32 devices in a mesh: seq: 8 (over y, x, core), fsdp: 4 (over z).
Axes of the slice: x: 2, y: 2, z: 4, core: 2. Of those that a mesh axis runs over, the one named last changes fastest.
Arguments:
- hidden_in: bfloat16 [4, 1024, 1024], P('fsdp', 'seq'), may hold values from -6 to 6
- cotangent: bfloat16 [4, 1024, 1024], P('fsdp', 'seq'), may hold values from -6 to 6
- segment_ids: int32 [4, 1024], P('fsdp'), may hold values from 0 to 7, never falling along the last dimension, each value on 1 to 512 neighbouring positions
- projection: float32 [1024, 3072], P('fsdp'), may hold values from -0.1875 to 0.1875
- projection_bias: float32 [3072], P('fsdp'), may hold values from -4 to 4
- output_weight: float32 [1024, 1024], P('fsdp'), may hold values from -1 to 1
- output_bias: float32 [1024], P('fsdp'), may hold values from -4 to 4
- first_gain: float32 [1024], P('fsdp'), may hold values from 0.5 to 1.5
- first_shift: float32 [1024], P('fsdp'), may hold values from -4 to 4
- up_weight: float32 [1024, 4096], P('fsdp'), may hold values from -0.1875 to 0.1875
- up_bias: float32 [4096], P('fsdp'), may hold values from -4 to 4
- down_weight: float32 [4096, 1024], P('fsdp'), may hold values from -0.09375 to 0.09375
- down_bias: float32 [1024], P('fsdp'), may hold values from -4 to 4
- second_gain: float32 [1024], P('fsdp'), may hold values from 0.5 to 1.5
- second_shift: float32 [1024], P('fsdp'), may hold values from -4 to 4
Outputs:
- layer_output: bfloat16 [4, 1024, 1024], P('fsdp', 'seq')
- input_grad: bfloat16 [4, 1024, 1024], P('fsdp', 'seq')
- projection_grad: float32 [1024, 3072], P('fsdp')
- projection_bias_grad: float32 [3072], P('fsdp')
- output_weight_grad: float32 [1024, 1024], P('fsdp')
- output_bias_grad: float32 [1024], P('fsdp')
- first_gain_grad: float32 [1024], P('fsdp')
- first_shift_grad: float32 [1024], P('fsdp')
- up_weight_grad: float32 [1024, 4096], P('fsdp')
- up_bias_grad: float32 [4096], P('fsdp')
- down_weight_grad: float32 [4096, 1024], P('fsdp')
- down_bias_grad: float32 [1024], P('fsdp')
- second_gain_grad: float32 [1024], P('fsdp')
- second_shift_grad: float32 [1024], P('fsdp')
The draws below stay inside these ranges and needn't reach their ends.
Inputs may be any that keep to these rules, and one draw needn't show every extreme that they name: `segment_ids`: in each sequence the numbers never fall and run through 0 to 7; equal numbers mark one document of 1 to 512 tokens, and some document has exactly 512.
All inputs are finite; a program needn't handle non-finite values.
Results may differ from the reference program's by a relative error of at most 0.02.
Values may be sent and summed in bfloat16 or wider, within the bound.
A program may use at most 192 MiB of HBM per device.

```python
import math
import jax
import jax.numpy as jnp
import numpy as np
from jax import lax

D = 1024
HEADS = 16
HEAD_DIM = 64
FF = 4096
L = 1024
SEQS = 4
DOCS = 8
MOST = 512


def levels(own_key, shape, cuts, low, largest):
    level = 1.0
    for position, parts in cuts:
        heights = jax.random.uniform(jax.random.fold_in(jax.random.fold_in(own_key, 6), position), (parts,), jnp.float32, low / len(cuts), largest / len(cuts))
        level = level * jnp.repeat(jnp.exp(heights), shape[position] // parts).reshape((-1,) + (1,) * (len(shape) - 1 - position))
    return level


def split_up(amount, total, most, skew):
    weights = [(1 << 20) // math.isqrt(standing ** skew) + 1 for standing in range(2, amount + 1)]
    rest, counts = total - most - (amount - 1), [1] * (amount - 1)
    while rest > 0:
        movable = [i for i in range(amount - 1) if counts[i] < most]
        pool, left = sum([weights[i] for i in movable]), rest
        for i in movable:
            extra = min(most - counts[i], max(1, left * weights[i] // pool), rest)
            counts[i] = counts[i] + extra
            rest = rest - extra
    return np.array([most] + counts)


def uneven(stream_key, number_of, total, reach, slope):
    if number_of == 2:
        one = jax.random.randint(stream_key, (), max(1, total - reach), min(reach, total - 1) + 1)
        return jnp.stack([one, total - one])
    tallies = jnp.asarray(split_up(number_of, total, reach, slope), jnp.int32)
    pairs = (number_of - 1) // 2
    giver, receiver = tallies[1:1 + 2 * pairs:2], tallies[2:2 + 2 * pairs:2]
    margin = jnp.minimum(giver - 1, reach - receiver)
    passed = jax.random.randint(jax.random.fold_in(stream_key, 1), (pairs,), 0, 1 << 20) % (margin + 1)
    tallies = tallies.at[1:1 + 2 * pairs:2].set(giver - passed).at[2:2 + 2 * pairs:2].set(receiver + passed)
    return tallies[jax.random.permutation(jax.random.fold_in(stream_key, 2), number_of)]


def normal_values(own_key, shape, width, most, cuts=(), held_as=jnp.bfloat16):
    result = width * jax.random.normal(own_key, shape, jnp.float32)
    if cuts:
        result = result * levels(own_key, shape, cuts, -0.22, 0.18)
    return jnp.clip(result, -most, most).astype(held_as)


def setup_inputs(seed: int = 0) -> dict:
    streams_of = jax.random.split(jax.random.key(seed), 16)
    return {
        "hidden_in": normal_values(streams_of[0], (SEQS, L, D), 1.0, 6.0, ((0, 4), (1, 8))),
        "cotangent": normal_values(streams_of[1], (SEQS, L, D), 1.0, 6.0, ((0, 4), (1, 8))),
        "segment_ids": jax.vmap(lambda own: jnp.searchsorted(jnp.cumsum(uneven(own, DOCS, L, MOST, 2)), jnp.arange(L), side="right"))(jax.random.split(streams_of[2], SEQS)).reshape((SEQS, L)).astype(jnp.int32),
        "projection": normal_values(streams_of[3], (D, 3 * D), D ** -0.5, 0.1875, ((0, 4),), jnp.float32),
        "projection_bias": normal_values(streams_of[4], (3 * D,), 0.3, 4.0, ((0, 4),), jnp.float32),
        "output_weight": normal_values(streams_of[5], (D, D), (D // 32) ** -0.5, 1.0, ((0, 4),), jnp.float32),
        "output_bias": normal_values(streams_of[6], (D,), 0.3, 4.0, ((0, 4),), jnp.float32),
        "first_gain": jnp.clip(1.0 + 0.1 * jax.random.normal(streams_of[7], (D,), jnp.float32), 0.5, 1.5),
        "first_shift": normal_values(streams_of[8], (D,), 0.3, 4.0, ((0, 4),), jnp.float32),
        "up_weight": normal_values(streams_of[9], (D, FF), D ** -0.5, 0.1875, ((0, 4),), jnp.float32),
        "up_bias": normal_values(streams_of[10], (FF,), 0.3, 4.0, ((0, 4),), jnp.float32),
        "down_weight": normal_values(streams_of[11], (FF, D), FF ** -0.5, 0.09375, ((0, 4),), jnp.float32),
        "down_bias": normal_values(streams_of[12], (D,), 0.3, 4.0, ((0, 4),), jnp.float32),
        "second_gain": jnp.clip(1.0 + 0.1 * jax.random.normal(streams_of[13], (D,), jnp.float32), 0.5, 1.5),
        "second_shift": normal_values(streams_of[14], (D,), 0.3, 4.0, ((0, 4),), jnp.float32),
    }


highest = lax.Precision.HIGHEST
norm_epsilon = 1e-05

@jax.custom_vjp
def low(v):
    return lax.optimization_barrier(v.astype(jnp.bfloat16)).astype(jnp.float32)

@jax.custom_vjp
def low_back(v):
    return v

def low_keep(v):
    return (low(v), None)

def low_pass(kept, grad):
    return (grad,)

def back_keep(v):
    return (v, None)

def back_low(kept, grad):
    return (low(grad),)
low.defvjp(low_keep, low_pass)
low_back.defvjp(back_keep, back_low)

def matmul(left, right):
    return jnp.dot(left, right, precision=highest)

def rotary(values, positions):
    half = values.shape[-1] // 2
    channel = jnp.arange(half).astype(jnp.float32)
    inverse = 10000.0 ** (-2.0 * channel / values.shape[-1])
    angles = positions[:, None] * inverse[None, :]
    cosine = jnp.cos(angles)[:, None, :]
    sine = jnp.sin(angles)[:, None, :]
    first = values[..., :half]
    second = values[..., half:]
    return jnp.concatenate([first * cosine - second * sine, second * cosine + first * sine], axis=-1)

def layer_norm(values, gain, shift):
    centre = values - lax.optimization_barrier(jnp.mean(values, axis=-1, keepdims=True))
    variance = lax.optimization_barrier(jnp.mean(centre * centre, axis=-1, keepdims=True))
    return centre * lax.rsqrt(variance + norm_epsilon) * gain + shift

def attend(keys_all, values_all, segments, query_block, segment_block):
    scores = jnp.einsum('qhd,khd->hqk', query_block, keys_all, precision=highest) * HEAD_DIM ** (-0.5)
    allowed = segment_block[:, None] == segments[None, :]
    scores = low_back(jnp.where(allowed[None], scores, -1e+30))
    weights = low(jax.nn.softmax(scores, axis=-1))
    return jnp.einsum('hqk,khd->qhd', weights, values_all, precision=highest)

def forward(tokens, params, segments):
    projection, projection_bias, output_weight, output_bias, first_gain, first_shift, up_weight, up_bias, down_weight, down_bias, second_gain, second_shift = [low(item) for item in params]
    length = tokens.shape[0]
    projected = low_back(matmul(tokens, projection) + projection_bias)
    heads = projected.reshape(length, 3, HEADS, HEAD_DIM)
    positions = jnp.arange(length).astype(jnp.float32)
    queries = rotary(heads[:, 0], positions)
    keys = rotary(heads[:, 1], positions)
    stacked = low_back(low(jnp.stack([queries, keys, heads[:, 2]])))
    block = min(512, length)
    count = length // block
    checked = jax.checkpoint(attend)
    context = lax.map(lambda pieces: checked(stacked[1], stacked[2], segments, pieces[0], pieces[1]), (stacked[0].reshape(count, block, HEADS, HEAD_DIM), segments.reshape(count, block)))
    context = low_back(low(context.reshape(length, HEADS * HEAD_DIM)))
    attended = low_back(matmul(context, output_weight) + output_bias)
    normed_one = layer_norm(tokens + attended, first_gain, first_shift)
    lifted = low_back(matmul(low(normed_one), up_weight) + up_bias)
    activated = low(jax.nn.gelu(lifted, approximate=False))
    lowered = low_back(matmul(activated, down_weight) + down_bias)
    return layer_norm(normed_one + lowered, second_gain, second_shift)

def reference(hidden_in, cotangent, segment_ids, projection, projection_bias, output_weight, output_bias, first_gain, first_shift, up_weight, up_bias, down_weight, down_bias, second_gain, second_shift):
    params = (projection, projection_bias, output_weight, output_bias, first_gain, first_shift, up_weight, up_bias, down_weight, down_bias, second_gain, second_shift)
    inputs = hidden_in.astype(jnp.float32)
    targets = cotangent.astype(jnp.float32)

    def per_sequence(totals, pieces):
        tokens, target, segments = pieces
        output, pullback = jax.vjp(lambda first, second: forward(first, second, segments), tokens, params)
        token_grad, param_grads = pullback(target)
        totals = jax.tree.map(lambda left, right: left + right, totals, param_grads)
        return (totals, (output.astype(jnp.bfloat16), token_grad.astype(jnp.bfloat16)))
    start = jax.tree.map(jnp.zeros_like, params)
    totals, (outputs, token_grads) = lax.scan(per_sequence, start, (inputs, targets, segment_ids))
    return (outputs, token_grads, totals[0], totals[1], totals[2], totals[3], totals[4], totals[5], totals[6], totals[7], totals[8], totals[9], totals[10], totals[11])
```

```python
from functools import partial

import jax
import jax.numpy as jnp
import numpy as np
from types import SimpleNamespace
from jax import lax
from jax.experimental import pallas as pl
from jax.experimental.pallas import tpu as pltpu
from jax.sharding import PartitionSpec as P

HEADS = 16
HEAD_DIM = 64


norm_epsilon = 1e-05


def rotary(values, positions):
    half = values.shape[-1] // 2
    channel = jnp.arange(half).astype(jnp.float32)
    inverse = 10000.0 ** (-2.0 * channel / values.shape[-1])
    angles = positions[:, None] * inverse[None, :]
    cosine = jnp.cos(angles)[:, None, :]
    sine = jnp.sin(angles)[:, None, :]
    first = values[..., :half]
    second = values[..., half:]
    return jnp.concatenate(
        [first * cosine - second * sine, second * cosine + first * sine], axis=-1
    )


def rotary_back(grads, positions):
    unused, pullback = jax.vjp(lambda inner: rotary(inner, positions), grads)
    return pullback(grads)[0]


def norm_forward(values, gain, shift):
    centre = values - jnp.mean(values, axis=-1, keepdims=True)
    inverse_root = lax.rsqrt(jnp.mean(centre * centre, axis=-1, keepdims=True) + norm_epsilon)
    normal = centre * inverse_root
    return (normal * gain + shift, normal, inverse_root)


def norm_backward(incoming, normal, inverse_root, gain):
    gain_grad = jnp.sum(incoming * normal, axis=0)
    shift_grad = jnp.sum(incoming, axis=0)
    scaled = incoming * gain
    inner = (
        scaled
        - jnp.mean(scaled, axis=-1, keepdims=True)
        - normal * jnp.mean(scaled * normal, axis=-1, keepdims=True)
    )
    return (inner * inverse_root, gain_grad, shift_grad)


def shards(
    hidden_in,
    cotangent,
    segment_ids,
    projection,
    projection_bias,
    output_weight,
    output_bias,
    first_gain,
    first_shift,
    up_weight,
    up_bias,
    down_weight,
    down_bias,
    second_gain,
    second_shift,
):
    bf16 = jnp.bfloat16
    f32 = jnp.float32
    tokens = hidden_in[0]
    local_rows = tokens.shape[0]
    width = tokens.shape[1]
    seq_rank = lax.axis_index("seq")
    positions = (seq_rank * local_rows + jnp.arange(local_rows)).astype(f32)
    segments = segment_ids[0]
    scale = HEAD_DIM ** (-0.5)
    attention_full = (
        lax.all_gather(projection.astype(bf16), "fsdp", axis=0, tiled=True),
        lax.all_gather(projection_bias.astype(bf16), "fsdp", axis=0, tiled=True),
        lax.all_gather(output_weight.astype(bf16), "fsdp", axis=0, tiled=True),
        lax.all_gather(output_bias.astype(bf16), "fsdp", axis=0, tiled=True),
        lax.all_gather(first_gain.astype(bf16), "fsdp", axis=0, tiled=True),
        lax.all_gather(first_shift.astype(bf16), "fsdp", axis=0, tiled=True),
    )
    proj_weight = attention_full[0]
    projected = jnp.dot(tokens, proj_weight, preferred_element_type=f32) + attention_full[1].astype(
        f32
    )
    heads = projected.reshape(local_rows, 3, HEADS, HEAD_DIM)
    queries = rotary(heads[:, 0], positions)
    keys = rotary(heads[:, 1], positions)
    stacked = jnp.stack([queries, keys, heads[:, 2]]).astype(bf16)
    spread = lax.all_to_all(stacked, "seq", split_axis=2, concat_axis=1, tiled=True)
    query_all = spread[0]
    key_all = spread[1]
    value_all = spread[2]
    length = query_all.shape[0]
    local_heads = query_all.shape[1]
    block = min(512, length)
    count = length // block
    query_blocks = query_all.reshape(count, block, local_heads, HEAD_DIM)
    segment_blocks = segments.reshape(count, block)

    def scores_of(query_block, segment_block):
        raw = jnp.einsum("qhd,khd->hqk", query_block, key_all, preferred_element_type=f32) * scale
        allowed = segment_block[:, None] == segments[None, :]
        return jnp.where(allowed[None], raw, -1e30)

    def forward_block(pieces):
        query_block, segment_block = pieces
        scores = scores_of(query_block, segment_block)
        row_max = jnp.max(scores, axis=-1, keepdims=True)
        exponent = jnp.exp(scores - row_max)
        total = jnp.sum(exponent, axis=-1, keepdims=True)
        weights = exponent / total
        context = jnp.einsum(
            "hqk,khd->qhd", weights.astype(bf16), value_all, preferred_element_type=f32
        )
        return (context.astype(bf16), (row_max + jnp.log(total))[..., 0])

    context_blocks, log_totals = lax.map(forward_block, (query_blocks, segment_blocks))
    context_heads = context_blocks.reshape(length, local_heads, HEAD_DIM)
    context_tokens = lax.all_to_all(
        context_heads, "seq", split_axis=0, concat_axis=1, tiled=True
    ).reshape(local_rows, width)
    attended = jnp.dot(
        context_tokens, attention_full[2], preferred_element_type=f32
    ) + attention_full[3].astype(f32)
    gain_one = attention_full[4].astype(f32)
    normed_one, normal_one, inverse_one = norm_forward(
        tokens.astype(f32) + attended, gain_one, attention_full[5].astype(f32)
    )
    feed_full = (
        lax.all_gather(up_weight.astype(bf16), "fsdp", axis=0, tiled=True),
        lax.all_gather(up_bias.astype(bf16), "fsdp", axis=0, tiled=True),
        lax.all_gather(down_weight.astype(bf16), "fsdp", axis=0, tiled=True),
        lax.all_gather(down_bias.astype(bf16), "fsdp", axis=0, tiled=True),
        lax.all_gather(second_gain.astype(bf16), "fsdp", axis=0, tiled=True),
        lax.all_gather(second_shift.astype(bf16), "fsdp", axis=0, tiled=True),
    )
    normed_low = normed_one.astype(bf16)
    lifted = jnp.dot(normed_low, feed_full[0], preferred_element_type=f32) + feed_full[1].astype(
        f32
    )
    activated = jax.nn.gelu(lifted, approximate=False).astype(bf16)
    lowered = jnp.dot(activated, feed_full[2], preferred_element_type=f32) + feed_full[3].astype(
        f32
    )
    gain_two = feed_full[4].astype(f32)
    layer_out, normal_two, inverse_two = norm_forward(
        normed_one + lowered, gain_two, feed_full[5].astype(f32)
    )
    feed_back = (
        lax.all_gather(up_weight.astype(bf16), "fsdp", axis=0, tiled=True),
        lax.all_gather(up_bias.astype(bf16), "fsdp", axis=0, tiled=True),
        lax.all_gather(down_weight.astype(bf16), "fsdp", axis=0, tiled=True),
        lax.all_gather(down_bias.astype(bf16), "fsdp", axis=0, tiled=True),
        lax.all_gather(second_gain.astype(bf16), "fsdp", axis=0, tiled=True),
        lax.all_gather(second_shift.astype(bf16), "fsdp", axis=0, tiled=True),
    )
    attention_back = (
        lax.all_gather(projection.astype(bf16), "fsdp", axis=0, tiled=True),
        lax.all_gather(projection_bias.astype(bf16), "fsdp", axis=0, tiled=True),
        lax.all_gather(output_weight.astype(bf16), "fsdp", axis=0, tiled=True),
        lax.all_gather(output_bias.astype(bf16), "fsdp", axis=0, tiled=True),
        lax.all_gather(first_gain.astype(bf16), "fsdp", axis=0, tiled=True),
        lax.all_gather(first_shift.astype(bf16), "fsdp", axis=0, tiled=True),
    )
    grad_two, second_gain_grad, second_shift_grad = norm_backward(
        cotangent[0].astype(f32), normal_two, inverse_two, gain_two
    )
    lowered_grad = grad_two.astype(bf16)
    down_weight_grad = jnp.einsum("tf,td->fd", activated, lowered_grad, preferred_element_type=f32)
    down_bias_grad = jnp.sum(lowered_grad.astype(f32), axis=0)
    active_grad = jnp.einsum("td,fd->tf", lowered_grad, feed_back[2], preferred_element_type=f32)
    unused, gelu_pull = jax.vjp(partial(jax.nn.gelu, approximate=False), lifted)
    lifted_grad = gelu_pull(active_grad)[0].astype(bf16)
    up_weight_grad = jnp.einsum("td,tf->df", normed_low, lifted_grad, preferred_element_type=f32)
    up_bias_grad = jnp.sum(lifted_grad.astype(f32), axis=0)
    normed_grad = grad_two + jnp.einsum(
        "tf,df->td", lifted_grad, feed_back[0], preferred_element_type=f32
    )
    grad_one, first_gain_grad, first_shift_grad = norm_backward(
        normed_grad, normal_one, inverse_one, attention_back[4].astype(f32)
    )
    attended_grad = grad_one.astype(bf16)
    output_weight_grad = jnp.einsum(
        "tc,td->cd", context_tokens, attended_grad, preferred_element_type=f32
    )
    output_bias_grad = jnp.sum(attended_grad.astype(f32), axis=0)
    context_grad = jnp.einsum(
        "td,cd->tc", attended_grad, attention_back[2], preferred_element_type=f32
    ).astype(bf16)
    context_grad = context_grad.reshape(local_rows, HEADS, HEAD_DIM)
    context_grad_heads = lax.all_to_all(
        context_grad, "seq", split_axis=1, concat_axis=0, tiled=True
    )
    grad_blocks = context_grad_heads.reshape(count, block, local_heads, HEAD_DIM)

    def backward_block(carry, pieces):
        key_grad, value_grad = carry
        query_block, segment_block, grad_block, log_block = pieces
        scores = scores_of(query_block, segment_block)
        weights = jnp.exp(scores - log_block[..., None])
        value_grad = value_grad + jnp.einsum(
            "hqk,qhd->khd", weights.astype(bf16), grad_block, preferred_element_type=f32
        )
        weight_grad = jnp.einsum("qhd,khd->hqk", grad_block, value_all, preferred_element_type=f32)
        centre = jnp.sum(weights * weight_grad, axis=-1, keepdims=True)
        score_grad = (weights * (weight_grad - centre)).astype(bf16)
        query_grad = (
            jnp.einsum("hqk,khd->qhd", score_grad, key_all, preferred_element_type=f32) * scale
        )
        key_grad = (
            key_grad
            + jnp.einsum("hqk,qhd->khd", score_grad, query_block, preferred_element_type=f32)
            * scale
        )
        return ((key_grad, value_grad), query_grad)

    zeros_heads = jnp.zeros((length, local_heads, HEAD_DIM), f32)
    (key_grad, value_grad), query_grad = lax.scan(
        backward_block,
        (zeros_heads, zeros_heads),
        (query_blocks, segment_blocks, grad_blocks, log_totals),
    )
    query_grad = query_grad.reshape(length, local_heads, HEAD_DIM)
    stacked_grad = jnp.stack([query_grad, key_grad, value_grad]).astype(bf16)
    token_heads = lax.all_to_all(stacked_grad, "seq", split_axis=1, concat_axis=2, tiled=True)
    query_back = rotary_back(token_heads[0].astype(f32), positions)
    key_back = rotary_back(token_heads[1].astype(f32), positions)
    projected_grad = jnp.stack([query_back, key_back, token_heads[2].astype(f32)], axis=1)
    projected_grad = projected_grad.reshape(local_rows, 3 * width).astype(bf16)
    projection_grad = jnp.einsum("td,te->de", tokens, projected_grad, preferred_element_type=f32)
    projection_bias_grad = jnp.sum(projected_grad.astype(f32), axis=0)
    input_grad = grad_one + jnp.einsum(
        "te,de->td", projected_grad, attention_back[0], preferred_element_type=f32
    )
    every_shard = (
        lax.psum_scatter(
            projection_grad.astype(jnp.bfloat16), "fsdp", scatter_dimension=0, tiled=True
        ).astype(jnp.float32),
        lax.psum_scatter(
            projection_bias_grad.astype(jnp.bfloat16), "fsdp", scatter_dimension=0, tiled=True
        ).astype(jnp.float32),
        lax.psum_scatter(
            output_weight_grad.astype(jnp.bfloat16), "fsdp", scatter_dimension=0, tiled=True
        ).astype(jnp.float32),
        lax.psum_scatter(
            output_bias_grad.astype(jnp.bfloat16), "fsdp", scatter_dimension=0, tiled=True
        ).astype(jnp.float32),
        lax.psum_scatter(
            first_gain_grad.astype(jnp.bfloat16), "fsdp", scatter_dimension=0, tiled=True
        ).astype(jnp.float32),
        lax.psum_scatter(
            first_shift_grad.astype(jnp.bfloat16), "fsdp", scatter_dimension=0, tiled=True
        ).astype(jnp.float32),
        lax.psum_scatter(
            up_weight_grad.astype(jnp.bfloat16), "fsdp", scatter_dimension=0, tiled=True
        ).astype(jnp.float32),
        lax.psum_scatter(
            up_bias_grad.astype(jnp.bfloat16), "fsdp", scatter_dimension=0, tiled=True
        ).astype(jnp.float32),
        lax.psum_scatter(
            down_weight_grad.astype(jnp.bfloat16), "fsdp", scatter_dimension=0, tiled=True
        ).astype(jnp.float32),
        lax.psum_scatter(
            down_bias_grad.astype(jnp.bfloat16), "fsdp", scatter_dimension=0, tiled=True
        ).astype(jnp.float32),
        lax.psum_scatter(
            second_gain_grad.astype(jnp.bfloat16), "fsdp", scatter_dimension=0, tiled=True
        ).astype(jnp.float32),
        lax.psum_scatter(
            second_shift_grad.astype(jnp.bfloat16), "fsdp", scatter_dimension=0, tiled=True
        ).astype(jnp.float32),
    )
    finals = (
        lax.psum(every_shard[0].astype(jnp.bfloat16), "seq").astype(jnp.float32),
        lax.psum(every_shard[1].astype(jnp.bfloat16), "seq").astype(jnp.float32),
        lax.psum(every_shard[2].astype(jnp.bfloat16), "seq").astype(jnp.float32),
        lax.psum(every_shard[3].astype(jnp.bfloat16), "seq").astype(jnp.float32),
        lax.psum(every_shard[4].astype(jnp.bfloat16), "seq").astype(jnp.float32),
        lax.psum(every_shard[5].astype(jnp.bfloat16), "seq").astype(jnp.float32),
        lax.psum(every_shard[6].astype(jnp.bfloat16), "seq").astype(jnp.float32),
        lax.psum(every_shard[7].astype(jnp.bfloat16), "seq").astype(jnp.float32),
        lax.psum(every_shard[8].astype(jnp.bfloat16), "seq").astype(jnp.float32),
        lax.psum(every_shard[9].astype(jnp.bfloat16), "seq").astype(jnp.float32),
        lax.psum(every_shard[10].astype(jnp.bfloat16), "seq").astype(jnp.float32),
        lax.psum(every_shard[11].astype(jnp.bfloat16), "seq").astype(jnp.float32),
    )
    return (
        layer_out.astype(bf16)[None],
        input_grad.astype(bf16)[None],
        finals[0],
        finals[1],
        finals[2],
        finals[3],
        finals[4],
        finals[5],
        finals[6],
        finals[7],
        finals[8],
        finals[9],
        finals[10],
        finals[11],
    )


MESH = pl.DeviceIdType.MESH
NN = (((1,), (0,)), ((), ()))
NT = (((1,), (1,)), ((), ()))
TN = (((0,), (0,)), ((), ()))
f32 = jnp.float32
bf16 = jnp.bfloat16
MASKED = -1e30


def mm(left, right, dims=NN):
    return lax.dot_general(left, right, dims, preferred_element_type=f32)


def block_of(index, size):
    return pl.ds(pl.multiple_of(index * size, size), size)


def flip(bit, other):
    return bit + other - 2 * bit * other


def fused_layer(sizes, *refs):
    r = SimpleNamespace(**dict(zip(sizes.names, refs)))
    T, D, L, F = sizes.T, sizes.D, sizes.L, sizes.F
    S, Z = 8, 4
    KW = D // Z
    UZ = F // Z
    C = 128
    T2 = 2 * T
    first_row = sizes.first_row
    ssem, rsem, lsem = r.ssem, r.rsem, r.lsem

    s = lax.axis_index("seq")
    z = lax.axis_index("fsdp")
    core, xbit, ybit = s % 2, (s // 2) % 2, s // 4
    zlow, zhigh = z % 2, z // 2

    def ps(k):
        return flip(core, k % 2) + 2 * flip(xbit, (k // 2) % 2) + 4 * flip(ybit, k // 4)

    def pz(k):
        return flip(zlow, k % 2) + 2 * flip(zhigh, k // 2)

    def chip_of(j):
        return flip(xbit, j % 2) + 2 * flip(ybit, j // 2)

    counter = [0, 0]
    pending = []

    def slots(n):
        counter[0] += n
        return counter[0] - n

    def remote(src, dst, slot, dev):
        return pltpu.make_async_remote_copy(
            src_ref=src, dst_ref=dst, send_sem=ssem.at[slot], recv_sem=rsem.at[slot],
            device_id=dev, device_id_type=MESH)

    def send(src, dst, slot, dev):
        copy = remote(src, dst, slot, dev)
        copy.start()
        pending.append(copy)
        return copy

    def drop(copies):
        for copy in copies:
            copy.wait_send()
        pending[:] = [other for other in pending if all(other is not copy for copy in copies)]

    def arrived(ref, slot):
        remote(ref, ref, slot, (ps(1), z)).wait_recv()

    def local(src, dst):
        copy = pltpu.make_async_copy(src, dst, lsem.at[counter[1]])
        counter[1] += 1
        copy.start()
        return copy

    class Gather:
        def __init__(self, place):
            self.place, self.base = place, slots(8)

        def start(self, src=None):
            mine = self.place(s)
            for k in (1, 2, 4, 6):
                send(mine if src is None else src, mine, self.base + k, (ps(k), z))

        def pass_on(self, k):
            there = self.place(ps(k))
            arrived(there, self.base + k)
            send(there, there, self.base + k + 1, (ps(1), z))

        def wait(self, k):
            arrived(self.place(ps(k)), self.base + k)

    class Spread:
        def __init__(self, place):
            self.place, self.base = place, slots(4)

        def start(self):
            mine = self.place(z)
            for k in (2, 1):
                send(mine, mine, self.base + k, (s, pz(k)))

        def pass_on(self):
            there = self.place(pz(2))
            arrived(there, self.base + 2)
            send(there, there, self.base + 3, (s, pz(1)))

        def wait(self):
            for k in (1, 3):
                arrived(self.place(pz(k)), self.base + k)

    class Fold:
        def __init__(self, parts, landing, passing):
            self.parts, self.landing, self.passing, self.base = parts, landing, passing, slots(3)

        def start(self):
            send(self.parts.at[pz(1)], self.landing.at[0], self.base, (s, pz(1)))
            send(self.parts.at[pz(3)], self.landing.at[1], self.base + 1, (s, pz(1)))

        def middle(self):
            arrived(self.landing.at[1], self.base + 1)
            self.passing[...] = (self.parts[pz(2)].astype(f32) + self.landing[1].astype(f32)).astype(bf16)
            send(self.passing, self.landing.at[2], self.base + 2, (s, pz(2)))

        def finish(self):
            arrived(self.landing.at[0], self.base)
            arrived(self.landing.at[2], self.base + 2)
            return (self.parts[z].astype(f32) + self.landing[0].astype(f32)
                    + self.landing[2].astype(f32)).astype(bf16)

    class Scatter:
        def __init__(self, parts, low, mid, high):
            self.parts, self.low, self.mid, self.high, self.base = parts, low, mid, high, slots(8)
            self.sent = []

        def pair(self, j):
            self.sent.append(send(self.parts.at[j, block_of(1 - core, T)], self.low.at[j],
                                  self.base + j, (ps(1), z)))

        def onward(self, j):
            arrived(self.low.at[j], self.base + j)
            own = self.parts[j, block_of(core, T), :].astype(f32)
            self.mid[j] = (own + self.low[j].astype(f32)).astype(bf16)
            self.sent.append(send(self.mid.at[j], self.high.at[j], self.base + 4 + j, (ps(2 * j), z)))

        def ready(self):
            arrived(self.low.at[0], self.base)
            for j in (1, 2, 3):
                arrived(self.high.at[j], self.base + 4 + j)

        def rows(self, at, n):
            own = self.parts[0, pl.ds(pl.multiple_of(core * T + at, n), n), :].astype(f32)
            total = own + self.low[0, pl.ds(at, n), :].astype(f32)
            for j in (1, 2, 3):
                total = total + self.high[j, pl.ds(at, n), :].astype(f32)
            return total

    def loop(count, body, unroll=1):
        def step(i, carry):
            body(i)
            return carry
        lax.fori_loop(0, count, step, 0, unroll=unroll)

    def at(i, n):
        return pl.multiple_of(i * n, n)

    vec, vecg = r.vec, r.vecg

    OUTPUT_BIAS, FIRST_GAIN, FIRST_SHIFT, DOWN_BIAS, SECOND_GAIN, SECOND_SHIFT, PROJECTION_BIAS, UP_BIAS = range(8)
    wide = ((first_row.output_bias, OUTPUT_BIAS), (first_row.first_gain, FIRST_GAIN),
            (first_row.first_shift, FIRST_SHIFT), (first_row.down_bias, DOWN_BIAS),
            (first_row.second_gain, SECOND_GAIN), (first_row.second_shift, SECOND_SHIFT))

    def row(i, width=D):
        return vec[i:i + 1, :width]

    lanes = lax.broadcasted_iota(jnp.int32, (T, C), 1)
    low_head = lanes < HEAD_DIM
    low_half = lanes % HEAD_DIM < HEAD_DIM // 2

    def swapped(w):
        return jnp.where(low_half, pltpu.roll(w, C - HEAD_DIM // 2, 1), pltpu.roll(w, HEAD_DIM // 2, 1))

    def stacked(w):
        nothing = jnp.zeros_like(w)
        return jnp.concatenate([jnp.where(low_head, w, nothing), jnp.where(low_head, nothing, w)], axis=0)

    def unstacked(w):
        return jnp.where(low_head, w[:T], w[T:])

    proj_loads = [local(r.proj.at[:, block_of(i * (D // C) + s, C)], r.st_proj.at[:, pl.ds(i * C, C)])
                  for i in range(3)]
    wo_load = local(r.wo.at[:, block_of(s, C)], r.st_wo)
    up_loads = [local(r.up.at[:, block_of(i * (D // C) + s, C)], r.st_up.at[:, pl.ds(i * C, C)])
                for i in range(Z)]
    dn_load = local(r.dn.at[block_of(s, UZ), :], r.st_dn)

    barrier = pltpu.get_barrier_semaphore()
    for k in range(1, S):
        pl.semaphore_signal(barrier, inc=1, device_id=(ps(k), z), device_id_type=MESH)
    for k in range(1, Z):
        pl.semaphore_signal(barrier, inc=1, device_id=(s, pz(k)), device_id_type=MESH)
    pl.semaphore_wait(barrier, S + Z - 2)

    x_ref, x_all = r.x, r.x_all
    w_qkv, w_o, w_up, w_dn = r.w_qkv, r.w_o, r.w_up, r.w_dn
    gather_x = Gather(lambda o: x_all.at[block_of(o, T)])
    gather_x.start(x_ref)
    spread_qkv = Spread(lambda p: w_qkv.at[block_of(p, KW)])
    spread_o = Spread(lambda p: w_o.at[block_of(p, KW), block_of(s, C)])
    spread_up = Spread(lambda p: w_up.at[block_of(p, KW)])
    spread_dn = Spread(lambda p: w_dn.at[block_of(p, UZ)])
    gather_o = Gather(lambda o: w_o.at[:, block_of(o, C)])

    for copy in proj_loads:
        copy.wait()
    w_qkv[block_of(z, KW), :] = r.st_proj[...].astype(bf16)
    spread_qkv.start()

    small_all = r.small_all
    small_base = slots(4)
    small_all[z] = r.small[...]
    for k in (1, 2, 3):
        send(r.small, small_all.at[z], small_base + k, (s, pz(k)))

    x_all[block_of(s, T), :] = x_ref[...]
    wo_load.wait()
    w_o[block_of(z, KW), block_of(s, C)] = r.st_wo[...].astype(bf16)
    spread_o.start()
    for copy in up_loads:
        copy.wait()
    w_up[block_of(z, KW), :] = r.st_up[...].astype(bf16)
    dn_load.wait()
    w_dn[block_of(z, UZ), :] = r.st_dn[...].astype(bf16)
    for i in range(8):
        vecg[i:i + 1, :] = jnp.zeros((1, D), f32)

    spread_qkv.pass_on()
    gather_x.pass_on(2)
    gather_x.pass_on(4)
    spread_o.pass_on()
    spread_up.start()
    gather_x.pass_on(6)
    for k in (1, 2, 3):
        arrived(small_all.at[pz(k)], small_base + k)
    for p in range(Z):
        for start, i in wide:
            for half in range(KW // C):
                at_row = start + half
                lane = (p * (KW // C) + half) * C
                vec[i:i + 1, lane:lane + C] = small_all[p, at_row:at_row + 1, :]
        vec[7:8, p * C:(p + 1) * C] = small_all[p, pl.ds(first_row.up_bias + s, 1), :]
    per = 3 * D // (C * Z)
    for t in range(3):
        number = t * (D // C) + s
        vec[6:7, t * C:(t + 1) * C] = small_all[number // per, pl.ds(first_row.projection_bias + number % per, 1), :]
    for k in (1, 3, 5, 7):
        gather_x.wait(k)

    x_t = r.x_t
    spread_qkv.wait()
    spread_o.wait()
    gather_o.start()
    q_ref, k_ref, v_ref = r.q, r.k, r.v
    scale = HEAD_DIM ** -0.5

    def project(i):
        here = pl.ds(at(i, T), T)
        out = mm(x_all[here, :], w_qkv[...]) + row(PROJECTION_BIAS, 3 * C)
        cosine, sine = r.cos[here, :], r.sin[here, :]
        q0, k0 = out[:, :C], out[:, C:2 * C]
        q_ref[here, :] = ((q0 * cosine + swapped(q0) * sine).astype(bf16).astype(f32) * scale).astype(bf16)
        k_ref[here, :] = (k0 * cosine + swapped(k0) * sine).astype(bf16)
        v_ref[here, :] = out[:, 2 * C:].astype(bf16)
    loop(L // T, project)

    s_buf, p_buf, col_a, col_b = r.s_buf, r.p_buf, r.col_a, r.col_b
    segr, segc = r.segr, r.segc
    lse, c_f, c_heads, c_tok = r.lse, r.c_f, r.c_heads, r.c_tok
    R = 16

    def attend(o):
        here = block_of(o, T)
        s_buf[...] = mm(stacked(q_ref[here, :]), k_ref[...], NT)

        def chunk(i):
            rows = pl.ds(at(i, R), R)
            same = segc[pl.ds(pl.multiple_of(o * T + (i % (T // R)) * R, R), R), :] == segr[...]
            score = jnp.where(same, s_buf[rows, :], MASKED)
            top = jnp.max(score, axis=-1, keepdims=True)
            power = jnp.exp(score - top)
            total = jnp.sum(power, axis=-1, keepdims=True)
            p_buf[rows, :] = power.astype(bf16)
            col_a[rows, :] = jnp.broadcast_to(1.0 / total, (R, C))
            col_b[rows, :] = jnp.broadcast_to(top + jnp.log(total), (R, C))
        loop(T2 // R, chunk)
        context = unstacked(mm(p_buf[...], v_ref[...]) * col_a[...])
        c_f[here, :] = context
        c_heads[here, :] = context.astype(bf16)
        for h in range(2):
            lse[h:h + 1, here] = jnp.transpose(col_b[h * T:(h + 1) * T, :])[0:1, :]

    c_base = slots(8)

    def c_copy(k):
        return remote(c_heads.at[block_of(ps(k), T)], c_tok.at[:, block_of(s, C)], c_base + k, (ps(k), z))

    def attend_and_send(i):
        k = 7 - i
        attend(ps(k))
        c_copy(k).start()

    loop(3, attend_and_send)
    spread_up.pass_on()
    spread_dn.start()
    loop(2, lambda i: attend_and_send(i + 3))
    gather_o.pass_on(2)
    gather_o.pass_on(4)
    loop(2, lambda i: attend_and_send(i + 5))
    attend(s)
    gather_o.pass_on(6)
    c_tok[:, block_of(s, C)] = c_heads[block_of(s, T), :]
    for k in (1, 3, 5, 7):
        gather_o.wait(k)
    for k in range(1, 8):
        arrived(c_tok.at[:, block_of(ps(k), C)], c_base + k)

    a_buf = r.a_buf
    a_buf[...] = mm(c_tok[...], w_o[...])
    n1, y1, r1, y_all = r.n1, r.y1, r.r1, r.y_all

    def norm(h):
        centre = h - jnp.mean(h, axis=-1, keepdims=True)
        root = lax.rsqrt(jnp.mean(centre * centre, axis=-1, keepdims=True) + norm_epsilon)
        return centre * root, root

    def first_norm(i):
        rows = pl.ds(at(i, R), R)
        normal, root = norm(x_ref[rows, :].astype(f32) + a_buf[rows, :] + row(OUTPUT_BIAS))
        out = normal * row(FIRST_GAIN) + row(FIRST_SHIFT)
        n1[rows, :] = normal
        r1[rows, :] = jnp.broadcast_to(root, (R, C))
        y1[rows, :] = out
        y_all[pl.ds(pl.multiple_of(s * T + i * R, R), R), :] = out.astype(bf16)
    loop(T // R, first_norm)
    gather_y = Gather(lambda o: y_all.at[block_of(o, T)])
    gather_y.start()

    u_buf, g_ref, d_ref, du_ref, dz_all = r.u_buf, r.g, r.d, r.du, r.dz_all
    parts, mid = r.parts, r.mid
    spread_dn.pass_on()
    spread_up.wait()
    E = 32

    def lift(j):
        q = chip_of(j)
        u_buf[...] = mm(y_all[block_of(q, T2), :], w_up[...])

        def chunk(i):
            rows = pl.ds(at(i, E), E)
            there = pl.ds(pl.multiple_of(q * T2 + i * E, E), E)
            u = u_buf[rows, :] + row(UP_BIAS, F)
            share = 0.5 + 0.5 * lax.erf(u * (0.5 ** 0.5))
            g_ref[there, :] = (u * share).astype(bf16)
            d_ref[there, :] = share + u * (jnp.exp(-0.5 * u * u) * 0.3989422804014327)
        loop(T2 // E, chunk)

    def lower(j):
        parts[j] = mm(g_ref[block_of(chip_of(j), T2), :], w_dn[...]).astype(bf16)

    fold_z = Scatter(parts, r.low0, mid, r.high0)
    gather_y.wait(1)
    lift(0)
    spread_dn.wait()
    lower(0)
    fold_z.pair(0)
    gather_y.pass_on(2)
    gather_y.pass_on(4)
    gather_y.wait(3)
    lift(1)
    lower(1)
    fold_z.pair(1)
    gather_y.wait(5)
    lift(2)
    fold_z.onward(1)
    lower(2)
    fold_z.pair(2)
    gather_y.pass_on(6)
    gather_y.wait(7)
    lift(3)
    fold_z.onward(2)
    lower(3)
    fold_z.pair(3)
    fold_z.onward(3)
    y_t, g_t = r.y_t, r.g_t

    def turn(src, dst, wide):
        def one(i):
            dst[:, pl.ds(at(i, T), T)] = jnp.transpose(src[pl.ds(at(i, T), T), :])
        loop(L // T, one)
    turn(g_ref, g_t, F)
    fold_z.ready()

    dh2, out_ref, ct_ref = r.dh2, r.out, r.ct

    def add_row(i, value):
        vecg[i:i + 1, :] = vecg[i:i + 1, :] + jnp.sum(value, axis=0, keepdims=True)

    def norm_back(incoming, normal, root, gain):
        scaled = incoming * gain
        return root * (scaled - jnp.mean(scaled, axis=-1, keepdims=True)
                       - normal * jnp.mean(scaled * normal, axis=-1, keepdims=True))

    def second_norm(i):
        start = at(i, R)
        rows = pl.ds(start, R)
        normal, root = norm(y1[rows, :] + fold_z.rows(start, R) + row(DOWN_BIAS))
        out_ref[rows, :] = (normal * row(SECOND_GAIN) + row(SECOND_SHIFT)).astype(bf16)
        e = ct_ref[rows, :].astype(f32)
        grad = norm_back(e, normal, root, row(SECOND_GAIN))
        dh2[rows, :] = grad
        dz = grad.astype(bf16)
        dz_all[pl.ds(pl.multiple_of(s * T + i * R, R), R), :] = dz
        add_row(3, dz.astype(f32))
        add_row(4, e * normal)
        add_row(5, e)
    loop(T // R, second_norm)
    gather_dz = Gather(lambda o: dz_all.at[block_of(o, T)])
    gather_dz.start()
    drop(fold_z.sent)

    colg = r.colg
    colg[...] = jnp.zeros((8, F), f32)

    def unlower(j):
        q = chip_of(j)
        u_buf[...] = mm(dz_all[block_of(q, T2), :], w_dn[...], NT)

        def chunk(i):
            rows = pl.ds(at(i, E), E)
            there = pl.ds(pl.multiple_of(q * T2 + i * E, E), E)
            du = (u_buf[rows, :] * d_ref[there, :]).astype(bf16)
            du_ref[there, :] = du
            colg[0:1, :] = colg[0:1, :] + jnp.sum(du.astype(f32), axis=0, keepdims=True)
        loop(T2 // E, chunk)

    def unlift(j):
        parts[j] = mm(du_ref[block_of(chip_of(j), T2), :], w_up[...], NT).astype(bf16)

    fold_y = Scatter(parts, r.low1, mid, r.high1)
    turn(y_all, y_t, D)
    gather_dz.wait(1)
    unlower(0)
    unlift(0)
    fold_y.pair(0)
    gather_dz.pass_on(2)
    gather_dz.pass_on(4)
    gather_dz.wait(3)
    unlower(1)
    unlift(1)
    fold_y.pair(1)
    gather_dz.wait(5)
    unlower(2)
    fold_y.onward(1)
    unlift(2)
    fold_y.pair(2)
    gather_dz.pass_on(6)
    gather_dz.wait(7)
    unlower(3)
    fold_y.onward(2)
    unlift(3)
    fold_y.pair(3)
    fold_y.onward(3)

    gd_part, gu_part = r.gd_part, r.gu_part

    def down_grad(i):
        gd_part[i] = mm(g_t[pl.ds(at(i, UZ), UZ), :], dz_all[...]).astype(bf16)
    loop(Z, down_grad)
    fold_dn = Fold(gd_part, r.gd_land, r.gd_pass)
    fold_dn.start()

    def up_grad(i):
        gu_part[i] = mm(y_t[pl.ds(at(i, KW), KW), :], du_ref[...]).astype(bf16)
    loop(Z, up_grad)
    fold_up = Fold(gu_part, r.gu_land, r.gu_pass)
    fold_up.start()
    fold_y.ready()

    dh1, da = r.dh1, r.da

    def first_back(i):
        start = at(i, R)
        rows = pl.ds(start, R)
        incoming = dh2[rows, :] + fold_y.rows(start, R)
        normal = n1[rows, :]
        grad = norm_back(incoming, normal, r1[rows, 0:1], row(FIRST_GAIN))
        dh1[rows, :] = grad
        low = grad.astype(bf16)
        da[rows, :] = low
        add_row(0, low.astype(f32))
        add_row(1, incoming * normal)
        add_row(2, incoming)
    loop(T // R, first_back)
    drop(fold_y.sent)

    dc_tok, dc = r.dc_tok, r.dc
    dc_tok[...] = mm(da[...], w_o[...], NT).astype(bf16)
    dc_base = slots(8)
    for k in (7, 6, 5, 4, 3, 2, 1):
        send(dc_tok.at[:, block_of(ps(k), C)], dc.at[block_of(s, T)], dc_base + k, (ps(k), z))
    dc[block_of(s, T), :] = dc_tok[:, block_of(s, C)]
    da_cols = r.da_cols
    da_base = slots(8)
    for k in (7, 6, 5, 4, 3, 2, 1):
        send(da.at[:, block_of(ps(k), C)], da_cols.at[block_of(s, T)], da_base + k, (ps(k), z))
    da_cols[block_of(s, T), :] = da[:, block_of(s, C)]
    vec_all = r.vec_all
    vec_base = slots(8)
    for k in (7, 6, 5, 4, 3, 2, 1):
        send(vecg, vec_all.at[s], vec_base + k, (ps(k), z))
    c_all = r.c_all
    c_all[block_of(s, T), :] = c_tok[...]
    gather_c = Gather(lambda o: c_all.at[block_of(o, T)])
    gather_c.start(c_tok)
    turn(x_all, x_t, D)
    for k in range(1, 8):
        arrived(dc.at[block_of(ps(k), T)], dc_base + k)

    delta, dp_buf, ds_buf, dq, dproj = r.delta, r.dp_buf, r.ds_buf, r.dq, r.dproj

    def deltas(i):
        here = pl.ds(at(i, T), T)
        turned = jnp.transpose(dc[here, :].astype(f32) * c_f[here, :])
        delta[0:1, here] = jnp.sum(turned[:HEAD_DIM], axis=0, keepdims=True)
        delta[1:2, here] = jnp.sum(turned[HEAD_DIM:], axis=0, keepdims=True)
        dq[here, :] = jnp.zeros((T, C), f32)
    loop(L // T, deltas)

    def attend_back(i):
        here = pl.ds(at(i, T), T)
        keys = stacked(k_ref[here, :])
        s_buf[...] = mm(keys, q_ref[...], NT)
        dp_buf[...] = mm(stacked(v_ref[here, :]), dc[...], NT)

        def chunk(n):
            rows = pl.ds(at(n, R), R)
            head = n // (T // R)
            same = segc[pl.ds(pl.multiple_of(i * T + (n % (T // R)) * R, R), R), :] == segr[...]
            weight = jnp.exp(jnp.where(same, s_buf[rows, :], MASKED) - lse[pl.ds(head, 1), :])
            p_buf[rows, :] = weight.astype(bf16)
            ds_buf[rows, :] = (weight * (dp_buf[rows, :] - delta[pl.ds(head, 1), :])).astype(bf16)
        loop(T2 // R, chunk)
        dv = unstacked(mm(p_buf[...], dc[...])).astype(bf16)
        dk = unstacked(mm(ds_buf[...], q_ref[...])).astype(bf16).astype(f32)
        dproj[here, 2 * C:] = dv
        dproj[here, C:2 * C] = (dk * r.cos[here, :] - swapped(dk) * r.sin[here, :]).astype(bf16)
        dq[...] = dq[...] + mm(ds_buf[...], keys, TN)

    go_part = r.go_part
    loop(3, attend_back)
    fold_dn.middle()
    gather_c.pass_on(2)
    gather_c.pass_on(4)
    loop(2, lambda i: attend_back(i + 3))
    fold_up.middle()
    gather_c.pass_on(6)
    gd_all, gu_all, go_all, gq_all = r.gd_all, r.gu_all, r.go_all, r.gq_all
    gather_gd = Gather(lambda o: gd_all.at[block_of(o, UZ)])
    gather_gu = Gather(lambda o: gu_all.at[o])
    gather_go = Gather(lambda o: go_all.at[:, block_of(o, C)])
    gather_gq = Gather(lambda o: gq_all.at[o])
    gd_all[block_of(s, UZ), :] = fold_dn.finish()
    gather_gd.start()
    for k in (1, 3, 5, 7):
        gather_c.wait(k)
    for k in range(1, 8):
        arrived(da_cols.at[block_of(ps(k), T)], da_base + k)

    def out_grad(i):
        go_part[i] = mm(c_all[:, pl.ds(at(i, KW), KW)], da_cols[...], TN).astype(bf16)
    loop(Z, out_grad)
    fold_o = Fold(go_part, r.go_land, r.go_pass)
    fold_o.start()
    vec_all[s] = vecg[...]
    for k in range(1, 8):
        arrived(vec_all.at[ps(k)], vec_base + k)
    vec_plane, vec_z = r.vec_plane, r.vec_z
    total = vec_all[0]
    for o in range(1, S):
        total = total + vec_all[o]
    vec_plane[...] = total
    vz_base = slots(4)
    for k in (1, 2, 3):
        send(vec_plane, vec_z.at[z], vz_base + k, (s, pz(k)))
    vec_z[z] = total
    loop(3, lambda i: attend_back(i + 5))

    def dq_rows(i):
        here = pl.ds(at(i, T), T)
        whole = (dq[here, :] * scale).astype(bf16).astype(f32)
        dproj[here, :C] = (whole * r.cos[here, :] - swapped(whole) * r.sin[here, :]).astype(bf16)
        colg[1:2, :3 * C] = colg[1:2, :3 * C] + jnp.sum(dproj[here, :].astype(f32), axis=0, keepdims=True)
    loop(L // T, dq_rows)

    gq_part = r.gq_part
    for k in (1, 3, 2, 0):
        gq_part[pz(k)] = mm(x_t[block_of(pz(k), KW), :], dproj[...]).astype(bf16)
        if k == 3:
            fold_qkv = Fold(gq_part, r.gq_land, r.gq_pass)
            fold_qkv.start()
    col_z = r.col_z
    cz_base = slots(4)
    for k in (1, 2, 3):
        send(colg, col_z.at[z], cz_base + k, (s, pz(k)))
    col_z[z] = colg[...]
    fold_x = Scatter(parts, r.low2, mid, r.high2)

    def unproject(j):
        parts[j] = mm(dproj[block_of(chip_of(j), T2), :], w_qkv[...], NT).astype(bf16)
        fold_x.pair(j)
    unproject(1)
    unproject(2)
    fold_x.onward(1)
    unproject(3)
    fold_x.onward(2)
    unproject(0)
    fold_x.onward(3)
    fold_o.middle()
    fold_qkv.middle()
    gu_all[s] = fold_up.finish()
    gather_gu.start()
    for k in (2, 4, 6):
        gather_gd.pass_on(k)
    go_all[:, block_of(s, C)] = fold_o.finish()
    gather_go.start()
    for k in (1, 2, 3):
        arrived(col_z.at[pz(k)], cz_base + k)
    col_all = r.col_all
    col_sum = r.col_sum
    col_sum[...] = col_z[0] + col_z[1] + col_z[2] + col_z[3]
    ca_base = slots(8)
    for k in range(1, 8):
        send(col_sum, col_all.at[s], ca_base + k, (ps(k), z))
    col_all[s] = col_sum[...]
    fold_x.ready()
    dx_ref = r.dx

    def input_back(i):
        start = at(i, R)
        rows = pl.ds(start, R)
        dx_ref[rows, :] = (dh1[rows, :] + fold_x.rows(start, R)).astype(bf16)
    loop(T // R, input_back)
    gq_all[s] = fold_qkv.finish()
    gather_gq.start()
    for k in (1, 3, 5, 7):
        gather_gd.wait(k)
    outs = [local(gd_all, r.gd)]
    for k in (2, 4, 6):
        gather_gu.pass_on(k)
    for k in (2, 4, 6):
        gather_go.pass_on(k)
    for k in (1, 3, 5, 7):
        gather_gu.wait(k)
    for o in range(S):
        for p in range(Z):
            lane = (p * S + o) * C
            outs.append(local(gu_all.at[o, :, pl.ds(p * C, C)], r.gu.at[:, pl.ds(lane, C)]))
    for k in (1, 3, 5, 7):
        gather_go.wait(k)
    outs.append(local(go_all, r.go))

    for k in (1, 2, 3):
        arrived(vec_z.at[pz(k)], vz_base + k)
    for k in range(1, 8):
        arrived(col_all.at[ps(k)], ca_base + k)
    vec_plane2 = r.vec_sum
    vec_plane2[...] = vec_z[0] + vec_z[1] + vec_z[2] + vec_z[3]
    gsm = r.gsm
    gsm[...] = jnp.zeros(gsm.shape, f32)
    for start, i in wide:
        for half in range(KW // C):
            at_row = start + half
            gsm[at_row:at_row + 1, :] = vec_plane2[i:i + 1, block_of(z * (KW // C) + half, C)]
    for o in range(S):
        at_row = first_row.up_bias + o
        gsm[at_row:at_row + 1, :] = col_all[o, 0:1, block_of(z, C)]
    for i in range(per):
        number = z * per + i
        at_row = first_row.projection_bias + i
        gsm[at_row:at_row + 1, :] = col_all[number % S, 1:2, block_of(number // S, C)]

    for k in (2, 4, 6):
        gather_gq.pass_on(k)
    for k in (1, 3, 5, 7):
        gather_gq.wait(k)
    for o in range(S):
        for t in range(3):
            lane = (t * S + o) * C
            outs.append(local(gq_all.at[o, :, pl.ds(t * C, C)], r.gq.at[:, pl.ds(lane, C)]))
    for copy in outs:
        copy.wait()
    for copy in pending:
        copy.wait_send()
    loop(7, lambda i: c_copy(7 - i).wait_send())


def fused_shards(*args):
    (hidden_in, cotangent, segment_ids, projection, projection_bias, output_weight, output_bias, first_gain,
     first_shift, up_weight, up_bias, down_weight, down_bias, second_gain, second_shift) = args
    T, D = hidden_in.shape[1:]
    L = segment_ids.shape[1]
    KW = projection.shape[0]
    F = up_weight.shape[1] // 8
    C, Z = 128, 4
    UZ = F // Z
    small = dict(projection_bias=projection_bias, output_bias=output_bias, first_gain=first_gain,
                 first_shift=first_shift, up_bias=up_bias, down_bias=down_bias, second_gain=second_gain,
                 second_shift=second_shift)
    starts, at_row = {}, 0
    for name, value in small.items():
        starts[name] = at_row
        at_row += value.shape[0] // C
    rows = -(-at_row // 8) * 8
    packed = jnp.concatenate(list(small.values())).astype(bf16).astype(f32).reshape(at_row, C)
    packed = jnp.pad(packed, ((0, rows - at_row), (0, 0)))

    half = HEAD_DIM // 2
    inverse = np.float32(10000.0) ** (np.float32(-2.0) * np.arange(half, dtype=np.float32) / np.float32(HEAD_DIM))
    angles = np.arange(L, dtype=np.float32)[:, None] * inverse.astype(np.float32)[None, :]
    cosine = np.tile(np.cos(angles), (1, C // half))
    sine = np.tile(np.concatenate([-np.sin(angles), np.sin(angles)], axis=1), (1, C // HEAD_DIM))

    inputs = dict(x=(hidden_in[0], 0), ct=(cotangent[0], 0), segr=(segment_ids, 0),
              segc=(segment_ids.reshape(L, 1), 0), cos=(jnp.asarray(cosine), 0), sin=(jnp.asarray(sine), 0),
              small=(packed, 0), proj=(projection, 1), wo=(output_weight, 1), up=(up_weight, 1),
              dn=(down_weight, 1))
    outputs = dict(out=((T, D), bf16, 0), dx=((T, D), bf16, 0), gsm=((rows, C), f32, 0),
               gq=(projection.shape, bf16, 1), go=(output_weight.shape, bf16, 1),
               gu=(up_weight.shape, bf16, 1), gd=(down_weight.shape, bf16, 1))
    PART = (4, T, D)
    scratch = dict(
        x_all=((L, D), bf16), x_t=((D, L), bf16), w_qkv=((D, 3 * C), bf16), st_proj=((KW, 3 * C), f32),
        w_o=((D, D), bf16), st_wo=((KW, C), f32), w_up=((D, F), bf16), st_up=((KW, F), f32),
        w_dn=((F, D), bf16), st_dn=((UZ, D), f32), small_all=((Z, rows, C), f32), vec=((8, D), f32),
        vecg=((8, D), f32), q=((L, C), bf16), k=((L, C), bf16), v=((L, C), bf16),
        s_buf=((2 * T, L), f32), dp_buf=((2 * T, L), f32), p_buf=((2 * T, L), bf16),
        ds_buf=((2 * T, L), bf16), col_a=((2 * T, C), f32), col_b=((2 * T, C), f32), lse=((8, L), f32),
        delta=((8, L), f32), c_f=((L, C), f32), c_heads=((L, C), bf16), c_tok=((T, D), bf16),
        a_buf=((T, D), f32), n1=((T, D), f32), y1=((T, D), f32), r1=((T, C), f32),
        y_all=((L, D), bf16), y_t=((D, L), bf16), u_buf=((2 * T, F), f32), g=((L, F), bf16),
        g_t=((F, L), bf16), d=((L, F), f32), du=((L, F), bf16), dz_all=((L, D), bf16),
        parts=((4, 2 * T, D), bf16), mid=((4, T, D), bf16), dh2=((T, D), f32), dh1=((T, D), f32),
        colg=((8, F), f32), gd_part=((Z, UZ, D), bf16), gd_land=((3, UZ, D), bf16), gd_pass=((UZ, D), bf16),
        gu_part=((Z, KW, F), bf16), gu_land=((3, KW, F), bf16), gu_pass=((KW, F), bf16),
        go_part=((Z, KW, C), bf16), go_land=((3, KW, C), bf16), go_pass=((KW, C), bf16),
        gq_part=((Z, KW, 3 * C), bf16), gq_land=((3, KW, 3 * C), bf16), gq_pass=((KW, 3 * C), bf16),
        gd_all=((8 * UZ, D), bf16), gu_all=((8, KW, F), bf16), go_all=((KW, D), bf16),
        gq_all=((8, KW, 3 * C), bf16), da=((T, D), bf16), dc_tok=((T, D), bf16), dc=((L, C), bf16),
        da_cols=((L, C), bf16), c_all=((L, D), bf16), dq=((L, C), f32), dproj=((L, 3 * C), bf16),
        vec_all=((8, 8, D), f32), vec_plane=((8, D), f32), vec_z=((Z, 8, D), f32), vec_sum=((8, D), f32),
        col_z=((Z, 8, F), f32), col_sum=((8, F), f32), col_all=((8, 8, F), f32),
        low0=(PART, bf16), high0=(PART, bf16), low1=(PART, bf16), high1=(PART, bf16), low2=(PART, bf16),
        high2=(PART, bf16), ssem=(SLOTS,), rsem=(SLOTS,), lsem=(LOCAL,))
    names = [*inputs, *outputs, *scratch]
    sizes = SimpleNamespace(names=names, T=T, D=D, L=L, F=F, first_row=SimpleNamespace(**starts))

    def spec(anywhere):
        return pl.BlockSpec(memory_space=pl.ANY if anywhere else pltpu.VMEM)
    results = pl.pallas_call(
        partial(fused_layer, sizes),
        out_shape=[jax.ShapeDtypeStruct(shape, dtype) for shape, dtype, _ in outputs.values()],
        in_specs=[spec(w) for _, w in inputs.values()],
        out_specs=[spec(w) for *_, w in outputs.values()],
        scratch_shapes=[pltpu.VMEM(*what) if len(what) == 2 else pltpu.SemaphoreType.DMA(what)
                        for what in scratch.values()],
        compiler_params=pltpu.CompilerParams(collective_id=0, has_side_effects=True, vmem_limit_bytes=67043328),
        name="fused_layer",
    )(*[value for value, _ in inputs.values()])
    out, dx, gsm, gq, go, gu, gd = results
    flat = gsm.reshape(-1)
    small_grads = [lax.slice(flat, (starts[name] * C,), (starts[name] * C + value.shape[0],))
                   for name, value in small.items()]
    pb, ob, g1, s1, ub, db, g2, s2 = small_grads
    return (out[None], dx[None], gq.astype(f32), pb, go.astype(f32), ob, g1, s1, gu.astype(f32), ub, gd.astype(f32),
            db, g2, s2)


SLOTS = 192
LOCAL = 80


def fits(mesh):
    return mesh.shape["seq"] == 8 and mesh.shape["fsdp"] == 4


def solution(mesh):
    return jax.shard_map(
        fused_shards if fits(mesh) else shards,
        mesh=mesh,
        in_specs=(
            P("fsdp", "seq", None),
            P("fsdp", "seq", None),
            P("fsdp", None),
            P("fsdp", None),
            P("fsdp"),
            P("fsdp", None),
            P("fsdp"),
            P("fsdp"),
            P("fsdp"),
            P("fsdp", None),
            P("fsdp"),
            P("fsdp", None),
            P("fsdp"),
            P("fsdp"),
            P("fsdp"),
        ),
        out_specs=(
            P("fsdp", "seq", None),
            P("fsdp", "seq", None),
            P("fsdp", None),
            P("fsdp"),
            P("fsdp", None),
            P("fsdp"),
            P("fsdp"),
            P("fsdp"),
            P("fsdp", None),
            P("fsdp"),
            P("fsdp", None),
            P("fsdp"),
            P("fsdp"),
            P("fsdp"),
        ),
        check_vma=False,
    )
```

```python
from functools import partial

import jax
import jax.numpy as jnp
import numpy as np
from types import SimpleNamespace
from jax import lax
from jax.experimental import pallas as pl
from jax.experimental.pallas import tpu as pltpu
from jax.sharding import PartitionSpec as P

HEADS = 16
HEAD_DIM = 64


norm_epsilon = 1e-05


def rotary(values, positions):
    half = values.shape[-1] // 2
    channel = jnp.arange(half).astype(jnp.float32)
    inverse = 10000.0 ** (-2.0 * channel / values.shape[-1])
    angles = positions[:, None] * inverse[None, :]
    cosine = jnp.cos(angles)[:, None, :]
    sine = jnp.sin(angles)[:, None, :]
    first = values[..., :half]
    second = values[..., half:]
    return jnp.concatenate(
        [first * cosine - second * sine, second * cosine + first * sine], axis=-1
    )


def rotary_back(grads, positions):
    unused, pullback = jax.vjp(lambda inner: rotary(inner, positions), grads)
    return pullback(grads)[0]


def norm_forward(values, gain, shift):
    centre = values - jnp.mean(values, axis=-1, keepdims=True)
    inverse_root = lax.rsqrt(jnp.mean(centre * centre, axis=-1, keepdims=True) + norm_epsilon)
    normal = centre * inverse_root
    return (normal * gain + shift, normal, inverse_root)


def norm_backward(incoming, normal, inverse_root, gain):
    gain_grad = jnp.sum(incoming * normal, axis=0)
    shift_grad = jnp.sum(incoming, axis=0)
    scaled = incoming * gain
    inner = (
        scaled
        - jnp.mean(scaled, axis=-1, keepdims=True)
        - normal * jnp.mean(scaled * normal, axis=-1, keepdims=True)
    )
    return (inner * inverse_root, gain_grad, shift_grad)


def shards(
    hidden_in,
    cotangent,
    segment_ids,
    projection,
    projection_bias,
    output_weight,
    output_bias,
    first_gain,
    first_shift,
    up_weight,
    up_bias,
    down_weight,
    down_bias,
    second_gain,
    second_shift,
):
    bf16 = jnp.bfloat16
    f32 = jnp.float32
    tokens = hidden_in[0]
    local_rows = tokens.shape[0]
    width = tokens.shape[1]
    seq_rank = lax.axis_index("seq")
    positions = (seq_rank * local_rows + jnp.arange(local_rows)).astype(f32)
    segments = segment_ids[0]
    scale = HEAD_DIM ** (-0.5)
    attention_full = (
        lax.all_gather(projection.astype(bf16), "fsdp", axis=0, tiled=True),
        lax.all_gather(projection_bias.astype(bf16), "fsdp", axis=0, tiled=True),
        lax.all_gather(output_weight.astype(bf16), "fsdp", axis=0, tiled=True),
        lax.all_gather(output_bias.astype(bf16), "fsdp", axis=0, tiled=True),
        lax.all_gather(first_gain.astype(bf16), "fsdp", axis=0, tiled=True),
        lax.all_gather(first_shift.astype(bf16), "fsdp", axis=0, tiled=True),
    )
    proj_weight = attention_full[0]
    projected = jnp.dot(tokens, proj_weight, preferred_element_type=f32) + attention_full[1].astype(
        f32
    )
    heads = projected.reshape(local_rows, 3, HEADS, HEAD_DIM)
    queries = rotary(heads[:, 0], positions)
    keys = rotary(heads[:, 1], positions)
    stacked = jnp.stack([queries, keys, heads[:, 2]]).astype(bf16)
    spread = lax.all_to_all(stacked, "seq", split_axis=2, concat_axis=1, tiled=True)
    query_all = spread[0]
    key_all = spread[1]
    value_all = spread[2]
    length = query_all.shape[0]
    local_heads = query_all.shape[1]
    block = min(512, length)
    count = length // block
    query_blocks = query_all.reshape(count, block, local_heads, HEAD_DIM)
    segment_blocks = segments.reshape(count, block)

    def scores_of(query_block, segment_block):
        raw = jnp.einsum("qhd,khd->hqk", query_block, key_all, preferred_element_type=f32) * scale
        allowed = segment_block[:, None] == segments[None, :]
        return jnp.where(allowed[None], raw, -1e30)

    def forward_block(pieces):
        query_block, segment_block = pieces
        scores = scores_of(query_block, segment_block)
        row_max = jnp.max(scores, axis=-1, keepdims=True)
        exponent = jnp.exp(scores - row_max)
        total = jnp.sum(exponent, axis=-1, keepdims=True)
        weights = exponent / total
        context = jnp.einsum(
            "hqk,khd->qhd", weights.astype(bf16), value_all, preferred_element_type=f32
        )
        return (context.astype(bf16), (row_max + jnp.log(total))[..., 0])

    context_blocks, log_totals = lax.map(forward_block, (query_blocks, segment_blocks))
    context_heads = context_blocks.reshape(length, local_heads, HEAD_DIM)
    context_tokens = lax.all_to_all(
        context_heads, "seq", split_axis=0, concat_axis=1, tiled=True
    ).reshape(local_rows, width)
    attended = jnp.dot(
        context_tokens, attention_full[2], preferred_element_type=f32
    ) + attention_full[3].astype(f32)
    gain_one = attention_full[4].astype(f32)
    normed_one, normal_one, inverse_one = norm_forward(
        tokens.astype(f32) + attended, gain_one, attention_full[5].astype(f32)
    )
    feed_full = (
        lax.all_gather(up_weight.astype(bf16), "fsdp", axis=0, tiled=True),
        lax.all_gather(up_bias.astype(bf16), "fsdp", axis=0, tiled=True),
        lax.all_gather(down_weight.astype(bf16), "fsdp", axis=0, tiled=True),
        lax.all_gather(down_bias.astype(bf16), "fsdp", axis=0, tiled=True),
        lax.all_gather(second_gain.astype(bf16), "fsdp", axis=0, tiled=True),
        lax.all_gather(second_shift.astype(bf16), "fsdp", axis=0, tiled=True),
    )
    normed_low = normed_one.astype(bf16)
    lifted = jnp.dot(normed_low, feed_full[0], preferred_element_type=f32) + feed_full[1].astype(
        f32
    )
    activated = jax.nn.gelu(lifted, approximate=False).astype(bf16)
    lowered = jnp.dot(activated, feed_full[2], preferred_element_type=f32) + feed_full[3].astype(
        f32
    )
    gain_two = feed_full[4].astype(f32)
    layer_out, normal_two, inverse_two = norm_forward(
        normed_one + lowered, gain_two, feed_full[5].astype(f32)
    )
    feed_back = (
        lax.all_gather(up_weight.astype(bf16), "fsdp", axis=0, tiled=True),
        lax.all_gather(up_bias.astype(bf16), "fsdp", axis=0, tiled=True),
        lax.all_gather(down_weight.astype(bf16), "fsdp", axis=0, tiled=True),
        lax.all_gather(down_bias.astype(bf16), "fsdp", axis=0, tiled=True),
        lax.all_gather(second_gain.astype(bf16), "fsdp", axis=0, tiled=True),
        lax.all_gather(second_shift.astype(bf16), "fsdp", axis=0, tiled=True),
    )
    attention_back = (
        lax.all_gather(projection.astype(bf16), "fsdp", axis=0, tiled=True),
        lax.all_gather(projection_bias.astype(bf16), "fsdp", axis=0, tiled=True),
        lax.all_gather(output_weight.astype(bf16), "fsdp", axis=0, tiled=True),
        lax.all_gather(output_bias.astype(bf16), "fsdp", axis=0, tiled=True),
        lax.all_gather(first_gain.astype(bf16), "fsdp", axis=0, tiled=True),
        lax.all_gather(first_shift.astype(bf16), "fsdp", axis=0, tiled=True),
    )
    grad_two, second_gain_grad, second_shift_grad = norm_backward(
        cotangent[0].astype(f32), normal_two, inverse_two, gain_two
    )
    lowered_grad = grad_two.astype(bf16)
    down_weight_grad = jnp.einsum("tf,td->fd", activated, lowered_grad, preferred_element_type=f32)
    down_bias_grad = jnp.sum(lowered_grad.astype(f32), axis=0)
    active_grad = jnp.einsum("td,fd->tf", lowered_grad, feed_back[2], preferred_element_type=f32)
    unused, gelu_pull = jax.vjp(partial(jax.nn.gelu, approximate=False), lifted)
    lifted_grad = gelu_pull(active_grad)[0].astype(bf16)
    up_weight_grad = jnp.einsum("td,tf->df", normed_low, lifted_grad, preferred_element_type=f32)
    up_bias_grad = jnp.sum(lifted_grad.astype(f32), axis=0)
    normed_grad = grad_two + jnp.einsum(
        "tf,df->td", lifted_grad, feed_back[0], preferred_element_type=f32
    )
    grad_one, first_gain_grad, first_shift_grad = norm_backward(
        normed_grad, normal_one, inverse_one, attention_back[4].astype(f32)
    )
    attended_grad = grad_one.astype(bf16)
    output_weight_grad = jnp.einsum(
        "tc,td->cd", context_tokens, attended_grad, preferred_element_type=f32
    )
    output_bias_grad = jnp.sum(attended_grad.astype(f32), axis=0)
    context_grad = jnp.einsum(
        "td,cd->tc", attended_grad, attention_back[2], preferred_element_type=f32
    ).astype(bf16)
    context_grad = context_grad.reshape(local_rows, HEADS, HEAD_DIM)
    context_grad_heads = lax.all_to_all(
        context_grad, "seq", split_axis=1, concat_axis=0, tiled=True
    )
    grad_blocks = context_grad_heads.reshape(count, block, local_heads, HEAD_DIM)

    def backward_block(carry, pieces):
        key_grad, value_grad = carry
        query_block, segment_block, grad_block, log_block = pieces
        scores = scores_of(query_block, segment_block)
        weights = jnp.exp(scores - log_block[..., None])
        value_grad = value_grad + jnp.einsum(
            "hqk,qhd->khd", weights.astype(bf16), grad_block, preferred_element_type=f32
        )
        weight_grad = jnp.einsum("qhd,khd->hqk", grad_block, value_all, preferred_element_type=f32)
        centre = jnp.sum(weights * weight_grad, axis=-1, keepdims=True)
        score_grad = (weights * (weight_grad - centre)).astype(bf16)
        query_grad = (
            jnp.einsum("hqk,khd->qhd", score_grad, key_all, preferred_element_type=f32) * scale
        )
        key_grad = (
            key_grad
            + jnp.einsum("hqk,qhd->khd", score_grad, query_block, preferred_element_type=f32)
            * scale
        )
        return ((key_grad, value_grad), query_grad)

    zeros_heads = jnp.zeros((length, local_heads, HEAD_DIM), f32)
    (key_grad, value_grad), query_grad = lax.scan(
        backward_block,
        (zeros_heads, zeros_heads),
        (query_blocks, segment_blocks, grad_blocks, log_totals),
    )
    query_grad = query_grad.reshape(length, local_heads, HEAD_DIM)
    stacked_grad = jnp.stack([query_grad, key_grad, value_grad]).astype(bf16)
    token_heads = lax.all_to_all(stacked_grad, "seq", split_axis=1, concat_axis=2, tiled=True)
    query_back = rotary_back(token_heads[0].astype(f32), positions)
    key_back = rotary_back(token_heads[1].astype(f32), positions)
    projected_grad = jnp.stack([query_back, key_back, token_heads[2].astype(f32)], axis=1)
    projected_grad = projected_grad.reshape(local_rows, 3 * width).astype(bf16)
    projection_grad = jnp.einsum("td,te->de", tokens, projected_grad, preferred_element_type=f32)
    projection_bias_grad = jnp.sum(projected_grad.astype(f32), axis=0)
    input_grad = grad_one + jnp.einsum(
        "te,de->td", projected_grad, attention_back[0], preferred_element_type=f32
    )
    every_shard = (
        lax.psum_scatter(
            projection_grad.astype(jnp.bfloat16), "fsdp", scatter_dimension=0, tiled=True
        ).astype(jnp.float32),
        lax.psum_scatter(
            projection_bias_grad.astype(jnp.bfloat16), "fsdp", scatter_dimension=0, tiled=True
        ).astype(jnp.float32),
        lax.psum_scatter(
            output_weight_grad.astype(jnp.bfloat16), "fsdp", scatter_dimension=0, tiled=True
        ).astype(jnp.float32),
        lax.psum_scatter(
            output_bias_grad.astype(jnp.bfloat16), "fsdp", scatter_dimension=0, tiled=True
        ).astype(jnp.float32),
        lax.psum_scatter(
            first_gain_grad.astype(jnp.bfloat16), "fsdp", scatter_dimension=0, tiled=True
        ).astype(jnp.float32),
        lax.psum_scatter(
            first_shift_grad.astype(jnp.bfloat16), "fsdp", scatter_dimension=0, tiled=True
        ).astype(jnp.float32),
        lax.psum_scatter(
            up_weight_grad.astype(jnp.bfloat16), "fsdp", scatter_dimension=0, tiled=True
        ).astype(jnp.float32),
        lax.psum_scatter(
            up_bias_grad.astype(jnp.bfloat16), "fsdp", scatter_dimension=0, tiled=True
        ).astype(jnp.float32),
        lax.psum_scatter(
            down_weight_grad.astype(jnp.bfloat16), "fsdp", scatter_dimension=0, tiled=True
        ).astype(jnp.float32),
        lax.psum_scatter(
            down_bias_grad.astype(jnp.bfloat16), "fsdp", scatter_dimension=0, tiled=True
        ).astype(jnp.float32),
        lax.psum_scatter(
            second_gain_grad.astype(jnp.bfloat16), "fsdp", scatter_dimension=0, tiled=True
        ).astype(jnp.float32),
        lax.psum_scatter(
            second_shift_grad.astype(jnp.bfloat16), "fsdp", scatter_dimension=0, tiled=True
        ).astype(jnp.float32),
    )
    finals = (
        lax.psum(every_shard[0].astype(jnp.bfloat16), "seq").astype(jnp.float32),
        lax.psum(every_shard[1].astype(jnp.bfloat16), "seq").astype(jnp.float32),
        lax.psum(every_shard[2].astype(jnp.bfloat16), "seq").astype(jnp.float32),
        lax.psum(every_shard[3].astype(jnp.bfloat16), "seq").astype(jnp.float32),
        lax.psum(every_shard[4].astype(jnp.bfloat16), "seq").astype(jnp.float32),
        lax.psum(every_shard[5].astype(jnp.bfloat16), "seq").astype(jnp.float32),
        lax.psum(every_shard[6].astype(jnp.bfloat16), "seq").astype(jnp.float32),
        lax.psum(every_shard[7].astype(jnp.bfloat16), "seq").astype(jnp.float32),
        lax.psum(every_shard[8].astype(jnp.bfloat16), "seq").astype(jnp.float32),
        lax.psum(every_shard[9].astype(jnp.bfloat16), "seq").astype(jnp.float32),
        lax.psum(every_shard[10].astype(jnp.bfloat16), "seq").astype(jnp.float32),
        lax.psum(every_shard[11].astype(jnp.bfloat16), "seq").astype(jnp.float32),
    )
    return (
        layer_out.astype(bf16)[None],
        input_grad.astype(bf16)[None],
        finals[0],
        finals[1],
        finals[2],
        finals[3],
        finals[4],
        finals[5],
        finals[6],
        finals[7],
        finals[8],
        finals[9],
        finals[10],
        finals[11],
    )


MESH = pl.DeviceIdType.MESH
NN = (((1,), (0,)), ((), ()))
NT = (((1,), (1,)), ((), ()))
TN = (((0,), (0,)), ((), ()))
f32 = jnp.float32
bf16 = jnp.bfloat16
MASKED = -1e30


def mm(left, right, dims=NN):
    return lax.dot_general(left, right, dims, preferred_element_type=f32)


def block_of(index, size):
    return pl.ds(pl.multiple_of(index * size, size), size)


def flip(bit, other):
    return bit + other - 2 * bit * other


def fused_layer(sizes, *refs):
    r = SimpleNamespace(**dict(zip(sizes.names, refs)))
    T, D, L, F = sizes.T, sizes.D, sizes.L, sizes.F
    S, Z = 8, 4
    KW = D // Z
    UZ = F // Z
    C = 128
    T2 = 2 * T
    first_row = sizes.first_row
    ssem, rsem, lsem = r.ssem, r.rsem, r.lsem

    s = lax.axis_index("seq")
    z = lax.axis_index("fsdp")
    core, xbit, ybit = s % 2, (s // 2) % 2, s // 4
    zlow, zhigh = z % 2, z // 2

    def ps(k):
        return flip(core, k % 2) + 2 * flip(xbit, (k // 2) % 2) + 4 * flip(ybit, k // 4)

    def pz(k):
        return flip(zlow, k % 2) + 2 * flip(zhigh, k // 2)

    def chip_of(j):
        return flip(xbit, j % 2) + 2 * flip(ybit, j // 2)

    counter = [0, 0]
    pending = []

    def slots(n):
        counter[0] += n
        return counter[0] - n

    def remote(src, dst, slot, dev):
        return pltpu.make_async_remote_copy(
            src_ref=src, dst_ref=dst, send_sem=ssem.at[slot], recv_sem=rsem.at[slot],
            device_id=dev, device_id_type=MESH)

    def send(src, dst, slot, dev):
        copy = remote(src, dst, slot, dev)
        copy.start()
        pending.append(copy)
        return copy

    def drop(copies):
        for copy in copies:
            copy.wait_send()
        pending[:] = [other for other in pending if all(other is not copy for copy in copies)]

    def arrived(ref, slot):
        remote(ref, ref, slot, (ps(1), z)).wait_recv()

    def local(src, dst):
        copy = pltpu.make_async_copy(src, dst, lsem.at[counter[1]])
        counter[1] += 1
        copy.start()
        return copy

    class Gather:
        def __init__(self, place):
            self.place, self.base = place, slots(9)

        def half(self, k, part):
            there = self.place(ps(k))
            n = there.shape[0] // 2
            return there.at[pl.ds(part * n, n)]

        def start(self, src=None):
            mine = self.place(s)
            for k in (2, 4, 1):
                send(mine if src is None else src, mine, self.base + k, (ps(k), z))

        def pass_on(self, k):
            there = self.place(ps(k))
            if k == 2:
                arrived(there, self.base + 2)
                send(self.half(2, 0), self.half(2, 0), self.base + 6, (ps(4), z))
            elif k == 4:
                arrived(there, self.base + 4)
                send(self.half(4, 1), self.half(4, 1), self.base + 8, (ps(2), z))
            else:
                arrived(self.half(6, 0), self.base + 6)
                arrived(self.half(6, 1), self.base + 8)
            send(there, there, self.base + k + 1, (ps(1), z))

        def pass_all(self):
            for k in (2, 4, 6):
                self.pass_on(k)

        def wait(self, *which):
            for k in which or (1, 3, 5, 7):
                arrived(self.place(ps(k)), self.base + k)

    class Spread:
        def __init__(self, place):
            self.place, self.base = place, slots(4)

        def start(self, *which):
            mine = self.place(z)
            for k in which or (2, 1):
                send(mine, mine, self.base + k, (s, pz(k)))

        def pass_on(self):
            there = self.place(pz(2))
            arrived(there, self.base + 2)
            send(there, there, self.base + 3, (s, pz(1)))

        def wait(self):
            for k in (1, 3):
                arrived(self.place(pz(k)), self.base + k)

    class Fold:
        def __init__(self, parts, landing, passing):
            self.parts, self.landing, self.passing, self.base = parts, landing, passing, slots(3)

        def start(self):
            send(self.parts.at[pz(1)], self.landing.at[0], self.base, (s, pz(1)))
            send(self.parts.at[pz(3)], self.landing.at[1], self.base + 1, (s, pz(1)))

        def middle(self):
            arrived(self.landing.at[1], self.base + 1)
            self.passing[...] = (self.parts[pz(2)].astype(f32) + self.landing[1].astype(f32)).astype(bf16)
            send(self.passing, self.landing.at[2], self.base + 2, (s, pz(2)))

        def finish(self):
            arrived(self.landing.at[0], self.base)
            arrived(self.landing.at[2], self.base + 2)
            return (self.parts[z].astype(f32) + self.landing[0].astype(f32)
                    + self.landing[2].astype(f32)).astype(bf16)

    class Scatter:
        def __init__(self, parts, low, mid, high):
            self.parts, self.low, self.mid, self.high, self.base = parts, low, mid, high, slots(8)
            self.sent = []

        def pair(self, j):
            self.sent.append(send(self.parts.at[j, block_of(1 - core, T)], self.low.at[j],
                                  self.base + j, (ps(1), z)))

        def onward(self, j):
            arrived(self.low.at[j], self.base + j)
            own = self.parts[j, block_of(core, T), :].astype(f32)
            self.mid[j] = (own + self.low[j].astype(f32)).astype(bf16)
            self.sent.append(send(self.mid.at[j], self.high.at[j], self.base + 4 + j, (ps(2 * j), z)))

        def ready(self):
            arrived(self.low.at[0], self.base)
            for j in (1, 2, 3):
                arrived(self.high.at[j], self.base + 4 + j)

        def rows(self, at, n):
            own = self.parts[0, pl.ds(pl.multiple_of(core * T + at, n), n), :].astype(f32)
            total = own + self.low[0, pl.ds(at, n), :].astype(f32)
            for j in (1, 2, 3):
                total = total + self.high[j, pl.ds(at, n), :].astype(f32)
            return total

    def loop(count, body, unroll=1):
        def step(i, carry):
            body(i)
            return carry
        lax.fori_loop(0, count, step, 0, unroll=unroll)

    def at(i, n):
        return pl.multiple_of(i * n, n)

    def turn(src, dst):
        def one(i):
            dst[:, pl.ds(at(i, T), T)] = jnp.transpose(src[pl.ds(at(i, T), T), :])
        loop(L // T, one)

    vec, vecg = r.vec, r.vecg

    OUTPUT_BIAS, FIRST_GAIN, FIRST_SHIFT, DOWN_BIAS, SECOND_GAIN, SECOND_SHIFT, PROJECTION_BIAS, UP_BIAS = range(8)
    wide = ((first_row.output_bias, OUTPUT_BIAS), (first_row.first_gain, FIRST_GAIN),
            (first_row.first_shift, FIRST_SHIFT), (first_row.down_bias, DOWN_BIAS),
            (first_row.second_gain, SECOND_GAIN), (first_row.second_shift, SECOND_SHIFT))

    def row(i, width=D):
        return vec[i:i + 1, :width]

    lanes = lax.broadcasted_iota(jnp.int32, (T, C), 1)
    low_head = lanes < HEAD_DIM

    def swapped(w):
        low_half = lax.broadcasted_iota(jnp.int32, w.shape, 1) % HEAD_DIM < HEAD_DIM // 2
        return jnp.where(low_half, pltpu.roll(w, C - HEAD_DIM // 2, 1), pltpu.roll(w, HEAD_DIM // 2, 1))

    def stacked(w):
        nothing = jnp.zeros_like(w)
        return jnp.concatenate([jnp.where(low_head, w, nothing), jnp.where(low_head, nothing, w)], axis=0)

    def unstacked(w):
        return jnp.where(low_head, w[:T], w[T:])

    barrier = pltpu.get_barrier_semaphore()
    for k in range(1, S):
        pl.semaphore_signal(barrier, inc=1, device_id=(ps(k), z), device_id_type=MESH)
    for k in range(1, Z):
        pl.semaphore_signal(barrier, inc=1, device_id=(s, pz(k)), device_id_type=MESH)
    proj_loads = [local(r.proj.at[:, block_of(i * (D // C) + s, C)], r.st_proj.at[:, pl.ds(i * C, C)])
                  for i in range(3)]
    wo_load = local(r.wo.at[:, block_of(s, C)], r.st_wo)
    up_loads = [local(r.up.at[:, block_of(i * (D // C) + s, C)], r.st_up.at[:, pl.ds(i * C, C)])
                for i in range(Z)]
    dn_load = local(r.dn.at[block_of(s, UZ), :], r.st_dn)
    pl.semaphore_wait(barrier, S + Z - 2)

    x_ref, x_all = r.x, r.x_all
    w_qkv, w_o, w_up, w_dn = r.w_qkv, r.w_o, r.w_up, r.w_dn
    gather_x = Gather(lambda o: x_all.at[block_of(o, T)])
    gather_x.start(x_ref)
    spread_qkv = Spread(lambda p: w_qkv.at[block_of(p, KW)])
    spread_o = Spread(lambda p: w_o.at[block_of(p, KW), block_of(s, C)])
    spread_up = Spread(lambda p: w_up.at[block_of(p, KW)])
    spread_dn = Spread(lambda p: w_dn.at[block_of(p, UZ)])
    gather_o = Gather(lambda o: w_o.at[:, block_of(o, C)])

    for copy in proj_loads:
        copy.wait()
    w_qkv[block_of(z, KW), :] = r.st_proj[...].astype(bf16)
    spread_qkv.start()

    small, small_all, seg_c, seg_r = r.small, r.small_all, r.seg_c, r.seg_r
    raw = ((r.b_projection, first_row.projection_bias), (r.b_output, first_row.output_bias),
           (r.gain1, first_row.first_gain), (r.shift1, first_row.first_shift), (r.b_up, first_row.up_bias),
           (r.b_down, first_row.down_bias), (r.gain2, first_row.second_gain), (r.shift2, first_row.second_shift))
    for ref, start in raw:
        for i in range(ref.shape[1] // C):
            small[start + i:start + i + 1, :] = ref[0:1, i * C:(i + 1) * C].astype(bf16).astype(f32)
    small_base = slots(4)
    x_all[block_of(s, T), :] = x_ref[...]
    wo_load.wait()
    w_o[block_of(z, KW), block_of(s, C)] = r.st_wo[...].astype(bf16)
    for copy in up_loads:
        copy.wait()
    w_up[block_of(z, KW), :] = r.st_up[...].astype(bf16)
    dn_load.wait()
    w_dn[block_of(z, UZ), :] = r.st_dn[...].astype(bf16)
    vecg[...] = jnp.zeros((8, D), f32)
    seg_r[...] = jnp.broadcast_to(r.seg[...].astype(f32), (8, L))

    def seg_turn(i):
        here = pl.ds(at(i, T), T)
        seg_c[here, :] = jnp.transpose(jnp.broadcast_to(seg_r[0:1, here], (T, T)))
    loop(L // T, seg_turn)

    spread_qkv.pass_on()
    small_all[z] = small[...]
    for k in (1, 2, 3):
        send(small, small_all.at[z], small_base + k, (s, pz(k)))
    spread_o.start()
    gather_x.pass_on(2)
    gather_x.pass_on(4)
    spread_up.start(2)
    gather_x.pass_on(6)
    gather_x.wait()
    x_t = r.x_t
    turn(x_all, x_t)
    spread_o.pass_on()
    spread_up.start(1)
    for k in (1, 2, 3):
        arrived(small_all.at[pz(k)], small_base + k)
    for p in range(Z):
        for start, i in wide:
            for half in range(KW // C):
                at_row = start + half
                lane = (p * (KW // C) + half) * C
                vec[i:i + 1, lane:lane + C] = small_all[p, at_row:at_row + 1, :]
        vec[7:8, p * C:(p + 1) * C] = small_all[p, pl.ds(first_row.up_bias + s, 1), :]
    per = 3 * D // (C * Z)
    for t in range(3):
        number = t * (D // C) + s
        vec[6:7, t * C:(t + 1) * C] = small_all[number // per, pl.ds(first_row.projection_bias + number % per, 1), :]

    spread_qkv.wait()
    q_ref, k_ref, v_ref = r.q, r.k, r.v
    scale = HEAD_DIM ** -0.5

    def project(i):
        here = pl.ds(at(i, T2), T2)
        out = mm(x_all[here, :], w_qkv[...]) + row(PROJECTION_BIAS, 3 * C)
        cosine, sine = r.cos[here, :], r.sin[here, :]
        q0, k0 = out[:, :C], out[:, C:2 * C]
        q_ref[here, :] = ((q0 * cosine + swapped(q0) * sine).astype(bf16).astype(f32) * scale).astype(bf16)
        k_ref[here, :] = (k0 * cosine + swapped(k0) * sine).astype(bf16)
        v_ref[here, :] = out[:, 2 * C:].astype(bf16)
    loop(L // T2, project)
    spread_o.wait()
    gather_o.start()

    lse, c_f, c_heads, c_tok = r.lse, r.c_f, r.c_heads, r.c_tok
    R = 16

    def same_document(here):
        return jnp.tile(seg_c[here, :], (1, L // C)) == seg_r[0:1, :]

    def both(w):
        return jnp.concatenate([w, w], axis=0)

    def attend(o):
        here = block_of(o, T)
        score = jnp.where(both(same_document(here)), mm(stacked(q_ref[here, :]), k_ref[...], NT), MASKED)
        top = jnp.max(score, axis=-1, keepdims=True)
        power = jnp.exp(score - top)
        total = jnp.sum(power, axis=-1, keepdims=True)
        context = unstacked(mm(power.astype(bf16), v_ref[...]) * (1.0 / total))
        c_f[here, :] = context
        c_heads[here, :] = context.astype(bf16)
        logs = jnp.broadcast_to(top + jnp.log(total), (T2, C))
        for h in range(2):
            lse[h:h + 1, here] = jnp.transpose(logs[h * T:(h + 1) * T, :])[0:1, :]

    c_base = slots(8)

    def c_copy(k):
        return remote(c_heads.at[block_of(ps(k), T)], c_tok.at[:, block_of(s, C)], c_base + k, (ps(k), z))

    def attend_and_send(i):
        k = 7 - i
        attend(ps(k))

        @pl.when(k > 0)
        def _():
            c_copy(k).start()
    loop(8, attend_and_send)
    spread_up.pass_on()
    spread_dn.start()
    c_tok[:, block_of(s, C)] = c_heads[block_of(s, T), :]
    gather_o.pass_on(2)
    gather_o.pass_on(4)
    gather_o.pass_on(6)
    gather_o.wait()
    for k in range(1, 8):
        arrived(c_tok.at[:, block_of(ps(k), C)], c_base + k)

    a_buf = r.a_buf
    a_buf[...] = mm(c_tok[...], w_o[...])
    n1, y1, r1, y_all = r.n1, r.y1, r.r1, r.y_all

    def norm(h):
        centre = h - jnp.mean(h, axis=-1, keepdims=True)
        root = lax.rsqrt(jnp.mean(centre * centre, axis=-1, keepdims=True) + norm_epsilon)
        return centre * root, root

    def first_norm(i):
        rows = pl.ds(at(i, R), R)
        normal, root = norm(x_ref[rows, :].astype(f32) + a_buf[rows, :] + row(OUTPUT_BIAS))
        out = normal * row(FIRST_GAIN) + row(FIRST_SHIFT)
        n1[rows, :] = normal
        r1[rows, :] = jnp.broadcast_to(root, (R, C))
        y1[rows, :] = out
        y_all[pl.ds(pl.multiple_of(s * T + i * R, R), R), :] = out.astype(bf16)
    loop(T // R, first_norm, 4)
    gather_y = Gather(lambda o: y_all.at[block_of(o, T)])
    gather_y.start()
    c_all = r.c_all
    gather_c = Gather(lambda o: c_all.at[block_of(o, T)])
    gather_c.start(c_tok)
    c_all[block_of(s, T), :] = c_tok[...]

    u_buf, g_ref, d_ref, du_ref, dz_all = r.u_buf, r.g, r.d, r.du, r.dz_all
    parts, mid = r.parts, r.mid
    spread_up.wait()
    E = 32

    def lift(j):
        q = chip_of(j)
        u_buf[...] = mm(y_all[block_of(q, T2), :], w_up[...])

        def chunk(i):
            rows = pl.ds(at(i, E), E)
            there = pl.ds(pl.multiple_of(q * T2 + i * E, E), E)
            u = u_buf[rows, :] + row(UP_BIAS, F)
            share = 0.5 + 0.5 * lax.erf(u * (0.5 ** 0.5))
            g_ref[there, :] = (u * share).astype(bf16)
            d_ref[there, :] = share + u * (jnp.exp(-0.5 * u * u) * 0.3989422804014327)
        loop(T2 // E, chunk)

    def lower(j):
        parts[j] = mm(g_ref[block_of(chip_of(j), T2), :], w_dn[...]).astype(bf16)

    fold_z = Scatter(parts, r.low0, mid, r.high0)
    y_t, g_t = r.y_t, r.g_t
    gather_y.wait(1)
    lift(0)
    gather_y.pass_on(2)
    gather_y.pass_on(4)
    gather_y.wait(3)
    lift(1)
    gather_y.wait(5)
    lift(2)
    spread_dn.pass_on()
    gather_y.pass_on(6)
    gather_y.wait(7)
    lift(3)
    gather_c.pass_on(2)
    gather_c.pass_on(4)
    turn(y_all, y_t)
    turn(g_ref, g_t)
    spread_dn.wait()
    for j in (3, 1, 2, 0):
        lower(j)
        fold_z.pair(j)
        if j == 1:
            fold_z.onward(3)
        if j == 2:
            fold_z.onward(1)
    fold_z.onward(2)
    gather_c.pass_on(6)
    gather_c.wait()
    fold_z.ready()

    dh2, out_ref, ct_ref = r.dh2, r.out, r.ct

    def add_row(i, value):
        vecg[i:i + 1, :] = vecg[i:i + 1, :] + jnp.sum(value, axis=0, keepdims=True)

    def norm_back(incoming, normal, root, gain):
        scaled = incoming * gain
        return root * (scaled - jnp.mean(scaled, axis=-1, keepdims=True)
                       - normal * jnp.mean(scaled * normal, axis=-1, keepdims=True))

    def second_norm(i):
        start = at(i, R)
        rows = pl.ds(start, R)
        normal, root = norm(y1[rows, :] + fold_z.rows(start, R) + row(DOWN_BIAS))
        out_ref[rows, :] = (normal * row(SECOND_GAIN) + row(SECOND_SHIFT)).astype(bf16)
        e = ct_ref[rows, :].astype(f32)
        grad = norm_back(e, normal, root, row(SECOND_GAIN))
        dh2[rows, :] = grad
        dz = grad.astype(bf16)
        dz_all[pl.ds(pl.multiple_of(s * T + i * R, R), R), :] = dz
        add_row(3, dz.astype(f32))
        add_row(4, e * normal)
        add_row(5, e)
    loop(T // R, second_norm, 2)
    gather_dz = Gather(lambda o: dz_all.at[block_of(o, T)])
    gather_dz.start()
    drop(fold_z.sent)

    colg = r.colg
    colg[...] = jnp.zeros((8, F), f32)

    def unlower(j):
        q = chip_of(j)
        u_buf[...] = mm(dz_all[block_of(q, T2), :], w_dn[...], NT)

        def chunk(i):
            rows = pl.ds(at(i, E), E)
            there = pl.ds(pl.multiple_of(q * T2 + i * E, E), E)
            du = (u_buf[rows, :] * d_ref[there, :]).astype(bf16)
            du_ref[there, :] = du
            colg[0:1, :] = colg[0:1, :] + jnp.sum(du.astype(f32), axis=0, keepdims=True)
        loop(T2 // E, chunk)

    def unlift(j):
        parts[j] = mm(du_ref[block_of(chip_of(j), T2), :], w_up[...], NT).astype(bf16)

    fold_y = Scatter(parts, r.low1, mid, r.high1)
    gd_part, gu_part = r.gd_part, r.gu_part
    fold_dn = Fold(gd_part, r.gd_land, r.gd_pass)
    fold_up = Fold(gu_part, r.gu_land, r.gu_pass)

    def down_grad(k):
        gd_part[pz(k)] = mm(g_t[block_of(pz(k), UZ), :], dz_all[...]).astype(bf16)

    def up_grad(k):
        gu_part[pz(k)] = mm(y_t[block_of(pz(k), KW), :], du_ref[...]).astype(bf16)

    gather_dz.wait(1)
    unlower(0)
    unlift(0)
    fold_y.pair(0)
    gather_dz.pass_on(2)
    gather_dz.pass_on(4)
    gather_dz.wait(3)
    unlower(1)
    unlift(1)
    fold_y.pair(1)
    gather_dz.wait(5)
    unlower(2)
    fold_y.onward(1)
    unlift(2)
    fold_y.pair(2)
    gather_dz.pass_on(6)
    fold_y.onward(2)
    gather_dz.wait(7)
    unlower(3)
    unlift(3)
    fold_y.pair(3)
    down_grad(1)
    down_grad(3)
    fold_dn.start()
    fold_y.onward(3)

    up_grad(1)
    up_grad(3)
    fold_up.start()
    down_grad(2)
    down_grad(0)
    up_grad(2)
    up_grad(0)
    fold_y.ready()

    dh1, da = r.dh1, r.da

    def first_back(i):
        start = at(i, R)
        rows = pl.ds(start, R)
        incoming = dh2[rows, :] + fold_y.rows(start, R)
        normal = n1[rows, :]
        grad = norm_back(incoming, normal, r1[rows, 0:1], row(FIRST_GAIN))
        dh1[rows, :] = grad
        low = grad.astype(bf16)
        da[rows, :] = low
        add_row(0, low.astype(f32))
        add_row(1, incoming * normal)
        add_row(2, incoming)
    loop(T // R, first_back, 2)
    drop(fold_y.sent)

    dc_tok, dc = r.dc_tok, r.dc
    dc_tok[...] = mm(da[...], w_o[...], NT).astype(bf16)
    dc_base = slots(8)
    for k in (7, 6, 5, 4, 3, 2, 1):
        send(dc_tok.at[:, block_of(ps(k), C)], dc.at[block_of(s, T)], dc_base + k, (ps(k), z))
    dc[block_of(s, T), :] = dc_tok[:, block_of(s, C)]
    da_cols = r.da_cols
    da_base = slots(8)
    for k in (7, 6, 5, 4, 3, 2, 1):
        send(da.at[:, block_of(ps(k), C)], da_cols.at[block_of(s, T)], da_base + k, (ps(k), z))
    da_cols[block_of(s, T), :] = da[:, block_of(s, C)]
    vec_all = r.vec_all
    vec_base = slots(8)
    for k in (7, 6, 5, 4, 3, 2, 1):
        send(vecg, vec_all.at[s], vec_base + k, (ps(k), z))
    fold_dn.middle()
    for k in range(1, 8):
        arrived(dc.at[block_of(ps(k), T)], dc_base + k)

    delta, dq, dproj = r.delta, r.dq, r.dproj

    def deltas(i):
        here = pl.ds(at(i, T), T)
        turned = jnp.transpose(dc[here, :].astype(f32) * c_f[here, :])
        delta[0:1, here] = jnp.sum(turned[:HEAD_DIM], axis=0, keepdims=True)
        delta[1:2, here] = jnp.sum(turned[HEAD_DIM:], axis=0, keepdims=True)
        dq[here, :] = jnp.zeros((T, C), f32)
    loop(L // T, deltas)

    def attend_back(i):
        here = pl.ds(at(i, T), T)
        same = same_document(here)
        k_here, v_here = k_ref[here, :], v_ref[here, :]
        keys, values, slopes = [], [], []
        for h in range(2):
            own = low_head if h == 0 else jnp.logical_not(low_head)
            nothing = jnp.zeros_like(k_here)
            key = jnp.where(own, k_here, nothing)
            weight = jnp.exp(jnp.where(same, mm(key, q_ref[...], NT), MASKED) - lse[h:h + 1, :])
            slope = mm(jnp.where(own, v_here, nothing), dc[...], NT) - delta[h:h + 1, :]
            slopes.append((weight * slope).astype(bf16))
            values.append(mm(weight.astype(bf16), dc[...]))
            keys.append(key)
        dv = jnp.where(low_head, values[0], values[1]).astype(bf16)
        dk = jnp.where(low_head, mm(slopes[0], q_ref[...]), mm(slopes[1], q_ref[...])).astype(bf16).astype(f32)
        dproj[here, 2 * C:] = dv
        dproj[here, C:2 * C] = (dk * r.cos[here, :] - swapped(dk) * r.sin[here, :]).astype(bf16)
        dq[...] = dq[...] + mm(jnp.concatenate(slopes, axis=0), jnp.concatenate(keys, axis=0), TN)

    gd_all, gu_all, go_all, gq_all = r.gd_all, r.gu_all, r.go_all, r.gq_all
    gather_gd = Gather(lambda o: gd_all.at[block_of(o, UZ)])
    gather_gu = Gather(lambda o: gu_all.at[o])
    gather_go = Gather(lambda o: go_all.at[:, block_of(o, C)])
    gather_gq = Gather(lambda o: gq_all.at[o])
    loop(L // T, attend_back)
    fold_up.middle()

    def dq_rows(i):
        here = pl.ds(at(i, T), T)
        whole = (dq[here, :] * scale).astype(bf16).astype(f32)
        dproj[here, :C] = (whole * r.cos[here, :] - swapped(whole) * r.sin[here, :]).astype(bf16)
        colg[1:2, :3 * C] = colg[1:2, :3 * C] + jnp.sum(dproj[here, :].astype(f32), axis=0, keepdims=True)
    loop(L // T, dq_rows)

    gq_part = r.gq_part
    fold_qkv = Fold(gq_part, r.gq_land, r.gq_pass)

    def projection_grad(k):
        gq_part[pz(k)] = mm(x_t[block_of(pz(k), KW), :], dproj[...]).astype(bf16)
    projection_grad(1)
    projection_grad(3)
    fold_qkv.start()
    fold_x = Scatter(parts, r.low2, mid, r.high2)

    def unproject(j):
        parts[j] = mm(dproj[block_of(chip_of(j), T2), :], w_qkv[...], NT).astype(bf16)
        fold_x.pair(j)
    unproject(3)
    unproject(1)
    fold_x.onward(3)
    unproject(2)
    fold_x.onward(1)
    unproject(0)
    fold_x.onward(2)
    for k in range(1, 8):
        arrived(da_cols.at[block_of(ps(k), T)], da_base + k)
    go_part = r.go_part
    fold_o = Fold(go_part, r.go_land, r.go_pass)

    def out_grad(k):
        go_part[pz(k)] = mm(c_all[:, block_of(pz(k), KW)], da_cols[...], TN).astype(bf16)
    out_grad(1)
    out_grad(3)
    fold_o.start()
    out_grad(2)
    out_grad(0)
    projection_grad(2)
    projection_grad(0)
    col_z = r.col_z
    cz_base = slots(4)
    for k in (1, 2, 3):
        send(colg, col_z.at[z], cz_base + k, (s, pz(k)))
    col_z[z] = colg[...]
    vec_all[s] = vecg[...]
    for k in range(1, 8):
        arrived(vec_all.at[ps(k)], vec_base + k)
    vec_plane, vec_z = r.vec_plane, r.vec_z
    total = vec_all[0]
    for o in range(1, S):
        total = total + vec_all[o]
    vec_plane[...] = total
    vz_base = slots(4)
    for k in (1, 2, 3):
        send(vec_plane, vec_z.at[z], vz_base + k, (s, pz(k)))
    vec_z[z] = total
    gd_all[block_of(s, UZ), :] = fold_dn.finish()
    gather_gd.start()
    fold_o.middle()
    gu_all[s] = fold_up.finish()
    gather_gu.start()
    fold_qkv.middle()
    gather_gd.pass_on(2)
    gather_gd.pass_on(4)
    fold_x.ready()
    dx_ref = r.dx

    def input_back(i):
        start = at(i, R)
        rows = pl.ds(start, R)
        dx_ref[rows, :] = (dh1[rows, :] + fold_x.rows(start, R)).astype(bf16)
    loop(T // R, input_back, 2)
    go_all[:, block_of(s, C)] = fold_o.finish()
    gather_go.start()
    gather_gd.pass_on(6)
    gather_gu.pass_on(2)
    gather_gu.pass_on(4)
    gq_all[s] = fold_qkv.finish()
    gather_gq.start()
    for k in (1, 2, 3):
        arrived(col_z.at[pz(k)], cz_base + k)
    col_all, col_sum = r.col_all, r.col_sum
    col_sum[...] = col_z[0] + col_z[1] + col_z[2] + col_z[3]
    ca_base = slots(8)
    for k in range(1, 8):
        send(col_sum, col_all.at[s], ca_base + k, (ps(k), z))
    col_all[s] = col_sum[...]
    gather_gu.pass_on(6)
    gather_go.pass_all()
    gather_gd.wait()
    outs = [local(gd_all, r.gd)]
    gather_gu.wait()
    for o in range(S):
        for p in range(Z):
            lane = (p * S + o) * C
            outs.append(local(gu_all.at[o, :, pl.ds(p * C, C)], r.gu.at[:, pl.ds(lane, C)]))
    gather_go.wait()
    outs.append(local(go_all, r.go))

    for k in (1, 2, 3):
        arrived(vec_z.at[pz(k)], vz_base + k)
    for k in range(1, 8):
        arrived(col_all.at[ps(k)], ca_base + k)
    vec_plane2 = r.vec_sum
    vec_plane2[...] = vec_z[0] + vec_z[1] + vec_z[2] + vec_z[3]
    gsm = r.gsm
    gsm[...] = jnp.zeros(gsm.shape, f32)
    for start, i in wide:
        for half in range(KW // C):
            at_row = start + half
            gsm[at_row:at_row + 1, :] = vec_plane2[i:i + 1, block_of(z * (KW // C) + half, C)]
    for o in range(S):
        at_row = first_row.up_bias + o
        gsm[at_row:at_row + 1, :] = col_all[o, 0:1, block_of(z, C)]
    for i in range(per):
        number = z * per + i
        at_row = first_row.projection_bias + i
        gsm[at_row:at_row + 1, :] = col_all[number % S, 1:2, block_of(number // S, C)]

    gather_gq.pass_all()
    gather_gq.wait()
    for o in range(S):
        for t in range(3):
            lane = (t * S + o) * C
            outs.append(local(gq_all.at[o, :, pl.ds(t * C, C)], r.gq.at[:, pl.ds(lane, C)]))
    for copy in outs:
        copy.wait()
    for copy in pending:
        copy.wait_send()
    loop(7, lambda i: c_copy(7 - i).wait_send())


def fused_shards(*args):
    (hidden_in, cotangent, segment_ids, projection, projection_bias, output_weight, output_bias, first_gain,
     first_shift, up_weight, up_bias, down_weight, down_bias, second_gain, second_shift) = args
    T, D = hidden_in.shape[1:]
    L = segment_ids.shape[1]
    KW = projection.shape[0]
    F = up_weight.shape[1] // 8
    C, Z = 128, 4
    UZ = F // Z
    small = dict(projection_bias=projection_bias, output_bias=output_bias, first_gain=first_gain,
                 first_shift=first_shift, up_bias=up_bias, down_bias=down_bias, second_gain=second_gain,
                 second_shift=second_shift)
    starts, at_row = {}, 0
    for name, value in small.items():
        starts[name] = at_row
        at_row += value.shape[0] // C
    rows = -(-at_row // 8) * 8
    half = HEAD_DIM // 2
    inverse = np.float32(10000.0) ** (np.float32(-2.0) * np.arange(half, dtype=np.float32) / np.float32(HEAD_DIM))
    angles = np.arange(L, dtype=np.float32)[:, None] * inverse.astype(np.float32)[None, :]
    cosine = np.tile(np.cos(angles), (1, C // half))
    sine = np.tile(np.concatenate([-np.sin(angles), np.sin(angles)], axis=1), (1, C // HEAD_DIM))

    inputs = dict(x=(hidden_in[0], 0), ct=(cotangent[0], 0), seg=(segment_ids, 0),
                  cos=(jnp.asarray(cosine), 0), sin=(jnp.asarray(sine), 0),
                  b_projection=(projection_bias[None], 0), b_output=(output_bias[None], 0),
                  gain1=(first_gain[None], 0), shift1=(first_shift[None], 0), b_up=(up_bias[None], 0),
                  b_down=(down_bias[None], 0), gain2=(second_gain[None], 0), shift2=(second_shift[None], 0),
                  proj=(projection, 1), wo=(output_weight, 1), up=(up_weight, 1), dn=(down_weight, 1))
    outputs = dict(out=((T, D), bf16, 0), dx=((T, D), bf16, 0), gsm=((rows, C), f32, 0),
               gq=(projection.shape, bf16, 1), go=(output_weight.shape, bf16, 1),
               gu=(up_weight.shape, bf16, 1), gd=(down_weight.shape, bf16, 1))
    PART = (4, T, D)
    scratch = dict(
        x_all=((L, D), bf16), x_t=((D, L), bf16), w_qkv=((D, 3 * C), bf16), st_proj=((KW, 3 * C), f32),
        w_o=((D, D), bf16), st_wo=((KW, C), f32), w_up=((D, F), bf16), st_up=((KW, F), f32),
        w_dn=((F, D), bf16), st_dn=((UZ, D), f32), small_all=((Z, rows, C), f32), vec=((8, D), f32),
        vecg=((8, D), f32), q=((L, C), bf16), k=((L, C), bf16), v=((L, C), bf16),
        seg_r=((8, L), f32), seg_c=((L, C), f32), small=((rows, C), f32), lse=((8, L), f32),
        delta=((8, L), f32), c_f=((L, C), f32), c_heads=((L, C), bf16), c_tok=((T, D), bf16),
        a_buf=((T, D), f32), n1=((T, D), f32), y1=((T, D), f32), r1=((T, C), f32),
        y_all=((L, D), bf16), y_t=((D, L), bf16), u_buf=((2 * T, F), f32), g=((L, F), bf16),
        g_t=((F, L), bf16), d=((L, F), f32), du=((L, F), bf16), dz_all=((L, D), bf16),
        parts=((4, 2 * T, D), bf16), mid=((4, T, D), bf16), dh2=((T, D), f32), dh1=((T, D), f32),
        colg=((8, F), f32), gd_part=((Z, UZ, D), bf16), gd_land=((3, UZ, D), bf16), gd_pass=((UZ, D), bf16),
        gu_part=((Z, KW, F), bf16), gu_land=((3, KW, F), bf16), gu_pass=((KW, F), bf16),
        go_part=((Z, KW, C), bf16), go_land=((3, KW, C), bf16), go_pass=((KW, C), bf16),
        gq_part=((Z, KW, 3 * C), bf16), gq_land=((3, KW, 3 * C), bf16), gq_pass=((KW, 3 * C), bf16),
        gd_all=((8 * UZ, D), bf16), gu_all=((8, KW, F), bf16), go_all=((KW, D), bf16),
        gq_all=((8, KW, 3 * C), bf16), da=((T, D), bf16), dc_tok=((T, D), bf16), dc=((L, C), bf16),
        da_cols=((L, C), bf16), c_all=((L, D), bf16), dq=((L, C), f32), dproj=((L, 3 * C), bf16),
        vec_all=((8, 8, D), f32), vec_plane=((8, D), f32), vec_z=((Z, 8, D), f32), vec_sum=((8, D), f32),
        col_z=((Z, 8, F), f32), col_sum=((8, F), f32), col_all=((8, 8, F), f32),
        low0=(PART, bf16), high0=(PART, bf16), low1=(PART, bf16), high1=(PART, bf16), low2=(PART, bf16),
        high2=(PART, bf16), ssem=(SLOTS,), rsem=(SLOTS,), lsem=(LOCAL,))
    names = [*inputs, *outputs, *scratch]
    sizes = SimpleNamespace(names=names, T=T, D=D, L=L, F=F, first_row=SimpleNamespace(**starts))

    def spec(anywhere):
        return pl.BlockSpec(memory_space=pl.ANY if anywhere else pltpu.VMEM)
    results = pl.pallas_call(
        partial(fused_layer, sizes),
        out_shape=[jax.ShapeDtypeStruct(shape, dtype) for shape, dtype, _ in outputs.values()],
        in_specs=[spec(w) for _, w in inputs.values()],
        out_specs=[spec(w) for *_, w in outputs.values()],
        scratch_shapes=[pltpu.VMEM(*what) if len(what) == 2 else pltpu.SemaphoreType.DMA(what)
                        for what in scratch.values()],
        compiler_params=pltpu.CompilerParams(collective_id=0, has_side_effects=True, vmem_limit_bytes=67043328),
        name="fused_layer",
    )(*[value for value, _ in inputs.values()])
    out, dx, gsm, gq, go, gu, gd = results
    steps = 8

    def tile(value):
        return pl.BlockSpec((value.shape[0] // steps, value.shape[1]), lambda i: (i, 0))

    def whole(n):
        return pl.BlockSpec((1, n), lambda i: (0, 0))
    wide = (gq, go, gu, gd)
    counts = [value.shape[0] for value in small.values()]
    results = pl.pallas_call(
        partial(widen, tuple(starts.values())),
        grid=(steps,),
        out_shape=[jax.ShapeDtypeStruct(value.shape, value.dtype) for value in (out, dx)]
        + [jax.ShapeDtypeStruct(value.shape, f32) for value in wide]
        + [jax.ShapeDtypeStruct((1, n), f32) for n in counts],
        in_specs=[tile(out), tile(dx), *map(tile, wide), pl.BlockSpec((rows, C), lambda i: (0, 0))],
        out_specs=[tile(out), tile(dx), *map(tile, wide), *map(whole, counts)],
        name="widen",
    )(out, dx, *wide, gsm)
    out, dx, gq, go, gu, gd = results[:6]
    pb, ob, g1, s1, ub, db, g2, s2 = [value[0] for value in results[6:]]
    return (out[None], dx[None], gq, pb, go, ob, g1, s1, gu, ub, gd, db, g2, s2)


def widen(starts, out, dx, gq, go, gu, gd, small, *results):
    for source, result in zip((out, dx, gq, go, gu, gd), results):
        result[...] = source[...].astype(result.dtype)
    for start, result in zip(starts, results[6:]):
        for i in range(result.shape[1] // 128):
            result[0:1, i * 128:(i + 1) * 128] = small[start + i:start + i + 1, :]


SLOTS = 200
LOCAL = 80


def fits(mesh):
    return mesh.shape["seq"] == 8 and mesh.shape["fsdp"] == 4


def solution(mesh):
    return jax.shard_map(
        fused_shards if fits(mesh) else shards,
        mesh=mesh,
        in_specs=(
            P("fsdp", "seq", None),
            P("fsdp", "seq", None),
            P("fsdp", None),
            P("fsdp", None),
            P("fsdp"),
            P("fsdp", None),
            P("fsdp"),
            P("fsdp"),
            P("fsdp"),
            P("fsdp", None),
            P("fsdp"),
            P("fsdp", None),
            P("fsdp"),
            P("fsdp"),
            P("fsdp"),
        ),
        out_specs=(
            P("fsdp", "seq", None),
            P("fsdp", "seq", None),
            P("fsdp", None),
            P("fsdp"),
            P("fsdp", None),
            P("fsdp"),
            P("fsdp"),
            P("fsdp"),
            P("fsdp", None),
            P("fsdp"),
            P("fsdp", None),
            P("fsdp"),
            P("fsdp"),
            P("fsdp"),
        ),
        check_vma=False,
    )
```

```python
from functools import partial

import jax
import jax.numpy as jnp
import numpy as np
import math
from types import SimpleNamespace
from jax import lax
from jax.experimental import pallas as pl
from jax.experimental.pallas import tpu as pltpu
from jax.sharding import PartitionSpec as P

HEADS = 16
HEAD_DIM = 64


norm_epsilon = 1e-05


def rotary(values, positions):
    half = values.shape[-1] // 2
    channel = jnp.arange(half).astype(jnp.float32)
    inverse = 10000.0 ** (-2.0 * channel / values.shape[-1])
    angles = positions[:, None] * inverse[None, :]
    cosine = jnp.cos(angles)[:, None, :]
    sine = jnp.sin(angles)[:, None, :]
    first = values[..., :half]
    second = values[..., half:]
    return jnp.concatenate(
        [first * cosine - second * sine, second * cosine + first * sine], axis=-1
    )


def rotary_back(grads, positions):
    unused, pullback = jax.vjp(lambda inner: rotary(inner, positions), grads)
    return pullback(grads)[0]


def norm_forward(values, gain, shift):
    centre = values - jnp.mean(values, axis=-1, keepdims=True)
    inverse_root = lax.rsqrt(jnp.mean(centre * centre, axis=-1, keepdims=True) + norm_epsilon)
    normal = centre * inverse_root
    return (normal * gain + shift, normal, inverse_root)


def norm_backward(incoming, normal, inverse_root, gain):
    gain_grad = jnp.sum(incoming * normal, axis=0)
    shift_grad = jnp.sum(incoming, axis=0)
    scaled = incoming * gain
    inner = (
        scaled
        - jnp.mean(scaled, axis=-1, keepdims=True)
        - normal * jnp.mean(scaled * normal, axis=-1, keepdims=True)
    )
    return (inner * inverse_root, gain_grad, shift_grad)


def shards(
    hidden_in,
    cotangent,
    segment_ids,
    projection,
    projection_bias,
    output_weight,
    output_bias,
    first_gain,
    first_shift,
    up_weight,
    up_bias,
    down_weight,
    down_bias,
    second_gain,
    second_shift,
):
    bf16 = jnp.bfloat16
    f32 = jnp.float32
    tokens = hidden_in[0]
    local_rows = tokens.shape[0]
    width = tokens.shape[1]
    seq_rank = lax.axis_index("seq")
    positions = (seq_rank * local_rows + jnp.arange(local_rows)).astype(f32)
    segments = segment_ids[0]
    scale = HEAD_DIM ** (-0.5)
    attention_full = (
        lax.all_gather(projection.astype(bf16), "fsdp", axis=0, tiled=True),
        lax.all_gather(projection_bias.astype(bf16), "fsdp", axis=0, tiled=True),
        lax.all_gather(output_weight.astype(bf16), "fsdp", axis=0, tiled=True),
        lax.all_gather(output_bias.astype(bf16), "fsdp", axis=0, tiled=True),
        lax.all_gather(first_gain.astype(bf16), "fsdp", axis=0, tiled=True),
        lax.all_gather(first_shift.astype(bf16), "fsdp", axis=0, tiled=True),
    )
    proj_weight = attention_full[0]
    projected = jnp.dot(tokens, proj_weight, preferred_element_type=f32) + attention_full[1].astype(
        f32
    )
    heads = projected.reshape(local_rows, 3, HEADS, HEAD_DIM)
    queries = rotary(heads[:, 0], positions)
    keys = rotary(heads[:, 1], positions)
    stacked = jnp.stack([queries, keys, heads[:, 2]]).astype(bf16)
    spread = lax.all_to_all(stacked, "seq", split_axis=2, concat_axis=1, tiled=True)
    query_all = spread[0]
    key_all = spread[1]
    value_all = spread[2]
    length = query_all.shape[0]
    local_heads = query_all.shape[1]
    block = min(512, length)
    count = length // block
    query_blocks = query_all.reshape(count, block, local_heads, HEAD_DIM)
    segment_blocks = segments.reshape(count, block)

    def scores_of(query_block, segment_block):
        raw = jnp.einsum("qhd,khd->hqk", query_block, key_all, preferred_element_type=f32) * scale
        allowed = segment_block[:, None] == segments[None, :]
        return jnp.where(allowed[None], raw, -1e30)

    def forward_block(pieces):
        query_block, segment_block = pieces
        scores = scores_of(query_block, segment_block)
        row_max = jnp.max(scores, axis=-1, keepdims=True)
        exponent = jnp.exp(scores - row_max)
        total = jnp.sum(exponent, axis=-1, keepdims=True)
        weights = exponent / total
        context = jnp.einsum(
            "hqk,khd->qhd", weights.astype(bf16), value_all, preferred_element_type=f32
        )
        return (context.astype(bf16), (row_max + jnp.log(total))[..., 0])

    context_blocks, log_totals = lax.map(forward_block, (query_blocks, segment_blocks))
    context_heads = context_blocks.reshape(length, local_heads, HEAD_DIM)
    context_tokens = lax.all_to_all(
        context_heads, "seq", split_axis=0, concat_axis=1, tiled=True
    ).reshape(local_rows, width)
    attended = jnp.dot(
        context_tokens, attention_full[2], preferred_element_type=f32
    ) + attention_full[3].astype(f32)
    gain_one = attention_full[4].astype(f32)
    normed_one, normal_one, inverse_one = norm_forward(
        tokens.astype(f32) + attended, gain_one, attention_full[5].astype(f32)
    )
    feed_full = (
        lax.all_gather(up_weight.astype(bf16), "fsdp", axis=0, tiled=True),
        lax.all_gather(up_bias.astype(bf16), "fsdp", axis=0, tiled=True),
        lax.all_gather(down_weight.astype(bf16), "fsdp", axis=0, tiled=True),
        lax.all_gather(down_bias.astype(bf16), "fsdp", axis=0, tiled=True),
        lax.all_gather(second_gain.astype(bf16), "fsdp", axis=0, tiled=True),
        lax.all_gather(second_shift.astype(bf16), "fsdp", axis=0, tiled=True),
    )
    normed_low = normed_one.astype(bf16)
    lifted = jnp.dot(normed_low, feed_full[0], preferred_element_type=f32) + feed_full[1].astype(
        f32
    )
    activated = jax.nn.gelu(lifted, approximate=False).astype(bf16)
    lowered = jnp.dot(activated, feed_full[2], preferred_element_type=f32) + feed_full[3].astype(
        f32
    )
    gain_two = feed_full[4].astype(f32)
    layer_out, normal_two, inverse_two = norm_forward(
        normed_one + lowered, gain_two, feed_full[5].astype(f32)
    )
    feed_back = (
        lax.all_gather(up_weight.astype(bf16), "fsdp", axis=0, tiled=True),
        lax.all_gather(up_bias.astype(bf16), "fsdp", axis=0, tiled=True),
        lax.all_gather(down_weight.astype(bf16), "fsdp", axis=0, tiled=True),
        lax.all_gather(down_bias.astype(bf16), "fsdp", axis=0, tiled=True),
        lax.all_gather(second_gain.astype(bf16), "fsdp", axis=0, tiled=True),
        lax.all_gather(second_shift.astype(bf16), "fsdp", axis=0, tiled=True),
    )
    attention_back = (
        lax.all_gather(projection.astype(bf16), "fsdp", axis=0, tiled=True),
        lax.all_gather(projection_bias.astype(bf16), "fsdp", axis=0, tiled=True),
        lax.all_gather(output_weight.astype(bf16), "fsdp", axis=0, tiled=True),
        lax.all_gather(output_bias.astype(bf16), "fsdp", axis=0, tiled=True),
        lax.all_gather(first_gain.astype(bf16), "fsdp", axis=0, tiled=True),
        lax.all_gather(first_shift.astype(bf16), "fsdp", axis=0, tiled=True),
    )
    grad_two, second_gain_grad, second_shift_grad = norm_backward(
        cotangent[0].astype(f32), normal_two, inverse_two, gain_two
    )
    lowered_grad = grad_two.astype(bf16)
    down_weight_grad = jnp.einsum("tf,td->fd", activated, lowered_grad, preferred_element_type=f32)
    down_bias_grad = jnp.sum(lowered_grad.astype(f32), axis=0)
    active_grad = jnp.einsum("td,fd->tf", lowered_grad, feed_back[2], preferred_element_type=f32)
    unused, gelu_pull = jax.vjp(partial(jax.nn.gelu, approximate=False), lifted)
    lifted_grad = gelu_pull(active_grad)[0].astype(bf16)
    up_weight_grad = jnp.einsum("td,tf->df", normed_low, lifted_grad, preferred_element_type=f32)
    up_bias_grad = jnp.sum(lifted_grad.astype(f32), axis=0)
    normed_grad = grad_two + jnp.einsum(
        "tf,df->td", lifted_grad, feed_back[0], preferred_element_type=f32
    )
    grad_one, first_gain_grad, first_shift_grad = norm_backward(
        normed_grad, normal_one, inverse_one, attention_back[4].astype(f32)
    )
    attended_grad = grad_one.astype(bf16)
    output_weight_grad = jnp.einsum(
        "tc,td->cd", context_tokens, attended_grad, preferred_element_type=f32
    )
    output_bias_grad = jnp.sum(attended_grad.astype(f32), axis=0)
    context_grad = jnp.einsum(
        "td,cd->tc", attended_grad, attention_back[2], preferred_element_type=f32
    ).astype(bf16)
    context_grad = context_grad.reshape(local_rows, HEADS, HEAD_DIM)
    context_grad_heads = lax.all_to_all(
        context_grad, "seq", split_axis=1, concat_axis=0, tiled=True
    )
    grad_blocks = context_grad_heads.reshape(count, block, local_heads, HEAD_DIM)

    def backward_block(carry, pieces):
        key_grad, value_grad = carry
        query_block, segment_block, grad_block, log_block = pieces
        scores = scores_of(query_block, segment_block)
        weights = jnp.exp(scores - log_block[..., None])
        value_grad = value_grad + jnp.einsum(
            "hqk,qhd->khd", weights.astype(bf16), grad_block, preferred_element_type=f32
        )
        weight_grad = jnp.einsum("qhd,khd->hqk", grad_block, value_all, preferred_element_type=f32)
        centre = jnp.sum(weights * weight_grad, axis=-1, keepdims=True)
        score_grad = (weights * (weight_grad - centre)).astype(bf16)
        query_grad = (
            jnp.einsum("hqk,khd->qhd", score_grad, key_all, preferred_element_type=f32) * scale
        )
        key_grad = (
            key_grad
            + jnp.einsum("hqk,qhd->khd", score_grad, query_block, preferred_element_type=f32)
            * scale
        )
        return ((key_grad, value_grad), query_grad)

    zeros_heads = jnp.zeros((length, local_heads, HEAD_DIM), f32)
    (key_grad, value_grad), query_grad = lax.scan(
        backward_block,
        (zeros_heads, zeros_heads),
        (query_blocks, segment_blocks, grad_blocks, log_totals),
    )
    query_grad = query_grad.reshape(length, local_heads, HEAD_DIM)
    stacked_grad = jnp.stack([query_grad, key_grad, value_grad]).astype(bf16)
    token_heads = lax.all_to_all(stacked_grad, "seq", split_axis=1, concat_axis=2, tiled=True)
    query_back = rotary_back(token_heads[0].astype(f32), positions)
    key_back = rotary_back(token_heads[1].astype(f32), positions)
    projected_grad = jnp.stack([query_back, key_back, token_heads[2].astype(f32)], axis=1)
    projected_grad = projected_grad.reshape(local_rows, 3 * width).astype(bf16)
    projection_grad = jnp.einsum("td,te->de", tokens, projected_grad, preferred_element_type=f32)
    projection_bias_grad = jnp.sum(projected_grad.astype(f32), axis=0)
    input_grad = grad_one + jnp.einsum(
        "te,de->td", projected_grad, attention_back[0], preferred_element_type=f32
    )
    every_shard = (
        lax.psum_scatter(
            projection_grad.astype(jnp.bfloat16), "fsdp", scatter_dimension=0, tiled=True
        ).astype(jnp.float32),
        lax.psum_scatter(
            projection_bias_grad.astype(jnp.bfloat16), "fsdp", scatter_dimension=0, tiled=True
        ).astype(jnp.float32),
        lax.psum_scatter(
            output_weight_grad.astype(jnp.bfloat16), "fsdp", scatter_dimension=0, tiled=True
        ).astype(jnp.float32),
        lax.psum_scatter(
            output_bias_grad.astype(jnp.bfloat16), "fsdp", scatter_dimension=0, tiled=True
        ).astype(jnp.float32),
        lax.psum_scatter(
            first_gain_grad.astype(jnp.bfloat16), "fsdp", scatter_dimension=0, tiled=True
        ).astype(jnp.float32),
        lax.psum_scatter(
            first_shift_grad.astype(jnp.bfloat16), "fsdp", scatter_dimension=0, tiled=True
        ).astype(jnp.float32),
        lax.psum_scatter(
            up_weight_grad.astype(jnp.bfloat16), "fsdp", scatter_dimension=0, tiled=True
        ).astype(jnp.float32),
        lax.psum_scatter(
            up_bias_grad.astype(jnp.bfloat16), "fsdp", scatter_dimension=0, tiled=True
        ).astype(jnp.float32),
        lax.psum_scatter(
            down_weight_grad.astype(jnp.bfloat16), "fsdp", scatter_dimension=0, tiled=True
        ).astype(jnp.float32),
        lax.psum_scatter(
            down_bias_grad.astype(jnp.bfloat16), "fsdp", scatter_dimension=0, tiled=True
        ).astype(jnp.float32),
        lax.psum_scatter(
            second_gain_grad.astype(jnp.bfloat16), "fsdp", scatter_dimension=0, tiled=True
        ).astype(jnp.float32),
        lax.psum_scatter(
            second_shift_grad.astype(jnp.bfloat16), "fsdp", scatter_dimension=0, tiled=True
        ).astype(jnp.float32),
    )
    finals = (
        lax.psum(every_shard[0].astype(jnp.bfloat16), "seq").astype(jnp.float32),
        lax.psum(every_shard[1].astype(jnp.bfloat16), "seq").astype(jnp.float32),
        lax.psum(every_shard[2].astype(jnp.bfloat16), "seq").astype(jnp.float32),
        lax.psum(every_shard[3].astype(jnp.bfloat16), "seq").astype(jnp.float32),
        lax.psum(every_shard[4].astype(jnp.bfloat16), "seq").astype(jnp.float32),
        lax.psum(every_shard[5].astype(jnp.bfloat16), "seq").astype(jnp.float32),
        lax.psum(every_shard[6].astype(jnp.bfloat16), "seq").astype(jnp.float32),
        lax.psum(every_shard[7].astype(jnp.bfloat16), "seq").astype(jnp.float32),
        lax.psum(every_shard[8].astype(jnp.bfloat16), "seq").astype(jnp.float32),
        lax.psum(every_shard[9].astype(jnp.bfloat16), "seq").astype(jnp.float32),
        lax.psum(every_shard[10].astype(jnp.bfloat16), "seq").astype(jnp.float32),
        lax.psum(every_shard[11].astype(jnp.bfloat16), "seq").astype(jnp.float32),
    )
    return (
        layer_out.astype(bf16)[None],
        input_grad.astype(bf16)[None],
        finals[0],
        finals[1],
        finals[2],
        finals[3],
        finals[4],
        finals[5],
        finals[6],
        finals[7],
        finals[8],
        finals[9],
        finals[10],
        finals[11],
    )


MESH = pl.DeviceIdType.MESH
NN = (((1,), (0,)), ((), ()))
NT = (((1,), (1,)), ((), ()))
TN = (((0,), (0,)), ((), ()))
f32 = jnp.float32
bf16 = jnp.bfloat16
MASKED = -1e30


def mm(left, right, dims=NN):
    return lax.dot_general(left, right, dims, preferred_element_type=f32)


def block_of(index, size):
    return pl.ds(pl.multiple_of(index * size, size), size)


def flip(bit, other):
    return bit + other - 2 * bit * other


def fused_layer(sizes, *refs):
    r = SimpleNamespace(**dict(zip(sizes.names, refs)))
    T, D, L, F = sizes.T, sizes.D, sizes.L, sizes.F
    S, Z = 8, 4
    KW = D // Z
    UZ = F // Z
    C = 128
    T2 = 2 * T
    first_row = sizes.first_row
    ssem, rsem, lsem = r.ssem, r.rsem, r.lsem

    s = lax.axis_index("seq")
    z = lax.axis_index("fsdp")
    core, xbit, ybit = s % 2, (s // 2) % 2, s // 4
    zlow, zhigh = z % 2, z // 2

    def ps(k):
        return flip(core, k % 2) + 2 * flip(xbit, (k // 2) % 2) + 4 * flip(ybit, k // 4)

    def pz(k):
        return flip(zlow, k % 2) + 2 * flip(zhigh, k // 2)

    def chip_of(j):
        return flip(xbit, j % 2) + 2 * flip(ybit, j // 2)

    counter = [0, 0, 0]
    closing = []

    def take(which, n=1):
        counter[which] += n
        return counter[which] - n

    def landings(n=1):
        return take(0, n)

    def size(ref):
        return math.prod(ref.shape) * jnp.dtype(ref.dtype).itemsize

    def extent(n):
        if n <= size(r.c_f):
            return r.c_f.at[pl.ds(0, n * L // size(r.c_f))]
        return r.y_all.at[pl.ds(0, n * L // size(r.y_all))]

    def arrived(ref, slot):
        pltpu.make_async_copy(ref, ref, rsem.at[slot]).wait()

    class Batch:
        def __init__(self, count, like):
            self.slot, self.bytes, self.open = take(1), count * size(like), True
            closing.append(self)

        def send(self, src, dst, slot, dev):
            pltpu.make_async_remote_copy(
                src_ref=src, dst_ref=dst, send_sem=ssem.at[self.slot], recv_sem=rsem.at[slot],
                device_id=dev, device_id_type=MESH).start()

        def close(self):
            if self.open:
                everything = extent(self.bytes)
                pltpu.make_async_copy(everything, everything, ssem.at[self.slot]).wait()
            self.open = False

    def local(src, dst):
        copy = pltpu.make_async_copy(src, dst, lsem.at[take(2)])
        copy.start()
        return copy

    class Gather:
        def __init__(self, place, at_once=True):
            self.place, self.at_once = place, at_once
            self.batch = Batch(7, place(0))
            self.near, self.across = landings(2), landings(2)
            self.other = landings() if at_once else landings(4)

        def half(self, k, part):
            there = self.place(ps(k))
            n = there.shape[0] // 2
            return there.at[pl.ds(part * n, n)]

        def start(self, src=None):
            mine = self.place(s)
            src = mine if src is None else src
            self.batch.send(src, mine, self.near, (ps(2), z))
            self.batch.send(src, mine, self.near + 1, (ps(4), z))
            self.batch.send(src, mine, self.other, (ps(1), z))

        def pass_on(self, k):
            there = self.place(ps(k))
            if k == 2:
                arrived(there, self.near)
                self.batch.send(self.half(2, 0), self.half(2, 0), self.across, (ps(4), z))
            elif k == 4:
                arrived(there, self.near + 1)
                self.batch.send(self.half(4, 1), self.half(4, 1), self.across + 1, (ps(2), z))
            else:
                arrived(self.half(6, 0), self.across)
                arrived(self.half(6, 1), self.across + 1)
            self.batch.send(there, there, self.other + (0 if self.at_once else k // 2), (ps(1), z))

        def pass_all(self):
            for k in (2, 4, 6):
                self.pass_on(k)

        def wait(self, k=None):
            if self.at_once:
                arrived(extent(4 * size(self.place(0))), self.other)
            else:
                arrived(self.place(ps(k)), self.other + k // 2)

    class Spread:
        def __init__(self, place):
            self.place, self.batch, self.base = place, Batch(3, place(0)), landings(3)

        def start(self, *which):
            mine = self.place(z)
            for k in which or (2, 1):
                self.batch.send(mine, mine, self.base + k - 1, (s, pz(k)))

        def pass_on(self):
            there = self.place(pz(2))
            arrived(there, self.base + 1)
            self.batch.send(there, there, self.base + 2, (s, pz(1)))

        def wait(self):
            for k in (1, 3):
                arrived(self.place(pz(k)), self.base + k - 1)

        def wait_all(self):
            for k in (1, 2, 3):
                arrived(self.place(pz(k)), self.base + k - 1)

    class Fold:
        def __init__(self, parts, landing, passing):
            self.parts, self.landing, self.passing = parts, landing, passing
            self.batch, self.base = Batch(3, passing), landings(3)

        def start(self):
            self.batch.send(self.parts.at[pz(3)], self.landing.at[1], self.base + 1, (s, pz(1)))
            self.batch.send(self.parts.at[pz(1)], self.landing.at[0], self.base, (s, pz(1)))

        def middle(self):
            arrived(self.landing.at[1], self.base + 1)
            self.passing[...] = (self.parts[pz(2)].astype(f32) + self.landing[1].astype(f32)).astype(bf16)
            self.batch.send(self.passing, self.landing.at[2], self.base + 2, (s, pz(2)))

        def finish(self):
            arrived(self.landing.at[0], self.base)
            arrived(self.landing.at[2], self.base + 2)
            return (self.parts[z].astype(f32) + self.landing[0].astype(f32)
                    + self.landing[2].astype(f32)).astype(bf16)

    class Scatter:
        def __init__(self, parts, low, mid, high):
            self.parts, self.low, self.mid, self.high = parts, low, mid, high
            self.batch, self.base, self.last = Batch(7, mid.at[0]), landings(4), landings()

        def pair(self, j):
            self.batch.send(self.parts.at[j, block_of(1 - core, T)], self.low.at[j], self.base + j, (ps(1), z))

        def onward(self, j):
            arrived(self.low.at[j], self.base + j)
            own = self.parts[j, block_of(core, T), :].astype(f32)
            self.mid[j] = (own + self.low[j].astype(f32)).astype(bf16)
            self.batch.send(self.mid.at[j], self.high.at[j], self.last, (ps(2 * j), z))

        def ready(self):
            arrived(self.low.at[0], self.base)
            arrived(self.high.at[pl.ds(1, 3)], self.last)

        def rows(self, at, n):
            own = self.parts[0, pl.ds(pl.multiple_of(core * T + at, n), n), :].astype(f32)
            total = own + self.low[0, pl.ds(at, n), :].astype(f32)
            for j in (1, 2, 3):
                total = total + self.high[j, pl.ds(at, n), :].astype(f32)
            return total

    class Share:
        def __init__(self, count, like):
            self.count, self.batch, self.slot, self.bytes = count, Batch(count, like), landings(), count * size(like)

        def plane(self, src, dst):
            for k in (6, 7, 2, 3, 4, 5, 1):
                self.batch.send(src(ps(k)), dst, self.slot, (ps(k), z))

        def column(self, src, dst):
            for k in (2, 3, 1):
                self.batch.send(src, dst, self.slot, (s, pz(k)))

        def wait(self):
            arrived(extent(self.bytes), self.slot)

    def loop(count, body, unroll=1):
        def step(i, carry):
            body(i)
            return carry
        lax.fori_loop(0, count, step, 0, unroll=unroll)

    def at(i, n):
        return pl.multiple_of(i * n, n)

    def turn(src, dst):
        def one(i):
            dst[:, pl.ds(at(i, T), T)] = jnp.transpose(src[pl.ds(at(i, T), T), :])
        loop(L // T, one)

    vec, vecg = r.vec, r.vecg

    OUTPUT_BIAS, FIRST_GAIN, FIRST_SHIFT, DOWN_BIAS, SECOND_GAIN, SECOND_SHIFT, PROJECTION_BIAS, UP_BIAS = range(8)
    wide = ((first_row.output_bias, OUTPUT_BIAS), (first_row.first_gain, FIRST_GAIN),
            (first_row.first_shift, FIRST_SHIFT), (first_row.down_bias, DOWN_BIAS),
            (first_row.second_gain, SECOND_GAIN), (first_row.second_shift, SECOND_SHIFT))

    def row(i, width=D):
        return vec[i:i + 1, :width]

    lanes = lax.broadcasted_iota(jnp.int32, (T, C), 1)
    low_head = lanes < HEAD_DIM

    def swapped(w):
        low_half = lax.broadcasted_iota(jnp.int32, w.shape, 1) % HEAD_DIM < HEAD_DIM // 2
        return jnp.where(low_half, pltpu.roll(w, C - HEAD_DIM // 2, 1), pltpu.roll(w, HEAD_DIM // 2, 1))

    def stacked(w):
        nothing = jnp.zeros_like(w)
        return jnp.concatenate([jnp.where(low_head, w, nothing), jnp.where(low_head, nothing, w)], axis=0)

    def unstacked(w):
        return jnp.where(low_head, w[:T], w[T:])

    barrier = pltpu.get_barrier_semaphore()
    for k in range(1, S):
        pl.semaphore_signal(barrier, inc=1, device_id=(ps(k), z), device_id_type=MESH)
    for k in range(1, Z):
        pl.semaphore_signal(barrier, inc=1, device_id=(s, pz(k)), device_id_type=MESH)
    x_ref, ct_ref = r.v_x, r.v_ct
    x_load = local(r.x, x_ref)
    wo_load = local(r.wo.at[:, block_of(s, C)], r.st_wo)
    proj_loads = [local(r.proj.at[:, block_of(i * (D // C) + s, C)], r.st_proj.at[:, pl.ds(i * C, C)])
                  for i in range(3)]
    raw = ((r.b_projection, r.v_projection, first_row.projection_bias), (r.b_output, r.v_output, first_row.output_bias),
           (r.gain1, r.v_gain1, first_row.first_gain), (r.shift1, r.v_shift1, first_row.first_shift),
           (r.b_up, r.v_up, first_row.up_bias), (r.b_down, r.v_down, first_row.down_bias),
           (r.gain2, r.v_gain2, first_row.second_gain), (r.shift2, r.v_shift2, first_row.second_shift))
    raw_loads = [local(source, ref) for source, ref, _ in raw]
    seg_load = local(r.seg, r.v_seg)
    up_loads = [local(r.up.at[:, block_of(i * (D // C) + s, C)], r.st_up.at[:, pl.ds(i * C, C)])
                for i in range(Z)]
    dn_load = local(r.dn.at[block_of(s, UZ), :], r.st_dn)
    late_loads = [local(r.cos, r.v_cos), local(r.sin, r.v_sin), local(r.ct, ct_ref)]
    cos_ref, sin_ref = r.v_cos, r.v_sin

    x_all, w_qkv, w_o, w_up, w_dn = r.x_all, r.w_qkv, r.w_o, r.w_up, r.w_dn
    gather_x = Gather(lambda o: x_all.at[block_of(o, T)])
    spread_qkv = Spread(lambda p: w_qkv.at[block_of(p, KW)])
    spread_o = Spread(lambda p: w_o.at[block_of(p, KW), block_of(s, C)])
    spread_up = Spread(lambda p: w_up.at[block_of(p, KW)])
    spread_dn = Spread(lambda p: w_dn.at[block_of(p, UZ)])
    gather_o = Gather(lambda o: w_o.at[:, block_of(o, C)])
    x_load.wait()
    pl.semaphore_wait(barrier, S + Z - 2)
    gather_x.start(x_ref)
    wo_load.wait()
    w_o[block_of(z, KW), block_of(s, C)] = r.st_wo[...].astype(bf16)
    spread_o.start(2, 3, 1)
    for copy in proj_loads:
        copy.wait()
    w_qkv[block_of(z, KW), :] = r.st_proj[...].astype(bf16)
    spread_qkv.start()

    small, small_all, seg_c, seg_r = r.small, r.small_all, r.seg_c, r.seg_r
    for copy, (_, ref, start) in zip(raw_loads, raw):
        copy.wait()
        for i in range(ref.shape[1] // C):
            small[start + i:start + i + 1, :] = ref[0:1, i * C:(i + 1) * C].astype(bf16).astype(f32)
    x_all[block_of(s, T), :] = x_ref[...]
    vecg[...] = jnp.zeros((8, D), f32)
    seg_load.wait()
    seg_r[...] = jnp.broadcast_to(r.v_seg[...].astype(f32), (8, L))

    def seg_turn(i):
        here = pl.ds(at(i, T), T)
        seg_c[here, :] = jnp.transpose(jnp.broadcast_to(seg_r[0:1, here], (T, T)))
    loop(L // T, seg_turn)
    for copy in up_loads:
        copy.wait()
    w_up[block_of(z, KW), :] = r.st_up[...].astype(bf16)
    dn_load.wait()
    w_dn[block_of(z, UZ), :] = r.st_dn[...].astype(bf16)
    share_small = Share(3, small)
    small_all[z] = small[...]

    gather_x.pass_on(2)
    gather_x.pass_on(4)
    spread_o.wait_all()
    gather_o.start()
    gather_x.pass_on(6)
    gather_x.wait()
    spread_qkv.pass_on()
    share_small.column(small, small_all.at[z])
    spread_up.start()
    x_t = r.x_t
    turn(x_all, x_t)
    for copy in late_loads:
        copy.wait()
    gather_o.pass_on(2)
    gather_o.pass_on(4)
    spread_qkv.wait()
    share_small.wait()
    for p in range(Z):
        for start, i in wide:
            for half in range(KW // C):
                at_row = start + half
                lane = (p * (KW // C) + half) * C
                vec[i:i + 1, lane:lane + C] = small_all[p, at_row:at_row + 1, :]
        vec[7:8, p * C:(p + 1) * C] = small_all[p, pl.ds(first_row.up_bias + s, 1), :]
    per = 3 * D // (C * Z)
    for t in range(3):
        number = t * (D // C) + s
        vec[6:7, t * C:(t + 1) * C] = small_all[number // per, pl.ds(first_row.projection_bias + number % per, 1), :]

    q_ref, k_ref, v_ref = r.q, r.k, r.v
    scale = HEAD_DIM ** -0.5

    def project(i):
        here = pl.ds(at(i, T2), T2)
        out = mm(x_all[here, :], w_qkv[...]) + row(PROJECTION_BIAS, 3 * C)
        cosine, sine = cos_ref[here, :], sin_ref[here, :]
        q0, k0 = out[:, :C], out[:, C:2 * C]
        q_ref[here, :] = ((q0 * cosine + swapped(q0) * sine).astype(bf16).astype(f32) * scale).astype(bf16)
        k_ref[here, :] = (k0 * cosine + swapped(k0) * sine).astype(bf16)
        v_ref[here, :] = out[:, 2 * C:].astype(bf16)
    loop(L // T2, project)
    gather_o.pass_on(6)

    lse, c_f, c_heads, c_tok = r.lse, r.c_f, r.c_heads, r.c_tok
    R = 16

    def same_document(here):
        return jnp.tile(seg_c[here, :], (1, L // C)) == seg_r[0:1, :]

    def both(w):
        return jnp.concatenate([w, w], axis=0)

    def attend(o):
        here = block_of(o, T)
        score = jnp.where(both(same_document(here)), mm(stacked(q_ref[here, :]), k_ref[...], NT), MASKED)
        top = jnp.max(score, axis=-1, keepdims=True)
        power = jnp.exp(score - top)
        total = jnp.sum(power, axis=-1, keepdims=True)
        context = unstacked(mm(power.astype(bf16), v_ref[...]) * (1.0 / total))
        c_f[here, :] = context
        c_heads[here, :] = context.astype(bf16)
        logs = jnp.broadcast_to(top + jnp.log(total), (T2, C))
        for h in range(2):
            lse[h:h + 1, here] = jnp.transpose(logs[h * T:(h + 1) * T, :])[0:1, :]

    share_c = Share(7, c_heads.at[pl.ds(0, T)])

    def attend_and_send(i):
        k = 7 - i
        attend(ps(k))

        @pl.when(k > 0)
        def _():
            share_c.batch.send(c_heads.at[block_of(ps(k), T)], c_tok.at[:, block_of(s, C)], share_c.slot, (ps(k), z))
    loop(8, attend_and_send)
    spread_up.pass_on()
    spread_dn.start()
    c_tok[:, block_of(s, C)] = c_heads[block_of(s, T), :]
    gather_o.wait()
    share_c.wait()

    a_buf = r.a_buf
    a_buf[...] = mm(c_tok[...], w_o[...])
    n1, y1, r1, y_all = r.n1, r.y1, r.r1, r.y_all

    def norm(h):
        centre = h - jnp.mean(h, axis=-1, keepdims=True)
        root = lax.rsqrt(jnp.mean(centre * centre, axis=-1, keepdims=True) + norm_epsilon)
        return centre * root, root

    def first_norm(i):
        rows = pl.ds(at(i, R), R)
        normal, root = norm(x_ref[rows, :].astype(f32) + a_buf[rows, :] + row(OUTPUT_BIAS))
        out = normal * row(FIRST_GAIN) + row(FIRST_SHIFT)
        n1[rows, :] = normal
        r1[rows, :] = jnp.broadcast_to(root, (R, C))
        y1[rows, :] = out
        y_all[pl.ds(pl.multiple_of(s * T + i * R, R), R), :] = out.astype(bf16)
    loop(T // R, first_norm, 4)
    gather_y = Gather(lambda o: y_all.at[block_of(o, T)], False)
    gather_y.start()
    c_all = r.c_all
    gather_c = Gather(lambda o: c_all.at[block_of(o, T)])
    c_all[block_of(s, T), :] = c_tok[...]

    u_buf, g_ref, d_ref, du_ref, dz_all = r.u_buf, r.g, r.d, r.du, r.dz_all
    parts, mid = r.parts, r.mid
    spread_up.wait()
    E = 32

    def lift(j):
        q = chip_of(j)
        u_buf[...] = mm(y_all[block_of(q, T2), :], w_up[...])

        def chunk(i):
            rows = pl.ds(at(i, E), E)
            there = pl.ds(pl.multiple_of(q * T2 + i * E, E), E)
            u = u_buf[rows, :] + row(UP_BIAS, F)
            share = 0.5 + 0.5 * lax.erf(u * (0.5 ** 0.5))
            g_ref[there, :] = (u * share).astype(bf16)
            d_ref[there, :] = share + u * (jnp.exp(-0.5 * u * u) * 0.3989422804014327)
        loop(T2 // E, chunk)

    def lower(j):
        parts[j] = mm(g_ref[block_of(chip_of(j), T2), :], w_dn[...]).astype(bf16)

    fold_z = Scatter(parts, r.low0, mid, r.high0)
    y_t, g_t = r.y_t, r.g_t
    gather_y.wait(1)
    lift(0)
    gather_y.pass_on(2)
    gather_y.pass_on(4)
    gather_y.wait(3)
    lift(1)
    gather_y.wait(5)
    lift(2)
    spread_dn.pass_on()
    gather_y.pass_on(6)
    gather_c.start(c_tok)
    gather_y.wait(7)
    lift(3)
    turn(y_all, y_t)
    turn(g_ref, g_t)
    spread_dn.wait()
    for j in (3, 1, 2, 0):
        lower(j)
        fold_z.pair(j)
        if j == 1:
            fold_z.onward(3)
        if j == 2:
            fold_z.onward(1)
    fold_z.onward(2)
    gather_c.pass_on(2)
    gather_c.pass_on(4)
    fold_z.ready()

    dh2, out_ref = r.dh2, r.v_out

    def add_row(i, value):
        vecg[i:i + 1, :] = vecg[i:i + 1, :] + jnp.sum(value, axis=0, keepdims=True)

    def norm_back(incoming, normal, root, gain):
        scaled = incoming * gain
        return root * (scaled - jnp.mean(scaled, axis=-1, keepdims=True)
                       - normal * jnp.mean(scaled * normal, axis=-1, keepdims=True))

    def second_norm(i):
        start = at(i, R)
        rows = pl.ds(start, R)
        normal, root = norm(y1[rows, :] + fold_z.rows(start, R) + row(DOWN_BIAS))
        out_ref[rows, :] = (normal * row(SECOND_GAIN) + row(SECOND_SHIFT)).astype(bf16)
        e = ct_ref[rows, :].astype(f32)
        grad = norm_back(e, normal, root, row(SECOND_GAIN))
        dh2[rows, :] = grad
        dz = grad.astype(bf16)
        dz_all[pl.ds(pl.multiple_of(s * T + i * R, R), R), :] = dz
        add_row(3, dz.astype(f32))
        add_row(4, e * normal)
        add_row(5, e)
    loop(T // R, second_norm, 2)
    outs = [local(out_ref, r.out)]
    gather_dz = Gather(lambda o: dz_all.at[block_of(o, T)], False)
    gather_dz.start()
    fold_z.batch.close()

    colg = r.colg
    colg[...] = jnp.zeros((8, F), f32)

    def unlower(j):
        q = chip_of(j)
        u_buf[...] = mm(dz_all[block_of(q, T2), :], w_dn[...], NT)

        def chunk(i):
            rows = pl.ds(at(i, E), E)
            there = pl.ds(pl.multiple_of(q * T2 + i * E, E), E)
            du = (u_buf[rows, :] * d_ref[there, :]).astype(bf16)
            du_ref[there, :] = du
            colg[0:1, :] = colg[0:1, :] + jnp.sum(du.astype(f32), axis=0, keepdims=True)
        loop(T2 // E, chunk)

    def unlift(j):
        parts[j] = mm(du_ref[block_of(chip_of(j), T2), :], w_up[...], NT).astype(bf16)

    fold_y = Scatter(parts, r.low1, mid, r.high1)
    gd_part, gu_part = r.gd_part, r.gu_part
    fold_dn = Fold(gd_part, r.gd_land, r.gd_pass)
    fold_up = Fold(gu_part, r.gu_land, r.gu_pass)

    def down_grad(k):
        gd_part[pz(k)] = mm(g_t[block_of(pz(k), UZ), :], dz_all[...]).astype(bf16)

    def up_grad(k):
        gu_part[pz(k)] = mm(y_t[block_of(pz(k), KW), :], du_ref[...]).astype(bf16)

    gather_c.pass_on(6)
    gather_dz.wait(1)
    unlower(0)
    unlift(0)
    fold_y.pair(0)
    gather_dz.pass_on(2)
    gather_dz.pass_on(4)
    gather_dz.wait(3)
    unlower(1)
    unlift(1)
    fold_y.pair(1)
    gather_dz.wait(5)
    unlower(2)
    fold_y.onward(1)
    unlift(2)
    fold_y.pair(2)
    gather_dz.pass_on(6)
    fold_y.onward(2)
    gather_dz.wait(7)
    unlower(3)
    unlift(3)
    fold_y.pair(3)
    down_grad(1)
    down_grad(3)
    fold_dn.start()
    fold_y.onward(3)

    up_grad(1)
    up_grad(3)
    down_grad(2)
    down_grad(0)
    up_grad(2)
    up_grad(0)
    gather_c.wait()
    fold_y.ready()

    dh1, da = r.dh1, r.da

    def first_back(i):
        start = at(i, R)
        rows = pl.ds(start, R)
        incoming = dh2[rows, :] + fold_y.rows(start, R)
        normal = n1[rows, :]
        grad = norm_back(incoming, normal, r1[rows, 0:1], row(FIRST_GAIN))
        dh1[rows, :] = grad
        low = grad.astype(bf16)
        da[rows, :] = low
        add_row(0, low.astype(f32))
        add_row(1, incoming * normal)
        add_row(2, incoming)
    loop(T // R, first_back, 2)
    fold_y.batch.close()

    dc_tok, dc = r.dc_tok, r.dc
    dc_tok[...] = mm(da[...], w_o[...], NT).astype(bf16)
    share_dc = Share(7, dc.at[pl.ds(0, T)])
    share_dc.plane(lambda o: dc_tok.at[:, block_of(o, C)], dc.at[block_of(s, T)])
    dc[block_of(s, T), :] = dc_tok[:, block_of(s, C)]
    da_cols = r.da_cols
    share_da = Share(7, da_cols.at[pl.ds(0, T)])
    share_da.plane(lambda o: da.at[:, block_of(o, C)], da_cols.at[block_of(s, T)])
    da_cols[block_of(s, T), :] = da[:, block_of(s, C)]
    vec_all = r.vec_all
    share_vec = Share(7, vecg)
    share_vec.plane(lambda o: vecg, vec_all.at[s])
    fold_dn.middle()
    fold_up.start()
    share_dc.wait()

    delta, dq, dproj = r.delta, r.dq, r.dproj

    def deltas(i):
        here = pl.ds(at(i, T), T)
        turned = jnp.transpose(dc[here, :].astype(f32) * c_f[here, :])
        delta[0:1, here] = jnp.sum(turned[:HEAD_DIM], axis=0, keepdims=True)
        delta[1:2, here] = jnp.sum(turned[HEAD_DIM:], axis=0, keepdims=True)
        dq[here, :] = jnp.zeros((T, C), f32)
    loop(L // T, deltas)

    def attend_back(i):
        here = pl.ds(at(i, T), T)
        same = same_document(here)
        k_here, v_here = k_ref[here, :], v_ref[here, :]
        keys, values, slopes = [], [], []
        for h in range(2):
            own = low_head if h == 0 else jnp.logical_not(low_head)
            nothing = jnp.zeros_like(k_here)
            key = jnp.where(own, k_here, nothing)
            weight = jnp.exp(jnp.where(same, mm(key, q_ref[...], NT), MASKED) - lse[h:h + 1, :])
            slope = mm(jnp.where(own, v_here, nothing), dc[...], NT) - delta[h:h + 1, :]
            slopes.append((weight * slope).astype(bf16))
            values.append(mm(weight.astype(bf16), dc[...]))
            keys.append(key)
        dv = jnp.where(low_head, values[0], values[1]).astype(bf16)
        dk = jnp.where(low_head, mm(slopes[0], q_ref[...]), mm(slopes[1], q_ref[...])).astype(bf16).astype(f32)
        dproj[here, 2 * C:] = dv
        dproj[here, C:2 * C] = (dk * cos_ref[here, :] - swapped(dk) * sin_ref[here, :]).astype(bf16)
        dq[...] = dq[...] + mm(jnp.concatenate(slopes, axis=0), jnp.concatenate(keys, axis=0), TN)

    gd_all, gu_all, go_all, gq_all = r.gd_all, r.gu_all, r.go_all, r.gq_all
    gather_gd = Gather(lambda o: gd_all.at[block_of(o, UZ)])
    gather_gu = Gather(lambda o: gu_all.at[o])
    gather_go = Gather(lambda o: go_all.at[:, block_of(o, C)])
    gather_gq = Gather(lambda o: gq_all.at[o])

    def attend_back_and_fold(i):
        attend_back(i)

        @pl.when(i == 3)
        def _():
            gd_all[block_of(s, UZ), :] = fold_dn.finish()
            gather_gd.start()
    loop(L // T, attend_back_and_fold)

    def dq_rows(i):
        here = pl.ds(at(i, T), T)
        whole = (dq[here, :] * scale).astype(bf16).astype(f32)
        dproj[here, :C] = (whole * cos_ref[here, :] - swapped(whole) * sin_ref[here, :]).astype(bf16)
        colg[1:2, :3 * C] = colg[1:2, :3 * C] + jnp.sum(dproj[here, :].astype(f32), axis=0, keepdims=True)
    loop(L // T, dq_rows)

    gq_part = r.gq_part
    fold_qkv = Fold(gq_part, r.gq_land, r.gq_pass)

    def projection_grad(k):
        gq_part[pz(k)] = mm(x_t[block_of(pz(k), KW), :], dproj[...]).astype(bf16)
    projection_grad(1)
    projection_grad(3)
    fold_up.middle()
    fold_qkv.start()
    gather_gd.pass_on(2)
    gather_gd.pass_on(4)
    fold_x = Scatter(parts, r.low2, mid, r.high2)

    def unproject(j):
        parts[j] = mm(dproj[block_of(chip_of(j), T2), :], w_qkv[...], NT).astype(bf16)
        fold_x.pair(j)
    unproject(3)
    unproject(1)
    fold_x.onward(3)
    unproject(2)
    fold_x.onward(1)
    unproject(0)
    fold_x.onward(2)
    share_da.wait()
    go_part = r.go_part
    fold_o = Fold(go_part, r.go_land, r.go_pass)

    def out_grad(k):
        go_part[pz(k)] = mm(c_all[:, block_of(pz(k), KW)], da_cols[...], TN).astype(bf16)
    out_grad(1)
    out_grad(3)
    fold_o.start()
    out_grad(2)
    out_grad(0)
    projection_grad(2)
    projection_grad(0)
    col_z = r.col_z
    share_col = Share(3, colg)
    share_col.column(colg, col_z.at[z])
    col_z[z] = colg[...]
    vec_all[s] = vecg[...]
    share_vec.wait()
    vec_plane, vec_z = r.vec_plane, r.vec_z
    total = vec_all[0]
    for o in range(1, S):
        total = total + vec_all[o]
    vec_plane[...] = total
    share_sum = Share(3, vec_plane)
    share_sum.column(vec_plane, vec_z.at[z])
    vec_z[z] = total
    gather_gd.pass_on(6)
    gu_all[s] = fold_up.finish()
    gather_gu.start()
    gather_gd.wait()
    outs.append(local(gd_all, r.gd))
    fold_x.ready()
    dx_ref = r.v_dx

    def input_back(i):
        start = at(i, R)
        rows = pl.ds(start, R)
        dx_ref[rows, :] = (dh1[rows, :] + fold_x.rows(start, R)).astype(bf16)
    loop(T // R, input_back, 2)
    outs.append(local(dx_ref, r.dx))
    fold_qkv.middle()
    gather_gu.pass_on(2)
    gather_gu.pass_on(4)
    share_col.wait()
    col_all, col_sum = r.col_all, r.col_sum
    col_sum[...] = col_z[0] + col_z[1] + col_z[2] + col_z[3]
    share_cols = Share(7, col_sum)
    share_cols.plane(lambda o: col_sum, col_all.at[s])
    col_all[s] = col_sum[...]
    fold_o.middle()
    gather_gu.pass_on(6)
    gq_all[s] = fold_qkv.finish()
    gather_gq.start()
    gather_gu.wait()
    outs.append(local(gu_all, r.gu))
    go_all[:, block_of(s, C)] = fold_o.finish()
    gather_go.start()

    share_sum.wait()
    share_cols.wait()
    vec_sum = r.vec_sum
    vec_sum[...] = vec_z[0] + vec_z[1] + vec_z[2] + vec_z[3]
    gsm = r.v_gsm
    gsm[...] = jnp.zeros(gsm.shape, f32)
    for start, i in wide:
        for half in range(KW // C):
            at_row = start + half
            gsm[at_row:at_row + 1, :] = vec_sum[i:i + 1, block_of(z * (KW // C) + half, C)]
    for o in range(S):
        at_row = first_row.up_bias + o
        gsm[at_row:at_row + 1, :] = col_all[o, 0:1, block_of(z, C)]
    for i in range(per):
        number = z * per + i
        at_row = first_row.projection_bias + i
        gsm[at_row:at_row + 1, :] = col_all[number % S, 1:2, block_of(number // S, C)]
    outs.append(local(gsm, r.gsm))
    gather_gq.pass_on(2)
    gather_gq.pass_on(4)
    gather_go.pass_all()
    gather_gq.pass_on(6)
    gather_go.wait()
    outs.append(local(go_all, r.go))
    gather_gq.wait()
    outs.append(local(gq_all, r.gq))
    for copy in outs:
        copy.wait()
    for batch in closing:
        batch.close()
    assert counter[0] <= LANDINGS and counter[1] <= BATCHES and counter[2] <= LOCAL, counter


def fused_shards(*args):
    (hidden_in, cotangent, segment_ids, projection, projection_bias, output_weight, output_bias, first_gain,
     first_shift, up_weight, up_bias, down_weight, down_bias, second_gain, second_shift) = args
    T, D = hidden_in.shape[1:]
    L = segment_ids.shape[1]
    KW = projection.shape[0]
    F = up_weight.shape[1] // 8
    C, Z = 128, 4
    UZ = F // Z
    small = dict(projection_bias=projection_bias, output_bias=output_bias, first_gain=first_gain,
                 first_shift=first_shift, up_bias=up_bias, down_bias=down_bias, second_gain=second_gain,
                 second_shift=second_shift)
    starts, at_row = {}, 0
    for name, value in small.items():
        starts[name] = at_row
        at_row += value.shape[0] // C
    rows = -(-at_row // 8) * 8
    half = HEAD_DIM // 2
    inverse = np.float32(10000.0) ** (np.float32(-2.0) * np.arange(half, dtype=np.float32) / np.float32(HEAD_DIM))
    angles = np.arange(L, dtype=np.float32)[:, None] * inverse.astype(np.float32)[None, :]
    cosine = np.tile(np.cos(angles), (1, C // half))
    sine = np.tile(np.concatenate([-np.sin(angles), np.sin(angles)], axis=1), (1, C // HEAD_DIM))

    inputs = dict(x=hidden_in[0], ct=cotangent[0], seg=segment_ids, cos=jnp.asarray(cosine), sin=jnp.asarray(sine),
                  b_projection=projection_bias[None], b_output=output_bias[None], gain1=first_gain[None],
                  shift1=first_shift[None], b_up=up_bias[None], b_down=down_bias[None], gain2=second_gain[None],
                  shift2=second_shift[None], proj=projection, wo=output_weight, up=up_weight, dn=down_weight)
    outputs = dict(out=((T, D), bf16), dx=((T, D), bf16), gsm=((rows, C), f32), gq=((8, KW, 3 * C), bf16),
                   go=((KW, D), bf16), gu=((8, KW, F), bf16), gd=((8 * UZ, D), bf16))
    landed = dict(v_x=inputs["x"], v_ct=inputs["ct"], v_seg=segment_ids, v_cos=inputs["cos"], v_sin=inputs["sin"],
                  v_projection=inputs["b_projection"], v_output=inputs["b_output"], v_gain1=inputs["gain1"],
                  v_shift1=inputs["shift1"], v_up=inputs["b_up"], v_down=inputs["b_down"], v_gain2=inputs["gain2"],
                  v_shift2=inputs["shift2"])
    PART = (4, T, D)
    scratch = {name: (value.shape, value.dtype) for name, value in landed.items()}
    scratch.update(
        v_out=((T, D), bf16), v_dx=((T, D), bf16), v_gsm=((rows, C), f32),
        x_all=((L, D), bf16), x_t=((D, L), bf16), w_qkv=((D, 3 * C), bf16), st_proj=((KW, 3 * C), f32),
        w_o=((D, D), bf16), st_wo=((KW, C), f32), w_up=((D, F), bf16), st_up=((KW, F), f32),
        w_dn=((F, D), bf16), st_dn=((UZ, D), f32), small_all=((Z, rows, C), f32), vec=((8, D), f32),
        vecg=((8, D), f32), q=((L, C), bf16), k=((L, C), bf16), v=((L, C), bf16),
        seg_r=((8, L), f32), seg_c=((L, C), f32), small=((rows, C), f32), lse=((8, L), f32),
        delta=((8, L), f32), c_f=((L, C), f32), c_heads=((L, C), bf16), c_tok=((T, D), bf16),
        a_buf=((T, D), f32), n1=((T, D), f32), y1=((T, D), f32), r1=((T, C), f32),
        y_all=((L, D), bf16), y_t=((D, L), bf16), u_buf=((2 * T, F), f32), g=((L, F), bf16),
        g_t=((F, L), bf16), d=((L, F), f32), du=((L, F), bf16), dz_all=((L, D), bf16),
        parts=((4, 2 * T, D), bf16), mid=((4, T, D), bf16), dh2=((T, D), f32), dh1=((T, D), f32),
        colg=((8, F), f32), gd_part=((Z, UZ, D), bf16), gd_land=((3, UZ, D), bf16), gd_pass=((UZ, D), bf16),
        gu_part=((Z, KW, F), bf16), gu_land=((3, KW, F), bf16), gu_pass=((KW, F), bf16),
        go_part=((Z, KW, C), bf16), go_land=((3, KW, C), bf16), go_pass=((KW, C), bf16),
        gq_part=((Z, KW, 3 * C), bf16), gq_land=((3, KW, 3 * C), bf16), gq_pass=((KW, 3 * C), bf16),
        gd_all=((8 * UZ, D), bf16), gu_all=((8, KW, F), bf16), go_all=((KW, D), bf16),
        gq_all=((8, KW, 3 * C), bf16), da=((T, D), bf16), dc_tok=((T, D), bf16), dc=((L, C), bf16),
        da_cols=((L, C), bf16), c_all=((L, D), bf16), dq=((L, C), f32), dproj=((L, 3 * C), bf16),
        vec_all=((8, 8, D), f32), vec_plane=((8, D), f32), vec_z=((Z, 8, D), f32), vec_sum=((8, D), f32),
        col_z=((Z, 8, F), f32), col_sum=((8, F), f32), col_all=((8, 8, F), f32),
        low0=(PART, bf16), high0=(PART, bf16), low1=(PART, bf16), high1=(PART, bf16), low2=(PART, bf16),
        high2=(PART, bf16), ssem=(BATCHES,), rsem=(LANDINGS,), lsem=(LOCAL,))
    names = [*inputs, *outputs, *scratch]
    sizes = SimpleNamespace(names=names, T=T, D=D, L=L, F=F, first_row=SimpleNamespace(**starts))

    anywhere = pl.BlockSpec(memory_space=pl.ANY)
    results = pl.pallas_call(
        partial(fused_layer, sizes),
        out_shape=[jax.ShapeDtypeStruct(*what) for what in outputs.values()],
        in_specs=[anywhere] * len(inputs),
        out_specs=[anywhere] * len(outputs),
        scratch_shapes=[pltpu.VMEM(*what) if len(what) == 2 else pltpu.SemaphoreType.DMA(what)
                        for what in scratch.values()],
        compiler_params=pltpu.CompilerParams(collective_id=0, has_side_effects=True, vmem_limit_bytes=67043328),
        name="fused_layer",
    )(*inputs.values())
    out, dx, gsm, gq, go, gu, gd = results
    steps = 8

    def tile(value):
        return pl.BlockSpec((value.shape[0] // steps, value.shape[1]), lambda i: (i, 0))

    def grouped(value):
        return pl.BlockSpec((8, value.shape[1] // steps, value.shape[2]), lambda i: (0, i, 0))

    def whole(n):
        return pl.BlockSpec((1, n), lambda i: (0, 0))
    wide = [jax.ShapeDtypeStruct(value.shape, f32) for value in (projection, output_weight, up_weight, down_weight)]
    counts = [value.shape[0] for value in small.values()]
    results = pl.pallas_call(
        partial(widen, tuple(starts.values())),
        grid=(steps,),
        out_shape=[jax.ShapeDtypeStruct((T, D), bf16)] * 2 + wide + [jax.ShapeDtypeStruct((1, n), f32) for n in counts],
        in_specs=[tile(out), tile(dx), grouped(gq), tile(go), grouped(gu), tile(gd),
                  pl.BlockSpec((rows, C), lambda i: (0, 0))],
        out_specs=[tile(out), tile(dx), *map(tile, wide), *map(whole, counts)],
        name="widen",
    )(out, dx, gq, go, gu, gd, gsm)
    out, dx, gq, go, gu, gd = results[:6]
    pb, ob, g1, s1, ub, db, g2, s2 = [value[0] for value in results[6:]]
    return (out[None], dx[None], gq, pb, go, ob, g1, s1, gu, ub, gd, db, g2, s2)


def widen(starts, out, dx, gq, go, gu, gd, small, *results):
    C = small.shape[1]
    for source, result in zip((out, dx), results):
        result[...] = source[...]
    results[3][...] = go[...].astype(f32)
    results[5][...] = gd[...].astype(f32)
    for source, result in ((gq, results[2]), (gu, results[4])):
        for o in range(source.shape[0]):
            for p in range(source.shape[2] // C):
                lane = (p * source.shape[0] + o) * C
                result[:, lane:lane + C] = source[o, :, p * C:(p + 1) * C].astype(f32)
    for start, result in zip(starts, results[6:]):
        for i in range(result.shape[1] // C):
            result[0:1, i * C:(i + 1) * C] = small[start + i:start + i + 1, :]


BATCHES = 36
LANDINGS = 112
LOCAL = 32


def fits(mesh):
    return mesh.shape["seq"] == 8 and mesh.shape["fsdp"] == 4


def solution(mesh):
    return jax.shard_map(
        fused_shards if fits(mesh) else shards,
        mesh=mesh,
        in_specs=(
            P("fsdp", "seq", None),
            P("fsdp", "seq", None),
            P("fsdp", None),
            P("fsdp", None),
            P("fsdp"),
            P("fsdp", None),
            P("fsdp"),
            P("fsdp"),
            P("fsdp"),
            P("fsdp", None),
            P("fsdp"),
            P("fsdp", None),
            P("fsdp"),
            P("fsdp"),
            P("fsdp"),
        ),
        out_specs=(
            P("fsdp", "seq", None),
            P("fsdp", "seq", None),
            P("fsdp", None),
            P("fsdp"),
            P("fsdp", None),
            P("fsdp"),
            P("fsdp"),
            P("fsdp"),
            P("fsdp", None),
            P("fsdp"),
            P("fsdp", None),
            P("fsdp"),
            P("fsdp"),
            P("fsdp"),
        ),
        check_vma=False,
    )
```

```python
from functools import partial

import jax
import jax.numpy as jnp
import numpy as np
import math
from types import SimpleNamespace
from jax import lax
from jax.experimental import pallas as pl
from jax.experimental.pallas import tpu as pltpu
from jax.sharding import PartitionSpec as P

HEADS = 16
HEAD_DIM = 64


norm_epsilon = 1e-05


def rotary(values, positions):
    half = values.shape[-1] // 2
    channel = jnp.arange(half).astype(jnp.float32)
    inverse = 10000.0 ** (-2.0 * channel / values.shape[-1])
    angles = positions[:, None] * inverse[None, :]
    cosine = jnp.cos(angles)[:, None, :]
    sine = jnp.sin(angles)[:, None, :]
    first = values[..., :half]
    second = values[..., half:]
    return jnp.concatenate(
        [first * cosine - second * sine, second * cosine + first * sine], axis=-1
    )


def rotary_back(grads, positions):
    unused, pullback = jax.vjp(lambda inner: rotary(inner, positions), grads)
    return pullback(grads)[0]


def norm_forward(values, gain, shift):
    centre = values - jnp.mean(values, axis=-1, keepdims=True)
    inverse_root = lax.rsqrt(jnp.mean(centre * centre, axis=-1, keepdims=True) + norm_epsilon)
    normal = centre * inverse_root
    return (normal * gain + shift, normal, inverse_root)


def norm_backward(incoming, normal, inverse_root, gain):
    gain_grad = jnp.sum(incoming * normal, axis=0)
    shift_grad = jnp.sum(incoming, axis=0)
    scaled = incoming * gain
    inner = (
        scaled
        - jnp.mean(scaled, axis=-1, keepdims=True)
        - normal * jnp.mean(scaled * normal, axis=-1, keepdims=True)
    )
    return (inner * inverse_root, gain_grad, shift_grad)


def shards(
    hidden_in,
    cotangent,
    segment_ids,
    projection,
    projection_bias,
    output_weight,
    output_bias,
    first_gain,
    first_shift,
    up_weight,
    up_bias,
    down_weight,
    down_bias,
    second_gain,
    second_shift,
):
    bf16 = jnp.bfloat16
    f32 = jnp.float32
    tokens = hidden_in[0]
    local_rows = tokens.shape[0]
    width = tokens.shape[1]
    seq_rank = lax.axis_index("seq")
    positions = (seq_rank * local_rows + jnp.arange(local_rows)).astype(f32)
    segments = segment_ids[0]
    scale = HEAD_DIM ** (-0.5)
    attention_full = (
        lax.all_gather(projection.astype(bf16), "fsdp", axis=0, tiled=True),
        lax.all_gather(projection_bias.astype(bf16), "fsdp", axis=0, tiled=True),
        lax.all_gather(output_weight.astype(bf16), "fsdp", axis=0, tiled=True),
        lax.all_gather(output_bias.astype(bf16), "fsdp", axis=0, tiled=True),
        lax.all_gather(first_gain.astype(bf16), "fsdp", axis=0, tiled=True),
        lax.all_gather(first_shift.astype(bf16), "fsdp", axis=0, tiled=True),
    )
    proj_weight = attention_full[0]
    projected = jnp.dot(tokens, proj_weight, preferred_element_type=f32) + attention_full[1].astype(
        f32
    )
    heads = projected.reshape(local_rows, 3, HEADS, HEAD_DIM)
    queries = rotary(heads[:, 0], positions)
    keys = rotary(heads[:, 1], positions)
    stacked = jnp.stack([queries, keys, heads[:, 2]]).astype(bf16)
    spread = lax.all_to_all(stacked, "seq", split_axis=2, concat_axis=1, tiled=True)
    query_all = spread[0]
    key_all = spread[1]
    value_all = spread[2]
    length = query_all.shape[0]
    local_heads = query_all.shape[1]
    block = min(512, length)
    count = length // block
    query_blocks = query_all.reshape(count, block, local_heads, HEAD_DIM)
    segment_blocks = segments.reshape(count, block)

    def scores_of(query_block, segment_block):
        raw = jnp.einsum("qhd,khd->hqk", query_block, key_all, preferred_element_type=f32) * scale
        allowed = segment_block[:, None] == segments[None, :]
        return jnp.where(allowed[None], raw, -1e30)

    def forward_block(pieces):
        query_block, segment_block = pieces
        scores = scores_of(query_block, segment_block)
        row_max = jnp.max(scores, axis=-1, keepdims=True)
        exponent = jnp.exp(scores - row_max)
        total = jnp.sum(exponent, axis=-1, keepdims=True)
        weights = exponent / total
        context = jnp.einsum(
            "hqk,khd->qhd", weights.astype(bf16), value_all, preferred_element_type=f32
        )
        return (context.astype(bf16), (row_max + jnp.log(total))[..., 0])

    context_blocks, log_totals = lax.map(forward_block, (query_blocks, segment_blocks))
    context_heads = context_blocks.reshape(length, local_heads, HEAD_DIM)
    context_tokens = lax.all_to_all(
        context_heads, "seq", split_axis=0, concat_axis=1, tiled=True
    ).reshape(local_rows, width)
    attended = jnp.dot(
        context_tokens, attention_full[2], preferred_element_type=f32
    ) + attention_full[3].astype(f32)
    gain_one = attention_full[4].astype(f32)
    normed_one, normal_one, inverse_one = norm_forward(
        tokens.astype(f32) + attended, gain_one, attention_full[5].astype(f32)
    )
    feed_full = (
        lax.all_gather(up_weight.astype(bf16), "fsdp", axis=0, tiled=True),
        lax.all_gather(up_bias.astype(bf16), "fsdp", axis=0, tiled=True),
        lax.all_gather(down_weight.astype(bf16), "fsdp", axis=0, tiled=True),
        lax.all_gather(down_bias.astype(bf16), "fsdp", axis=0, tiled=True),
        lax.all_gather(second_gain.astype(bf16), "fsdp", axis=0, tiled=True),
        lax.all_gather(second_shift.astype(bf16), "fsdp", axis=0, tiled=True),
    )
    normed_low = normed_one.astype(bf16)
    lifted = jnp.dot(normed_low, feed_full[0], preferred_element_type=f32) + feed_full[1].astype(
        f32
    )
    activated = jax.nn.gelu(lifted, approximate=False).astype(bf16)
    lowered = jnp.dot(activated, feed_full[2], preferred_element_type=f32) + feed_full[3].astype(
        f32
    )
    gain_two = feed_full[4].astype(f32)
    layer_out, normal_two, inverse_two = norm_forward(
        normed_one + lowered, gain_two, feed_full[5].astype(f32)
    )
    feed_back = (
        lax.all_gather(up_weight.astype(bf16), "fsdp", axis=0, tiled=True),
        lax.all_gather(up_bias.astype(bf16), "fsdp", axis=0, tiled=True),
        lax.all_gather(down_weight.astype(bf16), "fsdp", axis=0, tiled=True),
        lax.all_gather(down_bias.astype(bf16), "fsdp", axis=0, tiled=True),
        lax.all_gather(second_gain.astype(bf16), "fsdp", axis=0, tiled=True),
        lax.all_gather(second_shift.astype(bf16), "fsdp", axis=0, tiled=True),
    )
    attention_back = (
        lax.all_gather(projection.astype(bf16), "fsdp", axis=0, tiled=True),
        lax.all_gather(projection_bias.astype(bf16), "fsdp", axis=0, tiled=True),
        lax.all_gather(output_weight.astype(bf16), "fsdp", axis=0, tiled=True),
        lax.all_gather(output_bias.astype(bf16), "fsdp", axis=0, tiled=True),
        lax.all_gather(first_gain.astype(bf16), "fsdp", axis=0, tiled=True),
        lax.all_gather(first_shift.astype(bf16), "fsdp", axis=0, tiled=True),
    )
    grad_two, second_gain_grad, second_shift_grad = norm_backward(
        cotangent[0].astype(f32), normal_two, inverse_two, gain_two
    )
    lowered_grad = grad_two.astype(bf16)
    down_weight_grad = jnp.einsum("tf,td->fd", activated, lowered_grad, preferred_element_type=f32)
    down_bias_grad = jnp.sum(lowered_grad.astype(f32), axis=0)
    active_grad = jnp.einsum("td,fd->tf", lowered_grad, feed_back[2], preferred_element_type=f32)
    unused, gelu_pull = jax.vjp(partial(jax.nn.gelu, approximate=False), lifted)
    lifted_grad = gelu_pull(active_grad)[0].astype(bf16)
    up_weight_grad = jnp.einsum("td,tf->df", normed_low, lifted_grad, preferred_element_type=f32)
    up_bias_grad = jnp.sum(lifted_grad.astype(f32), axis=0)
    normed_grad = grad_two + jnp.einsum(
        "tf,df->td", lifted_grad, feed_back[0], preferred_element_type=f32
    )
    grad_one, first_gain_grad, first_shift_grad = norm_backward(
        normed_grad, normal_one, inverse_one, attention_back[4].astype(f32)
    )
    attended_grad = grad_one.astype(bf16)
    output_weight_grad = jnp.einsum(
        "tc,td->cd", context_tokens, attended_grad, preferred_element_type=f32
    )
    output_bias_grad = jnp.sum(attended_grad.astype(f32), axis=0)
    context_grad = jnp.einsum(
        "td,cd->tc", attended_grad, attention_back[2], preferred_element_type=f32
    ).astype(bf16)
    context_grad = context_grad.reshape(local_rows, HEADS, HEAD_DIM)
    context_grad_heads = lax.all_to_all(
        context_grad, "seq", split_axis=1, concat_axis=0, tiled=True
    )
    grad_blocks = context_grad_heads.reshape(count, block, local_heads, HEAD_DIM)

    def backward_block(carry, pieces):
        key_grad, value_grad = carry
        query_block, segment_block, grad_block, log_block = pieces
        scores = scores_of(query_block, segment_block)
        weights = jnp.exp(scores - log_block[..., None])
        value_grad = value_grad + jnp.einsum(
            "hqk,qhd->khd", weights.astype(bf16), grad_block, preferred_element_type=f32
        )
        weight_grad = jnp.einsum("qhd,khd->hqk", grad_block, value_all, preferred_element_type=f32)
        centre = jnp.sum(weights * weight_grad, axis=-1, keepdims=True)
        score_grad = (weights * (weight_grad - centre)).astype(bf16)
        query_grad = (
            jnp.einsum("hqk,khd->qhd", score_grad, key_all, preferred_element_type=f32) * scale
        )
        key_grad = (
            key_grad
            + jnp.einsum("hqk,qhd->khd", score_grad, query_block, preferred_element_type=f32)
            * scale
        )
        return ((key_grad, value_grad), query_grad)

    zeros_heads = jnp.zeros((length, local_heads, HEAD_DIM), f32)
    (key_grad, value_grad), query_grad = lax.scan(
        backward_block,
        (zeros_heads, zeros_heads),
        (query_blocks, segment_blocks, grad_blocks, log_totals),
    )
    query_grad = query_grad.reshape(length, local_heads, HEAD_DIM)
    stacked_grad = jnp.stack([query_grad, key_grad, value_grad]).astype(bf16)
    token_heads = lax.all_to_all(stacked_grad, "seq", split_axis=1, concat_axis=2, tiled=True)
    query_back = rotary_back(token_heads[0].astype(f32), positions)
    key_back = rotary_back(token_heads[1].astype(f32), positions)
    projected_grad = jnp.stack([query_back, key_back, token_heads[2].astype(f32)], axis=1)
    projected_grad = projected_grad.reshape(local_rows, 3 * width).astype(bf16)
    projection_grad = jnp.einsum("td,te->de", tokens, projected_grad, preferred_element_type=f32)
    projection_bias_grad = jnp.sum(projected_grad.astype(f32), axis=0)
    input_grad = grad_one + jnp.einsum(
        "te,de->td", projected_grad, attention_back[0], preferred_element_type=f32
    )
    every_shard = (
        lax.psum_scatter(
            projection_grad.astype(jnp.bfloat16), "fsdp", scatter_dimension=0, tiled=True
        ).astype(jnp.float32),
        lax.psum_scatter(
            projection_bias_grad.astype(jnp.bfloat16), "fsdp", scatter_dimension=0, tiled=True
        ).astype(jnp.float32),
        lax.psum_scatter(
            output_weight_grad.astype(jnp.bfloat16), "fsdp", scatter_dimension=0, tiled=True
        ).astype(jnp.float32),
        lax.psum_scatter(
            output_bias_grad.astype(jnp.bfloat16), "fsdp", scatter_dimension=0, tiled=True
        ).astype(jnp.float32),
        lax.psum_scatter(
            first_gain_grad.astype(jnp.bfloat16), "fsdp", scatter_dimension=0, tiled=True
        ).astype(jnp.float32),
        lax.psum_scatter(
            first_shift_grad.astype(jnp.bfloat16), "fsdp", scatter_dimension=0, tiled=True
        ).astype(jnp.float32),
        lax.psum_scatter(
            up_weight_grad.astype(jnp.bfloat16), "fsdp", scatter_dimension=0, tiled=True
        ).astype(jnp.float32),
        lax.psum_scatter(
            up_bias_grad.astype(jnp.bfloat16), "fsdp", scatter_dimension=0, tiled=True
        ).astype(jnp.float32),
        lax.psum_scatter(
            down_weight_grad.astype(jnp.bfloat16), "fsdp", scatter_dimension=0, tiled=True
        ).astype(jnp.float32),
        lax.psum_scatter(
            down_bias_grad.astype(jnp.bfloat16), "fsdp", scatter_dimension=0, tiled=True
        ).astype(jnp.float32),
        lax.psum_scatter(
            second_gain_grad.astype(jnp.bfloat16), "fsdp", scatter_dimension=0, tiled=True
        ).astype(jnp.float32),
        lax.psum_scatter(
            second_shift_grad.astype(jnp.bfloat16), "fsdp", scatter_dimension=0, tiled=True
        ).astype(jnp.float32),
    )
    finals = (
        lax.psum(every_shard[0].astype(jnp.bfloat16), "seq").astype(jnp.float32),
        lax.psum(every_shard[1].astype(jnp.bfloat16), "seq").astype(jnp.float32),
        lax.psum(every_shard[2].astype(jnp.bfloat16), "seq").astype(jnp.float32),
        lax.psum(every_shard[3].astype(jnp.bfloat16), "seq").astype(jnp.float32),
        lax.psum(every_shard[4].astype(jnp.bfloat16), "seq").astype(jnp.float32),
        lax.psum(every_shard[5].astype(jnp.bfloat16), "seq").astype(jnp.float32),
        lax.psum(every_shard[6].astype(jnp.bfloat16), "seq").astype(jnp.float32),
        lax.psum(every_shard[7].astype(jnp.bfloat16), "seq").astype(jnp.float32),
        lax.psum(every_shard[8].astype(jnp.bfloat16), "seq").astype(jnp.float32),
        lax.psum(every_shard[9].astype(jnp.bfloat16), "seq").astype(jnp.float32),
        lax.psum(every_shard[10].astype(jnp.bfloat16), "seq").astype(jnp.float32),
        lax.psum(every_shard[11].astype(jnp.bfloat16), "seq").astype(jnp.float32),
    )
    return (
        layer_out.astype(bf16)[None],
        input_grad.astype(bf16)[None],
        finals[0],
        finals[1],
        finals[2],
        finals[3],
        finals[4],
        finals[5],
        finals[6],
        finals[7],
        finals[8],
        finals[9],
        finals[10],
        finals[11],
    )


MESH = pl.DeviceIdType.MESH
NN = (((1,), (0,)), ((), ()))
NT = (((1,), (1,)), ((), ()))
TN = (((0,), (0,)), ((), ()))
f32 = jnp.float32
bf16 = jnp.bfloat16
MASKED = -1e30


def mm(left, right, dims=NN):
    return lax.dot_general(left, right, dims, preferred_element_type=f32)


def block_of(index, size):
    return pl.ds(pl.multiple_of(index * size, size), size)


def flip(bit, other):
    return bit + other - 2 * bit * other


def fused_layer(sizes, *refs):
    r = SimpleNamespace(**dict(zip(sizes.names, refs)))
    T, D, L, F = sizes.T, sizes.D, sizes.L, sizes.F
    S, Z = 8, 4
    KW = D // Z
    UZ = F // Z
    C = 128
    T2 = 2 * T
    first_row = sizes.first_row
    ssem, rsem, lsem = r.ssem, r.rsem, r.lsem

    s = lax.axis_index("seq")
    z = lax.axis_index("fsdp")
    core, xbit, ybit = s % 2, (s // 2) % 2, s // 4
    zlow, zhigh = z % 2, z // 2

    def ps(k):
        return flip(core, k % 2) + 2 * flip(xbit, (k // 2) % 2) + 4 * flip(ybit, k // 4)

    def pz(k):
        return flip(zlow, k % 2) + 2 * flip(zhigh, k // 2)

    def chip_of(j):
        return flip(xbit, j % 2) + 2 * flip(ybit, j // 2)

    counter = [0, 0, 0]
    closing = []

    def take(which, n=1):
        counter[which] += n
        return counter[which] - n

    def landings(n=1):
        return take(0, n)

    def size(ref):
        return math.prod(ref.shape) * jnp.dtype(ref.dtype).itemsize

    def extent(n):
        if n <= size(r.c_f):
            return r.c_f.at[pl.ds(0, n * L // size(r.c_f))]
        return r.y_all.at[pl.ds(0, n * L // size(r.y_all))]

    def arrived(ref, slot):
        pltpu.make_async_copy(ref, ref, rsem.at[slot]).wait()

    class Batch:
        def __init__(self, count, like):
            self.slot, self.bytes, self.open = take(1), count * size(like), True
            closing.append(self)

        def send(self, src, dst, slot, dev):
            pltpu.make_async_remote_copy(
                src_ref=src, dst_ref=dst, send_sem=ssem.at[self.slot], recv_sem=rsem.at[slot],
                device_id=dev, device_id_type=MESH).start()

        def close(self):
            if self.open:
                everything = extent(self.bytes)
                pltpu.make_async_copy(everything, everything, ssem.at[self.slot]).wait()
            self.open = False

    def local(src, dst):
        copy = pltpu.make_async_copy(src, dst, lsem.at[take(2)])
        copy.start()
        return copy

    class Gather:
        def __init__(self, place, at_once=True):
            self.place, self.at_once = place, at_once
            self.batch = Batch(7, place(0))
            self.near, self.across = landings(4), landings(2)
            self.other = landings() if at_once else landings(4)

        def part(self, ref, i):
            n = ref.shape[0] // 2
            return ref.at[pl.ds(i * n, n)]

        def start(self, src=None):
            mine = self.place(s)
            src = mine if src is None else src
            for slot, half, k in ((0, 0, 2), (3, 1, 4), (1, 1, 2), (2, 0, 4)):
                self.batch.send(self.part(src, half), self.part(mine, half), self.near + slot, (ps(k), z))
            self.batch.send(src, mine, self.other, (ps(1), z))

        def to_partner(self, k):
            there = self.place(ps(k))
            self.batch.send(there, there, self.other + (0 if self.at_once else k // 2), (ps(1), z))

        def pass_near(self):
            along_x, along_y = self.place(ps(2)), self.place(ps(4))
            first, second = self.part(along_x, 0), self.part(along_y, 1)
            arrived(first, self.near)
            self.batch.send(first, first, self.across, (ps(4), z))
            arrived(second, self.near + 3)
            self.batch.send(second, second, self.across + 1, (ps(2), z))
            arrived(self.part(along_x, 1), self.near + 1)
            self.to_partner(2)
            arrived(self.part(along_y, 0), self.near + 2)
            self.to_partner(4)

        def pass_far(self):
            far = self.place(ps(6))
            arrived(self.part(far, 0), self.across)
            arrived(self.part(far, 1), self.across + 1)
            self.to_partner(6)

        def pass_all(self):
            self.pass_near()
            self.pass_far()

        def wait(self, k=None):
            if self.at_once:
                arrived(extent(4 * size(self.place(0))), self.other)
            else:
                arrived(self.place(ps(k)), self.other + k // 2)

    class Spread:
        def __init__(self, place):
            self.place, self.batch, self.base = place, Batch(3, place(0)), landings(3)

        def start(self, *which):
            mine = self.place(z)
            for k in which or (2, 1):
                self.batch.send(mine, mine, self.base + k - 1, (s, pz(k)))

        def pass_on(self):
            there = self.place(pz(2))
            arrived(there, self.base + 1)
            self.batch.send(there, there, self.base + 2, (s, pz(1)))

        def wait(self):
            for k in (1, 3):
                arrived(self.place(pz(k)), self.base + k - 1)

        def wait_all(self):
            for k in (1, 2, 3):
                arrived(self.place(pz(k)), self.base + k - 1)

    class Fold:
        def __init__(self, parts, landing, passing):
            self.parts, self.landing, self.passing = parts, landing, passing
            self.batch, self.base = Batch(3, passing), landings(3)

        def start(self):
            self.batch.send(self.parts.at[pz(3)], self.landing.at[1], self.base + 1, (s, pz(1)))
            self.batch.send(self.parts.at[pz(1)], self.landing.at[0], self.base, (s, pz(1)))

        def middle(self):
            arrived(self.landing.at[1], self.base + 1)
            self.passing[...] = (self.parts[pz(2)].astype(f32) + self.landing[1].astype(f32)).astype(bf16)
            self.batch.send(self.passing, self.landing.at[2], self.base + 2, (s, pz(2)))

        def finish(self):
            arrived(self.landing.at[0], self.base)
            arrived(self.landing.at[2], self.base + 2)
            return (self.parts[z].astype(f32) + self.landing[0].astype(f32)
                    + self.landing[2].astype(f32)).astype(bf16)

    class Scatter:
        def __init__(self, parts, low, mid, high):
            self.parts, self.low, self.mid, self.high = parts, low, mid, high
            self.batch, self.base, self.far, self.last = Batch(7, mid.at[0]), landings(4), landings(2), landings()

        def half(self, ref, j, i):
            return ref.at[j, :, pl.ds(i * (D // 2), D // 2)]

        def send(self, j, i, slot, k):
            self.batch.send(self.half(self.mid, j, i), self.half(self.high, j, i), slot, (ps(k), z))

        def pair(self, j):
            self.batch.send(self.parts.at[j, block_of(1 - core, T)], self.low.at[j], self.base + j, (ps(1), z))

        def onward(self, j):
            arrived(self.low.at[j], self.base + j)
            own = self.parts[j, block_of(core, T), :].astype(f32)
            self.mid[j] = (own + self.low[j].astype(f32)).astype(bf16)
            if j == 1:
                self.send(1, 0, self.last, 2)
            elif j == 2:
                self.send(2, 1, self.last, 4)
            else:
                self.send(3, 0, self.far, 2)
                self.send(3, 1, self.far + 1, 4)

        def cross(self):
            for j, i, k in ((2, 0, 4), (1, 1, 2)):
                arrived(self.half(self.high, 3, i), self.far + i)
                ref = self.half(self.mid, j, i)
                ref[...] = (ref[...].astype(f32) + self.half(self.high, 3, i)[...].astype(f32)).astype(bf16)
                self.send(j, i, self.last, k)

        def ready(self):
            arrived(self.low.at[0], self.base)
            arrived(self.high.at[pl.ds(1, 2)], self.last)

        def rows(self, at, n):
            own = self.parts[0, pl.ds(pl.multiple_of(core * T + at, n), n), :].astype(f32)
            total = own + self.low[0, pl.ds(at, n), :].astype(f32)
            for j in (1, 2):
                total = total + self.high[j, pl.ds(at, n), :].astype(f32)
            return total

    class Share:
        def __init__(self, count, like):
            self.count, self.batch, self.slot, self.bytes = count, Batch(count, like), landings(), count * size(like)

        def plane(self, src, dst):
            for k in (6, 7, 2, 3, 4, 5, 1):
                self.batch.send(src(ps(k)), dst, self.slot, (ps(k), z))

        def column(self, src, dst):
            for k in (2, 3, 1):
                self.batch.send(src, dst, self.slot, (s, pz(k)))

        def wait(self):
            arrived(extent(self.bytes), self.slot)

    def loop(count, body, unroll=1):
        def step(i, carry):
            body(i)
            return carry
        lax.fori_loop(0, count, step, 0, unroll=unroll)

    def at(i, n):
        return pl.multiple_of(i * n, n)

    def turn(src, dst):
        def one(i):
            dst[:, pl.ds(at(i, T), T)] = jnp.transpose(src[pl.ds(at(i, T), T), :])
        loop(L // T, one)

    vec, vecg = r.vec, r.vecg

    OUTPUT_BIAS, FIRST_GAIN, FIRST_SHIFT, DOWN_BIAS, SECOND_GAIN, SECOND_SHIFT, PROJECTION_BIAS, UP_BIAS = range(8)
    wide = ((first_row.output_bias, OUTPUT_BIAS), (first_row.first_gain, FIRST_GAIN),
            (first_row.first_shift, FIRST_SHIFT), (first_row.down_bias, DOWN_BIAS),
            (first_row.second_gain, SECOND_GAIN), (first_row.second_shift, SECOND_SHIFT))

    def row(i, width=D):
        return vec[i:i + 1, :width]

    lanes = lax.broadcasted_iota(jnp.int32, (T, C), 1)
    low_head = lanes < HEAD_DIM

    def swapped(w):
        low_half = lax.broadcasted_iota(jnp.int32, w.shape, 1) % HEAD_DIM < HEAD_DIM // 2
        return jnp.where(low_half, pltpu.roll(w, C - HEAD_DIM // 2, 1), pltpu.roll(w, HEAD_DIM // 2, 1))

    def stacked(w):
        nothing = jnp.zeros_like(w)
        return jnp.concatenate([jnp.where(low_head, w, nothing), jnp.where(low_head, nothing, w)], axis=0)

    def unstacked(w):
        return jnp.where(low_head, w[:T], w[T:])

    barrier = pltpu.get_barrier_semaphore()
    for k in range(1, S):
        pl.semaphore_signal(barrier, inc=1, device_id=(ps(k), z), device_id_type=MESH)
    for k in range(1, Z):
        pl.semaphore_signal(barrier, inc=1, device_id=(s, pz(k)), device_id_type=MESH)
    x_ref, ct_ref = r.v_x, r.v_ct
    x_load = local(r.x, x_ref)
    wo_load = local(r.wo.at[:, block_of(s, C)], r.st_wo)
    proj_loads = [local(r.proj.at[:, block_of(i * (D // C) + s, C)], r.st_proj.at[:, pl.ds(i * C, C)])
                  for i in range(3)]
    raw = ((r.b_projection, r.v_projection, first_row.projection_bias), (r.b_output, r.v_output, first_row.output_bias),
           (r.gain1, r.v_gain1, first_row.first_gain), (r.shift1, r.v_shift1, first_row.first_shift),
           (r.b_up, r.v_up, first_row.up_bias), (r.b_down, r.v_down, first_row.down_bias),
           (r.gain2, r.v_gain2, first_row.second_gain), (r.shift2, r.v_shift2, first_row.second_shift))
    raw_loads = [local(source, ref) for source, ref, _ in raw]
    seg_load = local(r.seg, r.v_seg)
    up_loads = [local(r.up.at[:, block_of(i * (D // C) + s, C)], r.st_up.at[:, pl.ds(i * C, C)])
                for i in range(Z)]
    dn_load = local(r.dn.at[block_of(s, UZ), :], r.st_dn)
    late_loads = [local(r.cos, r.v_cos), local(r.sin, r.v_sin), local(r.ct, ct_ref)]
    cos_ref, sin_ref = r.v_cos, r.v_sin

    x_all, w_qkv, w_o, w_up, w_dn = r.x_all, r.w_qkv, r.w_o, r.w_up, r.w_dn
    gather_x = Gather(lambda o: x_all.at[block_of(o, T)])
    spread_qkv = Spread(lambda p: w_qkv.at[block_of(p, KW)])
    spread_o = Spread(lambda p: w_o.at[block_of(p, KW), block_of(s, C)])
    spread_up = Spread(lambda p: w_up.at[block_of(p, KW)])
    spread_dn = Spread(lambda p: w_dn.at[block_of(p, UZ)])
    gather_o = Gather(lambda o: w_o.at[:, block_of(o, C)])
    wo_load.wait()
    w_o[block_of(z, KW), block_of(s, C)] = r.st_wo[...].astype(bf16)
    for copy in proj_loads:
        copy.wait()
    w_qkv[block_of(z, KW), :] = r.st_proj[...].astype(bf16)
    x_load.wait()
    pl.semaphore_wait(barrier, S + Z - 2)
    spread_o.start(2, 3, 1)
    spread_qkv.start()
    gather_x.start(x_ref)

    small, small_all, seg_c, seg_r = r.small, r.small_all, r.seg_c, r.seg_r
    for copy, (_, ref, start) in zip(raw_loads, raw):
        copy.wait()
        if ref.shape[1] == C:
            small[start:start + ref.shape[0], :] = ref[...].astype(bf16).astype(f32)
        else:
            for i in range(ref.shape[1] // C):
                small[start + i:start + i + 1, :] = ref[0:1, i * C:(i + 1) * C].astype(bf16).astype(f32)
    x_all[block_of(s, T), :] = x_ref[...]
    vecg[...] = jnp.zeros((8, D), f32)
    seg_load.wait()
    seg_r[...] = jnp.broadcast_to(r.v_seg[...].astype(f32), (8, L))

    def seg_turn(i):
        here = pl.ds(at(i, T), T)
        seg_c[here, :] = jnp.transpose(jnp.broadcast_to(seg_r[0:1, here], (T, T)))
    loop(L // T, seg_turn)
    for copy in up_loads:
        copy.wait()
    w_up[block_of(z, KW), :] = r.st_up[...].astype(bf16)
    dn_load.wait()
    w_dn[block_of(z, UZ), :] = r.st_dn[...].astype(bf16)
    share_small = Share(3, small)
    small_all[z] = small[...]

    gather_x.pass_near()
    spread_o.wait_all()
    gather_o.start()
    gather_x.pass_far()
    gather_x.wait()
    spread_qkv.pass_on()
    share_small.column(small, small_all.at[z])
    spread_up.start()
    x_t = r.x_t
    turn(x_all, x_t)
    for copy in late_loads:
        copy.wait()
    gather_o.pass_near()
    spread_qkv.wait()
    share_small.wait()
    for p in range(Z):
        for start, i in wide:
            for half in range(KW // C):
                at_row = start + half
                lane = (p * (KW // C) + half) * C
                vec[i:i + 1, lane:lane + C] = small_all[p, at_row:at_row + 1, :]
        vec[7:8, p * C:(p + 1) * C] = small_all[p, pl.ds(first_row.up_bias + s, 1), :]
    per = 3 * D // (C * Z)
    for t in range(3):
        number = t * (D // C) + s
        vec[6:7, t * C:(t + 1) * C] = small_all[number // per, pl.ds(first_row.projection_bias + number % per, 1), :]

    q_ref, k_ref, v_ref = r.q, r.k, r.v
    scale = HEAD_DIM ** -0.5

    def project(i):
        here = pl.ds(at(i, T2), T2)
        out = mm(x_all[here, :], w_qkv[...]) + row(PROJECTION_BIAS, 3 * C)
        cosine, sine = cos_ref[here, :], sin_ref[here, :]
        q0, k0 = out[:, :C], out[:, C:2 * C]
        q_ref[here, :] = ((q0 * cosine + swapped(q0) * sine).astype(bf16).astype(f32) * scale).astype(bf16)
        k_ref[here, :] = (k0 * cosine + swapped(k0) * sine).astype(bf16)
        v_ref[here, :] = out[:, 2 * C:].astype(bf16)
    loop(L // T2, project)
    gather_o.pass_far()

    lse, c_f, c_heads, c_tok = r.lse, r.c_f, r.c_heads, r.c_tok
    R = 16

    def same_document(here):
        return jnp.tile(seg_c[here, :], (1, L // C)) == seg_r[0:1, :]

    def both(w):
        return jnp.concatenate([w, w], axis=0)

    def attend(o):
        here = block_of(o, T)
        score = jnp.where(both(same_document(here)), mm(stacked(q_ref[here, :]), k_ref[...], NT), MASKED)
        top = jnp.max(score, axis=-1, keepdims=True)
        power = jnp.exp(score - top)
        total = jnp.sum(power, axis=-1, keepdims=True)
        context = unstacked(mm(power.astype(bf16), v_ref[...]) * (1.0 / total))
        c_f[here, :] = context
        c_heads[here, :] = context.astype(bf16)
        logs = jnp.broadcast_to(top + jnp.log(total), (T2, C))
        for h in range(2):
            lse[h:h + 1, here] = jnp.transpose(logs[h * T:(h + 1) * T, :])[0:1, :]

    share_c = Share(7, c_heads.at[pl.ds(0, T)])

    def attend_and_send(i):
        k = 7 - i
        attend(ps(k))

        @pl.when(k > 0)
        def _():
            share_c.batch.send(c_heads.at[block_of(ps(k), T)], c_tok.at[:, block_of(s, C)], share_c.slot, (ps(k), z))
    loop(8, attend_and_send)
    spread_up.pass_on()
    spread_dn.start()
    c_tok[:, block_of(s, C)] = c_heads[block_of(s, T), :]
    gather_o.wait()
    share_c.wait()

    a_buf = r.a_buf
    a_buf[...] = mm(c_tok[...], w_o[...])
    n1, y1, r1, y_all = r.n1, r.y1, r.r1, r.y_all

    def norm(h):
        centre = h - jnp.mean(h, axis=-1, keepdims=True)
        root = lax.rsqrt(jnp.mean(centre * centre, axis=-1, keepdims=True) + norm_epsilon)
        return centre * root, root

    def first_norm(i):
        rows = pl.ds(at(i, R), R)
        normal, root = norm(x_ref[rows, :].astype(f32) + a_buf[rows, :] + row(OUTPUT_BIAS))
        out = normal * row(FIRST_GAIN) + row(FIRST_SHIFT)
        n1[rows, :] = normal
        r1[rows, :] = jnp.broadcast_to(root, (R, C))
        y1[rows, :] = out
        y_all[pl.ds(pl.multiple_of(s * T + i * R, R), R), :] = out.astype(bf16)
    loop(T // R, first_norm, 4)
    gather_y = Gather(lambda o: y_all.at[block_of(o, T)], False)
    gather_y.start()
    c_all = r.c_all
    gather_c = Gather(lambda o: c_all.at[block_of(o, T)])
    c_all[block_of(s, T), :] = c_tok[...]

    u_buf, g_ref, d_ref, du_ref, dz_all = r.u_buf, r.g, r.d, r.du, r.dz_all
    parts, mid = r.parts, r.mid
    spread_up.wait()
    E = 32

    def lift(j):
        q = chip_of(j)
        u_buf[...] = mm(y_all[block_of(q, T2), :], w_up[...])

        def chunk(i):
            rows = pl.ds(at(i, E), E)
            there = pl.ds(pl.multiple_of(q * T2 + i * E, E), E)
            u = u_buf[rows, :] + row(UP_BIAS, F)
            share = 0.5 + 0.5 * lax.erf(u * (0.5 ** 0.5))
            g_ref[there, :] = (u * share).astype(bf16)
            d_ref[there, :] = share + u * (jnp.exp(-0.5 * u * u) * 0.3989422804014327)
        loop(T2 // E, chunk)

    def lower(j):
        parts[j] = mm(g_ref[block_of(chip_of(j), T2), :], w_dn[...]).astype(bf16)

    fold_z = Scatter(parts, r.low0, mid, r.high0)
    y_t, g_t = r.y_t, r.g_t
    gather_y.wait(1)
    lift(0)
    gather_y.pass_near()
    gather_y.wait(3)
    lift(1)
    gather_y.wait(5)
    lift(2)
    spread_dn.pass_on()
    gather_y.pass_far()
    gather_c.start(c_tok)
    gather_y.wait(7)
    lift(3)
    turn(y_all, y_t)
    turn(g_ref, g_t)
    spread_dn.wait()
    for j in (3, 1, 2, 0):
        lower(j)
        fold_z.pair(j)
        if j == 1:
            fold_z.onward(3)
        if j == 2:
            fold_z.onward(1)
    fold_z.onward(2)
    fold_z.cross()
    gather_c.pass_near()
    fold_z.ready()

    dh2, out_ref = r.dh2, r.v_out

    def add_row(i, value):
        vecg[i:i + 1, :] = vecg[i:i + 1, :] + jnp.sum(value, axis=0, keepdims=True)

    def norm_back(incoming, normal, root, gain):
        scaled = incoming * gain
        return root * (scaled - jnp.mean(scaled, axis=-1, keepdims=True)
                       - normal * jnp.mean(scaled * normal, axis=-1, keepdims=True))

    def second_norm(i):
        start = at(i, R)
        rows = pl.ds(start, R)
        normal, root = norm(y1[rows, :] + fold_z.rows(start, R) + row(DOWN_BIAS))
        out_ref[rows, :] = (normal * row(SECOND_GAIN) + row(SECOND_SHIFT)).astype(bf16)
        e = ct_ref[rows, :].astype(f32)
        grad = norm_back(e, normal, root, row(SECOND_GAIN))
        dh2[rows, :] = grad
        dz = grad.astype(bf16)
        dz_all[pl.ds(pl.multiple_of(s * T + i * R, R), R), :] = dz
        add_row(3, dz.astype(f32))
        add_row(4, e * normal)
        add_row(5, e)
    loop(T // R, second_norm, 2)
    outs = [local(out_ref, r.out)]
    gather_dz = Gather(lambda o: dz_all.at[block_of(o, T)], False)
    gather_dz.start()
    fold_z.batch.close()

    colg = r.colg
    colg[...] = jnp.zeros((8, F), f32)

    def unlower(j):
        q = chip_of(j)
        u_buf[...] = mm(dz_all[block_of(q, T2), :], w_dn[...], NT)

        def chunk(i):
            rows = pl.ds(at(i, E), E)
            there = pl.ds(pl.multiple_of(q * T2 + i * E, E), E)
            du = (u_buf[rows, :] * d_ref[there, :]).astype(bf16)
            du_ref[there, :] = du
            colg[0:1, :] = colg[0:1, :] + jnp.sum(du.astype(f32), axis=0, keepdims=True)
        loop(T2 // E, chunk)

    def unlift(j):
        parts[j] = mm(du_ref[block_of(chip_of(j), T2), :], w_up[...], NT).astype(bf16)

    fold_y = Scatter(parts, r.low1, mid, r.high1)
    gd_part, gu_part = r.gd_part, r.gu_part
    fold_dn = Fold(gd_part, r.gd_land, r.gd_pass)
    fold_up = Fold(gu_part, r.gu_land, r.gu_pass)

    def down_grad(k):
        gd_part[pz(k)] = mm(g_t[block_of(pz(k), UZ), :], dz_all[...]).astype(bf16)

    def up_grad(k):
        gu_part[pz(k)] = mm(y_t[block_of(pz(k), KW), :], du_ref[...]).astype(bf16)

    gather_c.pass_far()
    gather_dz.wait(1)
    unlower(0)
    unlift(0)
    fold_y.pair(0)
    gather_dz.pass_near()
    gather_dz.wait(3)
    unlower(1)
    unlift(1)
    fold_y.pair(1)
    gather_dz.wait(5)
    unlower(2)
    fold_y.onward(1)
    unlift(2)
    fold_y.pair(2)
    gather_dz.pass_far()
    fold_y.onward(2)
    gather_dz.wait(7)
    unlower(3)
    unlift(3)
    fold_y.pair(3)
    down_grad(1)
    down_grad(3)
    fold_dn.start()
    fold_y.onward(3)

    up_grad(1)
    up_grad(3)
    down_grad(2)
    fold_y.cross()
    down_grad(0)
    up_grad(2)
    up_grad(0)
    gather_c.wait()
    fold_y.ready()

    dh1, da = r.dh1, r.da

    def first_back(i):
        start = at(i, R)
        rows = pl.ds(start, R)
        incoming = dh2[rows, :] + fold_y.rows(start, R)
        normal = n1[rows, :]
        grad = norm_back(incoming, normal, r1[rows, 0:1], row(FIRST_GAIN))
        dh1[rows, :] = grad
        low = grad.astype(bf16)
        da[rows, :] = low
        add_row(0, low.astype(f32))
        add_row(1, incoming * normal)
        add_row(2, incoming)
    loop(T // R, first_back, 2)
    fold_y.batch.close()

    dc_tok, dc = r.dc_tok, r.dc
    dc_tok[...] = mm(da[...], w_o[...], NT).astype(bf16)
    share_dc = Share(7, dc.at[pl.ds(0, T)])
    share_dc.plane(lambda o: dc_tok.at[:, block_of(o, C)], dc.at[block_of(s, T)])
    dc[block_of(s, T), :] = dc_tok[:, block_of(s, C)]
    da_cols = r.da_cols
    share_da = Share(7, da_cols.at[pl.ds(0, T)])
    share_da.plane(lambda o: da.at[:, block_of(o, C)], da_cols.at[block_of(s, T)])
    da_cols[block_of(s, T), :] = da[:, block_of(s, C)]
    vec_all = r.vec_all
    share_vec = Share(7, vecg)
    share_vec.plane(lambda o: vecg, vec_all.at[s])
    fold_dn.middle()
    fold_up.start()
    share_dc.wait()

    delta, dq, dproj = r.delta, r.dq, r.dproj

    def deltas(i):
        here = pl.ds(at(i, T), T)
        turned = jnp.transpose(dc[here, :].astype(f32) * c_f[here, :])
        delta[0:1, here] = jnp.sum(turned[:HEAD_DIM], axis=0, keepdims=True)
        delta[1:2, here] = jnp.sum(turned[HEAD_DIM:], axis=0, keepdims=True)
        dq[here, :] = jnp.zeros((T, C), f32)
    loop(L // T, deltas)

    def attend_back(i):
        here = pl.ds(at(i, T), T)
        same = same_document(here)
        k_here, v_here = k_ref[here, :], v_ref[here, :]
        keys, values, slopes = [], [], []
        for h in range(2):
            own = low_head if h == 0 else jnp.logical_not(low_head)
            nothing = jnp.zeros_like(k_here)
            key = jnp.where(own, k_here, nothing)
            weight = jnp.exp(jnp.where(same, mm(key, q_ref[...], NT), MASKED) - lse[h:h + 1, :])
            slope = mm(jnp.where(own, v_here, nothing), dc[...], NT) - delta[h:h + 1, :]
            slopes.append((weight * slope).astype(bf16))
            values.append(mm(weight.astype(bf16), dc[...]))
            keys.append(key)
        dv = jnp.where(low_head, values[0], values[1]).astype(bf16)
        dk = jnp.where(low_head, mm(slopes[0], q_ref[...]), mm(slopes[1], q_ref[...])).astype(bf16).astype(f32)
        dproj[here, 2 * C:] = dv
        dproj[here, C:2 * C] = (dk * cos_ref[here, :] - swapped(dk) * sin_ref[here, :]).astype(bf16)
        dq[...] = dq[...] + mm(jnp.concatenate(slopes, axis=0), jnp.concatenate(keys, axis=0), TN)

    gd_all, gu_all, go_all, gqk_all, gv_all = r.gd_all, r.gu_all, r.go_all, r.gqk_all, r.gv_all
    gather_gd = Gather(lambda o: gd_all.at[block_of(o, UZ)])
    gather_gu = Gather(lambda o: gu_all.at[o])
    gather_go = Gather(lambda o: go_all.at[:, block_of(o, C)])
    gather_gqk = Gather(lambda o: gqk_all.at[o])
    gather_gv = Gather(lambda o: gv_all.at[o])
    go_part = r.go_part
    fold_o = Fold(go_part, r.go_land, r.go_pass)

    def out_grad(k):
        go_part[pz(k)] = mm(c_all[:, block_of(pz(k), KW)], da_cols[...], TN).astype(bf16)

    def attend_back_and_fold(i):
        attend_back(i)

        @pl.when(i == 1)
        def _():
            share_da.wait()
            out_grad(1)
            out_grad(3)
            fold_o.start()

        @pl.when(i == 3)
        def _():
            out_grad(2)
            out_grad(0)
    loop(L // T, attend_back_and_fold)

    def dq_rows(i):
        here = pl.ds(at(i, T), T)
        whole = (dq[here, :] * scale).astype(bf16).astype(f32)
        dproj[here, :C] = (whole * cos_ref[here, :] - swapped(whole) * sin_ref[here, :]).astype(bf16)
        colg[1:2, :3 * C] = colg[1:2, :3 * C] + jnp.sum(dproj[here, :].astype(f32), axis=0, keepdims=True)
    loop(L // T, dq_rows)

    gqk_part, gv_part = r.gqk_part, r.gv_part
    fold_qk = Fold(gqk_part, r.gqk_land, r.gqk_pass)
    fold_v = Fold(gv_part, r.gv_land, r.gv_pass)

    def projection_grad(k):
        grad = mm(x_t[block_of(pz(k), KW), :], dproj[...]).astype(bf16)
        gqk_part[pz(k)] = grad[:, :2 * C]
        gv_part[pz(k)] = grad[:, 2 * C:]
    projection_grad(3)
    projection_grad(1)
    fold_qk.start()
    gd_all[block_of(s, UZ), :] = fold_dn.finish()
    gather_gd.start()
    fold_x = Scatter(parts, r.low2, mid, r.high2)

    def unproject(j):
        parts[j] = mm(dproj[block_of(chip_of(j), T2), :], w_qkv[...], NT).astype(bf16)
        fold_x.pair(j)
    unproject(3)
    unproject(1)
    fold_x.onward(3)
    fold_up.middle()
    fold_v.start()
    unproject(2)
    fold_x.onward(1)
    unproject(0)
    fold_x.onward(2)
    projection_grad(2)
    projection_grad(0)
    fold_x.cross()
    gather_gd.pass_near()
    col_z = r.col_z
    share_col = Share(3, colg)
    share_col.column(colg, col_z.at[z])
    col_z[z] = colg[...]
    vec_all[s] = vecg[...]
    share_vec.wait()
    vec_plane, vec_z = r.vec_plane, r.vec_z
    total = vec_all[0]
    for o in range(1, S):
        total = total + vec_all[o]
    vec_plane[...] = total
    share_sum = Share(3, vec_plane)
    share_sum.column(vec_plane, vec_z.at[z])
    vec_z[z] = total
    fold_o.middle()
    fold_qk.middle()
    gather_gd.pass_far()
    fold_x.ready()
    dx_ref = r.v_dx

    def input_back(i):
        start = at(i, R)
        rows = pl.ds(start, R)
        dx_ref[rows, :] = (dh1[rows, :] + fold_x.rows(start, R)).astype(bf16)
    loop(T // R, input_back, 2)
    outs.append(local(dx_ref, r.dx))
    gu_all[s] = fold_up.finish()
    gather_gu.start()
    fold_v.middle()
    go_all[:, block_of(s, C)] = fold_o.finish()
    gather_go.start()
    gather_gd.wait()
    outs.append(local(gd_all, r.gd))
    share_col.wait()
    col_all, col_sum = r.col_all, r.col_sum
    col_sum[...] = col_z[0] + col_z[1] + col_z[2] + col_z[3]
    share_cols = Share(7, col_sum)
    share_cols.plane(lambda o: col_sum, col_all.at[s])
    col_all[s] = col_sum[...]
    gather_gu.pass_near()
    gqk_all[s] = fold_qk.finish()
    gather_gqk.start()
    gather_go.pass_near()
    gather_gu.pass_far()
    gv_all[s] = fold_v.finish()
    gather_gv.start()
    gather_go.pass_far()
    gather_gu.wait()
    outs.append(local(gu_all, r.gu))
    gather_go.wait()
    outs.append(local(go_all, r.go))

    share_sum.wait()
    share_cols.wait()
    vec_sum = r.vec_sum
    vec_sum[...] = vec_z[0] + vec_z[1] + vec_z[2] + vec_z[3]
    gsm = r.v_gsm
    gsm[...] = jnp.zeros(gsm.shape, f32)
    for start, i in wide:
        for half in range(KW // C):
            at_row = start + half
            gsm[at_row:at_row + 1, :] = vec_sum[i:i + 1, block_of(z * (KW // C) + half, C)]
    for o in range(S):
        at_row = first_row.up_bias + o
        gsm[at_row:at_row + 1, :] = col_all[o, 0:1, block_of(z, C)]
    for i in range(per):
        number = z * per + i
        at_row = first_row.projection_bias + i
        gsm[at_row:at_row + 1, :] = col_all[number % S, 1:2, block_of(number // S, C)]
    outs.append(local(gsm, r.gsm))
    gather_gqk.pass_near()
    gather_gv.pass_near()
    gather_gqk.pass_far()
    gather_gv.pass_far()
    gather_gqk.wait()
    outs.append(local(gqk_all, r.gqk))
    gather_gv.wait()
    outs.append(local(gv_all, r.gv))
    for copy in outs:
        copy.wait()
    for batch in closing:
        batch.close()
    assert counter[0] <= LANDINGS and counter[1] <= BATCHES and counter[2] <= LOCAL, counter


def fused_shards(*args):
    (hidden_in, cotangent, segment_ids, projection, projection_bias, output_weight, output_bias, first_gain,
     first_shift, up_weight, up_bias, down_weight, down_bias, second_gain, second_shift) = args
    T, D = hidden_in.shape[1:]
    L = segment_ids.shape[1]
    KW = projection.shape[0]
    F = up_weight.shape[1] // 8
    C, Z = 128, 4
    UZ = F // Z
    small = dict(projection_bias=projection_bias, output_bias=output_bias, first_gain=first_gain,
                 first_shift=first_shift, up_bias=up_bias, down_bias=down_bias, second_gain=second_gain,
                 second_shift=second_shift)
    starts, at_row = {}, 0
    for name, value in small.items():
        starts[name] = at_row
        at_row += value.shape[0] // C
    rows = -(-at_row // 8) * 8
    half = HEAD_DIM // 2
    inverse = np.float32(10000.0) ** (np.float32(-2.0) * np.arange(half, dtype=np.float32) / np.float32(HEAD_DIM))
    angles = np.arange(L, dtype=np.float32)[:, None] * inverse.astype(np.float32)[None, :]
    cosine = np.tile(np.cos(angles), (1, C // half))
    sine = np.tile(np.concatenate([-np.sin(angles), np.sin(angles)], axis=1), (1, C // HEAD_DIM))

    inputs = dict(x=hidden_in[0], ct=cotangent[0], seg=segment_ids, cos=jnp.asarray(cosine), sin=jnp.asarray(sine),
                  b_projection=projection_bias.reshape(-1, C), b_output=output_bias[None], gain1=first_gain[None],
                  shift1=first_shift[None], b_up=up_bias[None], b_down=down_bias[None], gain2=second_gain[None],
                  shift2=second_shift[None], proj=projection, wo=output_weight, up=up_weight, dn=down_weight)
    outputs = dict(out=((T, D), bf16), dx=((T, D), bf16), gsm=((rows, C), f32), gqk=((8, KW, 2 * C), bf16), gv=((8, KW, C), bf16),
                   go=((KW, D), bf16), gu=((8, KW, F), bf16), gd=((8 * UZ, D), bf16))
    landed = dict(v_x=inputs["x"], v_ct=inputs["ct"], v_seg=segment_ids, v_cos=inputs["cos"], v_sin=inputs["sin"],
                  v_projection=inputs["b_projection"], v_output=inputs["b_output"], v_gain1=inputs["gain1"],
                  v_shift1=inputs["shift1"], v_up=inputs["b_up"], v_down=inputs["b_down"], v_gain2=inputs["gain2"],
                  v_shift2=inputs["shift2"])
    PART = (4, T, D)
    scratch = {name: (value.shape, value.dtype) for name, value in landed.items()}
    scratch.update(
        v_out=((T, D), bf16), v_dx=((T, D), bf16), v_gsm=((rows, C), f32),
        x_all=((L, D), bf16), x_t=((D, L), bf16), w_qkv=((D, 3 * C), bf16), st_proj=((KW, 3 * C), f32),
        w_o=((D, D), bf16), st_wo=((KW, C), f32), w_up=((D, F), bf16), st_up=((KW, F), f32),
        w_dn=((F, D), bf16), st_dn=((UZ, D), f32), small_all=((Z, rows, C), f32), vec=((8, D), f32),
        vecg=((8, D), f32), q=((L, C), bf16), k=((L, C), bf16), v=((L, C), bf16),
        seg_r=((8, L), f32), seg_c=((L, C), f32), small=((rows, C), f32), lse=((8, L), f32),
        delta=((8, L), f32), c_f=((L, C), f32), c_heads=((L, C), bf16), c_tok=((T, D), bf16),
        a_buf=((T, D), f32), n1=((T, D), f32), y1=((T, D), f32), r1=((T, C), f32),
        y_all=((L, D), bf16), y_t=((D, L), bf16), u_buf=((2 * T, F), f32), g=((L, F), bf16),
        g_t=((F, L), bf16), d=((L, F), f32), du=((L, F), bf16), dz_all=((L, D), bf16),
        parts=((4, 2 * T, D), bf16), mid=((4, T, D), bf16), dh2=((T, D), f32), dh1=((T, D), f32),
        colg=((8, F), f32), gd_part=((Z, UZ, D), bf16), gd_land=((3, UZ, D), bf16), gd_pass=((UZ, D), bf16),
        gu_part=((Z, KW, F), bf16), gu_land=((3, KW, F), bf16), gu_pass=((KW, F), bf16),
        go_part=((Z, KW, C), bf16), go_land=((3, KW, C), bf16), go_pass=((KW, C), bf16),
        gqk_part=((Z, KW, 2 * C), bf16), gqk_land=((3, KW, 2 * C), bf16), gqk_pass=((KW, 2 * C), bf16),
        gv_part=((Z, KW, C), bf16), gv_land=((3, KW, C), bf16), gv_pass=((KW, C), bf16),
        gd_all=((8 * UZ, D), bf16), gu_all=((8, KW, F), bf16), go_all=((KW, D), bf16),
        gqk_all=((8, KW, 2 * C), bf16), gv_all=((8, KW, C), bf16), da=((T, D), bf16), dc_tok=((T, D), bf16), dc=((L, C), bf16),
        da_cols=((L, C), bf16), c_all=((L, D), bf16), dq=((L, C), f32), dproj=((L, 3 * C), bf16),
        vec_all=((8, 8, D), f32), vec_plane=((8, D), f32), vec_z=((Z, 8, D), f32), vec_sum=((8, D), f32),
        col_z=((Z, 8, F), f32), col_sum=((8, F), f32), col_all=((8, 8, F), f32),
        low0=(PART, bf16), high0=(PART, bf16), low1=(PART, bf16), high1=(PART, bf16), low2=(PART, bf16),
        high2=(PART, bf16), ssem=(BATCHES,), rsem=(LANDINGS,), lsem=(LOCAL,))
    names = [*inputs, *outputs, *scratch]
    sizes = SimpleNamespace(names=names, T=T, D=D, L=L, F=F, first_row=SimpleNamespace(**starts))

    anywhere = pl.BlockSpec(memory_space=pl.ANY)
    results = pl.pallas_call(
        partial(fused_layer, sizes),
        out_shape=[jax.ShapeDtypeStruct(*what) for what in outputs.values()],
        in_specs=[anywhere] * len(inputs),
        out_specs=[anywhere] * len(outputs),
        scratch_shapes=[pltpu.VMEM(*what) if len(what) == 2 else pltpu.SemaphoreType.DMA(what)
                        for what in scratch.values()],
        compiler_params=pltpu.CompilerParams(collective_id=0, has_side_effects=True, vmem_limit_bytes=67043328),
        name="fused_layer",
    )(*inputs.values())
    out, dx, gsm, gqk, gv, go, gu, gd = results
    wide = [jax.ShapeDtypeStruct(value.shape, f32) for value in (projection, output_weight, up_weight, down_weight)]
    narrow = [jax.ShapeDtypeStruct((1, value.shape[0]) if value is not projection_bias else (value.shape[0] // C, C), f32)
              for value in small.values()]
    sources = [out, dx, gqk, gv, go, gu, gd, gsm]
    outcomes = [out, dx] + wide + narrow
    results = pl.pallas_call(
        partial(widen, tuple(starts.values())),
        out_shape=[jax.ShapeDtypeStruct(value.shape, value.dtype) for value in outcomes],
        in_specs=[anywhere] * len(sources),
        out_specs=[anywhere] * len(outcomes),
        scratch_shapes=[pltpu.VMEM(value.shape, value.dtype) for value in sources + outcomes[2:]]
        + [pltpu.SemaphoreType.DMA((LOCAL,))] * 2,
        compiler_params=pltpu.CompilerParams(vmem_limit_bytes=56 << 20),
        name="widen",
    )(*sources)
    out, dx, gq, go, gu, gd = results[:6]
    pb, ob, g1, s1, ub, db, g2, s2 = [value.reshape(-1) for value in results[6:]]
    return (out[None], dx[None], gq, pb, go, ob, g1, s1, gu, ub, gd, db, g2, s2)


def widen(starts, *refs):
    sources, results = refs[:8], refs[8:22]
    held, made, insem, outsem = refs[22:30], refs[30:42], refs[42], refs[43]
    out, dx, gqk, gv, go, gu, gd, gsm = held
    C = gsm.shape[1]
    count = [0, 0]

    def fetch(source, ref):
        copy = pltpu.make_async_copy(source, ref, insem.at[count[0]])
        count[0] += 1
        copy.start()
        return copy
    stores = []

    def store(ref, result):
        copy = pltpu.make_async_copy(ref, result, outsem.at[count[1]])
        count[1] += 1
        copy.start()
        stores.append(copy)

    def piece(i, at, n):
        window = (slice(None), pl.ds(at, n)) if len(held[i].shape) == 3 else (pl.ds(at, n),)
        return fetch(sources[i].at[window], held[i].at[window])

    def grouped(i, target, at, n, first):
        source, result = held[i], made[target]
        groups = source.shape[0]

        def step(j, carry):
            rows = pl.ds(pl.multiple_of(at + j * 32, 32), 32)
            for o in range(groups):
                for p in range(source.shape[2] // C):
                    lane = ((first + p) * groups + o) * C
                    result[rows, lane:lane + C] = source[o, rows, p * C:(p + 1) * C].astype(f32)
            return carry
        lax.fori_loop(0, n // 32, step, 0)

    def plain(i, target, at, n, _):
        source, result = held[i], made[target]

        def step(j, carry):
            rows = pl.ds(pl.multiple_of(at + j * 32, 32), 32)
            result[rows, :] = source[rows, :].astype(f32)
            return carry
        lax.fori_loop(0, n // 32, step, 0)

    work = []
    for i, target, n, body, first in ((5, 2, 64, grouped, 0), (6, 3, 256, plain, 0), (2, 0, 64, grouped, 0),
                                      (3, 0, 64, grouped, 2), (4, 1, 256, plain, 0)):
        total = held[i].shape[-2]
        for at in range(0, total, n):
            work.append((piece(i, at, n), i, target, at, n, body, first))
    whole = [fetch(sources[i], held[i]) for i in (0, 1, 7)]
    for copy, i, target, at, n, body, first in work:
        copy.wait()
        body(i, target, at, n, first)
        if i != 2:
            rows = pl.ds(at, n)
            store(made[target].at[rows], results[2 + target].at[rows])
    for copy in whole:
        copy.wait()
    store(out, results[0])
    store(dx, results[1])
    for start, ref, result in zip(starts, made[4:], results[6:]):
        if ref.shape[1] == C:
            ref[...] = gsm[start:start + ref.shape[0], :]
        else:
            for i in range(ref.shape[1] // C):
                ref[0:1, i * C:(i + 1) * C] = gsm[start + i:start + i + 1, :]
        store(ref, result)
    for copy in stores:
        copy.wait()


BATCHES = 38
LANDINGS = 144
LOCAL = 32


def fits(mesh):
    return mesh.shape["seq"] == 8 and mesh.shape["fsdp"] == 4


def solution(mesh):
    return jax.shard_map(
        fused_shards if fits(mesh) else shards,
        mesh=mesh,
        in_specs=(
            P("fsdp", "seq", None),
            P("fsdp", "seq", None),
            P("fsdp", None),
            P("fsdp", None),
            P("fsdp"),
            P("fsdp", None),
            P("fsdp"),
            P("fsdp"),
            P("fsdp"),
            P("fsdp", None),
            P("fsdp"),
            P("fsdp", None),
            P("fsdp"),
            P("fsdp"),
            P("fsdp"),
        ),
        out_specs=(
            P("fsdp", "seq", None),
            P("fsdp", "seq", None),
            P("fsdp", None),
            P("fsdp"),
            P("fsdp", None),
            P("fsdp"),
            P("fsdp"),
            P("fsdp"),
            P("fsdp", None),
            P("fsdp"),
            P("fsdp", None),
            P("fsdp"),
            P("fsdp"),
            P("fsdp"),
        ),
        check_vma=False,
    )
```

```python
from functools import partial

import jax
import jax.numpy as jnp
import numpy as np
import math
from types import SimpleNamespace
from jax import lax
from jax.experimental import pallas as pl
from jax.experimental.pallas import tpu as pltpu
from jax.sharding import PartitionSpec as P

HEADS = 16
HEAD_DIM = 64


norm_epsilon = 1e-05


def rotary(values, positions):
    half = values.shape[-1] // 2
    channel = jnp.arange(half).astype(jnp.float32)
    inverse = 10000.0 ** (-2.0 * channel / values.shape[-1])
    angles = positions[:, None] * inverse[None, :]
    cosine = jnp.cos(angles)[:, None, :]
    sine = jnp.sin(angles)[:, None, :]
    first = values[..., :half]
    second = values[..., half:]
    return jnp.concatenate(
        [first * cosine - second * sine, second * cosine + first * sine], axis=-1
    )


def rotary_back(grads, positions):
    unused, pullback = jax.vjp(lambda inner: rotary(inner, positions), grads)
    return pullback(grads)[0]


def norm_forward(values, gain, shift):
    centre = values - jnp.mean(values, axis=-1, keepdims=True)
    inverse_root = lax.rsqrt(jnp.mean(centre * centre, axis=-1, keepdims=True) + norm_epsilon)
    normal = centre * inverse_root
    return (normal * gain + shift, normal, inverse_root)


def norm_backward(incoming, normal, inverse_root, gain):
    gain_grad = jnp.sum(incoming * normal, axis=0)
    shift_grad = jnp.sum(incoming, axis=0)
    scaled = incoming * gain
    inner = (
        scaled
        - jnp.mean(scaled, axis=-1, keepdims=True)
        - normal * jnp.mean(scaled * normal, axis=-1, keepdims=True)
    )
    return (inner * inverse_root, gain_grad, shift_grad)


def shards(
    hidden_in,
    cotangent,
    segment_ids,
    projection,
    projection_bias,
    output_weight,
    output_bias,
    first_gain,
    first_shift,
    up_weight,
    up_bias,
    down_weight,
    down_bias,
    second_gain,
    second_shift,
):
    bf16 = jnp.bfloat16
    f32 = jnp.float32
    tokens = hidden_in[0]
    local_rows = tokens.shape[0]
    width = tokens.shape[1]
    seq_rank = lax.axis_index("seq")
    positions = (seq_rank * local_rows + jnp.arange(local_rows)).astype(f32)
    segments = segment_ids[0]
    scale = HEAD_DIM ** (-0.5)
    attention_full = (
        lax.all_gather(projection.astype(bf16), "fsdp", axis=0, tiled=True),
        lax.all_gather(projection_bias.astype(bf16), "fsdp", axis=0, tiled=True),
        lax.all_gather(output_weight.astype(bf16), "fsdp", axis=0, tiled=True),
        lax.all_gather(output_bias.astype(bf16), "fsdp", axis=0, tiled=True),
        lax.all_gather(first_gain.astype(bf16), "fsdp", axis=0, tiled=True),
        lax.all_gather(first_shift.astype(bf16), "fsdp", axis=0, tiled=True),
    )
    proj_weight = attention_full[0]
    projected = jnp.dot(tokens, proj_weight, preferred_element_type=f32) + attention_full[1].astype(
        f32
    )
    heads = projected.reshape(local_rows, 3, HEADS, HEAD_DIM)
    queries = rotary(heads[:, 0], positions)
    keys = rotary(heads[:, 1], positions)
    stacked = jnp.stack([queries, keys, heads[:, 2]]).astype(bf16)
    spread = lax.all_to_all(stacked, "seq", split_axis=2, concat_axis=1, tiled=True)
    query_all = spread[0]
    key_all = spread[1]
    value_all = spread[2]
    length = query_all.shape[0]
    local_heads = query_all.shape[1]
    block = min(512, length)
    count = length // block
    query_blocks = query_all.reshape(count, block, local_heads, HEAD_DIM)
    segment_blocks = segments.reshape(count, block)

    def scores_of(query_block, segment_block):
        raw = jnp.einsum("qhd,khd->hqk", query_block, key_all, preferred_element_type=f32) * scale
        allowed = segment_block[:, None] == segments[None, :]
        return jnp.where(allowed[None], raw, -1e30)

    def forward_block(pieces):
        query_block, segment_block = pieces
        scores = scores_of(query_block, segment_block)
        row_max = jnp.max(scores, axis=-1, keepdims=True)
        exponent = jnp.exp(scores - row_max)
        total = jnp.sum(exponent, axis=-1, keepdims=True)
        weights = exponent / total
        context = jnp.einsum(
            "hqk,khd->qhd", weights.astype(bf16), value_all, preferred_element_type=f32
        )
        return (context.astype(bf16), (row_max + jnp.log(total))[..., 0])

    context_blocks, log_totals = lax.map(forward_block, (query_blocks, segment_blocks))
    context_heads = context_blocks.reshape(length, local_heads, HEAD_DIM)
    context_tokens = lax.all_to_all(
        context_heads, "seq", split_axis=0, concat_axis=1, tiled=True
    ).reshape(local_rows, width)
    attended = jnp.dot(
        context_tokens, attention_full[2], preferred_element_type=f32
    ) + attention_full[3].astype(f32)
    gain_one = attention_full[4].astype(f32)
    normed_one, normal_one, inverse_one = norm_forward(
        tokens.astype(f32) + attended, gain_one, attention_full[5].astype(f32)
    )
    feed_full = (
        lax.all_gather(up_weight.astype(bf16), "fsdp", axis=0, tiled=True),
        lax.all_gather(up_bias.astype(bf16), "fsdp", axis=0, tiled=True),
        lax.all_gather(down_weight.astype(bf16), "fsdp", axis=0, tiled=True),
        lax.all_gather(down_bias.astype(bf16), "fsdp", axis=0, tiled=True),
        lax.all_gather(second_gain.astype(bf16), "fsdp", axis=0, tiled=True),
        lax.all_gather(second_shift.astype(bf16), "fsdp", axis=0, tiled=True),
    )
    normed_low = normed_one.astype(bf16)
    lifted = jnp.dot(normed_low, feed_full[0], preferred_element_type=f32) + feed_full[1].astype(
        f32
    )
    activated = jax.nn.gelu(lifted, approximate=False).astype(bf16)
    lowered = jnp.dot(activated, feed_full[2], preferred_element_type=f32) + feed_full[3].astype(
        f32
    )
    gain_two = feed_full[4].astype(f32)
    layer_out, normal_two, inverse_two = norm_forward(
        normed_one + lowered, gain_two, feed_full[5].astype(f32)
    )
    feed_back = (
        lax.all_gather(up_weight.astype(bf16), "fsdp", axis=0, tiled=True),
        lax.all_gather(up_bias.astype(bf16), "fsdp", axis=0, tiled=True),
        lax.all_gather(down_weight.astype(bf16), "fsdp", axis=0, tiled=True),
        lax.all_gather(down_bias.astype(bf16), "fsdp", axis=0, tiled=True),
        lax.all_gather(second_gain.astype(bf16), "fsdp", axis=0, tiled=True),
        lax.all_gather(second_shift.astype(bf16), "fsdp", axis=0, tiled=True),
    )
    attention_back = (
        lax.all_gather(projection.astype(bf16), "fsdp", axis=0, tiled=True),
        lax.all_gather(projection_bias.astype(bf16), "fsdp", axis=0, tiled=True),
        lax.all_gather(output_weight.astype(bf16), "fsdp", axis=0, tiled=True),
        lax.all_gather(output_bias.astype(bf16), "fsdp", axis=0, tiled=True),
        lax.all_gather(first_gain.astype(bf16), "fsdp", axis=0, tiled=True),
        lax.all_gather(first_shift.astype(bf16), "fsdp", axis=0, tiled=True),
    )
    grad_two, second_gain_grad, second_shift_grad = norm_backward(
        cotangent[0].astype(f32), normal_two, inverse_two, gain_two
    )
    lowered_grad = grad_two.astype(bf16)
    down_weight_grad = jnp.einsum("tf,td->fd", activated, lowered_grad, preferred_element_type=f32)
    down_bias_grad = jnp.sum(lowered_grad.astype(f32), axis=0)
    active_grad = jnp.einsum("td,fd->tf", lowered_grad, feed_back[2], preferred_element_type=f32)
    unused, gelu_pull = jax.vjp(partial(jax.nn.gelu, approximate=False), lifted)
    lifted_grad = gelu_pull(active_grad)[0].astype(bf16)
    up_weight_grad = jnp.einsum("td,tf->df", normed_low, lifted_grad, preferred_element_type=f32)
    up_bias_grad = jnp.sum(lifted_grad.astype(f32), axis=0)
    normed_grad = grad_two + jnp.einsum(
        "tf,df->td", lifted_grad, feed_back[0], preferred_element_type=f32
    )
    grad_one, first_gain_grad, first_shift_grad = norm_backward(
        normed_grad, normal_one, inverse_one, attention_back[4].astype(f32)
    )
    attended_grad = grad_one.astype(bf16)
    output_weight_grad = jnp.einsum(
        "tc,td->cd", context_tokens, attended_grad, preferred_element_type=f32
    )
    output_bias_grad = jnp.sum(attended_grad.astype(f32), axis=0)
    context_grad = jnp.einsum(
        "td,cd->tc", attended_grad, attention_back[2], preferred_element_type=f32
    ).astype(bf16)
    context_grad = context_grad.reshape(local_rows, HEADS, HEAD_DIM)
    context_grad_heads = lax.all_to_all(
        context_grad, "seq", split_axis=1, concat_axis=0, tiled=True
    )
    grad_blocks = context_grad_heads.reshape(count, block, local_heads, HEAD_DIM)

    def backward_block(carry, pieces):
        key_grad, value_grad = carry
        query_block, segment_block, grad_block, log_block = pieces
        scores = scores_of(query_block, segment_block)
        weights = jnp.exp(scores - log_block[..., None])
        value_grad = value_grad + jnp.einsum(
            "hqk,qhd->khd", weights.astype(bf16), grad_block, preferred_element_type=f32
        )
        weight_grad = jnp.einsum("qhd,khd->hqk", grad_block, value_all, preferred_element_type=f32)
        centre = jnp.sum(weights * weight_grad, axis=-1, keepdims=True)
        score_grad = (weights * (weight_grad - centre)).astype(bf16)
        query_grad = (
            jnp.einsum("hqk,khd->qhd", score_grad, key_all, preferred_element_type=f32) * scale
        )
        key_grad = (
            key_grad
            + jnp.einsum("hqk,qhd->khd", score_grad, query_block, preferred_element_type=f32)
            * scale
        )
        return ((key_grad, value_grad), query_grad)

    zeros_heads = jnp.zeros((length, local_heads, HEAD_DIM), f32)
    (key_grad, value_grad), query_grad = lax.scan(
        backward_block,
        (zeros_heads, zeros_heads),
        (query_blocks, segment_blocks, grad_blocks, log_totals),
    )
    query_grad = query_grad.reshape(length, local_heads, HEAD_DIM)
    stacked_grad = jnp.stack([query_grad, key_grad, value_grad]).astype(bf16)
    token_heads = lax.all_to_all(stacked_grad, "seq", split_axis=1, concat_axis=2, tiled=True)
    query_back = rotary_back(token_heads[0].astype(f32), positions)
    key_back = rotary_back(token_heads[1].astype(f32), positions)
    projected_grad = jnp.stack([query_back, key_back, token_heads[2].astype(f32)], axis=1)
    projected_grad = projected_grad.reshape(local_rows, 3 * width).astype(bf16)
    projection_grad = jnp.einsum("td,te->de", tokens, projected_grad, preferred_element_type=f32)
    projection_bias_grad = jnp.sum(projected_grad.astype(f32), axis=0)
    input_grad = grad_one + jnp.einsum(
        "te,de->td", projected_grad, attention_back[0], preferred_element_type=f32
    )
    every_shard = (
        lax.psum_scatter(
            projection_grad.astype(jnp.bfloat16), "fsdp", scatter_dimension=0, tiled=True
        ).astype(jnp.float32),
        lax.psum_scatter(
            projection_bias_grad.astype(jnp.bfloat16), "fsdp", scatter_dimension=0, tiled=True
        ).astype(jnp.float32),
        lax.psum_scatter(
            output_weight_grad.astype(jnp.bfloat16), "fsdp", scatter_dimension=0, tiled=True
        ).astype(jnp.float32),
        lax.psum_scatter(
            output_bias_grad.astype(jnp.bfloat16), "fsdp", scatter_dimension=0, tiled=True
        ).astype(jnp.float32),
        lax.psum_scatter(
            first_gain_grad.astype(jnp.bfloat16), "fsdp", scatter_dimension=0, tiled=True
        ).astype(jnp.float32),
        lax.psum_scatter(
            first_shift_grad.astype(jnp.bfloat16), "fsdp", scatter_dimension=0, tiled=True
        ).astype(jnp.float32),
        lax.psum_scatter(
            up_weight_grad.astype(jnp.bfloat16), "fsdp", scatter_dimension=0, tiled=True
        ).astype(jnp.float32),
        lax.psum_scatter(
            up_bias_grad.astype(jnp.bfloat16), "fsdp", scatter_dimension=0, tiled=True
        ).astype(jnp.float32),
        lax.psum_scatter(
            down_weight_grad.astype(jnp.bfloat16), "fsdp", scatter_dimension=0, tiled=True
        ).astype(jnp.float32),
        lax.psum_scatter(
            down_bias_grad.astype(jnp.bfloat16), "fsdp", scatter_dimension=0, tiled=True
        ).astype(jnp.float32),
        lax.psum_scatter(
            second_gain_grad.astype(jnp.bfloat16), "fsdp", scatter_dimension=0, tiled=True
        ).astype(jnp.float32),
        lax.psum_scatter(
            second_shift_grad.astype(jnp.bfloat16), "fsdp", scatter_dimension=0, tiled=True
        ).astype(jnp.float32),
    )
    finals = (
        lax.psum(every_shard[0].astype(jnp.bfloat16), "seq").astype(jnp.float32),
        lax.psum(every_shard[1].astype(jnp.bfloat16), "seq").astype(jnp.float32),
        lax.psum(every_shard[2].astype(jnp.bfloat16), "seq").astype(jnp.float32),
        lax.psum(every_shard[3].astype(jnp.bfloat16), "seq").astype(jnp.float32),
        lax.psum(every_shard[4].astype(jnp.bfloat16), "seq").astype(jnp.float32),
        lax.psum(every_shard[5].astype(jnp.bfloat16), "seq").astype(jnp.float32),
        lax.psum(every_shard[6].astype(jnp.bfloat16), "seq").astype(jnp.float32),
        lax.psum(every_shard[7].astype(jnp.bfloat16), "seq").astype(jnp.float32),
        lax.psum(every_shard[8].astype(jnp.bfloat16), "seq").astype(jnp.float32),
        lax.psum(every_shard[9].astype(jnp.bfloat16), "seq").astype(jnp.float32),
        lax.psum(every_shard[10].astype(jnp.bfloat16), "seq").astype(jnp.float32),
        lax.psum(every_shard[11].astype(jnp.bfloat16), "seq").astype(jnp.float32),
    )
    return (
        layer_out.astype(bf16)[None],
        input_grad.astype(bf16)[None],
        finals[0],
        finals[1],
        finals[2],
        finals[3],
        finals[4],
        finals[5],
        finals[6],
        finals[7],
        finals[8],
        finals[9],
        finals[10],
        finals[11],
    )


MESH = pl.DeviceIdType.MESH
NN = (((1,), (0,)), ((), ()))
NT = (((1,), (1,)), ((), ()))
TN = (((0,), (0,)), ((), ()))
f32 = jnp.float32
bf16 = jnp.bfloat16
MASKED = -1e30


def mm(left, right, dims=NN):
    return lax.dot_general(left, right, dims, preferred_element_type=f32)


def block_of(index, size):
    return pl.ds(pl.multiple_of(index * size, size), size)


def flip(bit, other):
    return bit + other - 2 * bit * other


def fused_layer(sizes, *refs):
    r = SimpleNamespace(**dict(zip(sizes.names, refs)))
    T, D, L, F = sizes.T, sizes.D, sizes.L, sizes.F
    S, Z = 8, 4
    KW = D // Z
    UZ = F // Z
    C = 128
    T2 = 2 * T
    first_row = sizes.first_row
    ssem, rsem, lsem = r.ssem, r.rsem, r.lsem

    s = lax.axis_index("seq")
    z = lax.axis_index("fsdp")
    core, xbit, ybit = s % 2, (s // 2) % 2, s // 4
    zlow, zhigh = z % 2, z // 2

    def ps(k):
        return flip(core, k % 2) + 2 * flip(xbit, (k // 2) % 2) + 4 * flip(ybit, k // 4)

    def pz(k):
        return flip(zlow, k % 2) + 2 * flip(zhigh, k // 2)

    def chip_of(j):
        return flip(xbit, j % 2) + 2 * flip(ybit, j // 2)

    counter = [0, 0, 0]
    closing = []

    def take(which, n=1):
        counter[which] += n
        return counter[which] - n

    def landings(n=1):
        return take(0, n)

    def size(ref):
        return math.prod(ref.shape) * jnp.dtype(ref.dtype).itemsize

    def extent(n):
        if n <= size(r.c_f):
            return r.c_f.at[pl.ds(0, n * L // size(r.c_f))]
        return r.y_all.at[pl.ds(0, n * L // size(r.y_all))]

    def arrived(ref, slot):
        pltpu.make_async_copy(ref, ref, rsem.at[slot]).wait()

    class Batch:
        def __init__(self, count, like):
            self.slot, self.bytes, self.open = take(1), count * size(like), True
            closing.append(self)

        def send(self, src, dst, slot, dev):
            pltpu.make_async_remote_copy(
                src_ref=src, dst_ref=dst, send_sem=ssem.at[self.slot], recv_sem=rsem.at[slot],
                device_id=dev, device_id_type=MESH).start()

        def close(self):
            if self.open:
                everything = extent(self.bytes)
                pltpu.make_async_copy(everything, everything, ssem.at[self.slot]).wait()
            self.open = False

    def local(src, dst):
        copy = pltpu.make_async_copy(src, dst, lsem.at[take(2)])
        copy.start()
        return copy

    class Gather:
        def __init__(self, place, at_once=True):
            self.place, self.at_once = place, at_once
            self.batch = Batch(7, place(0))
            self.near, self.across = landings(4), landings(2)
            self.other = landings() if at_once else landings(4)

        def part(self, ref, i):
            n = ref.shape[0] // 2
            return ref.at[pl.ds(i * n, n)]

        def start(self, src=None):
            mine = self.place(s)
            src = mine if src is None else src
            for slot, half, k in ((0, 0, 2), (3, 1, 4), (1, 1, 2), (2, 0, 4)):
                self.batch.send(self.part(src, half), self.part(mine, half), self.near + slot, (ps(k), z))
            self.batch.send(src, mine, self.other, (ps(1), z))

        def to_partner(self, k):
            there = self.place(ps(k))
            self.batch.send(there, there, self.other + (0 if self.at_once else k // 2), (ps(1), z))

        def pass_near(self):
            along_x, along_y = self.place(ps(2)), self.place(ps(4))
            first, second = self.part(along_x, 0), self.part(along_y, 1)
            arrived(first, self.near)
            self.batch.send(first, first, self.across, (ps(4), z))
            arrived(second, self.near + 3)
            self.batch.send(second, second, self.across + 1, (ps(2), z))
            arrived(self.part(along_x, 1), self.near + 1)
            self.to_partner(2)
            arrived(self.part(along_y, 0), self.near + 2)
            self.to_partner(4)

        def pass_far(self):
            far = self.place(ps(6))
            arrived(self.part(far, 0), self.across)
            arrived(self.part(far, 1), self.across + 1)
            self.to_partner(6)

        def pass_all(self):
            self.pass_near()
            self.pass_far()

        def wait(self, k=None):
            if self.at_once:
                arrived(extent(4 * size(self.place(0))), self.other)
            else:
                arrived(self.place(ps(k)), self.other + k // 2)

    class Spread:
        def __init__(self, place):
            self.place, self.batch, self.base = place, Batch(3, place(0)), landings(3)

        def start(self, *which):
            mine = self.place(z)
            for k in which or (2, 1):
                self.batch.send(mine, mine, self.base + k - 1, (s, pz(k)))

        def pass_on(self):
            there = self.place(pz(2))
            arrived(there, self.base + 1)
            self.batch.send(there, there, self.base + 2, (s, pz(1)))

        def wait(self):
            for k in (1, 3):
                arrived(self.place(pz(k)), self.base + k - 1)

        def wait_all(self):
            for k in (1, 2, 3):
                arrived(self.place(pz(k)), self.base + k - 1)

    class Fold:
        def __init__(self, parts, landing, passing, first=0, count=None):
            self.rows = pl.ds(first, count or passing.shape[0])
            self.parts, self.landing, self.passing = parts, landing, passing.at[self.rows]
            self.batch, self.base = Batch(3, self.passing), landings(3)

        def start(self):
            for i, k in ((1, 3), (0, 1)):
                self.batch.send(self.parts.at[pz(k), self.rows], self.landing.at[i, self.rows], self.base + i, (s, pz(1)))

        def middle(self):
            arrived(self.landing.at[1, self.rows], self.base + 1)
            self.passing[...] = (self.parts[pz(2), self.rows, :].astype(f32)
                                 + self.landing[1, self.rows, :].astype(f32)).astype(bf16)
            self.batch.send(self.passing, self.landing.at[2, self.rows], self.base + 2, (s, pz(2)))

        def finish(self):
            arrived(self.landing.at[0, self.rows], self.base)
            arrived(self.landing.at[2, self.rows], self.base + 2)
            return (self.parts[z, self.rows, :].astype(f32) + self.landing[0, self.rows, :].astype(f32)
                    + self.landing[2, self.rows, :].astype(f32)).astype(bf16)

    class Scatter:
        def __init__(self, parts, low, mid, high):
            self.parts, self.low, self.mid, self.high = parts, low, mid, high
            self.batch, self.base, self.far, self.last = Batch(7, mid.at[0]), landings(4), landings(2), landings()

        def half(self, ref, j, i):
            return ref.at[j, :, pl.ds(i * (D // 2), D // 2)]

        def send(self, j, i, slot, k):
            self.batch.send(self.half(self.mid, j, i), self.half(self.high, j, i), slot, (ps(k), z))

        def pair(self, j):
            self.batch.send(self.parts.at[j, block_of(1 - core, T)], self.low.at[j], self.base + j, (ps(1), z))

        def onward(self, j):
            arrived(self.low.at[j], self.base + j)
            own = self.parts[j, block_of(core, T), :].astype(f32)
            self.mid[j] = (own + self.low[j].astype(f32)).astype(bf16)
            if j == 1:
                self.send(1, 0, self.last, 2)
            elif j == 2:
                self.send(2, 1, self.last, 4)
            else:
                self.send(3, 0, self.far, 2)
                self.send(3, 1, self.far + 1, 4)

        def cross(self):
            for j, i, k in ((2, 0, 4), (1, 1, 2)):
                arrived(self.half(self.high, 3, i), self.far + i)
                ref = self.half(self.mid, j, i)
                ref[...] = (ref[...].astype(f32) + self.half(self.high, 3, i)[...].astype(f32)).astype(bf16)
                self.send(j, i, self.last, k)

        def ready(self):
            arrived(self.low.at[0], self.base)
            arrived(self.high.at[pl.ds(1, 2)], self.last)

        def rows(self, at, n):
            own = self.parts[0, pl.ds(pl.multiple_of(core * T + at, n), n), :].astype(f32)
            total = own + self.low[0, pl.ds(at, n), :].astype(f32)
            for j in (1, 2):
                total = total + self.high[j, pl.ds(at, n), :].astype(f32)
            return total

    class Share:
        def __init__(self, count, like):
            self.count, self.batch, self.slot, self.bytes = count, Batch(count, like), landings(), count * size(like)

        def plane(self, src, dst):
            for k in (6, 7, 2, 3, 4, 5, 1):
                self.batch.send(src(ps(k)), dst, self.slot, (ps(k), z))

        def column(self, src, dst):
            for k in (2, 3, 1):
                self.batch.send(src, dst, self.slot, (s, pz(k)))

        def wait(self):
            arrived(extent(self.bytes), self.slot)

    def loop(count, body, unroll=1):
        def step(i, carry):
            body(i)
            return carry
        lax.fori_loop(0, count, step, 0, unroll=unroll)

    def at(i, n):
        return pl.multiple_of(i * n, n)

    def turn(src, dst):
        def one(i):
            dst[:, pl.ds(at(i, T), T)] = jnp.transpose(src[pl.ds(at(i, T), T), :])
        loop(L // T, one)

    vec, vecg = r.vec, r.vecg

    OUTPUT_BIAS, FIRST_GAIN, FIRST_SHIFT, DOWN_BIAS, SECOND_GAIN, SECOND_SHIFT, PROJECTION_BIAS, UP_BIAS = range(8)
    wide = ((first_row.output_bias, OUTPUT_BIAS), (first_row.first_gain, FIRST_GAIN),
            (first_row.first_shift, FIRST_SHIFT), (first_row.down_bias, DOWN_BIAS),
            (first_row.second_gain, SECOND_GAIN), (first_row.second_shift, SECOND_SHIFT))

    def row(i, width=D):
        return vec[i:i + 1, :width]

    lanes = lax.broadcasted_iota(jnp.int32, (T, C), 1)
    low_head = lanes < HEAD_DIM

    def swapped(w):
        low_half = lax.broadcasted_iota(jnp.int32, w.shape, 1) % HEAD_DIM < HEAD_DIM // 2
        return jnp.where(low_half, pltpu.roll(w, C - HEAD_DIM // 2, 1), pltpu.roll(w, HEAD_DIM // 2, 1))

    def stacked(w):
        nothing = jnp.zeros_like(w)
        return jnp.concatenate([jnp.where(low_head, w, nothing), jnp.where(low_head, nothing, w)], axis=0)

    def unstacked(w):
        return jnp.where(low_head, w[:T], w[T:])

    barrier = pltpu.get_barrier_semaphore()
    for k in range(1, S):
        pl.semaphore_signal(barrier, inc=1, device_id=(ps(k), z), device_id_type=MESH)
    for k in range(1, Z):
        pl.semaphore_signal(barrier, inc=1, device_id=(s, pz(k)), device_id_type=MESH)
    x_ref, ct_ref = r.v_x, r.v_ct
    x_load = local(r.x, x_ref)
    wo_load = local(r.wo.at[:, block_of(s, C)], r.st_wo)
    proj_loads = [local(r.proj.at[:, block_of(i * (D // C) + s, C)], r.st_proj.at[:, pl.ds(i * C, C)])
                  for i in range(3)]
    raw = ((r.b_projection, r.v_projection, first_row.projection_bias), (r.b_output, r.v_output, first_row.output_bias),
           (r.gain1, r.v_gain1, first_row.first_gain), (r.shift1, r.v_shift1, first_row.first_shift),
           (r.b_up, r.v_up, first_row.up_bias), (r.b_down, r.v_down, first_row.down_bias),
           (r.gain2, r.v_gain2, first_row.second_gain), (r.shift2, r.v_shift2, first_row.second_shift))
    raw_loads = [local(source, ref) for source, ref, _ in raw]
    seg_load = local(r.seg, r.v_seg)
    up_loads = [local(r.up.at[:, block_of(i * (D // C) + s, C)], r.st_up.at[:, pl.ds(i * C, C)])
                for i in range(Z)]
    dn_load = local(r.dn.at[block_of(s, UZ), :], r.st_dn)
    late_loads = [local(r.cos, r.v_cos), local(r.sin, r.v_sin), local(r.ct, ct_ref)]
    cos_ref, sin_ref = r.v_cos, r.v_sin

    x_all, w_qkv, w_o, w_up, w_dn = r.x_all, r.w_qkv, r.w_o, r.w_up, r.w_dn
    gather_x = Gather(lambda o: x_all.at[block_of(o, T)])
    spread_qkv = Spread(lambda p: w_qkv.at[block_of(p, KW)])
    spread_o = Spread(lambda p: w_o.at[block_of(p, KW), block_of(s, C)])
    spread_up = Spread(lambda p: w_up.at[block_of(p, KW)])
    spread_dn = Spread(lambda p: w_dn.at[block_of(p, UZ)])
    gather_o = Gather(lambda o: w_o.at[:, block_of(o, C)])
    wo_load.wait()
    w_o[block_of(z, KW), block_of(s, C)] = r.st_wo[...].astype(bf16)
    for copy in proj_loads:
        copy.wait()
    w_qkv[block_of(z, KW), :] = r.st_proj[...].astype(bf16)
    x_load.wait()
    pl.semaphore_wait(barrier, S + Z - 2)
    spread_o.start(2, 3, 1)
    spread_qkv.start()
    gather_x.start(x_ref)

    small, small_all, seg_c, seg_r = r.small, r.small_all, r.seg_c, r.seg_r
    for copy, (_, ref, start) in zip(raw_loads, raw):
        copy.wait()
        if ref.shape[1] == C:
            small[start:start + ref.shape[0], :] = ref[...].astype(bf16).astype(f32)
        else:
            for i in range(ref.shape[1] // C):
                small[start + i:start + i + 1, :] = ref[0:1, i * C:(i + 1) * C].astype(bf16).astype(f32)
    x_all[block_of(s, T), :] = x_ref[...]
    vecg[...] = jnp.zeros((8, D), f32)
    seg_load.wait()
    seg_r[...] = jnp.broadcast_to(r.v_seg[...].astype(f32), (8, L))

    def seg_turn(i):
        here = pl.ds(at(i, T), T)
        seg_c[here, :] = jnp.transpose(jnp.broadcast_to(seg_r[0:1, here], (T, T)))
    loop(L // T, seg_turn)
    for copy in up_loads:
        copy.wait()
    w_up[block_of(z, KW), :] = r.st_up[...].astype(bf16)
    dn_load.wait()
    w_dn[block_of(z, UZ), :] = r.st_dn[...].astype(bf16)
    share_small = Share(3, small)
    small_all[z] = small[...]

    gather_x.pass_near()
    spread_o.wait_all()
    gather_o.start()
    gather_x.pass_far()
    gather_x.wait()
    spread_qkv.pass_on()
    share_small.column(small, small_all.at[z])
    spread_up.start()
    x_t = r.x_t
    turn(x_all, x_t)
    for copy in late_loads:
        copy.wait()
    gather_o.pass_near()
    spread_qkv.wait()
    share_small.wait()
    for p in range(Z):
        for start, i in wide:
            for half in range(KW // C):
                at_row = start + half
                lane = (p * (KW // C) + half) * C
                vec[i:i + 1, lane:lane + C] = small_all[p, at_row:at_row + 1, :]
        vec[7:8, p * C:(p + 1) * C] = small_all[p, pl.ds(first_row.up_bias + s, 1), :]
    per = 3 * D // (C * Z)
    for t in range(3):
        number = t * (D // C) + s
        vec[6:7, t * C:(t + 1) * C] = small_all[number // per, pl.ds(first_row.projection_bias + number % per, 1), :]

    q_ref, k_ref, v_ref = r.q, r.k, r.v
    scale = HEAD_DIM ** -0.5

    def project(i):
        here = pl.ds(at(i, T2), T2)
        out = mm(x_all[here, :], w_qkv[...]) + row(PROJECTION_BIAS, 3 * C)
        cosine, sine = cos_ref[here, :], sin_ref[here, :]
        q0, k0 = out[:, :C], out[:, C:2 * C]
        q_ref[here, :] = ((q0 * cosine + swapped(q0) * sine).astype(bf16).astype(f32) * scale).astype(bf16)
        k_ref[here, :] = (k0 * cosine + swapped(k0) * sine).astype(bf16)
        v_ref[here, :] = out[:, 2 * C:].astype(bf16)
    loop(L // T2, project)
    gather_o.pass_far()

    lse, c_f, c_heads, c_tok = r.lse, r.c_f, r.c_heads, r.c_tok
    R = 16

    def same_document(here):
        return jnp.tile(seg_c[here, :], (1, L // C)) == seg_r[0:1, :]

    def both(w):
        return jnp.concatenate([w, w], axis=0)

    def attend(o):
        here = block_of(o, T)
        score = jnp.where(both(same_document(here)), mm(stacked(q_ref[here, :]), k_ref[...], NT), MASKED)
        top = jnp.max(score, axis=-1, keepdims=True)
        power = jnp.exp(score - top)
        total = jnp.sum(power, axis=-1, keepdims=True)
        context = unstacked(mm(power.astype(bf16), v_ref[...]) * (1.0 / total))
        c_f[here, :] = context
        c_heads[here, :] = context.astype(bf16)
        logs = jnp.broadcast_to(top + jnp.log(total), (T2, C))
        for h in range(2):
            lse[h:h + 1, here] = jnp.transpose(logs[h * T:(h + 1) * T, :])[0:1, :]

    share_c = Share(7, c_heads.at[pl.ds(0, T)])

    def attend_and_send(i):
        k = 7 - i
        attend(ps(k))

        @pl.when(k > 0)
        def _():
            share_c.batch.send(c_heads.at[block_of(ps(k), T)], c_tok.at[:, block_of(s, C)], share_c.slot, (ps(k), z))
    loop(8, attend_and_send)
    spread_up.pass_on()
    spread_dn.start()
    c_tok[:, block_of(s, C)] = c_heads[block_of(s, T), :]
    gather_o.wait()
    share_c.wait()

    a_buf = r.a_buf
    a_buf[...] = mm(c_tok[...], w_o[...])
    n1, y1, r1, y_all = r.n1, r.y1, r.r1, r.y_all

    def norm(h):
        centre = h - jnp.mean(h, axis=-1, keepdims=True)
        root = lax.rsqrt(jnp.mean(centre * centre, axis=-1, keepdims=True) + norm_epsilon)
        return centre * root, root

    def first_norm(i):
        rows = pl.ds(at(i, R), R)
        normal, root = norm(x_ref[rows, :].astype(f32) + a_buf[rows, :] + row(OUTPUT_BIAS))
        out = normal * row(FIRST_GAIN) + row(FIRST_SHIFT)
        n1[rows, :] = normal
        r1[rows, :] = jnp.broadcast_to(root, (R, C))
        y1[rows, :] = out
        y_all[pl.ds(pl.multiple_of(s * T + i * R, R), R), :] = out.astype(bf16)
    loop(T // R, first_norm, 4)
    gather_y = Gather(lambda o: y_all.at[block_of(o, T)], False)
    gather_y.start()
    c_all = r.c_all
    gather_c = Gather(lambda o: c_all.at[block_of(o, T)])
    c_all[block_of(s, T), :] = c_tok[...]

    u_buf, g_ref, d_ref, du_ref, dz_all = r.u_buf, r.g, r.d, r.du, r.dz_all
    parts, mid = r.parts, r.mid
    spread_up.wait()
    E = 32

    def lift(j):
        q = chip_of(j)
        u_buf[...] = mm(y_all[block_of(q, T2), :], w_up[...])

        def chunk(i):
            rows = pl.ds(at(i, E), E)
            there = pl.ds(pl.multiple_of(q * T2 + i * E, E), E)
            u = u_buf[rows, :] + row(UP_BIAS, F)
            share = 0.5 + 0.5 * lax.erf(u * (0.5 ** 0.5))
            g_ref[there, :] = (u * share).astype(bf16)
            d_ref[there, :] = share + u * (jnp.exp(-0.5 * u * u) * 0.3989422804014327)
        loop(T2 // E, chunk)

    def lower(j):
        parts[j] = mm(g_ref[block_of(chip_of(j), T2), :], w_dn[...]).astype(bf16)

    fold_z = Scatter(parts, r.low0, mid, r.high0)
    y_t, g_t = r.y_t, r.g_t
    gather_y.wait(1)
    lift(0)
    gather_y.pass_near()
    gather_y.wait(3)
    lift(1)
    gather_y.wait(5)
    lift(2)
    spread_dn.pass_on()
    gather_y.pass_far()
    gather_c.start(c_tok)
    gather_y.wait(7)
    lift(3)
    turn(y_all, y_t)
    turn(g_ref, g_t)
    spread_dn.wait()
    for j in (3, 1, 2, 0):
        lower(j)
        fold_z.pair(j)
        if j == 1:
            fold_z.onward(3)
        if j == 2:
            fold_z.onward(1)
    fold_z.onward(2)
    fold_z.cross()
    gather_c.pass_near()
    fold_z.ready()

    dh2, out_ref = r.dh2, r.v_out

    def add_row(i, value):
        vecg[i:i + 1, :] = vecg[i:i + 1, :] + jnp.sum(value, axis=0, keepdims=True)

    def norm_back(incoming, normal, root, gain):
        scaled = incoming * gain
        return root * (scaled - jnp.mean(scaled, axis=-1, keepdims=True)
                       - normal * jnp.mean(scaled * normal, axis=-1, keepdims=True))

    def second_norm(i):
        start = at(i, R)
        rows = pl.ds(start, R)
        normal, root = norm(y1[rows, :] + fold_z.rows(start, R) + row(DOWN_BIAS))
        out_ref[rows, :] = (normal * row(SECOND_GAIN) + row(SECOND_SHIFT)).astype(bf16)
        e = ct_ref[rows, :].astype(f32)
        grad = norm_back(e, normal, root, row(SECOND_GAIN))
        dh2[rows, :] = grad
        dz = grad.astype(bf16)
        dz_all[pl.ds(pl.multiple_of(s * T + i * R, R), R), :] = dz
        add_row(3, dz.astype(f32))
        add_row(4, e * normal)
        add_row(5, e)
    loop(T // R, second_norm, 2)
    outs = [local(out_ref, r.out)]
    gather_dz = Gather(lambda o: dz_all.at[block_of(o, T)], False)
    gather_dz.start()
    fold_z.batch.close()

    colg = r.colg
    colg[...] = jnp.zeros((8, F), f32)

    def unlower(j):
        q = chip_of(j)
        u_buf[...] = mm(dz_all[block_of(q, T2), :], w_dn[...], NT)

        def chunk(i):
            rows = pl.ds(at(i, E), E)
            there = pl.ds(pl.multiple_of(q * T2 + i * E, E), E)
            du = (u_buf[rows, :] * d_ref[there, :]).astype(bf16)
            du_ref[there, :] = du
            colg[0:1, :] = colg[0:1, :] + jnp.sum(du.astype(f32), axis=0, keepdims=True)
        loop(T2 // E, chunk)

    def unlift(j):
        parts[j] = mm(du_ref[block_of(chip_of(j), T2), :], w_up[...], NT).astype(bf16)

    fold_y = Scatter(parts, r.low1, mid, r.high1)
    gd_part, gu_part = r.gd_part, r.gu_part
    folds_dn = [Fold(gd_part, r.gd_land, r.gd_pass, i * (UZ // 2), UZ // 2) for i in range(2)]
    folds_up = [Fold(gu_part, r.gu_land, r.gu_pass, i * (KW // 2), KW // 2) for i in range(2)]

    def down_grad(k):
        gd_part[pz(k)] = mm(g_t[block_of(pz(k), UZ), :], dz_all[...]).astype(bf16)

    def up_grad(k):
        gu_part[pz(k)] = mm(y_t[block_of(pz(k), KW), :], du_ref[...]).astype(bf16)

    gather_c.pass_far()
    gather_dz.wait(1)
    unlower(0)
    unlift(0)
    fold_y.pair(0)
    gather_dz.pass_near()
    gather_dz.wait(3)
    unlower(1)
    unlift(1)
    fold_y.pair(1)
    gather_dz.wait(5)
    unlower(2)
    fold_y.onward(1)
    unlift(2)
    fold_y.pair(2)
    gather_dz.pass_far()
    fold_y.onward(2)
    gather_dz.wait(7)
    down_grad(3)
    down_grad(1)
    folds_dn[0].start()
    folds_dn[1].start()
    unlower(3)
    unlift(3)
    fold_y.pair(3)
    up_grad(3)
    fold_y.onward(3)

    up_grad(1)
    down_grad(2)
    fold_y.cross()
    folds_dn[0].middle()
    folds_up[0].start()
    down_grad(0)
    up_grad(2)
    up_grad(0)
    gather_c.wait()
    fold_y.ready()

    dh1, da = r.dh1, r.da

    def first_back(i):
        start = at(i, R)
        rows = pl.ds(start, R)
        incoming = dh2[rows, :] + fold_y.rows(start, R)
        normal = n1[rows, :]
        grad = norm_back(incoming, normal, r1[rows, 0:1], row(FIRST_GAIN))
        dh1[rows, :] = grad
        low = grad.astype(bf16)
        da[rows, :] = low
        add_row(0, low.astype(f32))
        add_row(1, incoming * normal)
        add_row(2, incoming)
    loop(T // R, first_back, 2)
    fold_y.batch.close()

    dc_tok, dc = r.dc_tok, r.dc
    dc_tok[...] = mm(da[...], w_o[...], NT).astype(bf16)
    share_dc = Share(7, dc.at[pl.ds(0, T)])
    share_dc.plane(lambda o: dc_tok.at[:, block_of(o, C)], dc.at[block_of(s, T)])
    dc[block_of(s, T), :] = dc_tok[:, block_of(s, C)]
    da_cols = r.da_cols
    share_da = Share(7, da_cols.at[pl.ds(0, T)])
    share_da.plane(lambda o: da.at[:, block_of(o, C)], da_cols.at[block_of(s, T)])
    da_cols[block_of(s, T), :] = da[:, block_of(s, C)]
    vec_all = r.vec_all
    share_vec = Share(7, vecg)
    share_vec.plane(lambda o: vecg, vec_all.at[s])
    folds_dn[1].middle()
    folds_up[1].start()
    share_dc.wait()

    delta, dq, dproj = r.delta, r.dq, r.dproj

    def deltas(i):
        here = pl.ds(at(i, T), T)
        turned = jnp.transpose(dc[here, :].astype(f32) * c_f[here, :])
        delta[0:1, here] = jnp.sum(turned[:HEAD_DIM], axis=0, keepdims=True)
        delta[1:2, here] = jnp.sum(turned[HEAD_DIM:], axis=0, keepdims=True)
        dq[here, :] = jnp.zeros((T, C), f32)
    loop(L // T, deltas)

    def attend_back(i):
        here = pl.ds(at(i, T), T)
        same = same_document(here)
        k_here, v_here = k_ref[here, :], v_ref[here, :]
        keys, values, slopes = [], [], []
        for h in range(2):
            own = low_head if h == 0 else jnp.logical_not(low_head)
            nothing = jnp.zeros_like(k_here)
            key = jnp.where(own, k_here, nothing)
            weight = jnp.exp(jnp.where(same, mm(key, q_ref[...], NT), MASKED) - lse[h:h + 1, :])
            slope = mm(jnp.where(own, v_here, nothing), dc[...], NT) - delta[h:h + 1, :]
            slopes.append((weight * slope).astype(bf16))
            values.append(mm(weight.astype(bf16), dc[...]))
            keys.append(key)
        dv = jnp.where(low_head, values[0], values[1]).astype(bf16)
        dk = jnp.where(low_head, mm(slopes[0], q_ref[...]), mm(slopes[1], q_ref[...])).astype(bf16).astype(f32)
        dproj[here, 2 * C:] = dv
        dproj[here, C:2 * C] = (dk * cos_ref[here, :] - swapped(dk) * sin_ref[here, :]).astype(bf16)
        dq[...] = dq[...] + mm(jnp.concatenate(slopes, axis=0), jnp.concatenate(keys, axis=0), TN)

    gd_all, gu_all, go_all, gqk_all, gv_all = r.gd_all, r.gu_all, r.go_all, r.gqk_all, r.gv_all
    gather_gd = Gather(lambda o: gd_all.at[block_of(o, UZ)])
    gather_gu = Gather(lambda o: gu_all.at[o])
    gather_go = Gather(lambda o: go_all.at[:, block_of(o, C)])
    gather_gqk = Gather(lambda o: gqk_all.at[o])
    gather_gv = Gather(lambda o: gv_all.at[o])
    go_part = r.go_part
    fold_o = Fold(go_part, r.go_land, r.go_pass)

    def out_grad(k):
        go_part[pz(k)] = mm(c_all[:, block_of(pz(k), KW)], da_cols[...], TN).astype(bf16)

    def attend_back_and_fold(i):
        attend_back(i)

        @pl.when(i == 4)
        def _():
            share_da.wait()
            for k in (3, 1, 2, 0):
                out_grad(k)
            fold_o.start()

        @pl.when(i == 6)
        def _():
            folds_up[0].middle()
    loop(L // T, attend_back_and_fold)

    for i in range(2):
        gd_all[pl.ds(pl.multiple_of(s * UZ + i * (UZ // 2), UZ // 2), UZ // 2), :] = folds_dn[i].finish()
    gather_gd.start()

    def dq_rows(i):
        here = pl.ds(at(i, T), T)
        whole = (dq[here, :] * scale).astype(bf16).astype(f32)
        dproj[here, :C] = (whole * cos_ref[here, :] - swapped(whole) * sin_ref[here, :]).astype(bf16)
        colg[1:2, :3 * C] = colg[1:2, :3 * C] + jnp.sum(dproj[here, :].astype(f32), axis=0, keepdims=True)
    loop(L // T, dq_rows)

    gqk_part, gv_part = r.gqk_part, r.gv_part
    fold_qk = Fold(gqk_part, r.gqk_land, r.gqk_pass)
    fold_v = Fold(gv_part, r.gv_land, r.gv_pass)

    def projection_grad(k):
        grad = mm(x_t[block_of(pz(k), KW), :], dproj[...]).astype(bf16)
        gqk_part[pz(k)] = grad[:, :2 * C]
        gv_part[pz(k)] = grad[:, 2 * C:]
    projection_grad(3)
    projection_grad(1)
    fold_x = Scatter(parts, r.low2, mid, r.high2)

    def unproject(j):
        parts[j] = mm(dproj[block_of(chip_of(j), T2), :], w_qkv[...], NT).astype(bf16)
        fold_x.pair(j)
    fold_qk.start()
    unproject(3)
    unproject(1)
    fold_x.onward(3)
    folds_up[1].middle()
    fold_v.start()
    unproject(2)
    fold_x.onward(1)
    unproject(0)
    fold_x.onward(2)
    projection_grad(2)
    projection_grad(0)
    fold_x.cross()
    gather_gd.pass_near()
    col_z = r.col_z
    share_col = Share(3, colg)
    share_col.column(colg, col_z.at[z])
    col_z[z] = colg[...]
    vec_all[s] = vecg[...]
    share_vec.wait()
    vec_plane, vec_z = r.vec_plane, r.vec_z
    total = vec_all[0]
    for o in range(1, S):
        total = total + vec_all[o]
    vec_plane[...] = total
    share_sum = Share(3, vec_plane)
    share_sum.column(vec_plane, vec_z.at[z])
    vec_z[z] = total
    gather_gd.pass_far()
    fold_o.middle()
    fold_x.ready()
    dx_ref = r.v_dx

    def input_back(i):
        start = at(i, R)
        rows = pl.ds(start, R)
        dx_ref[rows, :] = (dh1[rows, :] + fold_x.rows(start, R)).astype(bf16)
    loop(T // R, input_back, 2)
    outs.append(local(dx_ref, r.dx))
    for i in range(2):
        gu_all[s, pl.ds(i * (KW // 2), KW // 2), :] = folds_up[i].finish()
    gather_gu.start()
    fold_qk.middle()
    gather_gd.wait()
    outs.append(local(gd_all, r.gd))
    share_col.wait()
    col_all, col_sum = r.col_all, r.col_sum
    col_sum[...] = col_z[0] + col_z[1] + col_z[2] + col_z[3]
    share_cols = Share(7, col_sum)
    share_cols.plane(lambda o: col_sum, col_all.at[s])
    col_all[s] = col_sum[...]
    fold_v.middle()
    gather_gu.pass_near()
    go_all[:, block_of(s, C)] = fold_o.finish()
    gather_go.start()
    gqk_all[s] = fold_qk.finish()
    gather_gqk.start()
    gv_all[s] = fold_v.finish()
    gather_gv.start()
    gather_gu.pass_far()
    gather_go.pass_near()
    gather_gqk.pass_near()
    gather_gv.pass_near()
    gather_gu.wait()
    outs.append(local(gu_all, r.gu))

    share_sum.wait()
    share_cols.wait()
    vec_sum = r.vec_sum
    vec_sum[...] = vec_z[0] + vec_z[1] + vec_z[2] + vec_z[3]
    gsm = r.v_gsm
    gsm[...] = jnp.zeros(gsm.shape, f32)
    for start, i in wide:
        for half in range(KW // C):
            at_row = start + half
            gsm[at_row:at_row + 1, :] = vec_sum[i:i + 1, block_of(z * (KW // C) + half, C)]
    for o in range(S):
        at_row = first_row.up_bias + o
        gsm[at_row:at_row + 1, :] = col_all[o, 0:1, block_of(z, C)]
    for i in range(per):
        number = z * per + i
        at_row = first_row.projection_bias + i
        gsm[at_row:at_row + 1, :] = col_all[number % S, 1:2, block_of(number // S, C)]
    outs.append(local(gsm, r.gsm))
    gather_go.pass_far()
    gather_gqk.pass_far()
    gather_gv.pass_far()
    gather_go.wait()
    outs.append(local(go_all, r.go))
    gather_gqk.wait()
    outs.append(local(gqk_all, r.gqk))
    gather_gv.wait()
    outs.append(local(gv_all, r.gv))
    for copy in outs:
        copy.wait()
    for batch in closing:
        batch.close()
    assert counter[0] <= LANDINGS and counter[1] <= BATCHES and counter[2] <= LOCAL, counter


def fused_shards(*args):
    (hidden_in, cotangent, segment_ids, projection, projection_bias, output_weight, output_bias, first_gain,
     first_shift, up_weight, up_bias, down_weight, down_bias, second_gain, second_shift) = args
    T, D = hidden_in.shape[1:]
    L = segment_ids.shape[1]
    KW = projection.shape[0]
    F = up_weight.shape[1] // 8
    C, Z = 128, 4
    UZ = F // Z
    small = dict(projection_bias=projection_bias, output_bias=output_bias, first_gain=first_gain,
                 first_shift=first_shift, up_bias=up_bias, down_bias=down_bias, second_gain=second_gain,
                 second_shift=second_shift)
    starts, at_row = {}, 0
    for name, value in small.items():
        starts[name] = at_row
        at_row += value.shape[0] // C
    rows = -(-at_row // 8) * 8
    half = HEAD_DIM // 2
    inverse = np.float32(10000.0) ** (np.float32(-2.0) * np.arange(half, dtype=np.float32) / np.float32(HEAD_DIM))
    angles = np.arange(L, dtype=np.float32)[:, None] * inverse.astype(np.float32)[None, :]
    cosine = np.tile(np.cos(angles), (1, C // half))
    sine = np.tile(np.concatenate([-np.sin(angles), np.sin(angles)], axis=1), (1, C // HEAD_DIM))

    inputs = dict(x=hidden_in[0], ct=cotangent[0], seg=segment_ids, cos=jnp.asarray(cosine), sin=jnp.asarray(sine),
                  b_projection=projection_bias.reshape(-1, C), b_output=output_bias[None], gain1=first_gain[None],
                  shift1=first_shift[None], b_up=up_bias[None], b_down=down_bias[None], gain2=second_gain[None],
                  shift2=second_shift[None], proj=projection, wo=output_weight, up=up_weight, dn=down_weight)
    outputs = dict(out=((T, D), bf16), dx=((T, D), bf16), gsm=((rows, C), f32), gqk=((8, KW, 2 * C), bf16), gv=((8, KW, C), bf16),
                   go=((KW, D), bf16), gu=((8, KW, F), bf16), gd=((8 * UZ, D), bf16))
    landed = dict(v_x=inputs["x"], v_ct=inputs["ct"], v_seg=segment_ids, v_cos=inputs["cos"], v_sin=inputs["sin"],
                  v_projection=inputs["b_projection"], v_output=inputs["b_output"], v_gain1=inputs["gain1"],
                  v_shift1=inputs["shift1"], v_up=inputs["b_up"], v_down=inputs["b_down"], v_gain2=inputs["gain2"],
                  v_shift2=inputs["shift2"])
    PART = (4, T, D)
    scratch = {name: (value.shape, value.dtype) for name, value in landed.items()}
    scratch.update(
        v_out=((T, D), bf16), v_dx=((T, D), bf16), v_gsm=((rows, C), f32),
        x_all=((L, D), bf16), x_t=((D, L), bf16), w_qkv=((D, 3 * C), bf16), st_proj=((KW, 3 * C), f32),
        w_o=((D, D), bf16), st_wo=((KW, C), f32), w_up=((D, F), bf16), st_up=((KW, F), f32),
        w_dn=((F, D), bf16), st_dn=((UZ, D), f32), small_all=((Z, rows, C), f32), vec=((8, D), f32),
        vecg=((8, D), f32), q=((L, C), bf16), k=((L, C), bf16), v=((L, C), bf16),
        seg_r=((8, L), f32), seg_c=((L, C), f32), small=((rows, C), f32), lse=((8, L), f32),
        delta=((8, L), f32), c_f=((L, C), f32), c_heads=((L, C), bf16), c_tok=((T, D), bf16),
        a_buf=((T, D), f32), n1=((T, D), f32), y1=((T, D), f32), r1=((T, C), f32),
        y_all=((L, D), bf16), y_t=((D, L), bf16), u_buf=((2 * T, F), f32), g=((L, F), bf16),
        g_t=((F, L), bf16), d=((L, F), f32), du=((L, F), bf16), dz_all=((L, D), bf16),
        parts=((4, 2 * T, D), bf16), mid=((4, T, D), bf16), dh2=((T, D), f32), dh1=((T, D), f32),
        colg=((8, F), f32), gd_part=((Z, UZ, D), bf16), gd_land=((3, UZ, D), bf16), gd_pass=((UZ, D), bf16),
        gu_part=((Z, KW, F), bf16), gu_land=((3, KW, F), bf16), gu_pass=((KW, F), bf16),
        go_part=((Z, KW, C), bf16), go_land=((3, KW, C), bf16), go_pass=((KW, C), bf16),
        gqk_part=((Z, KW, 2 * C), bf16), gqk_land=((3, KW, 2 * C), bf16), gqk_pass=((KW, 2 * C), bf16),
        gv_part=((Z, KW, C), bf16), gv_land=((3, KW, C), bf16), gv_pass=((KW, C), bf16),
        gd_all=((8 * UZ, D), bf16), gu_all=((8, KW, F), bf16), go_all=((KW, D), bf16),
        gqk_all=((8, KW, 2 * C), bf16), gv_all=((8, KW, C), bf16), da=((T, D), bf16), dc_tok=((T, D), bf16), dc=((L, C), bf16),
        da_cols=((L, C), bf16), c_all=((L, D), bf16), dq=((L, C), f32), dproj=((L, 3 * C), bf16),
        vec_all=((8, 8, D), f32), vec_plane=((8, D), f32), vec_z=((Z, 8, D), f32), vec_sum=((8, D), f32),
        col_z=((Z, 8, F), f32), col_sum=((8, F), f32), col_all=((8, 8, F), f32),
        low0=(PART, bf16), high0=(PART, bf16), low1=(PART, bf16), high1=(PART, bf16), low2=(PART, bf16),
        high2=(PART, bf16), ssem=(BATCHES,), rsem=(LANDINGS,), lsem=(LOCAL,))
    names = [*inputs, *outputs, *scratch]
    sizes = SimpleNamespace(names=names, T=T, D=D, L=L, F=F, first_row=SimpleNamespace(**starts))

    anywhere = pl.BlockSpec(memory_space=pl.ANY)
    results = pl.pallas_call(
        partial(fused_layer, sizes),
        out_shape=[jax.ShapeDtypeStruct(*what) for what in outputs.values()],
        in_specs=[anywhere] * len(inputs),
        out_specs=[anywhere] * len(outputs),
        scratch_shapes=[pltpu.VMEM(*what) if len(what) == 2 else pltpu.SemaphoreType.DMA(what)
                        for what in scratch.values()],
        compiler_params=pltpu.CompilerParams(collective_id=0, has_side_effects=True, vmem_limit_bytes=67043328),
        name="fused_layer",
    )(*inputs.values())
    out, dx, gsm, gqk, gv, go, gu, gd = results
    wide = [jax.ShapeDtypeStruct(value.shape, f32) for value in (projection, output_weight, up_weight, down_weight)]
    narrow = [jax.ShapeDtypeStruct((1, value.shape[0]) if value is not projection_bias else (value.shape[0] // C, C), f32)
              for value in small.values()]
    sources = [out, dx, gqk, gv, go, gu, gd, gsm]
    outcomes = [out, dx] + wide + narrow
    results = pl.pallas_call(
        partial(widen, tuple(starts.values())),
        out_shape=[jax.ShapeDtypeStruct(value.shape, value.dtype) for value in outcomes],
        in_specs=[anywhere] * len(sources),
        out_specs=[anywhere] * len(outcomes),
        scratch_shapes=[pltpu.VMEM(value.shape, value.dtype) for value in sources + outcomes[2:]]
        + [pltpu.SemaphoreType.DMA((LOCAL,))] * 2,
        compiler_params=pltpu.CompilerParams(vmem_limit_bytes=56 << 20),
        name="widen",
    )(*sources)
    out, dx, gq, go, gu, gd = results[:6]
    pb, ob, g1, s1, ub, db, g2, s2 = [value.reshape(-1) for value in results[6:]]
    return (out[None], dx[None], gq, pb, go, ob, g1, s1, gu, ub, gd, db, g2, s2)


def widen(starts, *refs):
    sources, results = refs[:8], refs[8:22]
    held, made, insem, outsem = refs[22:30], refs[30:42], refs[42], refs[43]
    out, dx, gqk, gv, go, gu, gd, gsm = held
    C = gsm.shape[1]
    count = [0, 0]

    def fetch(source, ref):
        copy = pltpu.make_async_copy(source, ref, insem.at[count[0]])
        count[0] += 1
        copy.start()
        return copy
    stores = []

    def store(ref, result):
        copy = pltpu.make_async_copy(ref, result, outsem.at[count[1]])
        count[1] += 1
        copy.start()
        stores.append(copy)

    def piece(i, at, n):
        window = (slice(None), pl.ds(at, n)) if len(held[i].shape) == 3 else (pl.ds(at, n),)
        return fetch(sources[i].at[window], held[i].at[window])

    def grouped(i, target, at, n, first):
        source, result = held[i], made[target]
        groups = source.shape[0]

        def step(j, carry):
            rows = pl.ds(pl.multiple_of(at + j * 32, 32), 32)
            for o in range(groups):
                for p in range(source.shape[2] // C):
                    lane = ((first + p) * groups + o) * C
                    result[rows, lane:lane + C] = source[o, rows, p * C:(p + 1) * C].astype(f32)
            return carry
        lax.fori_loop(0, n // 32, step, 0)

    def plain(i, target, at, n, _):
        source, result = held[i], made[target]

        def step(j, carry):
            rows = pl.ds(pl.multiple_of(at + j * 32, 32), 32)
            result[rows, :] = source[rows, :].astype(f32)
            return carry
        lax.fori_loop(0, n // 32, step, 0)

    work = []
    for i, target, n, body, first in ((5, 2, 64, grouped, 0), (6, 3, 256, plain, 0), (2, 0, 64, grouped, 0),
                                      (3, 0, 64, grouped, 2), (4, 1, 256, plain, 0)):
        total = held[i].shape[-2]
        for at in range(0, total, n):
            work.append((piece(i, at, n), i, target, at, n, body, first))
    whole = [fetch(sources[i], held[i]) for i in (0, 1, 7)]
    for copy, i, target, at, n, body, first in work:
        copy.wait()
        body(i, target, at, n, first)
        if i != 2:
            rows = pl.ds(at, n)
            store(made[target].at[rows], results[2 + target].at[rows])
    for copy in whole:
        copy.wait()
    store(out, results[0])
    store(dx, results[1])
    for start, ref, result in zip(starts, made[4:], results[6:]):
        if ref.shape[1] == C:
            ref[...] = gsm[start:start + ref.shape[0], :]
        else:
            for i in range(ref.shape[1] // C):
                ref[0:1, i * C:(i + 1) * C] = gsm[start + i:start + i + 1, :]
        store(ref, result)
    for copy in stores:
        copy.wait()


BATCHES = 42
LANDINGS = 148
LOCAL = 32


def fits(mesh):
    return mesh.shape["seq"] == 8 and mesh.shape["fsdp"] == 4


def solution(mesh):
    return jax.shard_map(
        fused_shards if fits(mesh) else shards,
        mesh=mesh,
        in_specs=(
            P("fsdp", "seq", None),
            P("fsdp", "seq", None),
            P("fsdp", None),
            P("fsdp", None),
            P("fsdp"),
            P("fsdp", None),
            P("fsdp"),
            P("fsdp"),
            P("fsdp"),
            P("fsdp", None),
            P("fsdp"),
            P("fsdp", None),
            P("fsdp"),
            P("fsdp"),
            P("fsdp"),
        ),
        out_specs=(
            P("fsdp", "seq", None),
            P("fsdp", "seq", None),
            P("fsdp", None),
            P("fsdp"),
            P("fsdp", None),
            P("fsdp"),
            P("fsdp"),
            P("fsdp"),
            P("fsdp", None),
            P("fsdp"),
            P("fsdp", None),
            P("fsdp"),
            P("fsdp"),
            P("fsdp"),
        ),
        check_vma=False,
    )
```

```python
from functools import partial

import jax
import jax.numpy as jnp
import numpy as np
import math
from types import SimpleNamespace
from jax import lax
from jax.experimental import pallas as pl
from jax.experimental.pallas import tpu as pltpu
from jax.sharding import PartitionSpec as P

HEADS = 16
HEAD_DIM = 64


norm_epsilon = 1e-05


def rotary(values, positions):
    half = values.shape[-1] // 2
    channel = jnp.arange(half).astype(jnp.float32)
    inverse = 10000.0 ** (-2.0 * channel / values.shape[-1])
    angles = positions[:, None] * inverse[None, :]
    cosine = jnp.cos(angles)[:, None, :]
    sine = jnp.sin(angles)[:, None, :]
    first = values[..., :half]
    second = values[..., half:]
    return jnp.concatenate(
        [first * cosine - second * sine, second * cosine + first * sine], axis=-1
    )


def rotary_back(grads, positions):
    unused, pullback = jax.vjp(lambda inner: rotary(inner, positions), grads)
    return pullback(grads)[0]


def norm_forward(values, gain, shift):
    centre = values - jnp.mean(values, axis=-1, keepdims=True)
    inverse_root = lax.rsqrt(jnp.mean(centre * centre, axis=-1, keepdims=True) + norm_epsilon)
    normal = centre * inverse_root
    return (normal * gain + shift, normal, inverse_root)


def norm_backward(incoming, normal, inverse_root, gain):
    gain_grad = jnp.sum(incoming * normal, axis=0)
    shift_grad = jnp.sum(incoming, axis=0)
    scaled = incoming * gain
    inner = (
        scaled
        - jnp.mean(scaled, axis=-1, keepdims=True)
        - normal * jnp.mean(scaled * normal, axis=-1, keepdims=True)
    )
    return (inner * inverse_root, gain_grad, shift_grad)


def shards(
    hidden_in,
    cotangent,
    segment_ids,
    projection,
    projection_bias,
    output_weight,
    output_bias,
    first_gain,
    first_shift,
    up_weight,
    up_bias,
    down_weight,
    down_bias,
    second_gain,
    second_shift,
):
    bf16 = jnp.bfloat16
    f32 = jnp.float32
    tokens = hidden_in[0]
    local_rows = tokens.shape[0]
    width = tokens.shape[1]
    seq_rank = lax.axis_index("seq")
    positions = (seq_rank * local_rows + jnp.arange(local_rows)).astype(f32)
    segments = segment_ids[0]
    scale = HEAD_DIM ** (-0.5)
    attention_full = (
        lax.all_gather(projection.astype(bf16), "fsdp", axis=0, tiled=True),
        lax.all_gather(projection_bias.astype(bf16), "fsdp", axis=0, tiled=True),
        lax.all_gather(output_weight.astype(bf16), "fsdp", axis=0, tiled=True),
        lax.all_gather(output_bias.astype(bf16), "fsdp", axis=0, tiled=True),
        lax.all_gather(first_gain.astype(bf16), "fsdp", axis=0, tiled=True),
        lax.all_gather(first_shift.astype(bf16), "fsdp", axis=0, tiled=True),
    )
    proj_weight = attention_full[0]
    projected = jnp.dot(tokens, proj_weight, preferred_element_type=f32) + attention_full[1].astype(
        f32
    )
    heads = projected.reshape(local_rows, 3, HEADS, HEAD_DIM)
    queries = rotary(heads[:, 0], positions)
    keys = rotary(heads[:, 1], positions)
    stacked = jnp.stack([queries, keys, heads[:, 2]]).astype(bf16)
    spread = lax.all_to_all(stacked, "seq", split_axis=2, concat_axis=1, tiled=True)
    query_all = spread[0]
    key_all = spread[1]
    value_all = spread[2]
    length = query_all.shape[0]
    local_heads = query_all.shape[1]
    block = min(512, length)
    count = length // block
    query_blocks = query_all.reshape(count, block, local_heads, HEAD_DIM)
    segment_blocks = segments.reshape(count, block)

    def scores_of(query_block, segment_block):
        raw = jnp.einsum("qhd,khd->hqk", query_block, key_all, preferred_element_type=f32) * scale
        allowed = segment_block[:, None] == segments[None, :]
        return jnp.where(allowed[None], raw, -1e30)

    def forward_block(pieces):
        query_block, segment_block = pieces
        scores = scores_of(query_block, segment_block)
        row_max = jnp.max(scores, axis=-1, keepdims=True)
        exponent = jnp.exp(scores - row_max)
        total = jnp.sum(exponent, axis=-1, keepdims=True)
        weights = exponent / total
        context = jnp.einsum(
            "hqk,khd->qhd", weights.astype(bf16), value_all, preferred_element_type=f32
        )
        return (context.astype(bf16), (row_max + jnp.log(total))[..., 0])

    context_blocks, log_totals = lax.map(forward_block, (query_blocks, segment_blocks))
    context_heads = context_blocks.reshape(length, local_heads, HEAD_DIM)
    context_tokens = lax.all_to_all(
        context_heads, "seq", split_axis=0, concat_axis=1, tiled=True
    ).reshape(local_rows, width)
    attended = jnp.dot(
        context_tokens, attention_full[2], preferred_element_type=f32
    ) + attention_full[3].astype(f32)
    gain_one = attention_full[4].astype(f32)
    normed_one, normal_one, inverse_one = norm_forward(
        tokens.astype(f32) + attended, gain_one, attention_full[5].astype(f32)
    )
    feed_full = (
        lax.all_gather(up_weight.astype(bf16), "fsdp", axis=0, tiled=True),
        lax.all_gather(up_bias.astype(bf16), "fsdp", axis=0, tiled=True),
        lax.all_gather(down_weight.astype(bf16), "fsdp", axis=0, tiled=True),
        lax.all_gather(down_bias.astype(bf16), "fsdp", axis=0, tiled=True),
        lax.all_gather(second_gain.astype(bf16), "fsdp", axis=0, tiled=True),
        lax.all_gather(second_shift.astype(bf16), "fsdp", axis=0, tiled=True),
    )
    normed_low = normed_one.astype(bf16)
    lifted = jnp.dot(normed_low, feed_full[0], preferred_element_type=f32) + feed_full[1].astype(
        f32
    )
    activated = jax.nn.gelu(lifted, approximate=False).astype(bf16)
    lowered = jnp.dot(activated, feed_full[2], preferred_element_type=f32) + feed_full[3].astype(
        f32
    )
    gain_two = feed_full[4].astype(f32)
    layer_out, normal_two, inverse_two = norm_forward(
        normed_one + lowered, gain_two, feed_full[5].astype(f32)
    )
    feed_back = (
        lax.all_gather(up_weight.astype(bf16), "fsdp", axis=0, tiled=True),
        lax.all_gather(up_bias.astype(bf16), "fsdp", axis=0, tiled=True),
        lax.all_gather(down_weight.astype(bf16), "fsdp", axis=0, tiled=True),
        lax.all_gather(down_bias.astype(bf16), "fsdp", axis=0, tiled=True),
        lax.all_gather(second_gain.astype(bf16), "fsdp", axis=0, tiled=True),
        lax.all_gather(second_shift.astype(bf16), "fsdp", axis=0, tiled=True),
    )
    attention_back = (
        lax.all_gather(projection.astype(bf16), "fsdp", axis=0, tiled=True),
        lax.all_gather(projection_bias.astype(bf16), "fsdp", axis=0, tiled=True),
        lax.all_gather(output_weight.astype(bf16), "fsdp", axis=0, tiled=True),
        lax.all_gather(output_bias.astype(bf16), "fsdp", axis=0, tiled=True),
        lax.all_gather(first_gain.astype(bf16), "fsdp", axis=0, tiled=True),
        lax.all_gather(first_shift.astype(bf16), "fsdp", axis=0, tiled=True),
    )
    grad_two, second_gain_grad, second_shift_grad = norm_backward(
        cotangent[0].astype(f32), normal_two, inverse_two, gain_two
    )
    lowered_grad = grad_two.astype(bf16)
    down_weight_grad = jnp.einsum("tf,td->fd", activated, lowered_grad, preferred_element_type=f32)
    down_bias_grad = jnp.sum(lowered_grad.astype(f32), axis=0)
    active_grad = jnp.einsum("td,fd->tf", lowered_grad, feed_back[2], preferred_element_type=f32)
    unused, gelu_pull = jax.vjp(partial(jax.nn.gelu, approximate=False), lifted)
    lifted_grad = gelu_pull(active_grad)[0].astype(bf16)
    up_weight_grad = jnp.einsum("td,tf->df", normed_low, lifted_grad, preferred_element_type=f32)
    up_bias_grad = jnp.sum(lifted_grad.astype(f32), axis=0)
    normed_grad = grad_two + jnp.einsum(
        "tf,df->td", lifted_grad, feed_back[0], preferred_element_type=f32
    )
    grad_one, first_gain_grad, first_shift_grad = norm_backward(
        normed_grad, normal_one, inverse_one, attention_back[4].astype(f32)
    )
    attended_grad = grad_one.astype(bf16)
    output_weight_grad = jnp.einsum(
        "tc,td->cd", context_tokens, attended_grad, preferred_element_type=f32
    )
    output_bias_grad = jnp.sum(attended_grad.astype(f32), axis=0)
    context_grad = jnp.einsum(
        "td,cd->tc", attended_grad, attention_back[2], preferred_element_type=f32
    ).astype(bf16)
    context_grad = context_grad.reshape(local_rows, HEADS, HEAD_DIM)
    context_grad_heads = lax.all_to_all(
        context_grad, "seq", split_axis=1, concat_axis=0, tiled=True
    )
    grad_blocks = context_grad_heads.reshape(count, block, local_heads, HEAD_DIM)

    def backward_block(carry, pieces):
        key_grad, value_grad = carry
        query_block, segment_block, grad_block, log_block = pieces
        scores = scores_of(query_block, segment_block)
        weights = jnp.exp(scores - log_block[..., None])
        value_grad = value_grad + jnp.einsum(
            "hqk,qhd->khd", weights.astype(bf16), grad_block, preferred_element_type=f32
        )
        weight_grad = jnp.einsum("qhd,khd->hqk", grad_block, value_all, preferred_element_type=f32)
        centre = jnp.sum(weights * weight_grad, axis=-1, keepdims=True)
        score_grad = (weights * (weight_grad - centre)).astype(bf16)
        query_grad = (
            jnp.einsum("hqk,khd->qhd", score_grad, key_all, preferred_element_type=f32) * scale
        )
        key_grad = (
            key_grad
            + jnp.einsum("hqk,qhd->khd", score_grad, query_block, preferred_element_type=f32)
            * scale
        )
        return ((key_grad, value_grad), query_grad)

    zeros_heads = jnp.zeros((length, local_heads, HEAD_DIM), f32)
    (key_grad, value_grad), query_grad = lax.scan(
        backward_block,
        (zeros_heads, zeros_heads),
        (query_blocks, segment_blocks, grad_blocks, log_totals),
    )
    query_grad = query_grad.reshape(length, local_heads, HEAD_DIM)
    stacked_grad = jnp.stack([query_grad, key_grad, value_grad]).astype(bf16)
    token_heads = lax.all_to_all(stacked_grad, "seq", split_axis=1, concat_axis=2, tiled=True)
    query_back = rotary_back(token_heads[0].astype(f32), positions)
    key_back = rotary_back(token_heads[1].astype(f32), positions)
    projected_grad = jnp.stack([query_back, key_back, token_heads[2].astype(f32)], axis=1)
    projected_grad = projected_grad.reshape(local_rows, 3 * width).astype(bf16)
    projection_grad = jnp.einsum("td,te->de", tokens, projected_grad, preferred_element_type=f32)
    projection_bias_grad = jnp.sum(projected_grad.astype(f32), axis=0)
    input_grad = grad_one + jnp.einsum(
        "te,de->td", projected_grad, attention_back[0], preferred_element_type=f32
    )
    every_shard = (
        lax.psum_scatter(
            projection_grad.astype(jnp.bfloat16), "fsdp", scatter_dimension=0, tiled=True
        ).astype(jnp.float32),
        lax.psum_scatter(
            projection_bias_grad.astype(jnp.bfloat16), "fsdp", scatter_dimension=0, tiled=True
        ).astype(jnp.float32),
        lax.psum_scatter(
            output_weight_grad.astype(jnp.bfloat16), "fsdp", scatter_dimension=0, tiled=True
        ).astype(jnp.float32),
        lax.psum_scatter(
            output_bias_grad.astype(jnp.bfloat16), "fsdp", scatter_dimension=0, tiled=True
        ).astype(jnp.float32),
        lax.psum_scatter(
            first_gain_grad.astype(jnp.bfloat16), "fsdp", scatter_dimension=0, tiled=True
        ).astype(jnp.float32),
        lax.psum_scatter(
            first_shift_grad.astype(jnp.bfloat16), "fsdp", scatter_dimension=0, tiled=True
        ).astype(jnp.float32),
        lax.psum_scatter(
            up_weight_grad.astype(jnp.bfloat16), "fsdp", scatter_dimension=0, tiled=True
        ).astype(jnp.float32),
        lax.psum_scatter(
            up_bias_grad.astype(jnp.bfloat16), "fsdp", scatter_dimension=0, tiled=True
        ).astype(jnp.float32),
        lax.psum_scatter(
            down_weight_grad.astype(jnp.bfloat16), "fsdp", scatter_dimension=0, tiled=True
        ).astype(jnp.float32),
        lax.psum_scatter(
            down_bias_grad.astype(jnp.bfloat16), "fsdp", scatter_dimension=0, tiled=True
        ).astype(jnp.float32),
        lax.psum_scatter(
            second_gain_grad.astype(jnp.bfloat16), "fsdp", scatter_dimension=0, tiled=True
        ).astype(jnp.float32),
        lax.psum_scatter(
            second_shift_grad.astype(jnp.bfloat16), "fsdp", scatter_dimension=0, tiled=True
        ).astype(jnp.float32),
    )
    finals = (
        lax.psum(every_shard[0].astype(jnp.bfloat16), "seq").astype(jnp.float32),
        lax.psum(every_shard[1].astype(jnp.bfloat16), "seq").astype(jnp.float32),
        lax.psum(every_shard[2].astype(jnp.bfloat16), "seq").astype(jnp.float32),
        lax.psum(every_shard[3].astype(jnp.bfloat16), "seq").astype(jnp.float32),
        lax.psum(every_shard[4].astype(jnp.bfloat16), "seq").astype(jnp.float32),
        lax.psum(every_shard[5].astype(jnp.bfloat16), "seq").astype(jnp.float32),
        lax.psum(every_shard[6].astype(jnp.bfloat16), "seq").astype(jnp.float32),
        lax.psum(every_shard[7].astype(jnp.bfloat16), "seq").astype(jnp.float32),
        lax.psum(every_shard[8].astype(jnp.bfloat16), "seq").astype(jnp.float32),
        lax.psum(every_shard[9].astype(jnp.bfloat16), "seq").astype(jnp.float32),
        lax.psum(every_shard[10].astype(jnp.bfloat16), "seq").astype(jnp.float32),
        lax.psum(every_shard[11].astype(jnp.bfloat16), "seq").astype(jnp.float32),
    )
    return (
        layer_out.astype(bf16)[None],
        input_grad.astype(bf16)[None],
        finals[0],
        finals[1],
        finals[2],
        finals[3],
        finals[4],
        finals[5],
        finals[6],
        finals[7],
        finals[8],
        finals[9],
        finals[10],
        finals[11],
    )


MESH = pl.DeviceIdType.MESH
NN = (((1,), (0,)), ((), ()))
NT = (((1,), (1,)), ((), ()))
TN = (((0,), (0,)), ((), ()))
f32 = jnp.float32
bf16 = jnp.bfloat16
MASKED = -1e30


def mm(left, right, dims=NN):
    return lax.dot_general(left, right, dims, preferred_element_type=f32)


def block_of(index, size):
    return pl.ds(pl.multiple_of(index * size, size), size)


def flip(bit, other):
    return bit + other - 2 * bit * other


def fused_layer(sizes, *refs):
    r = SimpleNamespace(**dict(zip(sizes.names, refs)))
    T, D, L, F = sizes.T, sizes.D, sizes.L, sizes.F
    S, Z = 8, 4
    KW = D // Z
    UZ = F // Z
    C = 128
    T2 = 2 * T
    first_row = sizes.first_row
    ssem, rsem, lsem = r.ssem, r.rsem, r.lsem

    s = lax.axis_index("seq")
    z = lax.axis_index("fsdp")
    core, xbit, ybit = s % 2, (s // 2) % 2, s // 4
    zlow, zhigh = z % 2, z // 2

    def ps(k):
        return flip(core, k % 2) + 2 * flip(xbit, (k // 2) % 2) + 4 * flip(ybit, k // 4)

    def pz(k):
        return flip(zlow, k % 2) + 2 * flip(zhigh, k // 2)

    def chip_of(j):
        return flip(xbit, j % 2) + 2 * flip(ybit, j // 2)

    counter = [0, 0, 0]
    closing = []

    def take(which, n=1):
        counter[which] += n
        return counter[which] - n

    def landings(n=1):
        return take(0, n)

    def size(ref):
        return math.prod(ref.shape) * jnp.dtype(ref.dtype).itemsize

    def extent(n):
        if n <= size(r.c_f):
            return r.c_f.at[pl.ds(0, n * L // size(r.c_f))]
        return r.y_all.at[pl.ds(0, n * L // size(r.y_all))]

    def arrived(ref, slot):
        pltpu.make_async_copy(ref, ref, rsem.at[slot]).wait()

    class Batch:
        def __init__(self, count, like):
            self.slot, self.bytes, self.open = take(1), count * size(like), True
            closing.append(self)

        def send(self, src, dst, slot, dev):
            pltpu.make_async_remote_copy(
                src_ref=src, dst_ref=dst, send_sem=ssem.at[self.slot], recv_sem=rsem.at[slot],
                device_id=dev, device_id_type=MESH).start()

        def close(self):
            if self.open:
                everything = extent(self.bytes)
                pltpu.make_async_copy(everything, everything, ssem.at[self.slot]).wait()
            self.open = False

    def local(src, dst):
        copy = pltpu.make_async_copy(src, dst, lsem.at[take(2)])
        copy.start()
        return copy

    class Gather:
        def __init__(self, place, at_once=True):
            self.place, self.at_once = place, at_once
            self.batch = Batch(7, place(0))
            self.near, self.across = landings(4), landings(2)
            self.other = landings() if at_once else landings(4)

        def part(self, ref, i):
            n = ref.shape[0] // 2
            return ref.at[pl.ds(i * n, n)]

        def start(self, src=None):
            mine = self.place(s)
            src = mine if src is None else src
            for slot, half, k in ((0, 0, 2), (3, 1, 4), (1, 1, 2), (2, 0, 4)):
                self.batch.send(self.part(src, half), self.part(mine, half), self.near + slot, (ps(k), z))
            self.batch.send(src, mine, self.other, (ps(1), z))

        def to_partner(self, k):
            there = self.place(ps(k))
            self.batch.send(there, there, self.other + (0 if self.at_once else k // 2), (ps(1), z))

        def pass_near(self):
            along_x, along_y = self.place(ps(2)), self.place(ps(4))
            first, second = self.part(along_x, 0), self.part(along_y, 1)
            arrived(first, self.near)
            self.batch.send(first, first, self.across, (ps(4), z))
            arrived(second, self.near + 3)
            self.batch.send(second, second, self.across + 1, (ps(2), z))
            arrived(self.part(along_x, 1), self.near + 1)
            self.to_partner(2)
            arrived(self.part(along_y, 0), self.near + 2)
            self.to_partner(4)

        def pass_far(self):
            far = self.place(ps(6))
            arrived(self.part(far, 0), self.across)
            arrived(self.part(far, 1), self.across + 1)
            self.to_partner(6)

        def pass_all(self):
            self.pass_near()
            self.pass_far()

        def wait(self, k=None):
            if self.at_once:
                arrived(extent(4 * size(self.place(0))), self.other)
            else:
                arrived(self.place(ps(k)), self.other + k // 2)

    class Spread:
        def __init__(self, place):
            self.place, self.batch, self.base = place, Batch(3, place(0)), landings(3)

        def start(self, *which):
            mine = self.place(z)
            for k in which or (2, 1):
                self.batch.send(mine, mine, self.base + k - 1, (s, pz(k)))

        def pass_on(self):
            there = self.place(pz(2))
            arrived(there, self.base + 1)
            self.batch.send(there, there, self.base + 2, (s, pz(1)))

        def wait(self):
            for k in (1, 3):
                arrived(self.place(pz(k)), self.base + k - 1)

        def wait_all(self):
            for k in (1, 2, 3):
                arrived(self.place(pz(k)), self.base + k - 1)

    class Fold:
        def __init__(self, parts, landing, passing, first=0, count=None):
            self.rows = pl.ds(first, count or passing.shape[0])
            self.parts, self.landing, self.passing = parts, landing, passing.at[self.rows]
            self.batch, self.base = Batch(3, self.passing), landings(3)

        def start(self):
            for i, k in ((1, 3), (0, 1)):
                self.batch.send(self.parts.at[pz(k), self.rows], self.landing.at[i, self.rows], self.base + i, (s, pz(1)))

        def middle(self):
            arrived(self.landing.at[1, self.rows], self.base + 1)
            self.passing[...] = (self.parts[pz(2), self.rows, :].astype(f32)
                                 + self.landing[1, self.rows, :].astype(f32)).astype(bf16)
            self.batch.send(self.passing, self.landing.at[2, self.rows], self.base + 2, (s, pz(2)))

        def finish(self):
            arrived(self.landing.at[0, self.rows], self.base)
            arrived(self.landing.at[2, self.rows], self.base + 2)
            return (self.parts[z, self.rows, :].astype(f32) + self.landing[0, self.rows, :].astype(f32)
                    + self.landing[2, self.rows, :].astype(f32)).astype(bf16)

    class Scatter:
        def __init__(self, parts, low, mid, high, first=0, count=T):
            self.parts, self.low, self.mid, self.high = parts, low, mid, high
            self.first, self.count, self.window = first, count, pl.ds(first, count)
            self.batch = Batch(7, mid.at[0, self.window])
            self.base, self.far, self.last = landings(4), landings(2), landings()

        def rows_of(self, which):
            return pl.ds(pl.multiple_of(which * T + self.first, self.count), self.count)

        def half(self, ref, j, i):
            return ref.at[j, self.window, pl.ds(i * (D // 2), D // 2)]

        def send(self, j, i, slot, k):
            self.batch.send(self.half(self.mid, j, i), self.half(self.high, j, i), slot, (ps(k), z))

        def pair(self, j):
            self.batch.send(self.parts.at[j, self.rows_of(1 - core)], self.low.at[j, self.window],
                            self.base + j, (ps(1), z))

        def onward(self, j):
            arrived(self.low.at[j, self.window], self.base + j)
            own = self.parts[j, self.rows_of(core), :].astype(f32)
            self.mid[j, self.window, :] = (own + self.low[j, self.window, :].astype(f32)).astype(bf16)
            if j == 1:
                self.send(1, 0, self.last, 2)
            elif j == 2:
                self.send(2, 1, self.last, 4)
            else:
                self.send(3, 0, self.far, 2)
                self.send(3, 1, self.far + 1, 4)

        def cross(self):
            for j, i, k in ((2, 0, 4), (1, 1, 2)):
                arrived(self.half(self.high, 3, i), self.far + i)
                ref = self.half(self.mid, j, i)
                ref[...] = (ref[...].astype(f32) + self.half(self.high, 3, i)[...].astype(f32)).astype(bf16)
                self.send(j, i, self.last, k)

        def ready(self):
            arrived(self.low.at[0, self.window], self.base)
            arrived(self.high.at[pl.ds(1, 2), self.window], self.last)

        def rows(self, at, n):
            own = self.parts[0, pl.ds(pl.multiple_of(core * T + at, n), n), :].astype(f32)
            total = own + self.low[0, pl.ds(at, n), :].astype(f32)
            for j in (1, 2):
                total = total + self.high[j, pl.ds(at, n), :].astype(f32)
            return total

    class Share:
        def __init__(self, count, like):
            self.count, self.batch, self.slot, self.bytes = count, Batch(count, like), landings(), count * size(like)

        def plane(self, src, dst):
            for k in (6, 7, 2, 3, 4, 5, 1):
                self.batch.send(src(ps(k)), dst, self.slot, (ps(k), z))

        def column(self, src, dst):
            for k in (2, 3, 1):
                self.batch.send(src, dst, self.slot, (s, pz(k)))

        def wait(self):
            arrived(extent(self.bytes), self.slot)

    def loop(count, body, unroll=1):
        def step(i, carry):
            body(i)
            return carry
        lax.fori_loop(0, count, step, 0, unroll=unroll)

    def at(i, n):
        return pl.multiple_of(i * n, n)

    def turn(src, dst):
        def one(i):
            dst[:, pl.ds(at(i, T), T)] = jnp.transpose(src[pl.ds(at(i, T), T), :])
        loop(L // T, one)

    vec, vecg = r.vec, r.vecg

    OUTPUT_BIAS, FIRST_GAIN, FIRST_SHIFT, DOWN_BIAS, SECOND_GAIN, SECOND_SHIFT, PROJECTION_BIAS, UP_BIAS = range(8)
    wide = ((first_row.output_bias, OUTPUT_BIAS), (first_row.first_gain, FIRST_GAIN),
            (first_row.first_shift, FIRST_SHIFT), (first_row.down_bias, DOWN_BIAS),
            (first_row.second_gain, SECOND_GAIN), (first_row.second_shift, SECOND_SHIFT))

    def row(i, width=D):
        return vec[i:i + 1, :width]

    lanes = lax.broadcasted_iota(jnp.int32, (T, C), 1)
    low_head = lanes < HEAD_DIM

    def swapped(w):
        low_half = lax.broadcasted_iota(jnp.int32, w.shape, 1) % HEAD_DIM < HEAD_DIM // 2
        return jnp.where(low_half, pltpu.roll(w, C - HEAD_DIM // 2, 1), pltpu.roll(w, HEAD_DIM // 2, 1))

    def stacked(w):
        nothing = jnp.zeros_like(w)
        return jnp.concatenate([jnp.where(low_head, w, nothing), jnp.where(low_head, nothing, w)], axis=0)

    def unstacked(w):
        return jnp.where(low_head, w[:T], w[T:])

    barrier = pltpu.get_barrier_semaphore()
    for k in range(1, S):
        pl.semaphore_signal(barrier, inc=1, device_id=(ps(k), z), device_id_type=MESH)
    for k in range(1, Z):
        pl.semaphore_signal(barrier, inc=1, device_id=(s, pz(k)), device_id_type=MESH)
    x_ref, ct_ref = r.v_x, r.v_ct
    x_load = local(r.x, x_ref)
    wo_load = local(r.wo.at[:, block_of(s, C)], r.st_wo)
    proj_loads = [local(r.proj.at[:, block_of(i * (D // C) + s, C)], r.st_proj.at[:, pl.ds(i * C, C)])
                  for i in range(3)]
    raw = ((r.b_projection, r.v_projection, first_row.projection_bias), (r.b_output, r.v_output, first_row.output_bias),
           (r.gain1, r.v_gain1, first_row.first_gain), (r.shift1, r.v_shift1, first_row.first_shift),
           (r.b_up, r.v_up, first_row.up_bias), (r.b_down, r.v_down, first_row.down_bias),
           (r.gain2, r.v_gain2, first_row.second_gain), (r.shift2, r.v_shift2, first_row.second_shift))
    raw_loads = [local(source, ref) for source, ref, _ in raw]
    seg_load = local(r.seg, r.v_seg)
    up_loads = [local(r.up.at[:, block_of(i * (D // C) + s, C)], r.st_up.at[:, pl.ds(i * C, C)])
                for i in range(Z)]
    dn_load = local(r.dn.at[block_of(s, UZ), :], r.st_dn)
    late_loads = [local(r.cos, r.v_cos), local(r.sin, r.v_sin), local(r.ct, ct_ref)]
    cos_ref, sin_ref = r.v_cos, r.v_sin

    x_all, w_qkv, w_o, w_up, w_dn = r.x_all, r.w_qkv, r.w_o, r.w_up, r.w_dn
    gather_x = Gather(lambda o: x_all.at[block_of(o, T)])
    spread_qkv = Spread(lambda p: w_qkv.at[block_of(p, KW)])
    spread_o = Spread(lambda p: w_o.at[block_of(p, KW), block_of(s, C)])
    spread_up = Spread(lambda p: w_up.at[block_of(p, KW)])
    spread_dn = Spread(lambda p: w_dn.at[block_of(p, UZ)])
    gather_o = Gather(lambda o: w_o.at[:, block_of(o, C)])
    wo_load.wait()
    w_o[block_of(z, KW), block_of(s, C)] = r.st_wo[...].astype(bf16)
    for copy in proj_loads:
        copy.wait()
    w_qkv[block_of(z, KW), :] = r.st_proj[...].astype(bf16)
    x_load.wait()
    pl.semaphore_wait(barrier, S + Z - 2)
    spread_o.start(2, 3, 1)
    spread_qkv.start()
    gather_x.start(x_ref)

    small, small_all, seg_c, seg_r = r.small, r.small_all, r.seg_c, r.seg_r
    for copy, (_, ref, start) in zip(raw_loads, raw):
        copy.wait()
        if ref.shape[1] == C:
            small[start:start + ref.shape[0], :] = ref[...].astype(bf16).astype(f32)
        else:
            for i in range(ref.shape[1] // C):
                small[start + i:start + i + 1, :] = ref[0:1, i * C:(i + 1) * C].astype(bf16).astype(f32)
    x_all[block_of(s, T), :] = x_ref[...]
    vecg[...] = jnp.zeros((8, D), f32)
    seg_load.wait()
    seg_r[...] = jnp.broadcast_to(r.v_seg[...].astype(f32), (8, L))

    def seg_turn(i):
        here = pl.ds(at(i, T), T)
        seg_c[here, :] = jnp.transpose(jnp.broadcast_to(seg_r[0:1, here], (T, T)))
    loop(L // T, seg_turn)
    for copy in up_loads:
        copy.wait()
    w_up[block_of(z, KW), :] = r.st_up[...].astype(bf16)
    dn_load.wait()
    w_dn[block_of(z, UZ), :] = r.st_dn[...].astype(bf16)
    share_small = Share(3, small)
    small_all[z] = small[...]

    gather_x.pass_near()
    spread_o.wait_all()
    gather_o.start()
    gather_x.pass_far()
    gather_x.wait()
    spread_qkv.pass_on()
    share_small.column(small, small_all.at[z])
    spread_up.start()
    x_t = r.x_t
    turn(x_all, x_t)
    for copy in late_loads:
        copy.wait()
    gather_o.pass_near()
    spread_qkv.wait()
    share_small.wait()
    for p in range(Z):
        for start, i in wide:
            for half in range(KW // C):
                at_row = start + half
                lane = (p * (KW // C) + half) * C
                vec[i:i + 1, lane:lane + C] = small_all[p, at_row:at_row + 1, :]
        vec[7:8, p * C:(p + 1) * C] = small_all[p, pl.ds(first_row.up_bias + s, 1), :]
    per = 3 * D // (C * Z)
    for t in range(3):
        number = t * (D // C) + s
        vec[6:7, t * C:(t + 1) * C] = small_all[number // per, pl.ds(first_row.projection_bias + number % per, 1), :]

    q_ref, k_ref, v_ref = r.q, r.k, r.v
    scale = HEAD_DIM ** -0.5

    def project(i):
        here = pl.ds(at(i, T2), T2)
        out = mm(x_all[here, :], w_qkv[...]) + row(PROJECTION_BIAS, 3 * C)
        cosine, sine = cos_ref[here, :], sin_ref[here, :]
        q0, k0 = out[:, :C], out[:, C:2 * C]
        q_ref[here, :] = ((q0 * cosine + swapped(q0) * sine).astype(bf16).astype(f32) * scale).astype(bf16)
        k_ref[here, :] = (k0 * cosine + swapped(k0) * sine).astype(bf16)
        v_ref[here, :] = out[:, 2 * C:].astype(bf16)
    loop(L // T2, project)
    gather_o.pass_far()

    lse, c_f, c_heads, c_tok = r.lse, r.c_f, r.c_heads, r.c_tok
    R = 16

    def same_document(here):
        return jnp.tile(seg_c[here, :], (1, L // C)) == seg_r[0:1, :]

    def both(w):
        return jnp.concatenate([w, w], axis=0)

    def attend(o):
        here = block_of(o, T)
        score = jnp.where(both(same_document(here)), mm(stacked(q_ref[here, :]), k_ref[...], NT), MASKED)
        top = jnp.max(score, axis=-1, keepdims=True)
        power = jnp.exp(score - top)
        total = jnp.sum(power, axis=-1, keepdims=True)
        context = unstacked(mm(power.astype(bf16), v_ref[...]) * (1.0 / total))
        c_f[here, :] = context
        c_heads[here, :] = context.astype(bf16)
        logs = jnp.broadcast_to(top + jnp.log(total), (T2, C))
        for h in range(2):
            lse[h:h + 1, here] = jnp.transpose(logs[h * T:(h + 1) * T, :])[0:1, :]

    share_c = Share(7, c_heads.at[pl.ds(0, T)])

    def attend_and_send(i):
        k = 7 - i
        attend(ps(k))

        @pl.when(k > 0)
        def _():
            share_c.batch.send(c_heads.at[block_of(ps(k), T)], c_tok.at[:, block_of(s, C)], share_c.slot, (ps(k), z))
    loop(8, attend_and_send)
    spread_up.pass_on()
    spread_dn.start()
    c_tok[:, block_of(s, C)] = c_heads[block_of(s, T), :]
    gather_o.wait()
    share_c.wait()

    a_buf = r.a_buf
    a_buf[...] = mm(c_tok[...], w_o[...])
    n1, y1, r1, y_all = r.n1, r.y1, r.r1, r.y_all

    def norm(h):
        centre = h - jnp.mean(h, axis=-1, keepdims=True)
        root = lax.rsqrt(jnp.mean(centre * centre, axis=-1, keepdims=True) + norm_epsilon)
        return centre * root, root

    def first_norm(i):
        rows = pl.ds(at(i, R), R)
        normal, root = norm(x_ref[rows, :].astype(f32) + a_buf[rows, :] + row(OUTPUT_BIAS))
        out = normal * row(FIRST_GAIN) + row(FIRST_SHIFT)
        n1[rows, :] = normal
        r1[rows, :] = jnp.broadcast_to(root, (R, C))
        y1[rows, :] = out
        y_all[pl.ds(pl.multiple_of(s * T + i * R, R), R), :] = out.astype(bf16)
    loop(T // R, first_norm, 4)
    gather_y = Gather(lambda o: y_all.at[block_of(o, T)], False)
    gather_y.start()
    c_all = r.c_all
    gather_c = Gather(lambda o: c_all.at[block_of(o, T)])
    c_all[block_of(s, T), :] = c_tok[...]

    u_buf, g_ref, d_ref, du_ref, dz_all = r.u_buf, r.g, r.d, r.du, r.dz_all
    parts, mid = r.parts, r.mid
    spread_up.wait()
    E = 32

    def lift(j):
        q = chip_of(j)
        u_buf[...] = mm(y_all[block_of(q, T2), :], w_up[...])

        def chunk(i):
            rows = pl.ds(at(i, E), E)
            there = pl.ds(pl.multiple_of(q * T2 + i * E, E), E)
            u = u_buf[rows, :] + row(UP_BIAS, F)
            share = 0.5 + 0.5 * lax.erf(u * (0.5 ** 0.5))
            g_ref[there, :] = (u * share).astype(bf16)
            d_ref[there, :] = share + u * (jnp.exp(-0.5 * u * u) * 0.3989422804014327)
        loop(T2 // E, chunk)

    def lower(j):
        parts[j] = mm(g_ref[block_of(chip_of(j), T2), :], w_dn[...]).astype(bf16)

    H = T // 2
    folds_z = [Scatter(parts, r.low0, mid, r.high0, i * H, H) for i in range(2)]
    y_t, g_t = r.y_t, r.g_t
    gather_y.wait(1)
    lift(0)
    gather_y.pass_near()
    gather_y.wait(3)
    lift(1)
    gather_y.wait(5)
    lift(2)
    spread_dn.pass_on()
    gather_y.pass_far()
    gather_c.start(c_tok)
    gather_y.wait(7)
    lift(3)
    turn(y_all, y_t)
    turn(g_ref, g_t)
    spread_dn.wait()
    for j in (3, 1, 2):
        lower(j)
        for fold in folds_z:
            fold.pair(j)
    for j in (3, 1, 2):
        folds_z[0].onward(j)
    folds_z[1].onward(3)
    lower(0)
    for fold in folds_z:
        fold.pair(0)
    folds_z[0].cross()
    folds_z[1].onward(1)
    folds_z[1].onward(2)
    folds_z[1].cross()
    folds_z[0].ready()

    dh2, out_ref = r.dh2, r.v_out

    def add_row(i, value):
        vecg[i:i + 1, :] = vecg[i:i + 1, :] + jnp.sum(value, axis=0, keepdims=True)

    def norm_back(incoming, normal, root, gain):
        scaled = incoming * gain
        return root * (scaled - jnp.mean(scaled, axis=-1, keepdims=True)
                       - normal * jnp.mean(scaled * normal, axis=-1, keepdims=True))

    def second_norm(i):
        start = at(i, R)
        rows = pl.ds(start, R)
        normal, root = norm(y1[rows, :] + folds_z[0].rows(start, R) + row(DOWN_BIAS))
        out_ref[rows, :] = (normal * row(SECOND_GAIN) + row(SECOND_SHIFT)).astype(bf16)
        e = ct_ref[rows, :].astype(f32)
        grad = norm_back(e, normal, root, row(SECOND_GAIN))
        dh2[rows, :] = grad
        dz = grad.astype(bf16)
        dz_all[pl.ds(pl.multiple_of(s * T + i * R, R), R), :] = dz
        add_row(3, dz.astype(f32))
        add_row(4, e * normal)
        add_row(5, e)
    gathers_dz = [Gather(lambda o, i=i: dz_all.at[block_of(2 * o + i, H)], False) for i in range(2)]
    loop(H // R, second_norm, 2)
    gathers_dz[0].start()
    folds_z[1].ready()
    loop(H // R, lambda i: second_norm(i + H // R), 2)
    gathers_dz[1].start()
    outs = [local(out_ref, r.out)]
    for fold in folds_z:
        fold.batch.close()

    colg = r.colg
    colg[...] = jnp.zeros((8, F), f32)

    def unlower(j):
        q = chip_of(j)
        u_buf[...] = mm(dz_all[block_of(q, T2), :], w_dn[...], NT)

        def chunk(i):
            rows = pl.ds(at(i, E), E)
            there = pl.ds(pl.multiple_of(q * T2 + i * E, E), E)
            du = (u_buf[rows, :] * d_ref[there, :]).astype(bf16)
            du_ref[there, :] = du
            colg[0:1, :] = colg[0:1, :] + jnp.sum(du.astype(f32), axis=0, keepdims=True)
        loop(T2 // E, chunk)

    def unlift(j):
        parts[j] = mm(du_ref[block_of(chip_of(j), T2), :], w_up[...], NT).astype(bf16)

    fold_y = Scatter(parts, r.low1, mid, r.high1)
    gd_part, gu_part = r.gd_part, r.gu_part
    folds_dn = [Fold(gd_part, r.gd_land, r.gd_pass, i * (UZ // 2), UZ // 2) for i in range(2)]
    folds_up = [Fold(gu_part, r.gu_land, r.gu_pass, i * (KW // 2), KW // 2) for i in range(2)]

    def down_grad(k):
        gd_part[pz(k)] = mm(g_t[block_of(pz(k), UZ), :], dz_all[...]).astype(bf16)

    def up_grad(k):
        gu_part[pz(k)] = mm(y_t[block_of(pz(k), KW), :], du_ref[...]).astype(bf16)

    def dz_wait(k):
        for gather in gathers_dz:
            gather.wait(k)
    dz_wait(1)
    unlower(0)
    unlift(0)
    fold_y.pair(0)
    gathers_dz[0].pass_near()
    gathers_dz[1].pass_near()
    dz_wait(3)
    unlower(1)
    unlift(1)
    fold_y.pair(1)
    gathers_dz[0].pass_far()
    dz_wait(5)
    unlower(2)
    fold_y.onward(1)
    unlift(2)
    fold_y.pair(2)
    gathers_dz[1].pass_far()
    fold_y.onward(2)
    dz_wait(7)
    down_grad(3)
    down_grad(1)
    folds_dn[0].start()
    folds_dn[1].start()
    unlower(3)
    unlift(3)
    fold_y.pair(3)
    up_grad(3)
    fold_y.onward(3)

    up_grad(1)
    down_grad(2)
    fold_y.cross()
    folds_dn[0].middle()
    folds_up[0].start()
    down_grad(0)
    up_grad(2)
    up_grad(0)
    fold_y.ready()

    dh1, da = r.dh1, r.da

    def first_back(i):
        start = at(i, R)
        rows = pl.ds(start, R)
        incoming = dh2[rows, :] + fold_y.rows(start, R)
        normal = n1[rows, :]
        grad = norm_back(incoming, normal, r1[rows, 0:1], row(FIRST_GAIN))
        dh1[rows, :] = grad
        low = grad.astype(bf16)
        da[rows, :] = low
        add_row(0, low.astype(f32))
        add_row(1, incoming * normal)
        add_row(2, incoming)
    loop(T // R, first_back, 2)
    fold_y.batch.close()

    dc_tok, dc = r.dc_tok, r.dc
    dc_tok[...] = mm(da[...], w_o[...], NT).astype(bf16)
    share_dc = Share(7, dc.at[pl.ds(0, T)])
    share_dc.plane(lambda o: dc_tok.at[:, block_of(o, C)], dc.at[block_of(s, T)])
    dc[block_of(s, T), :] = dc_tok[:, block_of(s, C)]
    da_cols = r.da_cols
    share_da = Share(7, da_cols.at[pl.ds(0, T)])
    share_da.plane(lambda o: da.at[:, block_of(o, C)], da_cols.at[block_of(s, T)])
    da_cols[block_of(s, T), :] = da[:, block_of(s, C)]
    vec_z, vec_all = r.vec_z, r.vec_all
    share_vec = Share(3, vec_z.at[0])
    for k in (2, 3, 1):
        share_vec.batch.send(vecg.at[:, block_of(pz(k), KW)], vec_z.at[z], share_vec.slot, (s, pz(k)))
    vec_z[z] = vecg[:, block_of(z, KW)]
    folds_dn[1].middle()
    folds_up[1].start()
    share_dc.wait()

    delta, dq, dproj = r.delta, r.dq, r.dproj

    def deltas(i):
        here = pl.ds(at(i, T), T)
        turned = jnp.transpose(dc[here, :].astype(f32) * c_f[here, :])
        delta[0:1, here] = jnp.sum(turned[:HEAD_DIM], axis=0, keepdims=True)
        delta[1:2, here] = jnp.sum(turned[HEAD_DIM:], axis=0, keepdims=True)
        dq[here, :] = jnp.zeros((T, C), f32)
    loop(L // T, deltas)

    def attend_back(i):
        here = pl.ds(at(i, T), T)
        same = same_document(here)
        k_here, v_here = k_ref[here, :], v_ref[here, :]
        keys, values, slopes = [], [], []
        for h in range(2):
            own = low_head if h == 0 else jnp.logical_not(low_head)
            nothing = jnp.zeros_like(k_here)
            key = jnp.where(own, k_here, nothing)
            weight = jnp.exp(jnp.where(same, mm(key, q_ref[...], NT), MASKED) - lse[h:h + 1, :])
            slope = mm(jnp.where(own, v_here, nothing), dc[...], NT) - delta[h:h + 1, :]
            slopes.append((weight * slope).astype(bf16))
            values.append(mm(weight.astype(bf16), dc[...]))
            keys.append(key)
        dv = jnp.where(low_head, values[0], values[1]).astype(bf16)
        dk = jnp.where(low_head, mm(slopes[0], q_ref[...]), mm(slopes[1], q_ref[...])).astype(bf16).astype(f32)
        dproj[here, 2 * C:] = dv
        dproj[here, C:2 * C] = (dk * cos_ref[here, :] - swapped(dk) * sin_ref[here, :]).astype(bf16)
        dq[...] = dq[...] + mm(jnp.concatenate(slopes, axis=0), jnp.concatenate(keys, axis=0), TN)

    gd_all, gu_all, go_all, gqk_all, gv_all = r.gd_all, r.gu_all, r.go_all, r.gqk_all, r.gv_all
    gather_gd = Gather(lambda o: gd_all.at[block_of(o, UZ)])
    gather_gu = Gather(lambda o: gu_all.at[o])
    gather_go = Gather(lambda o: go_all.at[:, block_of(o, C)])
    gather_gqk = Gather(lambda o: gqk_all.at[o])
    gather_gv = Gather(lambda o: gv_all.at[o])
    go_part = r.go_part
    fold_o = Fold(go_part, r.go_land, r.go_pass)

    def out_grad(k):
        go_part[pz(k)] = mm(c_all[:, block_of(pz(k), KW)], da_cols[...], TN).astype(bf16)

    def attend_back_and_fold(i):
        attend_back(i)

        @pl.when(i == 0)
        def _():
            gather_c.pass_near()

        @pl.when(i == 5)
        def _():
            for part in range(2):
                at_row = pl.multiple_of(s * UZ + part * (UZ // 2), UZ // 2)
                gd_all[pl.ds(at_row, UZ // 2), :] = folds_dn[part].finish()
            gather_gd.start()

        @pl.when(i == 6)
        def _():
            folds_up[0].middle()
            gather_c.pass_far()
    loop(L // T, attend_back_and_fold)


    def dq_rows(i):
        here = pl.ds(at(i, T), T)
        whole = (dq[here, :] * scale).astype(bf16).astype(f32)
        dproj[here, :C] = (whole * cos_ref[here, :] - swapped(whole) * sin_ref[here, :]).astype(bf16)
        colg[1:2, :3 * C] = colg[1:2, :3 * C] + jnp.sum(dproj[here, :].astype(f32), axis=0, keepdims=True)
    loop(L // T, dq_rows)

    gqk_part, gv_part = r.gqk_part, r.gv_part
    fold_qk = Fold(gqk_part, r.gqk_land, r.gqk_pass)
    fold_v = Fold(gv_part, r.gv_land, r.gv_pass)

    def projection_grad(k):
        grad = mm(x_t[block_of(pz(k), KW), :], dproj[...]).astype(bf16)
        gqk_part[pz(k)] = grad[:, :2 * C]
        gv_part[pz(k)] = grad[:, 2 * C:]
    projection_grad(3)
    projection_grad(1)
    fold_x = Scatter(parts, r.low2, mid, r.high2)

    def unproject(j):
        parts[j] = mm(dproj[block_of(chip_of(j), T2), :], w_qkv[...], NT).astype(bf16)
        fold_x.pair(j)
    fold_qk.start()
    unproject(3)
    unproject(1)
    fold_x.onward(3)
    folds_up[1].middle()
    fold_v.start()
    unproject(2)
    fold_x.onward(1)
    unproject(0)
    fold_x.onward(2)
    gather_c.wait()
    share_da.wait()
    for k in (3, 1):
        out_grad(k)
    fold_o.start()
    for k in (2, 0):
        out_grad(k)
    projection_grad(2)
    projection_grad(0)
    fold_x.cross()
    gather_gd.pass_near()
    col_z, col_own = r.col_z, r.col_own
    col_own[...] = jnp.zeros((8, C), f32)
    for i in range(Z):
        col_own[i:i + 1, :] = colg[0:1, i * C:(i + 1) * C]
    for i in range(3):
        col_own[Z + i:Z + i + 1, :] = colg[1:2, i * C:(i + 1) * C]
    share_col = Share(3, col_own)
    share_col.column(col_own, col_z.at[z])
    col_z[z] = col_own[...]
    share_vec.wait()
    vec_sum = r.vec_sum
    vec_sum[...] = vec_z[0] + vec_z[1] + vec_z[2] + vec_z[3]
    share_sum = Share(7, vec_sum)
    share_sum.plane(lambda o: vec_sum, vec_all.at[s])
    vec_all[s] = vec_sum[...]
    for i in range(2):
        gu_all[s, pl.ds(i * (KW // 2), KW // 2), :] = folds_up[i].finish()
    gather_gu.start()
    fold_qk.middle()

    @pl.when(zhigh == 1)
    def _():
        fold_v.middle()
        fold_o.middle()
    gather_gd.pass_far()
    fold_x.ready()
    dx_ref = r.v_dx

    def input_back(i):
        start = at(i, R)
        rows = pl.ds(start, R)
        dx_ref[rows, :] = (dh1[rows, :] + fold_x.rows(start, R)).astype(bf16)
    loop(T // R, input_back, 2)
    outs.append(local(dx_ref, r.dx))
    gather_gd.wait()
    outs.append(local(gd_all, r.gd))
    gather_gu.pass_near()

    @pl.when(zhigh == 0)
    def _():
        fold_v.middle()
        fold_o.middle()
    gqk_all[s] = fold_qk.finish()
    gather_gqk.start()
    gv_all[s] = fold_v.finish()
    gather_gv.start()
    go_all[:, block_of(s, C)] = fold_o.finish()
    gather_go.start()
    gather_gu.pass_far()
    share_col.wait()
    col_all, col_sum = r.col_all, r.col_sum
    col_sum[...] = col_z[0] + col_z[1] + col_z[2] + col_z[3]
    share_cols = Share(7, col_sum)
    share_cols.plane(lambda o: col_sum, col_all.at[s])
    col_all[s] = col_sum[...]
    gather_gqk.pass_near()
    gather_gv.pass_near()
    gather_gu.wait()
    outs.append(local(gu_all, r.gu))

    share_sum.wait()
    share_cols.wait()
    total = vec_all[0]
    for o in range(1, S):
        total = total + vec_all[o]
    gsm = r.v_gsm
    gsm[...] = jnp.zeros(gsm.shape, f32)
    for start, i in wide:
        for half in range(KW // C):
            gsm[start + half:start + half + 1, :] = total[i:i + 1, half * C:(half + 1) * C]
    for o in range(S):
        at_row = first_row.up_bias + o
        gsm[at_row:at_row + 1, :] = col_all[o, pl.ds(z, 1), :]
    for i in range(per):
        number = z * per + i
        at_row = first_row.projection_bias + i
        gsm[at_row:at_row + 1, :] = col_all[number % S, pl.ds(Z + number // S, 1), :]
    outs.append(local(gsm, r.gsm))
    gather_go.pass_near()
    gather_gqk.pass_far()
    gather_gv.pass_far()
    gather_go.pass_far()
    gather_go.wait()
    outs.append(local(go_all, r.go))
    gather_gqk.wait()
    outs.append(local(gqk_all, r.gqk))
    gather_gv.wait()
    outs.append(local(gv_all, r.gv))
    for copy in outs:
        copy.wait()
    for batch in closing:
        batch.close()
    assert counter[0] <= LANDINGS and counter[1] <= BATCHES and counter[2] <= LOCAL, counter


def fused_shards(*args):
    (hidden_in, cotangent, segment_ids, projection, projection_bias, output_weight, output_bias, first_gain,
     first_shift, up_weight, up_bias, down_weight, down_bias, second_gain, second_shift) = args
    T, D = hidden_in.shape[1:]
    L = segment_ids.shape[1]
    KW = projection.shape[0]
    F = up_weight.shape[1] // 8
    C, Z = 128, 4
    UZ = F // Z
    small = dict(projection_bias=projection_bias, output_bias=output_bias, first_gain=first_gain,
                 first_shift=first_shift, up_bias=up_bias, down_bias=down_bias, second_gain=second_gain,
                 second_shift=second_shift)
    starts, at_row = {}, 0
    for name, value in small.items():
        starts[name] = at_row
        at_row += value.shape[0] // C
    rows = -(-at_row // 8) * 8
    half = HEAD_DIM // 2
    inverse = np.float32(10000.0) ** (np.float32(-2.0) * np.arange(half, dtype=np.float32) / np.float32(HEAD_DIM))
    angles = np.arange(L, dtype=np.float32)[:, None] * inverse.astype(np.float32)[None, :]
    cosine = np.tile(np.cos(angles), (1, C // half))
    sine = np.tile(np.concatenate([-np.sin(angles), np.sin(angles)], axis=1), (1, C // HEAD_DIM))

    inputs = dict(x=hidden_in[0], ct=cotangent[0], seg=segment_ids, cos=jnp.asarray(cosine), sin=jnp.asarray(sine),
                  b_projection=projection_bias.reshape(-1, C), b_output=output_bias[None], gain1=first_gain[None],
                  shift1=first_shift[None], b_up=up_bias[None], b_down=down_bias[None], gain2=second_gain[None],
                  shift2=second_shift[None], proj=projection, wo=output_weight, up=up_weight, dn=down_weight)
    outputs = dict(out=((T, D), bf16), dx=((T, D), bf16), gsm=((rows, C), f32), gqk=((8, KW, 2 * C), bf16), gv=((8, KW, C), bf16),
                   go=((KW, D), bf16), gu=((8, KW, F), bf16), gd=((8 * UZ, D), bf16))
    landed = dict(v_x=inputs["x"], v_ct=inputs["ct"], v_seg=segment_ids, v_cos=inputs["cos"], v_sin=inputs["sin"],
                  v_projection=inputs["b_projection"], v_output=inputs["b_output"], v_gain1=inputs["gain1"],
                  v_shift1=inputs["shift1"], v_up=inputs["b_up"], v_down=inputs["b_down"], v_gain2=inputs["gain2"],
                  v_shift2=inputs["shift2"])
    PART = (4, T, D)
    scratch = {name: (value.shape, value.dtype) for name, value in landed.items()}
    scratch.update(
        v_out=((T, D), bf16), v_dx=((T, D), bf16), v_gsm=((rows, C), f32),
        x_all=((L, D), bf16), x_t=((D, L), bf16), w_qkv=((D, 3 * C), bf16), st_proj=((KW, 3 * C), f32),
        w_o=((D, D), bf16), st_wo=((KW, C), f32), w_up=((D, F), bf16), st_up=((KW, F), f32),
        w_dn=((F, D), bf16), st_dn=((UZ, D), f32), small_all=((Z, rows, C), f32), vec=((8, D), f32),
        vecg=((8, D), f32), q=((L, C), bf16), k=((L, C), bf16), v=((L, C), bf16),
        seg_r=((8, L), f32), seg_c=((L, C), f32), small=((rows, C), f32), lse=((8, L), f32),
        delta=((8, L), f32), c_f=((L, C), f32), c_heads=((L, C), bf16), c_tok=((T, D), bf16),
        a_buf=((T, D), f32), n1=((T, D), f32), y1=((T, D), f32), r1=((T, C), f32),
        y_all=((L, D), bf16), y_t=((D, L), bf16), u_buf=((2 * T, F), f32), g=((L, F), bf16),
        g_t=((F, L), bf16), d=((L, F), f32), du=((L, F), bf16), dz_all=((L, D), bf16),
        parts=((4, 2 * T, D), bf16), mid=((4, T, D), bf16), dh2=((T, D), f32), dh1=((T, D), f32),
        colg=((8, F), f32), gd_part=((Z, UZ, D), bf16), gd_land=((3, UZ, D), bf16), gd_pass=((UZ, D), bf16),
        gu_part=((Z, KW, F), bf16), gu_land=((3, KW, F), bf16), gu_pass=((KW, F), bf16),
        go_part=((Z, KW, C), bf16), go_land=((3, KW, C), bf16), go_pass=((KW, C), bf16),
        gqk_part=((Z, KW, 2 * C), bf16), gqk_land=((3, KW, 2 * C), bf16), gqk_pass=((KW, 2 * C), bf16),
        gv_part=((Z, KW, C), bf16), gv_land=((3, KW, C), bf16), gv_pass=((KW, C), bf16),
        gd_all=((8 * UZ, D), bf16), gu_all=((8, KW, F), bf16), go_all=((KW, D), bf16),
        gqk_all=((8, KW, 2 * C), bf16), gv_all=((8, KW, C), bf16), da=((T, D), bf16), dc_tok=((T, D), bf16), dc=((L, C), bf16),
        da_cols=((L, C), bf16), c_all=((L, D), bf16), dq=((L, C), f32), dproj=((L, 3 * C), bf16),
        vec_all=((8, 8, KW), f32), vec_z=((Z, 8, KW), f32), vec_sum=((8, KW), f32), col_own=((8, C), f32),
        col_z=((Z, 8, C), f32), col_sum=((8, C), f32), col_all=((8, 8, C), f32),
        low0=(PART, bf16), high0=(PART, bf16), low1=(PART, bf16), high1=(PART, bf16), low2=(PART, bf16),
        high2=(PART, bf16), ssem=(BATCHES,), rsem=(LANDINGS,), lsem=(LOCAL,))
    names = [*inputs, *outputs, *scratch]
    sizes = SimpleNamespace(names=names, T=T, D=D, L=L, F=F, first_row=SimpleNamespace(**starts))

    anywhere = pl.BlockSpec(memory_space=pl.ANY)
    results = pl.pallas_call(
        partial(fused_layer, sizes),
        out_shape=[jax.ShapeDtypeStruct(*what) for what in outputs.values()],
        in_specs=[anywhere] * len(inputs),
        out_specs=[anywhere] * len(outputs),
        scratch_shapes=[pltpu.VMEM(*what) if len(what) == 2 else pltpu.SemaphoreType.DMA(what)
                        for what in scratch.values()],
        compiler_params=pltpu.CompilerParams(collective_id=0, has_side_effects=True, vmem_limit_bytes=67043328),
        name="fused_layer",
    )(*inputs.values())
    out, dx, gsm, gqk, gv, go, gu, gd = results
    wide = [jax.ShapeDtypeStruct(value.shape, f32) for value in (projection, output_weight, up_weight, down_weight)]
    narrow = [jax.ShapeDtypeStruct((1, value.shape[0]) if value is not projection_bias else (value.shape[0] // C, C), f32)
              for value in small.values()]
    sources = [out, dx, gqk, gv, go, gu, gd, gsm]
    outcomes = [out, dx] + wide + narrow
    results = pl.pallas_call(
        partial(widen, tuple(starts.values())),
        out_shape=[jax.ShapeDtypeStruct(value.shape, value.dtype) for value in outcomes],
        in_specs=[anywhere] * len(sources),
        out_specs=[anywhere] * len(outcomes),
        scratch_shapes=[pltpu.VMEM(value.shape, value.dtype) for value in sources + outcomes[2:]]
        + [pltpu.SemaphoreType.DMA((LOCAL,))] * 2,
        compiler_params=pltpu.CompilerParams(vmem_limit_bytes=56 << 20),
        name="widen",
    )(*sources)
    out, dx, gq, go, gu, gd = results[:6]
    pb, ob, g1, s1, ub, db, g2, s2 = [value.reshape(-1) for value in results[6:]]
    return (out[None], dx[None], gq, pb, go, ob, g1, s1, gu, ub, gd, db, g2, s2)


def widen(starts, *refs):
    sources, results = refs[:8], refs[8:22]
    held, made, insem, outsem = refs[22:30], refs[30:42], refs[42], refs[43]
    out, dx, gqk, gv, go, gu, gd, gsm = held
    C = gsm.shape[1]
    count = [0, 0]

    def fetch(source, ref):
        copy = pltpu.make_async_copy(source, ref, insem.at[count[0]])
        count[0] += 1
        copy.start()
        return copy
    stores = []

    def store(ref, result):
        copy = pltpu.make_async_copy(ref, result, outsem.at[count[1]])
        count[1] += 1
        copy.start()
        stores.append(copy)

    def piece(i, at, n):
        window = (slice(None), pl.ds(at, n)) if len(held[i].shape) == 3 else (pl.ds(at, n),)
        return fetch(sources[i].at[window], held[i].at[window])

    def grouped(i, target, at, n, first):
        source, result = held[i], made[target]
        groups = source.shape[0]

        def step(j, carry):
            rows = pl.ds(pl.multiple_of(at + j * 32, 32), 32)
            for o in range(groups):
                for p in range(source.shape[2] // C):
                    lane = ((first + p) * groups + o) * C
                    result[rows, lane:lane + C] = source[o, rows, p * C:(p + 1) * C].astype(f32)
            return carry
        lax.fori_loop(0, n // 32, step, 0)

    def plain(i, target, at, n, _):
        source, result = held[i], made[target]

        def step(j, carry):
            rows = pl.ds(pl.multiple_of(at + j * 32, 32), 32)
            result[rows, :] = source[rows, :].astype(f32)
            return carry
        lax.fori_loop(0, n // 32, step, 0)

    work = []
    for i, target, n, body, first in ((5, 2, 64, grouped, 0), (6, 3, 256, plain, 0), (2, 0, 64, grouped, 0),
                                      (3, 0, 64, grouped, 2), (4, 1, 256, plain, 0)):
        total = held[i].shape[-2]
        for at in range(0, total, n):
            work.append((piece(i, at, n), i, target, at, n, body, first))
    whole = [fetch(sources[i], held[i]) for i in (0, 1, 7)]
    for copy, i, target, at, n, body, first in work:
        copy.wait()
        body(i, target, at, n, first)
        if i != 2:
            rows = pl.ds(at, n)
            store(made[target].at[rows], results[2 + target].at[rows])
    for copy in whole:
        copy.wait()
    store(out, results[0])
    store(dx, results[1])
    for start, ref, result in zip(starts, made[4:], results[6:]):
        if ref.shape[1] == C:
            ref[...] = gsm[start:start + ref.shape[0], :]
        else:
            for i in range(ref.shape[1] // C):
                ref[0:1, i * C:(i + 1) * C] = gsm[start + i:start + i + 1, :]
        store(ref, result)
    for copy in stores:
        copy.wait()


BATCHES = 44
LANDINGS = 166
LOCAL = 32


def fits(mesh):
    return mesh.shape["seq"] == 8 and mesh.shape["fsdp"] == 4


def solution(mesh):
    return jax.shard_map(
        fused_shards if fits(mesh) else shards,
        mesh=mesh,
        in_specs=(
            P("fsdp", "seq", None),
            P("fsdp", "seq", None),
            P("fsdp", None),
            P("fsdp", None),
            P("fsdp"),
            P("fsdp", None),
            P("fsdp"),
            P("fsdp"),
            P("fsdp"),
            P("fsdp", None),
            P("fsdp"),
            P("fsdp", None),
            P("fsdp"),
            P("fsdp"),
            P("fsdp"),
        ),
        out_specs=(
            P("fsdp", "seq", None),
            P("fsdp", "seq", None),
            P("fsdp", None),
            P("fsdp"),
            P("fsdp", None),
            P("fsdp"),
            P("fsdp"),
            P("fsdp"),
            P("fsdp", None),
            P("fsdp"),
            P("fsdp", None),
            P("fsdp"),
            P("fsdp"),
            P("fsdp"),
        ),
        check_vma=False,
    )
```

```python
from functools import partial

import jax
import jax.numpy as jnp
import numpy as np
import math
from types import SimpleNamespace
from jax import lax
from jax.experimental import pallas as pl
from jax.experimental.pallas import tpu as pltpu
from jax.sharding import PartitionSpec as P

HEADS = 16
HEAD_DIM = 64


norm_epsilon = 1e-05


def rotary(values, positions):
    half = values.shape[-1] // 2
    channel = jnp.arange(half).astype(jnp.float32)
    inverse = 10000.0 ** (-2.0 * channel / values.shape[-1])
    angles = positions[:, None] * inverse[None, :]
    cosine = jnp.cos(angles)[:, None, :]
    sine = jnp.sin(angles)[:, None, :]
    first = values[..., :half]
    second = values[..., half:]
    return jnp.concatenate(
        [first * cosine - second * sine, second * cosine + first * sine], axis=-1
    )


def rotary_back(grads, positions):
    unused, pullback = jax.vjp(lambda inner: rotary(inner, positions), grads)
    return pullback(grads)[0]


def norm_forward(values, gain, shift):
    centre = values - jnp.mean(values, axis=-1, keepdims=True)
    inverse_root = lax.rsqrt(jnp.mean(centre * centre, axis=-1, keepdims=True) + norm_epsilon)
    normal = centre * inverse_root
    return (normal * gain + shift, normal, inverse_root)


def norm_backward(incoming, normal, inverse_root, gain):
    gain_grad = jnp.sum(incoming * normal, axis=0)
    shift_grad = jnp.sum(incoming, axis=0)
    scaled = incoming * gain
    inner = (
        scaled
        - jnp.mean(scaled, axis=-1, keepdims=True)
        - normal * jnp.mean(scaled * normal, axis=-1, keepdims=True)
    )
    return (inner * inverse_root, gain_grad, shift_grad)


def shards(
    hidden_in,
    cotangent,
    segment_ids,
    projection,
    projection_bias,
    output_weight,
    output_bias,
    first_gain,
    first_shift,
    up_weight,
    up_bias,
    down_weight,
    down_bias,
    second_gain,
    second_shift,
):
    bf16 = jnp.bfloat16
    f32 = jnp.float32
    tokens = hidden_in[0]
    local_rows = tokens.shape[0]
    width = tokens.shape[1]
    seq_rank = lax.axis_index("seq")
    positions = (seq_rank * local_rows + jnp.arange(local_rows)).astype(f32)
    segments = segment_ids[0]
    scale = HEAD_DIM ** (-0.5)
    attention_full = (
        lax.all_gather(projection.astype(bf16), "fsdp", axis=0, tiled=True),
        lax.all_gather(projection_bias.astype(bf16), "fsdp", axis=0, tiled=True),
        lax.all_gather(output_weight.astype(bf16), "fsdp", axis=0, tiled=True),
        lax.all_gather(output_bias.astype(bf16), "fsdp", axis=0, tiled=True),
        lax.all_gather(first_gain.astype(bf16), "fsdp", axis=0, tiled=True),
        lax.all_gather(first_shift.astype(bf16), "fsdp", axis=0, tiled=True),
    )
    proj_weight = attention_full[0]
    projected = jnp.dot(tokens, proj_weight, preferred_element_type=f32) + attention_full[1].astype(
        f32
    )
    heads = projected.reshape(local_rows, 3, HEADS, HEAD_DIM)
    queries = rotary(heads[:, 0], positions)
    keys = rotary(heads[:, 1], positions)
    stacked = jnp.stack([queries, keys, heads[:, 2]]).astype(bf16)
    spread = lax.all_to_all(stacked, "seq", split_axis=2, concat_axis=1, tiled=True)
    query_all = spread[0]
    key_all = spread[1]
    value_all = spread[2]
    length = query_all.shape[0]
    local_heads = query_all.shape[1]
    block = min(512, length)
    count = length // block
    query_blocks = query_all.reshape(count, block, local_heads, HEAD_DIM)
    segment_blocks = segments.reshape(count, block)

    def scores_of(query_block, segment_block):
        raw = jnp.einsum("qhd,khd->hqk", query_block, key_all, preferred_element_type=f32) * scale
        allowed = segment_block[:, None] == segments[None, :]
        return jnp.where(allowed[None], raw, -1e30)

    def forward_block(pieces):
        query_block, segment_block = pieces
        scores = scores_of(query_block, segment_block)
        row_max = jnp.max(scores, axis=-1, keepdims=True)
        exponent = jnp.exp(scores - row_max)
        total = jnp.sum(exponent, axis=-1, keepdims=True)
        weights = exponent / total
        context = jnp.einsum(
            "hqk,khd->qhd", weights.astype(bf16), value_all, preferred_element_type=f32
        )
        return (context.astype(bf16), (row_max + jnp.log(total))[..., 0])

    context_blocks, log_totals = lax.map(forward_block, (query_blocks, segment_blocks))
    context_heads = context_blocks.reshape(length, local_heads, HEAD_DIM)
    context_tokens = lax.all_to_all(
        context_heads, "seq", split_axis=0, concat_axis=1, tiled=True
    ).reshape(local_rows, width)
    attended = jnp.dot(
        context_tokens, attention_full[2], preferred_element_type=f32
    ) + attention_full[3].astype(f32)
    gain_one = attention_full[4].astype(f32)
    normed_one, normal_one, inverse_one = norm_forward(
        tokens.astype(f32) + attended, gain_one, attention_full[5].astype(f32)
    )
    feed_full = (
        lax.all_gather(up_weight.astype(bf16), "fsdp", axis=0, tiled=True),
        lax.all_gather(up_bias.astype(bf16), "fsdp", axis=0, tiled=True),
        lax.all_gather(down_weight.astype(bf16), "fsdp", axis=0, tiled=True),
        lax.all_gather(down_bias.astype(bf16), "fsdp", axis=0, tiled=True),
        lax.all_gather(second_gain.astype(bf16), "fsdp", axis=0, tiled=True),
        lax.all_gather(second_shift.astype(bf16), "fsdp", axis=0, tiled=True),
    )
    normed_low = normed_one.astype(bf16)
    lifted = jnp.dot(normed_low, feed_full[0], preferred_element_type=f32) + feed_full[1].astype(
        f32
    )
    activated = jax.nn.gelu(lifted, approximate=False).astype(bf16)
    lowered = jnp.dot(activated, feed_full[2], preferred_element_type=f32) + feed_full[3].astype(
        f32
    )
    gain_two = feed_full[4].astype(f32)
    layer_out, normal_two, inverse_two = norm_forward(
        normed_one + lowered, gain_two, feed_full[5].astype(f32)
    )
    feed_back = (
        lax.all_gather(up_weight.astype(bf16), "fsdp", axis=0, tiled=True),
        lax.all_gather(up_bias.astype(bf16), "fsdp", axis=0, tiled=True),
        lax.all_gather(down_weight.astype(bf16), "fsdp", axis=0, tiled=True),
        lax.all_gather(down_bias.astype(bf16), "fsdp", axis=0, tiled=True),
        lax.all_gather(second_gain.astype(bf16), "fsdp", axis=0, tiled=True),
        lax.all_gather(second_shift.astype(bf16), "fsdp", axis=0, tiled=True),
    )
    attention_back = (
        lax.all_gather(projection.astype(bf16), "fsdp", axis=0, tiled=True),
        lax.all_gather(projection_bias.astype(bf16), "fsdp", axis=0, tiled=True),
        lax.all_gather(output_weight.astype(bf16), "fsdp", axis=0, tiled=True),
        lax.all_gather(output_bias.astype(bf16), "fsdp", axis=0, tiled=True),
        lax.all_gather(first_gain.astype(bf16), "fsdp", axis=0, tiled=True),
        lax.all_gather(first_shift.astype(bf16), "fsdp", axis=0, tiled=True),
    )
    grad_two, second_gain_grad, second_shift_grad = norm_backward(
        cotangent[0].astype(f32), normal_two, inverse_two, gain_two
    )
    lowered_grad = grad_two.astype(bf16)
    down_weight_grad = jnp.einsum("tf,td->fd", activated, lowered_grad, preferred_element_type=f32)
    down_bias_grad = jnp.sum(lowered_grad.astype(f32), axis=0)
    active_grad = jnp.einsum("td,fd->tf", lowered_grad, feed_back[2], preferred_element_type=f32)
    unused, gelu_pull = jax.vjp(partial(jax.nn.gelu, approximate=False), lifted)
    lifted_grad = gelu_pull(active_grad)[0].astype(bf16)
    up_weight_grad = jnp.einsum("td,tf->df", normed_low, lifted_grad, preferred_element_type=f32)
    up_bias_grad = jnp.sum(lifted_grad.astype(f32), axis=0)
    normed_grad = grad_two + jnp.einsum(
        "tf,df->td", lifted_grad, feed_back[0], preferred_element_type=f32
    )
    grad_one, first_gain_grad, first_shift_grad = norm_backward(
        normed_grad, normal_one, inverse_one, attention_back[4].astype(f32)
    )
    attended_grad = grad_one.astype(bf16)
    output_weight_grad = jnp.einsum(
        "tc,td->cd", context_tokens, attended_grad, preferred_element_type=f32
    )
    output_bias_grad = jnp.sum(attended_grad.astype(f32), axis=0)
    context_grad = jnp.einsum(
        "td,cd->tc", attended_grad, attention_back[2], preferred_element_type=f32
    ).astype(bf16)
    context_grad = context_grad.reshape(local_rows, HEADS, HEAD_DIM)
    context_grad_heads = lax.all_to_all(
        context_grad, "seq", split_axis=1, concat_axis=0, tiled=True
    )
    grad_blocks = context_grad_heads.reshape(count, block, local_heads, HEAD_DIM)

    def backward_block(carry, pieces):
        key_grad, value_grad = carry
        query_block, segment_block, grad_block, log_block = pieces
        scores = scores_of(query_block, segment_block)
        weights = jnp.exp(scores - log_block[..., None])
        value_grad = value_grad + jnp.einsum(
            "hqk,qhd->khd", weights.astype(bf16), grad_block, preferred_element_type=f32
        )
        weight_grad = jnp.einsum("qhd,khd->hqk", grad_block, value_all, preferred_element_type=f32)
        centre = jnp.sum(weights * weight_grad, axis=-1, keepdims=True)
        score_grad = (weights * (weight_grad - centre)).astype(bf16)
        query_grad = (
            jnp.einsum("hqk,khd->qhd", score_grad, key_all, preferred_element_type=f32) * scale
        )
        key_grad = (
            key_grad
            + jnp.einsum("hqk,qhd->khd", score_grad, query_block, preferred_element_type=f32)
            * scale
        )
        return ((key_grad, value_grad), query_grad)

    zeros_heads = jnp.zeros((length, local_heads, HEAD_DIM), f32)
    (key_grad, value_grad), query_grad = lax.scan(
        backward_block,
        (zeros_heads, zeros_heads),
        (query_blocks, segment_blocks, grad_blocks, log_totals),
    )
    query_grad = query_grad.reshape(length, local_heads, HEAD_DIM)
    stacked_grad = jnp.stack([query_grad, key_grad, value_grad]).astype(bf16)
    token_heads = lax.all_to_all(stacked_grad, "seq", split_axis=1, concat_axis=2, tiled=True)
    query_back = rotary_back(token_heads[0].astype(f32), positions)
    key_back = rotary_back(token_heads[1].astype(f32), positions)
    projected_grad = jnp.stack([query_back, key_back, token_heads[2].astype(f32)], axis=1)
    projected_grad = projected_grad.reshape(local_rows, 3 * width).astype(bf16)
    projection_grad = jnp.einsum("td,te->de", tokens, projected_grad, preferred_element_type=f32)
    projection_bias_grad = jnp.sum(projected_grad.astype(f32), axis=0)
    input_grad = grad_one + jnp.einsum(
        "te,de->td", projected_grad, attention_back[0], preferred_element_type=f32
    )
    every_shard = (
        lax.psum_scatter(
            projection_grad.astype(jnp.bfloat16), "fsdp", scatter_dimension=0, tiled=True
        ).astype(jnp.float32),
        lax.psum_scatter(
            projection_bias_grad.astype(jnp.bfloat16), "fsdp", scatter_dimension=0, tiled=True
        ).astype(jnp.float32),
        lax.psum_scatter(
            output_weight_grad.astype(jnp.bfloat16), "fsdp", scatter_dimension=0, tiled=True
        ).astype(jnp.float32),
        lax.psum_scatter(
            output_bias_grad.astype(jnp.bfloat16), "fsdp", scatter_dimension=0, tiled=True
        ).astype(jnp.float32),
        lax.psum_scatter(
            first_gain_grad.astype(jnp.bfloat16), "fsdp", scatter_dimension=0, tiled=True
        ).astype(jnp.float32),
        lax.psum_scatter(
            first_shift_grad.astype(jnp.bfloat16), "fsdp", scatter_dimension=0, tiled=True
        ).astype(jnp.float32),
        lax.psum_scatter(
            up_weight_grad.astype(jnp.bfloat16), "fsdp", scatter_dimension=0, tiled=True
        ).astype(jnp.float32),
        lax.psum_scatter(
            up_bias_grad.astype(jnp.bfloat16), "fsdp", scatter_dimension=0, tiled=True
        ).astype(jnp.float32),
        lax.psum_scatter(
            down_weight_grad.astype(jnp.bfloat16), "fsdp", scatter_dimension=0, tiled=True
        ).astype(jnp.float32),
        lax.psum_scatter(
            down_bias_grad.astype(jnp.bfloat16), "fsdp", scatter_dimension=0, tiled=True
        ).astype(jnp.float32),
        lax.psum_scatter(
            second_gain_grad.astype(jnp.bfloat16), "fsdp", scatter_dimension=0, tiled=True
        ).astype(jnp.float32),
        lax.psum_scatter(
            second_shift_grad.astype(jnp.bfloat16), "fsdp", scatter_dimension=0, tiled=True
        ).astype(jnp.float32),
    )
    finals = (
        lax.psum(every_shard[0].astype(jnp.bfloat16), "seq").astype(jnp.float32),
        lax.psum(every_shard[1].astype(jnp.bfloat16), "seq").astype(jnp.float32),
        lax.psum(every_shard[2].astype(jnp.bfloat16), "seq").astype(jnp.float32),
        lax.psum(every_shard[3].astype(jnp.bfloat16), "seq").astype(jnp.float32),
        lax.psum(every_shard[4].astype(jnp.bfloat16), "seq").astype(jnp.float32),
        lax.psum(every_shard[5].astype(jnp.bfloat16), "seq").astype(jnp.float32),
        lax.psum(every_shard[6].astype(jnp.bfloat16), "seq").astype(jnp.float32),
        lax.psum(every_shard[7].astype(jnp.bfloat16), "seq").astype(jnp.float32),
        lax.psum(every_shard[8].astype(jnp.bfloat16), "seq").astype(jnp.float32),
        lax.psum(every_shard[9].astype(jnp.bfloat16), "seq").astype(jnp.float32),
        lax.psum(every_shard[10].astype(jnp.bfloat16), "seq").astype(jnp.float32),
        lax.psum(every_shard[11].astype(jnp.bfloat16), "seq").astype(jnp.float32),
    )
    return (
        layer_out.astype(bf16)[None],
        input_grad.astype(bf16)[None],
        finals[0],
        finals[1],
        finals[2],
        finals[3],
        finals[4],
        finals[5],
        finals[6],
        finals[7],
        finals[8],
        finals[9],
        finals[10],
        finals[11],
    )


MESH = pl.DeviceIdType.MESH
NN = (((1,), (0,)), ((), ()))
NT = (((1,), (1,)), ((), ()))
TN = (((0,), (0,)), ((), ()))
f32 = jnp.float32
bf16 = jnp.bfloat16
MASKED = -1e30


def mm(left, right, dims=NN):
    return lax.dot_general(left, right, dims, preferred_element_type=f32)


def block_of(index, size):
    return pl.ds(pl.multiple_of(index * size, size), size)


def flip(bit, other):
    return bit + other - 2 * bit * other


def fused_layer(sizes, *refs):
    r = SimpleNamespace(**dict(zip(sizes.names, refs)))
    T, D, L, F = sizes.T, sizes.D, sizes.L, sizes.F
    S, Z = 8, 4
    KW = D // Z
    UZ = F // Z
    C = 128
    T2 = 2 * T
    first_row = sizes.first_row
    ssem, rsem, lsem = r.ssem, r.rsem, r.lsem

    s = lax.axis_index("seq")
    z = lax.axis_index("fsdp")
    core, xbit, ybit = s % 2, (s // 2) % 2, s // 4
    zlow, zhigh = z % 2, z // 2

    def ps(k):
        return flip(core, k % 2) + 2 * flip(xbit, (k // 2) % 2) + 4 * flip(ybit, k // 4)

    def pz(k):
        return flip(zlow, k % 2) + 2 * flip(zhigh, k // 2)

    def chip_of(j):
        return flip(xbit, j % 2) + 2 * flip(ybit, j // 2)

    counter = [0, 0, 0]
    closing = []

    def take(which, n=1):
        counter[which] += n
        return counter[which] - n

    def landings(n=1):
        return take(0, n)

    def size(ref):
        return math.prod(ref.shape) * jnp.dtype(ref.dtype).itemsize

    def extent(n):
        if n <= size(r.c_f):
            return r.c_f.at[pl.ds(0, n * L // size(r.c_f))]
        return r.y_all.at[pl.ds(0, n * L // size(r.y_all))]

    def arrived(ref, slot):
        pltpu.make_async_copy(ref, ref, rsem.at[slot]).wait()

    class Batch:
        def __init__(self, count, like):
            self.slot, self.bytes, self.open = take(1), count * size(like), True
            closing.append(self)

        def send(self, src, dst, slot, dev):
            pltpu.make_async_remote_copy(
                src_ref=src, dst_ref=dst, send_sem=ssem.at[self.slot], recv_sem=rsem.at[slot],
                device_id=dev, device_id_type=MESH).start()

        def close(self):
            if self.open:
                everything = extent(self.bytes)
                pltpu.make_async_copy(everything, everything, ssem.at[self.slot]).wait()
            self.open = False

    def local(src, dst):
        copy = pltpu.make_async_copy(src, dst, lsem.at[take(2)])
        copy.start()
        return copy

    class Gather:
        def __init__(self, place, at_once=True):
            self.place, self.at_once = place, at_once
            self.batch = Batch(7, place(0))
            self.near, self.across = landings(4), landings(2)
            self.other = landings() if at_once else landings(4)

        def part(self, ref, i):
            n = ref.shape[0] // 2
            return ref.at[pl.ds(i * n, n)]

        def start(self, src=None):
            mine = self.place(s)
            src = mine if src is None else src
            for slot, half, k in ((0, 0, 2), (3, 1, 4), (1, 1, 2), (2, 0, 4)):
                self.batch.send(self.part(src, half), self.part(mine, half), self.near + slot, (ps(k), z))
            self.batch.send(src, mine, self.other, (ps(1), z))

        def to_partner(self, k):
            there = self.place(ps(k))
            self.batch.send(there, there, self.other + (0 if self.at_once else k // 2), (ps(1), z))

        def pass_near(self):
            along_x, along_y = self.place(ps(2)), self.place(ps(4))
            first, second = self.part(along_x, 0), self.part(along_y, 1)
            arrived(first, self.near)
            self.batch.send(first, first, self.across, (ps(4), z))
            arrived(second, self.near + 3)
            self.batch.send(second, second, self.across + 1, (ps(2), z))
            arrived(self.part(along_x, 1), self.near + 1)
            self.to_partner(2)
            arrived(self.part(along_y, 0), self.near + 2)
            self.to_partner(4)

        def pass_far(self):
            far = self.place(ps(6))
            arrived(self.part(far, 0), self.across)
            arrived(self.part(far, 1), self.across + 1)
            self.to_partner(6)

        def pass_all(self):
            self.pass_near()
            self.pass_far()

        def wait(self, k=None):
            if self.at_once:
                arrived(extent(4 * size(self.place(0))), self.other)
            else:
                arrived(self.place(ps(k)), self.other + k // 2)

    class Spread:
        def __init__(self, place):
            self.place, self.batch, self.base = place, Batch(3, place(0)), landings(3)

        def start(self, *which):
            mine = self.place(z)
            for k in which or (2, 1):
                self.batch.send(mine, mine, self.base + k - 1, (s, pz(k)))

        def pass_on(self):
            there = self.place(pz(2))
            arrived(there, self.base + 1)
            self.batch.send(there, there, self.base + 2, (s, pz(1)))

        def wait(self):
            for k in (1, 3):
                arrived(self.place(pz(k)), self.base + k - 1)

        def wait_all(self):
            for k in (1, 2, 3):
                arrived(self.place(pz(k)), self.base + k - 1)

    class Fold:
        def __init__(self, parts, landing, passing, first=0, count=None):
            self.rows = pl.ds(first, count or passing.shape[0])
            self.parts, self.landing, self.passing = parts, landing, passing.at[self.rows]
            self.batch, self.base = Batch(3, self.passing), landings(3)

        def start(self):
            for i, k in ((1, 3), (0, 1)):
                self.batch.send(self.parts.at[pz(k), self.rows], self.landing.at[i, self.rows], self.base + i, (s, pz(1)))

        def middle(self):
            arrived(self.landing.at[1, self.rows], self.base + 1)
            self.passing[...] = (self.parts[pz(2), self.rows, :].astype(f32)
                                 + self.landing[1, self.rows, :].astype(f32)).astype(bf16)
            self.batch.send(self.passing, self.landing.at[2, self.rows], self.base + 2, (s, pz(2)))

        def finish(self):
            arrived(self.landing.at[0, self.rows], self.base)
            arrived(self.landing.at[2, self.rows], self.base + 2)
            return (self.parts[z, self.rows, :].astype(f32) + self.landing[0, self.rows, :].astype(f32)
                    + self.landing[2, self.rows, :].astype(f32)).astype(bf16)

    class Scatter:
        def __init__(self, parts, low, mid, high, first=0, count=T):
            self.parts, self.low, self.mid, self.high = parts, low, mid, high
            self.first, self.count, self.window = first, count, pl.ds(first, count)
            self.batch = Batch(7, mid.at[0, self.window])
            self.base, self.far, self.last = landings(4), landings(2), landings()

        def rows_of(self, which):
            return pl.ds(pl.multiple_of(which * T + self.first, self.count), self.count)

        def half(self, ref, j, i):
            return ref.at[j, self.window, pl.ds(i * (D // 2), D // 2)]

        def send(self, j, i, slot, k):
            self.batch.send(self.half(self.mid, j, i), self.half(self.high, j, i), slot, (ps(k), z))

        def pair(self, j):
            self.batch.send(self.parts.at[j, self.rows_of(1 - core)], self.low.at[j, self.window],
                            self.base + j, (ps(1), z))

        def onward(self, j):
            arrived(self.low.at[j, self.window], self.base + j)
            own = self.parts[j, self.rows_of(core), :].astype(f32)
            self.mid[j, self.window, :] = (own + self.low[j, self.window, :].astype(f32)).astype(bf16)
            if j == 1:
                self.send(1, 0, self.last, 2)
            elif j == 2:
                self.send(2, 1, self.last, 4)
            else:
                self.send(3, 0, self.far, 2)
                self.send(3, 1, self.far + 1, 4)

        def cross(self):
            for j, i, k in ((2, 0, 4), (1, 1, 2)):
                arrived(self.half(self.high, 3, i), self.far + i)
                ref = self.half(self.mid, j, i)
                ref[...] = (ref[...].astype(f32) + self.half(self.high, 3, i)[...].astype(f32)).astype(bf16)
                self.send(j, i, self.last, k)

        def ready(self):
            arrived(self.low.at[0, self.window], self.base)
            arrived(self.high.at[pl.ds(1, 2), self.window], self.last)

        def rows(self, at, n):
            own = self.parts[0, pl.ds(pl.multiple_of(core * T + at, n), n), :].astype(f32)
            total = own + self.low[0, pl.ds(at, n), :].astype(f32)
            for j in (1, 2):
                total = total + self.high[j, pl.ds(at, n), :].astype(f32)
            return total

    class Share:
        def __init__(self, count, like):
            self.count, self.batch, self.slot, self.bytes = count, Batch(count, like), landings(), count * size(like)

        def plane(self, src, dst):
            for k in (6, 7, 2, 3, 4, 5, 1):
                self.batch.send(src(ps(k)), dst, self.slot, (ps(k), z))

        def column(self, src, dst):
            for k in (2, 3, 1):
                self.batch.send(src, dst, self.slot, (s, pz(k)))

        def wait(self):
            arrived(extent(self.bytes), self.slot)

    def loop(count, body, unroll=1):
        def step(i, carry):
            body(i)
            return carry
        lax.fori_loop(0, count, step, 0, unroll=unroll)

    def at(i, n):
        return pl.multiple_of(i * n, n)

    def turn(src, dst):
        def one(i):
            dst[:, pl.ds(at(i, T), T)] = jnp.transpose(src[pl.ds(at(i, T), T), :])
        loop(L // T, one)

    vec, vecg = r.vec, r.vecg

    OUTPUT_BIAS, FIRST_GAIN, FIRST_SHIFT, DOWN_BIAS, SECOND_GAIN, SECOND_SHIFT, PROJECTION_BIAS, UP_BIAS = range(8)
    wide = ((first_row.output_bias, OUTPUT_BIAS), (first_row.first_gain, FIRST_GAIN),
            (first_row.first_shift, FIRST_SHIFT), (first_row.down_bias, DOWN_BIAS),
            (first_row.second_gain, SECOND_GAIN), (first_row.second_shift, SECOND_SHIFT))

    def row(i, width=D):
        return vec[i:i + 1, :width]

    lanes = lax.broadcasted_iota(jnp.int32, (T, C), 1)
    low_head = lanes < HEAD_DIM

    def swapped(w):
        low_half = lax.broadcasted_iota(jnp.int32, w.shape, 1) % HEAD_DIM < HEAD_DIM // 2
        return jnp.where(low_half, pltpu.roll(w, C - HEAD_DIM // 2, 1), pltpu.roll(w, HEAD_DIM // 2, 1))

    def stacked(w):
        nothing = jnp.zeros_like(w)
        return jnp.concatenate([jnp.where(low_head, w, nothing), jnp.where(low_head, nothing, w)], axis=0)

    def unstacked(w):
        return jnp.where(low_head, w[:T], w[T:])

    barrier = pltpu.get_barrier_semaphore()
    for k in range(1, S):
        pl.semaphore_signal(barrier, inc=1, device_id=(ps(k), z), device_id_type=MESH)
    for k in range(1, Z):
        pl.semaphore_signal(barrier, inc=1, device_id=(s, pz(k)), device_id_type=MESH)
    x_ref, ct_ref = r.v_x, r.v_ct
    x_load = local(r.x, x_ref)
    wo_load = local(r.wo.at[:, block_of(s, C)], r.st_wo)
    proj_loads = [local(r.proj.at[:, block_of(i * (D // C) + s, C)], r.st_proj.at[:, pl.ds(i * C, C)])
                  for i in range(3)]
    raw = ((r.b_projection, r.v_projection, first_row.projection_bias), (r.b_output, r.v_output, first_row.output_bias),
           (r.gain1, r.v_gain1, first_row.first_gain), (r.shift1, r.v_shift1, first_row.first_shift),
           (r.b_up, r.v_up, first_row.up_bias), (r.b_down, r.v_down, first_row.down_bias),
           (r.gain2, r.v_gain2, first_row.second_gain), (r.shift2, r.v_shift2, first_row.second_shift))
    raw_loads = [local(source, ref) for source, ref, _ in raw]
    seg_load = local(r.seg, r.v_seg)
    up_loads = [local(r.up.at[:, block_of(i * (D // C) + s, C)], r.st_up.at[:, pl.ds(i * C, C)])
                for i in range(Z)]
    dn_load = local(r.dn.at[block_of(s, UZ), :], r.st_dn)
    late_loads = [local(r.cos, r.v_cos), local(r.sin, r.v_sin), local(r.ct, ct_ref)]
    cos_ref, sin_ref = r.v_cos, r.v_sin

    x_all, w_qkv, w_o, w_up, w_dn = r.x_all, r.w_qkv, r.w_o, r.w_up, r.w_dn
    gather_x = Gather(lambda o: x_all.at[block_of(o, T)])
    spread_qkv = Spread(lambda p: w_qkv.at[block_of(p, KW)])
    spread_o = Spread(lambda p: w_o.at[block_of(p, KW), block_of(s, C)])
    spread_up = Spread(lambda p: w_up.at[block_of(p, KW)])
    spread_dn = Spread(lambda p: w_dn.at[block_of(p, UZ)])
    gather_o = Gather(lambda o: w_o.at[:, block_of(o, C)])
    wo_load.wait()
    w_o[block_of(z, KW), block_of(s, C)] = r.st_wo[...].astype(bf16)
    for copy in proj_loads:
        copy.wait()
    w_qkv[block_of(z, KW), :] = r.st_proj[...].astype(bf16)
    x_load.wait()
    pl.semaphore_wait(barrier, S + Z - 2)
    spread_o.start(2, 3, 1)
    spread_qkv.start()
    gather_x.start(x_ref)

    small, small_all, seg_c, seg_r = r.small, r.small_all, r.seg_c, r.seg_r
    for copy, (_, ref, start) in zip(raw_loads, raw):
        copy.wait()
        if ref.shape[1] == C:
            small[start:start + ref.shape[0], :] = ref[...].astype(bf16).astype(f32)
        else:
            for i in range(ref.shape[1] // C):
                small[start + i:start + i + 1, :] = ref[0:1, i * C:(i + 1) * C].astype(bf16).astype(f32)
    x_all[block_of(s, T), :] = x_ref[...]
    vecg[...] = jnp.zeros((8, D), f32)
    seg_load.wait()
    seg_r[...] = jnp.broadcast_to(r.v_seg[...].astype(f32), (8, L))

    def seg_turn(i):
        here = pl.ds(at(i, T), T)
        seg_c[here, :] = jnp.transpose(jnp.broadcast_to(seg_r[0:1, here], (T, T)))
    loop(L // T, seg_turn)
    for copy in up_loads:
        copy.wait()
    w_up[block_of(z, KW), :] = r.st_up[...].astype(bf16)
    dn_load.wait()
    w_dn[block_of(z, UZ), :] = r.st_dn[...].astype(bf16)
    share_small = Share(3, small)
    small_all[z] = small[...]

    gather_x.pass_near()
    spread_o.wait_all()
    gather_o.start()
    gather_x.pass_far()
    gather_x.wait()
    spread_qkv.pass_on()
    share_small.column(small, small_all.at[z])
    spread_up.start()
    x_t = r.x_t
    turn(x_all, x_t)
    for copy in late_loads:
        copy.wait()
    gather_o.pass_near()
    spread_qkv.wait()
    share_small.wait()
    for p in range(Z):
        for start, i in wide:
            for half in range(KW // C):
                at_row = start + half
                lane = (p * (KW // C) + half) * C
                vec[i:i + 1, lane:lane + C] = small_all[p, at_row:at_row + 1, :]
        vec[7:8, p * C:(p + 1) * C] = small_all[p, pl.ds(first_row.up_bias + s, 1), :]
    per = 3 * D // (C * Z)
    for t in range(3):
        number = t * (D // C) + s
        vec[6:7, t * C:(t + 1) * C] = small_all[number // per, pl.ds(first_row.projection_bias + number % per, 1), :]

    q_ref, k_ref, v_ref = r.q, r.k, r.v
    scale = HEAD_DIM ** -0.5

    def project(i):
        here = pl.ds(at(i, T2), T2)
        out = mm(x_all[here, :], w_qkv[...]) + row(PROJECTION_BIAS, 3 * C)
        cosine, sine = cos_ref[here, :], sin_ref[here, :]
        q0, k0 = out[:, :C], out[:, C:2 * C]
        q_ref[here, :] = ((q0 * cosine + swapped(q0) * sine).astype(bf16).astype(f32) * scale).astype(bf16)
        k_ref[here, :] = (k0 * cosine + swapped(k0) * sine).astype(bf16)
        v_ref[here, :] = out[:, 2 * C:].astype(bf16)
    loop(L // T2, project)
    gather_o.pass_far()

    lse, c_f, c_heads, c_tok = r.lse, r.c_f, r.c_heads, r.c_tok
    R = 16

    def same_document(here):
        return jnp.tile(seg_c[here, :], (1, L // C)) == seg_r[0:1, :]

    def both(w):
        return jnp.concatenate([w, w], axis=0)

    def attend(o):
        here = block_of(o, T)
        score = jnp.where(both(same_document(here)), mm(stacked(q_ref[here, :]), k_ref[...], NT), MASKED)
        top = jnp.max(score, axis=-1, keepdims=True)
        power = jnp.exp(score - top)
        total = jnp.sum(power, axis=-1, keepdims=True)
        context = unstacked(mm(power.astype(bf16), v_ref[...]) * (1.0 / total))
        c_f[here, :] = context
        c_heads[here, :] = context.astype(bf16)
        logs = jnp.broadcast_to(top + jnp.log(total), (T2, C))
        for h in range(2):
            lse[h:h + 1, here] = jnp.transpose(logs[h * T:(h + 1) * T, :])[0:1, :]

    share_c = Share(7, c_heads.at[pl.ds(0, T)])

    def attend_and_send(i):
        k = 7 - i
        attend(ps(k))

        @pl.when(k > 0)
        def _():
            share_c.batch.send(c_heads.at[block_of(ps(k), T)], c_tok.at[:, block_of(s, C)], share_c.slot, (ps(k), z))
    loop(8, attend_and_send)
    spread_up.pass_on()
    spread_dn.start()
    c_tok[:, block_of(s, C)] = c_heads[block_of(s, T), :]
    gather_o.wait()
    share_c.wait()

    a_buf = r.a_buf
    a_buf[...] = mm(c_tok[...], w_o[...])
    n1, y1, r1, y_all = r.n1, r.y1, r.r1, r.y_all

    def norm(h):
        centre = h - jnp.mean(h, axis=-1, keepdims=True)
        root = lax.rsqrt(jnp.mean(centre * centre, axis=-1, keepdims=True) + norm_epsilon)
        return centre * root, root

    def first_norm(i):
        rows = pl.ds(at(i, R), R)
        normal, root = norm(x_ref[rows, :].astype(f32) + a_buf[rows, :] + row(OUTPUT_BIAS))
        out = normal * row(FIRST_GAIN) + row(FIRST_SHIFT)
        n1[rows, :] = normal
        r1[rows, :] = jnp.broadcast_to(root, (R, C))
        y1[rows, :] = out
        y_all[pl.ds(pl.multiple_of(s * T + i * R, R), R), :] = out.astype(bf16)
    loop(T // R, first_norm, 4)
    gather_y = Gather(lambda o: y_all.at[block_of(o, T)], False)
    gather_y.start()
    c_all = r.c_all
    gather_c = Gather(lambda o: c_all.at[block_of(o, T)])
    c_all[block_of(s, T), :] = c_tok[...]

    u_buf, g_ref, d_ref, du_ref, dz_all = r.u_buf, r.g, r.d, r.du, r.dz_all
    parts, mid = r.parts, r.mid
    spread_up.wait()
    E = 32

    def lift(j):
        q = chip_of(j)
        u_buf[...] = mm(y_all[block_of(q, T2), :], w_up[...])

        def chunk(i):
            rows = pl.ds(at(i, E), E)
            there = pl.ds(pl.multiple_of(q * T2 + i * E, E), E)
            u = u_buf[rows, :] + row(UP_BIAS, F)
            share = 0.5 + 0.5 * lax.erf(u * (0.5 ** 0.5))
            g_ref[there, :] = (u * share).astype(bf16)
            d_ref[there, :] = share + u * (jnp.exp(-0.5 * u * u) * 0.3989422804014327)
        loop(T2 // E, chunk)

    def lower(j):
        parts[j] = mm(g_ref[block_of(chip_of(j), T2), :], w_dn[...]).astype(bf16)

    H = T // 2
    folds_z = [Scatter(parts, r.low0, mid, r.high0, i * H, H) for i in range(2)]
    y_t, g_t = r.y_t, r.g_t
    gather_y.wait(1)
    lift(0)
    gather_y.pass_near()
    gather_y.wait(3)
    lift(1)
    gather_y.wait(5)
    lift(2)
    spread_dn.pass_on()
    gather_y.pass_far()
    gather_c.start(c_tok)
    gather_y.wait(7)
    lift(3)
    turn(y_all, y_t)
    turn(g_ref, g_t)
    spread_dn.wait()
    for j in (3, 1, 2):
        lower(j)
        for fold in folds_z:
            fold.pair(j)
    for j in (3, 1, 2):
        folds_z[0].onward(j)
    folds_z[1].onward(3)
    lower(0)
    for fold in folds_z:
        fold.pair(0)
    folds_z[0].cross()
    folds_z[1].onward(1)
    folds_z[1].onward(2)
    folds_z[1].cross()
    folds_z[0].ready()

    dh2, out_ref = r.dh2, r.out

    def add_row(i, value):
        vecg[i:i + 1, :] = vecg[i:i + 1, :] + jnp.sum(value, axis=0, keepdims=True)

    def norm_back(incoming, normal, root, gain):
        scaled = incoming * gain
        return root * (scaled - jnp.mean(scaled, axis=-1, keepdims=True)
                       - normal * jnp.mean(scaled * normal, axis=-1, keepdims=True))

    def second_norm(i):
        start = at(i, R)
        rows = pl.ds(start, R)
        normal, root = norm(y1[rows, :] + folds_z[0].rows(start, R) + row(DOWN_BIAS))
        out_ref[rows, :] = (normal * row(SECOND_GAIN) + row(SECOND_SHIFT)).astype(bf16)
        e = ct_ref[rows, :].astype(f32)
        grad = norm_back(e, normal, root, row(SECOND_GAIN))
        dh2[rows, :] = grad
        dz = grad.astype(bf16)
        dz_all[pl.ds(pl.multiple_of(s * T + i * R, R), R), :] = dz
        add_row(3, dz.astype(f32))
        add_row(4, e * normal)
        add_row(5, e)
    gathers_dz = [Gather(lambda o, i=i: dz_all.at[block_of(2 * o + i, H)], False) for i in range(2)]
    loop(H // R, second_norm, 2)
    gathers_dz[0].start()
    folds_z[1].ready()
    loop(H // R, lambda i: second_norm(i + H // R), 2)
    gathers_dz[1].start()
    for fold in folds_z:
        fold.batch.close()

    colg = r.colg
    colg[...] = jnp.zeros((8, F), f32)

    def unlower(j):
        q = chip_of(j)
        u_buf[...] = mm(dz_all[block_of(q, T2), :], w_dn[...], NT)

        def chunk(i):
            rows = pl.ds(at(i, E), E)
            there = pl.ds(pl.multiple_of(q * T2 + i * E, E), E)
            du = (u_buf[rows, :] * d_ref[there, :]).astype(bf16)
            du_ref[there, :] = du
            colg[0:1, :] = colg[0:1, :] + jnp.sum(du.astype(f32), axis=0, keepdims=True)
        loop(T2 // E, chunk)

    def unlift(j):
        parts[j] = mm(du_ref[block_of(chip_of(j), T2), :], w_up[...], NT).astype(bf16)

    fold_y = Scatter(parts, r.low1, mid, r.high1)
    gd_part, gu_part = r.gd_part, r.gu_part
    folds_dn = [Fold(gd_part, r.gd_land, r.gd_pass, i * (UZ // 2), UZ // 2) for i in range(2)]
    folds_up = [Fold(gu_part, r.gu_land, r.gu_pass, i * (KW // 2), KW // 2) for i in range(2)]

    def down_grad(k):
        gd_part[pz(k)] = mm(g_t[block_of(pz(k), UZ), :], dz_all[...]).astype(bf16)

    def up_grad(k):
        gu_part[pz(k)] = mm(y_t[block_of(pz(k), KW), :], du_ref[...]).astype(bf16)

    def dz_wait(k):
        for gather in gathers_dz:
            gather.wait(k)
    dz_wait(1)
    unlower(0)
    unlift(0)
    fold_y.pair(0)
    gathers_dz[0].pass_near()
    gathers_dz[1].pass_near()
    dz_wait(3)
    unlower(1)
    unlift(1)
    fold_y.pair(1)
    gathers_dz[0].pass_far()
    dz_wait(5)
    unlower(2)
    fold_y.onward(1)
    unlift(2)
    fold_y.pair(2)
    gathers_dz[1].pass_far()
    fold_y.onward(2)
    dz_wait(7)
    down_grad(3)
    down_grad(1)
    folds_dn[0].start()
    folds_dn[1].start()
    unlower(3)
    unlift(3)
    fold_y.pair(3)
    up_grad(3)
    fold_y.onward(3)

    up_grad(1)
    down_grad(2)
    fold_y.cross()
    folds_dn[0].middle()
    folds_up[0].start()
    down_grad(0)
    up_grad(2)
    up_grad(0)
    fold_y.ready()

    dh1, da = r.dh1, r.da

    def first_back(i):
        start = at(i, R)
        rows = pl.ds(start, R)
        incoming = dh2[rows, :] + fold_y.rows(start, R)
        normal = n1[rows, :]
        grad = norm_back(incoming, normal, r1[rows, 0:1], row(FIRST_GAIN))
        dh1[rows, :] = grad
        low = grad.astype(bf16)
        da[rows, :] = low
        add_row(0, low.astype(f32))
        add_row(1, incoming * normal)
        add_row(2, incoming)
    loop(T // R, first_back, 2)
    fold_y.batch.close()

    dc_tok, dc = r.dc_tok, r.dc
    dc_tok[...] = mm(da[...], w_o[...], NT).astype(bf16)
    share_dc = Share(7, dc.at[pl.ds(0, T)])
    share_dc.plane(lambda o: dc_tok.at[:, block_of(o, C)], dc.at[block_of(s, T)])
    dc[block_of(s, T), :] = dc_tok[:, block_of(s, C)]
    da_cols = r.da_cols
    share_da = Share(7, da_cols.at[pl.ds(0, T)])
    share_da.plane(lambda o: da.at[:, block_of(o, C)], da_cols.at[block_of(s, T)])
    da_cols[block_of(s, T), :] = da[:, block_of(s, C)]
    vec_z, vec_all = r.vec_z, r.vec_all
    share_vec = Share(3, vec_z.at[0])
    for k in (2, 3, 1):
        share_vec.batch.send(vecg.at[:, block_of(pz(k), KW)], vec_z.at[z], share_vec.slot, (s, pz(k)))
    vec_z[z] = vecg[:, block_of(z, KW)]
    folds_dn[1].middle()
    folds_up[1].start()
    share_dc.wait()

    delta, dq, dproj = r.delta, r.dq, r.dproj

    def deltas(i):
        here = pl.ds(at(i, T), T)
        turned = jnp.transpose(dc[here, :].astype(f32) * c_f[here, :])
        delta[0:1, here] = jnp.sum(turned[:HEAD_DIM], axis=0, keepdims=True)
        delta[1:2, here] = jnp.sum(turned[HEAD_DIM:], axis=0, keepdims=True)
        dq[here, :] = jnp.zeros((T, C), f32)
    loop(L // T, deltas)

    def attend_back(i):
        here = pl.ds(at(i, T), T)
        same = same_document(here)
        k_here, v_here = k_ref[here, :], v_ref[here, :]
        keys, values, slopes = [], [], []
        for h in range(2):
            own = low_head if h == 0 else jnp.logical_not(low_head)
            nothing = jnp.zeros_like(k_here)
            key = jnp.where(own, k_here, nothing)
            weight = jnp.exp(jnp.where(same, mm(key, q_ref[...], NT), MASKED) - lse[h:h + 1, :])
            slope = mm(jnp.where(own, v_here, nothing), dc[...], NT) - delta[h:h + 1, :]
            slopes.append((weight * slope).astype(bf16))
            values.append(mm(weight.astype(bf16), dc[...]))
            keys.append(key)
        dv = jnp.where(low_head, values[0], values[1]).astype(bf16)
        dk = jnp.where(low_head, mm(slopes[0], q_ref[...]), mm(slopes[1], q_ref[...])).astype(bf16).astype(f32)
        dproj[here, 2 * C:] = dv
        dproj[here, C:2 * C] = (dk * cos_ref[here, :] - swapped(dk) * sin_ref[here, :]).astype(bf16)
        dq[...] = dq[...] + mm(jnp.concatenate(slopes, axis=0), jnp.concatenate(keys, axis=0), TN)

    gd_all, gu_all, go_all, gqk_all, gv_all = r.gd, r.gu, r.go, r.gqk, r.gv
    gather_gd = Gather(lambda o: gd_all.at[block_of(o, UZ)])
    gather_gu = Gather(lambda o: gu_all.at[o])
    gather_go = Gather(lambda o: go_all.at[:, block_of(o, C)])
    gather_gqk = Gather(lambda o: gqk_all.at[o])
    gather_gv = Gather(lambda o: gv_all.at[o])
    go_part = r.go_part
    fold_o = Fold(go_part, r.go_land, r.go_pass)

    def out_grad(k):
        go_part[pz(k)] = mm(c_all[:, block_of(pz(k), KW)], da_cols[...], TN).astype(bf16)

    def attend_back_and_fold(i):
        attend_back(i)

        @pl.when(i == 0)
        def _():
            gather_c.pass_near()

        @pl.when(i == 5)
        def _():
            for part in range(2):
                at_row = pl.multiple_of(s * UZ + part * (UZ // 2), UZ // 2)
                gd_all[pl.ds(at_row, UZ // 2), :] = folds_dn[part].finish()
            gather_gd.start()

        @pl.when(i == 6)
        def _():
            folds_up[0].middle()
            gather_c.pass_far()
    loop(L // T, attend_back_and_fold)


    def dq_rows(i):
        here = pl.ds(at(i, T), T)
        whole = (dq[here, :] * scale).astype(bf16).astype(f32)
        dproj[here, :C] = (whole * cos_ref[here, :] - swapped(whole) * sin_ref[here, :]).astype(bf16)
        colg[1:2, :3 * C] = colg[1:2, :3 * C] + jnp.sum(dproj[here, :].astype(f32), axis=0, keepdims=True)
    loop(L // T, dq_rows)

    gqk_part, gv_part = r.gqk_part, r.gv_part
    fold_qk = Fold(gqk_part, r.gqk_land, r.gqk_pass)
    fold_v = Fold(gv_part, r.gv_land, r.gv_pass)

    def projection_grad(k):
        grad = mm(x_t[block_of(pz(k), KW), :], dproj[...]).astype(bf16)
        gqk_part[pz(k)] = grad[:, :2 * C]
        gv_part[pz(k)] = grad[:, 2 * C:]
    projection_grad(3)
    projection_grad(1)
    fold_x = Scatter(parts, r.low2, mid, r.high2)

    def unproject(j):
        parts[j] = mm(dproj[block_of(chip_of(j), T2), :], w_qkv[...], NT).astype(bf16)
        fold_x.pair(j)
    fold_qk.start()
    unproject(3)
    unproject(1)
    fold_x.onward(3)
    folds_up[1].middle()
    fold_v.start()
    unproject(2)
    fold_x.onward(1)
    unproject(0)
    fold_x.onward(2)
    gather_c.wait()
    share_da.wait()
    for k in (3, 1):
        out_grad(k)
    fold_o.start()
    for k in (2, 0):
        out_grad(k)
    projection_grad(2)
    projection_grad(0)
    fold_x.cross()
    gather_gd.pass_near()
    col_z, col_own = r.col_z, r.col_own
    col_own[...] = jnp.zeros((8, C), f32)
    for i in range(Z):
        col_own[i:i + 1, :] = colg[0:1, i * C:(i + 1) * C]
    for i in range(3):
        col_own[Z + i:Z + i + 1, :] = colg[1:2, i * C:(i + 1) * C]
    share_col = Share(3, col_own)
    share_col.column(col_own, col_z.at[z])
    col_z[z] = col_own[...]
    share_vec.wait()
    vec_sum = r.vec_sum
    vec_sum[...] = vec_z[0] + vec_z[1] + vec_z[2] + vec_z[3]
    share_sum = Share(7, vec_sum)
    share_sum.plane(lambda o: vec_sum, vec_all.at[s])
    vec_all[s] = vec_sum[...]
    for i in range(2):
        gu_all[s, pl.ds(i * (KW // 2), KW // 2), :] = folds_up[i].finish()
    gather_gu.start()
    fold_qk.middle()

    @pl.when(zhigh == 1)
    def _():
        fold_v.middle()
        fold_o.middle()
    gather_gd.pass_far()
    fold_x.ready()
    dx_ref = r.dx

    def input_back(i):
        start = at(i, R)
        rows = pl.ds(start, R)
        dx_ref[rows, :] = (dh1[rows, :] + fold_x.rows(start, R)).astype(bf16)
    loop(T // R, input_back, 2)
    gather_gd.wait()
    gather_gu.pass_near()

    @pl.when(zhigh == 0)
    def _():
        fold_v.middle()
        fold_o.middle()
    gqk_all[s] = fold_qk.finish()
    gather_gqk.start()
    gv_all[s] = fold_v.finish()
    gather_gv.start()
    go_all[:, block_of(s, C)] = fold_o.finish()
    gather_go.start()
    gather_gu.pass_far()
    share_col.wait()
    col_all, col_sum = r.col_all, r.col_sum
    col_sum[...] = col_z[0] + col_z[1] + col_z[2] + col_z[3]
    share_cols = Share(7, col_sum)
    share_cols.plane(lambda o: col_sum, col_all.at[s])
    col_all[s] = col_sum[...]
    gather_gqk.pass_near()
    gather_gv.pass_near()
    gather_gu.wait()

    share_sum.wait()
    share_cols.wait()
    total = vec_all[0]
    for o in range(1, S):
        total = total + vec_all[o]
    gsm = r.gsm
    gsm[...] = jnp.zeros(gsm.shape, f32)
    for start, i in wide:
        for half in range(KW // C):
            gsm[start + half:start + half + 1, :] = total[i:i + 1, half * C:(half + 1) * C]
    for o in range(S):
        at_row = first_row.up_bias + o
        gsm[at_row:at_row + 1, :] = col_all[o, pl.ds(z, 1), :]
    for i in range(per):
        number = z * per + i
        at_row = first_row.projection_bias + i
        gsm[at_row:at_row + 1, :] = col_all[number % S, pl.ds(Z + number // S, 1), :]
    gather_go.pass_near()
    gather_gqk.pass_far()
    gather_gv.pass_far()
    gather_go.pass_far()
    gather_go.wait()
    gather_gqk.wait()
    gather_gv.wait()
    for batch in closing:
        batch.close()
    assert counter[0] <= LANDINGS and counter[1] <= BATCHES and counter[2] <= LOCAL, counter


def fused_shards(*args):
    (hidden_in, cotangent, segment_ids, projection, projection_bias, output_weight, output_bias, first_gain,
     first_shift, up_weight, up_bias, down_weight, down_bias, second_gain, second_shift) = args
    T, D = hidden_in.shape[1:]
    L = segment_ids.shape[1]
    KW = projection.shape[0]
    F = up_weight.shape[1] // 8
    C, Z = 128, 4
    UZ = F // Z
    small = dict(projection_bias=projection_bias, output_bias=output_bias, first_gain=first_gain,
                 first_shift=first_shift, up_bias=up_bias, down_bias=down_bias, second_gain=second_gain,
                 second_shift=second_shift)
    starts, at_row = {}, 0
    for name, value in small.items():
        starts[name] = at_row
        at_row += value.shape[0] // C
    rows = -(-at_row // 8) * 8
    half = HEAD_DIM // 2
    inverse = np.float32(10000.0) ** (np.float32(-2.0) * np.arange(half, dtype=np.float32) / np.float32(HEAD_DIM))
    angles = np.arange(L, dtype=np.float32)[:, None] * inverse.astype(np.float32)[None, :]
    cosine = np.tile(np.cos(angles), (1, C // half))
    sine = np.tile(np.concatenate([-np.sin(angles), np.sin(angles)], axis=1), (1, C // HEAD_DIM))

    inputs = dict(x=hidden_in[0], ct=cotangent[0], seg=segment_ids, cos=jnp.asarray(cosine), sin=jnp.asarray(sine),
                  b_projection=projection_bias.reshape(-1, C), b_output=output_bias[None], gain1=first_gain[None],
                  shift1=first_shift[None], b_up=up_bias[None], b_down=down_bias[None], gain2=second_gain[None],
                  shift2=second_shift[None], proj=projection, wo=output_weight, up=up_weight, dn=down_weight)
    outputs = dict(out=((T, D), bf16), dx=((T, D), bf16), gsm=((rows, C), f32), gqk=((8, KW, 2 * C), bf16), gv=((8, KW, C), bf16),
                   go=((KW, D), bf16), gu=((8, KW, F), bf16), gd=((8 * UZ, D), bf16))
    landed = dict(v_x=inputs["x"], v_ct=inputs["ct"], v_seg=segment_ids, v_cos=inputs["cos"], v_sin=inputs["sin"],
                  v_projection=inputs["b_projection"], v_output=inputs["b_output"], v_gain1=inputs["gain1"],
                  v_shift1=inputs["shift1"], v_up=inputs["b_up"], v_down=inputs["b_down"], v_gain2=inputs["gain2"],
                  v_shift2=inputs["shift2"])
    PART = (4, T, D)
    scratch = {name: (value.shape, value.dtype) for name, value in landed.items()}
    scratch.update(
        x_all=((L, D), bf16), x_t=((D, L), bf16), w_qkv=((D, 3 * C), bf16), st_proj=((KW, 3 * C), f32),
        w_o=((D, D), bf16), st_wo=((KW, C), f32), w_up=((D, F), bf16), st_up=((KW, F), f32),
        w_dn=((F, D), bf16), st_dn=((UZ, D), f32), small_all=((Z, rows, C), f32), vec=((8, D), f32),
        vecg=((8, D), f32), q=((L, C), bf16), k=((L, C), bf16), v=((L, C), bf16),
        seg_r=((8, L), f32), seg_c=((L, C), f32), small=((rows, C), f32), lse=((8, L), f32),
        delta=((8, L), f32), c_f=((L, C), f32), c_heads=((L, C), bf16), c_tok=((T, D), bf16),
        a_buf=((T, D), f32), n1=((T, D), f32), y1=((T, D), f32), r1=((T, C), f32),
        y_all=((L, D), bf16), y_t=((D, L), bf16), u_buf=((2 * T, F), f32), g=((L, F), bf16),
        g_t=((F, L), bf16), d=((L, F), f32), du=((L, F), bf16), dz_all=((L, D), bf16),
        parts=((4, 2 * T, D), bf16), mid=((4, T, D), bf16), dh2=((T, D), f32), dh1=((T, D), f32),
        colg=((8, F), f32), gd_part=((Z, UZ, D), bf16), gd_land=((3, UZ, D), bf16), gd_pass=((UZ, D), bf16),
        gu_part=((Z, KW, F), bf16), gu_land=((3, KW, F), bf16), gu_pass=((KW, F), bf16),
        go_part=((Z, KW, C), bf16), go_land=((3, KW, C), bf16), go_pass=((KW, C), bf16),
        gqk_part=((Z, KW, 2 * C), bf16), gqk_land=((3, KW, 2 * C), bf16), gqk_pass=((KW, 2 * C), bf16),
        gv_part=((Z, KW, C), bf16), gv_land=((3, KW, C), bf16), gv_pass=((KW, C), bf16),
        da=((T, D), bf16), dc_tok=((T, D), bf16), dc=((L, C), bf16),
        da_cols=((L, C), bf16), c_all=((L, D), bf16), dq=((L, C), f32), dproj=((L, 3 * C), bf16),
        vec_all=((8, 8, KW), f32), vec_z=((Z, 8, KW), f32), vec_sum=((8, KW), f32), col_own=((8, C), f32),
        col_z=((Z, 8, C), f32), col_sum=((8, C), f32), col_all=((8, 8, C), f32),
        low0=(PART, bf16), high0=(PART, bf16), low1=(PART, bf16), high1=(PART, bf16), low2=(PART, bf16),
        high2=(PART, bf16), ssem=(BATCHES,), rsem=(LANDINGS,), lsem=(LOCAL,))
    names = [*inputs, *outputs, *scratch]
    sizes = SimpleNamespace(names=names, T=T, D=D, L=L, F=F, first_row=SimpleNamespace(**starts))

    anywhere, near = pl.BlockSpec(memory_space=pl.ANY), pl.BlockSpec(memory_space=pltpu.VMEM)
    results = pl.pallas_call(
        partial(fused_layer, sizes),
        out_shape=[pltpu.VMEM(*what) for what in outputs.values()],
        in_specs=[anywhere] * len(inputs),
        out_specs=[near] * len(outputs),
        scratch_shapes=[pltpu.VMEM(*what) if len(what) == 2 else pltpu.SemaphoreType.DMA(what)
                        for what in scratch.values()],
        compiler_params=pltpu.CompilerParams(collective_id=0, has_side_effects=True, vmem_limit_bytes=57 << 20),
        name="fused_layer",
    )(*inputs.values())
    out, dx, gsm, gqk, gv, go, gu, gd = results
    wide = [jax.ShapeDtypeStruct(value.shape, f32) for value in (projection, output_weight, up_weight, down_weight)]
    narrow = [jax.ShapeDtypeStruct((1, value.shape[0]) if value is not projection_bias else (value.shape[0] // C, C), f32)
              for value in small.values()]
    sources = [out, dx, gqk, gv, go, gu, gd, gsm]
    outcomes = [out, dx] + wide + narrow
    results = pl.pallas_call(
        partial(widen, tuple(starts.values())),
        out_shape=[jax.ShapeDtypeStruct(value.shape, value.dtype) for value in outcomes],
        in_specs=[near] * len(sources),
        out_specs=[anywhere] * len(outcomes),
        scratch_shapes=[pltpu.VMEM(value.shape, value.dtype) for value in outcomes[2:]]
        + [pltpu.SemaphoreType.DMA((LOCAL,))],
        compiler_params=pltpu.CompilerParams(vmem_limit_bytes=20 << 20),
        name="widen",
    )(*sources)
    out, dx, gq, go, gu, gd = results[:6]
    pb, ob, g1, s1, ub, db, g2, s2 = [value.reshape(-1) for value in results[6:]]
    return (out[None], dx[None], gq, pb, go, ob, g1, s1, gu, ub, gd, db, g2, s2)


def widen(starts, *refs):
    held, results, made, outsem = refs[:8], refs[8:22], refs[22:34], refs[34]
    out, dx, gqk, gv, go, gu, gd, gsm = held
    C = gsm.shape[1]
    stores = []

    def store(ref, result):
        copy = pltpu.make_async_copy(ref, result, outsem.at[len(stores)])
        copy.start()
        stores.append(copy)

    def grouped(i, target, at, n, first):
        source, result = held[i], made[target]
        groups = source.shape[0]

        def step(j, carry):
            rows = pl.ds(pl.multiple_of(at + j * 32, 32), 32)
            for o in range(groups):
                for p in range(source.shape[2] // C):
                    lane = ((first + p) * groups + o) * C
                    result[rows, lane:lane + C] = source[o, rows, p * C:(p + 1) * C].astype(f32)
            return carry
        lax.fori_loop(0, n // 32, step, 0)

    def plain(i, target, at, n, _):
        source, result = held[i], made[target]

        def step(j, carry):
            rows = pl.ds(pl.multiple_of(at + j * 32, 32), 32)
            result[rows, :] = source[rows, :].astype(f32)
            return carry
        lax.fori_loop(0, n // 32, step, 0)

    store(out, results[0])
    store(dx, results[1])
    work = []
    for i, target, n, body, first in ((5, 2, 64, grouped, 0), (6, 3, 256, plain, 0), (2, 0, 64, grouped, 0),
                                      (3, 0, 64, grouped, 2), (4, 1, 256, plain, 0)):
        total = held[i].shape[-2]
        for at in range(0, total, n):
            work.append((i, target, at, n, body, first))
    for i, target, at, n, body, first in work:
        body(i, target, at, n, first)
        if i != 2:
            rows = pl.ds(at, n)
            store(made[target].at[rows], results[2 + target].at[rows])
    for start, ref, result in zip(starts, made[4:], results[6:]):
        if ref.shape[1] == C:
            ref[...] = gsm[start:start + ref.shape[0], :]
        else:
            for i in range(ref.shape[1] // C):
                ref[0:1, i * C:(i + 1) * C] = gsm[start + i:start + i + 1, :]
        store(ref, result)
    for copy in stores:
        copy.wait()


BATCHES = 44
LANDINGS = 166
LOCAL = 32


def fits(mesh):
    return mesh.shape["seq"] == 8 and mesh.shape["fsdp"] == 4


def solution(mesh):
    return jax.shard_map(
        fused_shards if fits(mesh) else shards,
        mesh=mesh,
        in_specs=(
            P("fsdp", "seq", None),
            P("fsdp", "seq", None),
            P("fsdp", None),
            P("fsdp", None),
            P("fsdp"),
            P("fsdp", None),
            P("fsdp"),
            P("fsdp"),
            P("fsdp"),
            P("fsdp", None),
            P("fsdp"),
            P("fsdp", None),
            P("fsdp"),
            P("fsdp"),
            P("fsdp"),
        ),
        out_specs=(
            P("fsdp", "seq", None),
            P("fsdp", "seq", None),
            P("fsdp", None),
            P("fsdp"),
            P("fsdp", None),
            P("fsdp"),
            P("fsdp"),
            P("fsdp"),
            P("fsdp", None),
            P("fsdp"),
            P("fsdp", None),
            P("fsdp"),
            P("fsdp"),
            P("fsdp"),
        ),
        check_vma=False,
    )
```

```python
from functools import partial

import jax
import jax.numpy as jnp
import numpy as np
import math
from types import SimpleNamespace
from jax import lax
from jax.experimental import pallas as pl
from jax.experimental.pallas import tpu as pltpu
from jax.sharding import PartitionSpec as P

HEADS = 16
HEAD_DIM = 64


norm_epsilon = 1e-05


def rotary(values, positions):
    half = values.shape[-1] // 2
    channel = jnp.arange(half).astype(jnp.float32)
    inverse = 10000.0 ** (-2.0 * channel / values.shape[-1])
    angles = positions[:, None] * inverse[None, :]
    cosine = jnp.cos(angles)[:, None, :]
    sine = jnp.sin(angles)[:, None, :]
    first = values[..., :half]
    second = values[..., half:]
    return jnp.concatenate(
        [first * cosine - second * sine, second * cosine + first * sine], axis=-1
    )


def rotary_back(grads, positions):
    unused, pullback = jax.vjp(lambda inner: rotary(inner, positions), grads)
    return pullback(grads)[0]


def norm_forward(values, gain, shift):
    centre = values - jnp.mean(values, axis=-1, keepdims=True)
    inverse_root = lax.rsqrt(jnp.mean(centre * centre, axis=-1, keepdims=True) + norm_epsilon)
    normal = centre * inverse_root
    return (normal * gain + shift, normal, inverse_root)


def norm_backward(incoming, normal, inverse_root, gain):
    gain_grad = jnp.sum(incoming * normal, axis=0)
    shift_grad = jnp.sum(incoming, axis=0)
    scaled = incoming * gain
    inner = (
        scaled
        - jnp.mean(scaled, axis=-1, keepdims=True)
        - normal * jnp.mean(scaled * normal, axis=-1, keepdims=True)
    )
    return (inner * inverse_root, gain_grad, shift_grad)


def shards(
    hidden_in,
    cotangent,
    segment_ids,
    projection,
    projection_bias,
    output_weight,
    output_bias,
    first_gain,
    first_shift,
    up_weight,
    up_bias,
    down_weight,
    down_bias,
    second_gain,
    second_shift,
):
    bf16 = jnp.bfloat16
    f32 = jnp.float32
    tokens = hidden_in[0]
    local_rows = tokens.shape[0]
    width = tokens.shape[1]
    seq_rank = lax.axis_index("seq")
    positions = (seq_rank * local_rows + jnp.arange(local_rows)).astype(f32)
    segments = segment_ids[0]
    scale = HEAD_DIM ** (-0.5)
    attention_full = (
        lax.all_gather(projection.astype(bf16), "fsdp", axis=0, tiled=True),
        lax.all_gather(projection_bias.astype(bf16), "fsdp", axis=0, tiled=True),
        lax.all_gather(output_weight.astype(bf16), "fsdp", axis=0, tiled=True),
        lax.all_gather(output_bias.astype(bf16), "fsdp", axis=0, tiled=True),
        lax.all_gather(first_gain.astype(bf16), "fsdp", axis=0, tiled=True),
        lax.all_gather(first_shift.astype(bf16), "fsdp", axis=0, tiled=True),
    )
    proj_weight = attention_full[0]
    projected = jnp.dot(tokens, proj_weight, preferred_element_type=f32) + attention_full[1].astype(
        f32
    )
    heads = projected.reshape(local_rows, 3, HEADS, HEAD_DIM)
    queries = rotary(heads[:, 0], positions)
    keys = rotary(heads[:, 1], positions)
    stacked = jnp.stack([queries, keys, heads[:, 2]]).astype(bf16)
    spread = lax.all_to_all(stacked, "seq", split_axis=2, concat_axis=1, tiled=True)
    query_all = spread[0]
    key_all = spread[1]
    value_all = spread[2]
    length = query_all.shape[0]
    local_heads = query_all.shape[1]
    block = min(512, length)
    count = length // block
    query_blocks = query_all.reshape(count, block, local_heads, HEAD_DIM)
    segment_blocks = segments.reshape(count, block)

    def scores_of(query_block, segment_block):
        raw = jnp.einsum("qhd,khd->hqk", query_block, key_all, preferred_element_type=f32) * scale
        allowed = segment_block[:, None] == segments[None, :]
        return jnp.where(allowed[None], raw, -1e30)

    def forward_block(pieces):
        query_block, segment_block = pieces
        scores = scores_of(query_block, segment_block)
        row_max = jnp.max(scores, axis=-1, keepdims=True)
        exponent = jnp.exp(scores - row_max)
        total = jnp.sum(exponent, axis=-1, keepdims=True)
        weights = exponent / total
        context = jnp.einsum(
            "hqk,khd->qhd", weights.astype(bf16), value_all, preferred_element_type=f32
        )
        return (context.astype(bf16), (row_max + jnp.log(total))[..., 0])

    context_blocks, log_totals = lax.map(forward_block, (query_blocks, segment_blocks))
    context_heads = context_blocks.reshape(length, local_heads, HEAD_DIM)
    context_tokens = lax.all_to_all(
        context_heads, "seq", split_axis=0, concat_axis=1, tiled=True
    ).reshape(local_rows, width)
    attended = jnp.dot(
        context_tokens, attention_full[2], preferred_element_type=f32
    ) + attention_full[3].astype(f32)
    gain_one = attention_full[4].astype(f32)
    normed_one, normal_one, inverse_one = norm_forward(
        tokens.astype(f32) + attended, gain_one, attention_full[5].astype(f32)
    )
    feed_full = (
        lax.all_gather(up_weight.astype(bf16), "fsdp", axis=0, tiled=True),
        lax.all_gather(up_bias.astype(bf16), "fsdp", axis=0, tiled=True),
        lax.all_gather(down_weight.astype(bf16), "fsdp", axis=0, tiled=True),
        lax.all_gather(down_bias.astype(bf16), "fsdp", axis=0, tiled=True),
        lax.all_gather(second_gain.astype(bf16), "fsdp", axis=0, tiled=True),
        lax.all_gather(second_shift.astype(bf16), "fsdp", axis=0, tiled=True),
    )
    normed_low = normed_one.astype(bf16)
    lifted = jnp.dot(normed_low, feed_full[0], preferred_element_type=f32) + feed_full[1].astype(
        f32
    )
    activated = jax.nn.gelu(lifted, approximate=False).astype(bf16)
    lowered = jnp.dot(activated, feed_full[2], preferred_element_type=f32) + feed_full[3].astype(
        f32
    )
    gain_two = feed_full[4].astype(f32)
    layer_out, normal_two, inverse_two = norm_forward(
        normed_one + lowered, gain_two, feed_full[5].astype(f32)
    )
    feed_back = (
        lax.all_gather(up_weight.astype(bf16), "fsdp", axis=0, tiled=True),
        lax.all_gather(up_bias.astype(bf16), "fsdp", axis=0, tiled=True),
        lax.all_gather(down_weight.astype(bf16), "fsdp", axis=0, tiled=True),
        lax.all_gather(down_bias.astype(bf16), "fsdp", axis=0, tiled=True),
        lax.all_gather(second_gain.astype(bf16), "fsdp", axis=0, tiled=True),
        lax.all_gather(second_shift.astype(bf16), "fsdp", axis=0, tiled=True),
    )
    attention_back = (
        lax.all_gather(projection.astype(bf16), "fsdp", axis=0, tiled=True),
        lax.all_gather(projection_bias.astype(bf16), "fsdp", axis=0, tiled=True),
        lax.all_gather(output_weight.astype(bf16), "fsdp", axis=0, tiled=True),
        lax.all_gather(output_bias.astype(bf16), "fsdp", axis=0, tiled=True),
        lax.all_gather(first_gain.astype(bf16), "fsdp", axis=0, tiled=True),
        lax.all_gather(first_shift.astype(bf16), "fsdp", axis=0, tiled=True),
    )
    grad_two, second_gain_grad, second_shift_grad = norm_backward(
        cotangent[0].astype(f32), normal_two, inverse_two, gain_two
    )
    lowered_grad = grad_two.astype(bf16)
    down_weight_grad = jnp.einsum("tf,td->fd", activated, lowered_grad, preferred_element_type=f32)
    down_bias_grad = jnp.sum(lowered_grad.astype(f32), axis=0)
    active_grad = jnp.einsum("td,fd->tf", lowered_grad, feed_back[2], preferred_element_type=f32)
    unused, gelu_pull = jax.vjp(partial(jax.nn.gelu, approximate=False), lifted)
    lifted_grad = gelu_pull(active_grad)[0].astype(bf16)
    up_weight_grad = jnp.einsum("td,tf->df", normed_low, lifted_grad, preferred_element_type=f32)
    up_bias_grad = jnp.sum(lifted_grad.astype(f32), axis=0)
    normed_grad = grad_two + jnp.einsum(
        "tf,df->td", lifted_grad, feed_back[0], preferred_element_type=f32
    )
    grad_one, first_gain_grad, first_shift_grad = norm_backward(
        normed_grad, normal_one, inverse_one, attention_back[4].astype(f32)
    )
    attended_grad = grad_one.astype(bf16)
    output_weight_grad = jnp.einsum(
        "tc,td->cd", context_tokens, attended_grad, preferred_element_type=f32
    )
    output_bias_grad = jnp.sum(attended_grad.astype(f32), axis=0)
    context_grad = jnp.einsum(
        "td,cd->tc", attended_grad, attention_back[2], preferred_element_type=f32
    ).astype(bf16)
    context_grad = context_grad.reshape(local_rows, HEADS, HEAD_DIM)
    context_grad_heads = lax.all_to_all(
        context_grad, "seq", split_axis=1, concat_axis=0, tiled=True
    )
    grad_blocks = context_grad_heads.reshape(count, block, local_heads, HEAD_DIM)

    def backward_block(carry, pieces):
        key_grad, value_grad = carry
        query_block, segment_block, grad_block, log_block = pieces
        scores = scores_of(query_block, segment_block)
        weights = jnp.exp(scores - log_block[..., None])
        value_grad = value_grad + jnp.einsum(
            "hqk,qhd->khd", weights.astype(bf16), grad_block, preferred_element_type=f32
        )
        weight_grad = jnp.einsum("qhd,khd->hqk", grad_block, value_all, preferred_element_type=f32)
        centre = jnp.sum(weights * weight_grad, axis=-1, keepdims=True)
        score_grad = (weights * (weight_grad - centre)).astype(bf16)
        query_grad = (
            jnp.einsum("hqk,khd->qhd", score_grad, key_all, preferred_element_type=f32) * scale
        )
        key_grad = (
            key_grad
            + jnp.einsum("hqk,qhd->khd", score_grad, query_block, preferred_element_type=f32)
            * scale
        )
        return ((key_grad, value_grad), query_grad)

    zeros_heads = jnp.zeros((length, local_heads, HEAD_DIM), f32)
    (key_grad, value_grad), query_grad = lax.scan(
        backward_block,
        (zeros_heads, zeros_heads),
        (query_blocks, segment_blocks, grad_blocks, log_totals),
    )
    query_grad = query_grad.reshape(length, local_heads, HEAD_DIM)
    stacked_grad = jnp.stack([query_grad, key_grad, value_grad]).astype(bf16)
    token_heads = lax.all_to_all(stacked_grad, "seq", split_axis=1, concat_axis=2, tiled=True)
    query_back = rotary_back(token_heads[0].astype(f32), positions)
    key_back = rotary_back(token_heads[1].astype(f32), positions)
    projected_grad = jnp.stack([query_back, key_back, token_heads[2].astype(f32)], axis=1)
    projected_grad = projected_grad.reshape(local_rows, 3 * width).astype(bf16)
    projection_grad = jnp.einsum("td,te->de", tokens, projected_grad, preferred_element_type=f32)
    projection_bias_grad = jnp.sum(projected_grad.astype(f32), axis=0)
    input_grad = grad_one + jnp.einsum(
        "te,de->td", projected_grad, attention_back[0], preferred_element_type=f32
    )
    every_shard = (
        lax.psum_scatter(
            projection_grad.astype(jnp.bfloat16), "fsdp", scatter_dimension=0, tiled=True
        ).astype(jnp.float32),
        lax.psum_scatter(
            projection_bias_grad.astype(jnp.bfloat16), "fsdp", scatter_dimension=0, tiled=True
        ).astype(jnp.float32),
        lax.psum_scatter(
            output_weight_grad.astype(jnp.bfloat16), "fsdp", scatter_dimension=0, tiled=True
        ).astype(jnp.float32),
        lax.psum_scatter(
            output_bias_grad.astype(jnp.bfloat16), "fsdp", scatter_dimension=0, tiled=True
        ).astype(jnp.float32),
        lax.psum_scatter(
            first_gain_grad.astype(jnp.bfloat16), "fsdp", scatter_dimension=0, tiled=True
        ).astype(jnp.float32),
        lax.psum_scatter(
            first_shift_grad.astype(jnp.bfloat16), "fsdp", scatter_dimension=0, tiled=True
        ).astype(jnp.float32),
        lax.psum_scatter(
            up_weight_grad.astype(jnp.bfloat16), "fsdp", scatter_dimension=0, tiled=True
        ).astype(jnp.float32),
        lax.psum_scatter(
            up_bias_grad.astype(jnp.bfloat16), "fsdp", scatter_dimension=0, tiled=True
        ).astype(jnp.float32),
        lax.psum_scatter(
            down_weight_grad.astype(jnp.bfloat16), "fsdp", scatter_dimension=0, tiled=True
        ).astype(jnp.float32),
        lax.psum_scatter(
            down_bias_grad.astype(jnp.bfloat16), "fsdp", scatter_dimension=0, tiled=True
        ).astype(jnp.float32),
        lax.psum_scatter(
            second_gain_grad.astype(jnp.bfloat16), "fsdp", scatter_dimension=0, tiled=True
        ).astype(jnp.float32),
        lax.psum_scatter(
            second_shift_grad.astype(jnp.bfloat16), "fsdp", scatter_dimension=0, tiled=True
        ).astype(jnp.float32),
    )
    finals = (
        lax.psum(every_shard[0].astype(jnp.bfloat16), "seq").astype(jnp.float32),
        lax.psum(every_shard[1].astype(jnp.bfloat16), "seq").astype(jnp.float32),
        lax.psum(every_shard[2].astype(jnp.bfloat16), "seq").astype(jnp.float32),
        lax.psum(every_shard[3].astype(jnp.bfloat16), "seq").astype(jnp.float32),
        lax.psum(every_shard[4].astype(jnp.bfloat16), "seq").astype(jnp.float32),
        lax.psum(every_shard[5].astype(jnp.bfloat16), "seq").astype(jnp.float32),
        lax.psum(every_shard[6].astype(jnp.bfloat16), "seq").astype(jnp.float32),
        lax.psum(every_shard[7].astype(jnp.bfloat16), "seq").astype(jnp.float32),
        lax.psum(every_shard[8].astype(jnp.bfloat16), "seq").astype(jnp.float32),
        lax.psum(every_shard[9].astype(jnp.bfloat16), "seq").astype(jnp.float32),
        lax.psum(every_shard[10].astype(jnp.bfloat16), "seq").astype(jnp.float32),
        lax.psum(every_shard[11].astype(jnp.bfloat16), "seq").astype(jnp.float32),
    )
    return (
        layer_out.astype(bf16)[None],
        input_grad.astype(bf16)[None],
        finals[0],
        finals[1],
        finals[2],
        finals[3],
        finals[4],
        finals[5],
        finals[6],
        finals[7],
        finals[8],
        finals[9],
        finals[10],
        finals[11],
    )


MESH = pl.DeviceIdType.MESH
NN = (((1,), (0,)), ((), ()))
NT = (((1,), (1,)), ((), ()))
TN = (((0,), (0,)), ((), ()))
f32 = jnp.float32
bf16 = jnp.bfloat16
MASKED = -1e30


def mm(left, right, dims=NN):
    return lax.dot_general(left, right, dims, preferred_element_type=f32)


def block_of(index, size):
    return pl.ds(pl.multiple_of(index * size, size), size)


def flip(bit, other):
    return bit + other - 2 * bit * other


def fused_layer(sizes, *refs):
    r = SimpleNamespace(**dict(zip(sizes.names, refs)))
    T, D, L, F = sizes.T, sizes.D, sizes.L, sizes.F
    S, Z = 8, 4
    KW = D // Z
    UZ = F // Z
    C = 128
    T2 = 2 * T
    first_row = sizes.first_row
    ssem, rsem, lsem = r.ssem, r.rsem, r.lsem

    s = lax.axis_index("seq")
    z = lax.axis_index("fsdp")
    core, xbit, ybit = s % 2, (s // 2) % 2, s // 4
    zlow, zhigh = z % 2, z // 2

    def ps(k):
        return flip(core, k % 2) + 2 * flip(xbit, (k // 2) % 2) + 4 * flip(ybit, k // 4)

    def pz(k):
        return flip(zlow, k % 2) + 2 * flip(zhigh, k // 2)

    def chip_of(j):
        return flip(xbit, j % 2) + 2 * flip(ybit, j // 2)

    counter = [0, 0, 0]
    closing = []

    def take(which, n=1):
        counter[which] += n
        return counter[which] - n

    def landings(n=1):
        return take(0, n)

    def size(ref):
        return math.prod(ref.shape) * jnp.dtype(ref.dtype).itemsize

    def extent(n):
        if n <= size(r.c_f):
            return r.c_f.at[pl.ds(0, n * L // size(r.c_f))]
        return r.y_all.at[pl.ds(0, n * L // size(r.y_all))]

    def arrived(ref, slot):
        pltpu.make_async_copy(ref, ref, rsem.at[slot]).wait()

    class Batch:
        def __init__(self, count, like):
            self.slot, self.bytes, self.open = take(1), count * size(like), True
            closing.append(self)

        def send(self, src, dst, slot, dev):
            pltpu.make_async_remote_copy(
                src_ref=src, dst_ref=dst, send_sem=ssem.at[self.slot], recv_sem=rsem.at[slot],
                device_id=dev, device_id_type=MESH).start()

        def close(self):
            if self.open:
                everything = extent(self.bytes)
                pltpu.make_async_copy(everything, everything, ssem.at[self.slot]).wait()
            self.open = False

    def local(src, dst):
        copy = pltpu.make_async_copy(src, dst, lsem.at[take(2)])
        copy.start()
        return copy

    class Gather:
        def __init__(self, place, at_once=True):
            self.place, self.at_once = place, at_once
            self.batch = Batch(7, place(0))
            self.near, self.across = landings(4), landings(2)
            self.other = landings() if at_once else landings(4)

        def part(self, ref, i):
            n = ref.shape[0] // 2
            return ref.at[pl.ds(i * n, n)]

        def start(self, src=None):
            mine = self.place(s)
            src = mine if src is None else src
            for slot, half, k in ((0, 0, 2), (3, 1, 4), (1, 1, 2), (2, 0, 4)):
                self.batch.send(self.part(src, half), self.part(mine, half), self.near + slot, (ps(k), z))
            self.batch.send(src, mine, self.other, (ps(1), z))

        def to_partner(self, k):
            there = self.place(ps(k))
            self.batch.send(there, there, self.other + (0 if self.at_once else k // 2), (ps(1), z))

        def pass_near(self):
            along_x, along_y = self.place(ps(2)), self.place(ps(4))
            first, second = self.part(along_x, 0), self.part(along_y, 1)
            arrived(first, self.near)
            self.batch.send(first, first, self.across, (ps(4), z))
            arrived(second, self.near + 3)
            self.batch.send(second, second, self.across + 1, (ps(2), z))
            arrived(self.part(along_x, 1), self.near + 1)
            self.to_partner(2)
            arrived(self.part(along_y, 0), self.near + 2)
            self.to_partner(4)

        def pass_far(self):
            far = self.place(ps(6))
            arrived(self.part(far, 0), self.across)
            arrived(self.part(far, 1), self.across + 1)
            self.to_partner(6)

        def pass_all(self):
            self.pass_near()
            self.pass_far()

        def wait(self, k=None):
            if self.at_once:
                arrived(extent(4 * size(self.place(0))), self.other)
            else:
                arrived(self.place(ps(k)), self.other + k // 2)

    class Spread:
        def __init__(self, place):
            self.place, self.batch, self.base = place, Batch(3, place(0)), landings(3)

        def start(self, *which):
            mine = self.place(z)
            for k in which or (2, 1):
                self.batch.send(mine, mine, self.base + k - 1, (s, pz(k)))

        def pass_on(self):
            there = self.place(pz(2))
            arrived(there, self.base + 1)
            self.batch.send(there, there, self.base + 2, (s, pz(1)))

        def wait(self):
            for k in (1, 3):
                arrived(self.place(pz(k)), self.base + k - 1)

        def wait_all(self):
            for k in (1, 2, 3):
                arrived(self.place(pz(k)), self.base + k - 1)

    class Fold:
        def __init__(self, parts, landing, passing, first=0, count=None):
            self.rows = pl.ds(first, count or passing.shape[0])
            self.parts, self.landing, self.passing = parts, landing, passing.at[self.rows]
            self.batch, self.base = Batch(3, self.passing), landings(3)

        def start(self):
            for i, k in ((1, 3), (0, 1)):
                self.batch.send(self.parts.at[pz(k), self.rows], self.landing.at[i, self.rows], self.base + i, (s, pz(1)))

        def middle(self):
            arrived(self.landing.at[1, self.rows], self.base + 1)
            self.passing[...] = (self.parts[pz(2), self.rows, :].astype(f32)
                                 + self.landing[1, self.rows, :].astype(f32)).astype(bf16)
            self.batch.send(self.passing, self.landing.at[2, self.rows], self.base + 2, (s, pz(2)))

        def finish(self):
            arrived(self.landing.at[0, self.rows], self.base)
            arrived(self.landing.at[2, self.rows], self.base + 2)
            return (self.parts[z, self.rows, :].astype(f32) + self.landing[0, self.rows, :].astype(f32)
                    + self.landing[2, self.rows, :].astype(f32)).astype(bf16)

    class Scatter:
        def __init__(self, parts, low, mid, high, first=0, count=T):
            self.parts, self.low, self.mid, self.high = parts, low, mid, high
            self.first, self.count, self.window = first, count, pl.ds(first, count)
            self.batch = Batch(7, mid.at[0, self.window])
            self.base, self.far, self.last = landings(4), landings(2), landings()

        def rows_of(self, which):
            return pl.ds(pl.multiple_of(which * T + self.first, self.count), self.count)

        def half(self, ref, j, i):
            return ref.at[j, self.window, pl.ds(i * (D // 2), D // 2)]

        def send(self, j, i, slot, k):
            self.batch.send(self.half(self.mid, j, i), self.half(self.high, j, i), slot, (ps(k), z))

        def pair(self, j):
            self.batch.send(self.parts.at[j, self.rows_of(1 - core)], self.low.at[j, self.window],
                            self.base + j, (ps(1), z))

        def onward(self, j):
            arrived(self.low.at[j, self.window], self.base + j)
            own = self.parts[j, self.rows_of(core), :].astype(f32)
            self.mid[j, self.window, :] = (own + self.low[j, self.window, :].astype(f32)).astype(bf16)
            if j == 1:
                self.send(1, 0, self.last, 2)
            elif j == 2:
                self.send(2, 1, self.last, 4)
            else:
                self.send(3, 0, self.far, 2)
                self.send(3, 1, self.far + 1, 4)

        def cross(self):
            for j, i, k in ((2, 0, 4), (1, 1, 2)):
                arrived(self.half(self.high, 3, i), self.far + i)
                ref = self.half(self.mid, j, i)
                ref[...] = (ref[...].astype(f32) + self.half(self.high, 3, i)[...].astype(f32)).astype(bf16)
                self.send(j, i, self.last, k)

        def ready(self):
            arrived(self.low.at[0, self.window], self.base)
            arrived(self.high.at[pl.ds(1, 2), self.window], self.last)

        def rows(self, at, n):
            own = self.parts[0, pl.ds(pl.multiple_of(core * T + at, n), n), :].astype(f32)
            total = own + self.low[0, pl.ds(at, n), :].astype(f32)
            for j in (1, 2):
                total = total + self.high[j, pl.ds(at, n), :].astype(f32)
            return total

    class Share:
        def __init__(self, count, like):
            self.count, self.batch, self.slot, self.bytes = count, Batch(count, like), landings(), count * size(like)

        def plane(self, src, dst):
            for k in (6, 7, 2, 3, 4, 5, 1):
                self.batch.send(src(ps(k)), dst, self.slot, (ps(k), z))

        def column(self, src, dst):
            for k in (2, 3, 1):
                self.batch.send(src, dst, self.slot, (s, pz(k)))

        def wait(self):
            arrived(extent(self.bytes), self.slot)

    def loop(count, body, unroll=1):
        def step(i, carry):
            body(i)
            return carry
        lax.fori_loop(0, count, step, 0, unroll=unroll)

    def at(i, n):
        return pl.multiple_of(i * n, n)

    def turn(src, dst):
        def one(i):
            dst[:, pl.ds(at(i, T), T)] = jnp.transpose(src[pl.ds(at(i, T), T), :])
        loop(L // T, one)

    vec, vecg = r.vec, r.vecg

    OUTPUT_BIAS, FIRST_GAIN, FIRST_SHIFT, DOWN_BIAS, SECOND_GAIN, SECOND_SHIFT, PROJECTION_BIAS, UP_BIAS = range(8)
    wide = ((first_row.output_bias, OUTPUT_BIAS), (first_row.first_gain, FIRST_GAIN),
            (first_row.first_shift, FIRST_SHIFT), (first_row.down_bias, DOWN_BIAS),
            (first_row.second_gain, SECOND_GAIN), (first_row.second_shift, SECOND_SHIFT))

    def row(i, width=D):
        return vec[i:i + 1, :width]

    lanes = lax.broadcasted_iota(jnp.int32, (T, C), 1)
    low_head = lanes < HEAD_DIM

    def swapped(w):
        low_half = lax.broadcasted_iota(jnp.int32, w.shape, 1) % HEAD_DIM < HEAD_DIM // 2
        return jnp.where(low_half, pltpu.roll(w, C - HEAD_DIM // 2, 1), pltpu.roll(w, HEAD_DIM // 2, 1))

    def stacked(w):
        nothing = jnp.zeros_like(w)
        return jnp.concatenate([jnp.where(low_head, w, nothing), jnp.where(low_head, nothing, w)], axis=0)

    def unstacked(w):
        return jnp.where(low_head, w[:T], w[T:])

    barrier = pltpu.get_barrier_semaphore()
    for k in range(1, S):
        pl.semaphore_signal(barrier, inc=1, device_id=(ps(k), z), device_id_type=MESH)
    for k in range(1, Z):
        pl.semaphore_signal(barrier, inc=1, device_id=(s, pz(k)), device_id_type=MESH)
    x_ref, ct_ref = r.v_x, r.v_ct
    x_load = local(r.x, x_ref)
    wo_load = local(r.wo.at[:, block_of(s, C)], r.st_wo)
    proj_loads = [local(r.proj.at[:, block_of(i * (D // C) + s, C)], r.st_proj.at[:, pl.ds(i * C, C)])
                  for i in range(3)]
    raw = ((r.b_projection, r.v_projection, first_row.projection_bias), (r.b_output, r.v_output, first_row.output_bias),
           (r.gain1, r.v_gain1, first_row.first_gain), (r.shift1, r.v_shift1, first_row.first_shift),
           (r.b_up, r.v_up, first_row.up_bias), (r.b_down, r.v_down, first_row.down_bias),
           (r.gain2, r.v_gain2, first_row.second_gain), (r.shift2, r.v_shift2, first_row.second_shift))
    raw_loads = [local(source, ref) for source, ref, _ in raw]
    seg_load = local(r.seg, r.v_seg)
    up_loads = [local(r.up.at[:, block_of(i * (D // C) + s, C)], r.st_up.at[:, pl.ds(i * C, C)])
                for i in range(Z)]
    dn_load = local(r.dn.at[block_of(s, UZ), :], r.st_dn)
    late_loads = [local(r.cos, r.v_cos), local(r.sin, r.v_sin), local(r.ct, ct_ref)]
    cos_ref, sin_ref = r.v_cos, r.v_sin

    x_all, w_qkv, w_o, w_up, w_dn = r.x_all, r.w_qkv, r.w_o, r.w_up, r.w_dn
    gather_x = Gather(lambda o: x_all.at[block_of(o, T)])
    spread_qkv = Spread(lambda p: w_qkv.at[block_of(p, KW)])
    spread_o = Spread(lambda p: w_o.at[block_of(p, KW), block_of(s, C)])
    spread_up = Spread(lambda p: w_up.at[block_of(p, KW)])
    spread_dn = Spread(lambda p: w_dn.at[block_of(p, UZ)])
    gather_o = Gather(lambda o: w_o.at[:, block_of(o, C)])
    wo_load.wait()
    w_o[block_of(z, KW), block_of(s, C)] = r.st_wo[...].astype(bf16)
    for copy in proj_loads:
        copy.wait()
    w_qkv[block_of(z, KW), :] = r.st_proj[...].astype(bf16)
    x_load.wait()
    pl.semaphore_wait(barrier, S + Z - 2)
    spread_o.start(2, 3, 1)
    spread_qkv.start()
    gather_x.start(x_ref)

    small, small_all, seg_c, seg_r = r.small, r.small_all, r.seg_c, r.seg_r
    for copy, (_, ref, start) in zip(raw_loads, raw):
        copy.wait()
        if ref.shape[1] == C:
            small[start:start + ref.shape[0], :] = ref[...].astype(bf16).astype(f32)
        else:
            for i in range(ref.shape[1] // C):
                small[start + i:start + i + 1, :] = ref[0:1, i * C:(i + 1) * C].astype(bf16).astype(f32)
    x_all[block_of(s, T), :] = x_ref[...]
    vecg[...] = jnp.zeros((8, D), f32)
    seg_load.wait()
    seg_r[...] = jnp.broadcast_to(r.v_seg[...].astype(f32), (8, L))

    def seg_turn(i):
        here = pl.ds(at(i, T), T)
        seg_c[here, :] = jnp.transpose(jnp.broadcast_to(seg_r[0:1, here], (T, T)))
    loop(L // T, seg_turn)
    for copy in up_loads:
        copy.wait()
    w_up[block_of(z, KW), :] = r.st_up[...].astype(bf16)
    dn_load.wait()
    w_dn[block_of(z, UZ), :] = r.st_dn[...].astype(bf16)
    share_small = Share(3, small)
    small_all[z] = small[...]

    gather_x.pass_near()
    spread_o.wait_all()
    gather_o.start()
    gather_x.pass_far()
    gather_x.wait()
    spread_qkv.pass_on()
    share_small.column(small, small_all.at[z])
    spread_up.start()
    x_t = r.x_t
    turn(x_all, x_t)
    for copy in late_loads:
        copy.wait()
    gather_o.pass_near()
    spread_qkv.wait()
    share_small.wait()
    for p in range(Z):
        for start, i in wide:
            for half in range(KW // C):
                at_row = start + half
                lane = (p * (KW // C) + half) * C
                vec[i:i + 1, lane:lane + C] = small_all[p, at_row:at_row + 1, :]
        vec[7:8, p * C:(p + 1) * C] = small_all[p, pl.ds(first_row.up_bias + s, 1), :]
    per = 3 * D // (C * Z)
    for t in range(3):
        number = t * (D // C) + s
        vec[6:7, t * C:(t + 1) * C] = small_all[number // per, pl.ds(first_row.projection_bias + number % per, 1), :]

    q_ref, k_ref, v_ref = r.q, r.k, r.v
    scale = HEAD_DIM ** -0.5

    def project(i):
        here = pl.ds(at(i, T2), T2)
        out = mm(x_all[here, :], w_qkv[...]) + row(PROJECTION_BIAS, 3 * C)
        cosine, sine = cos_ref[here, :], sin_ref[here, :]
        q0, k0 = out[:, :C], out[:, C:2 * C]
        q_ref[here, :] = ((q0 * cosine + swapped(q0) * sine).astype(bf16).astype(f32) * scale).astype(bf16)
        k_ref[here, :] = (k0 * cosine + swapped(k0) * sine).astype(bf16)
        v_ref[here, :] = out[:, 2 * C:].astype(bf16)
    loop(L // T2, project)
    gather_o.pass_far()

    lse, c_f, c_heads, c_tok = r.lse, r.c_f, r.c_heads, r.c_tok
    R = 16

    def same_document(here):
        return jnp.tile(seg_c[here, :], (1, L // C)) == seg_r[0:1, :]

    def both(w):
        return jnp.concatenate([w, w], axis=0)

    def attend(o):
        here = block_of(o, T)
        score = jnp.where(both(same_document(here)), mm(stacked(q_ref[here, :]), k_ref[...], NT), MASKED)
        top = jnp.max(score, axis=-1, keepdims=True)
        power = jnp.exp(score - top)
        total = jnp.sum(power, axis=-1, keepdims=True)
        context = unstacked(mm(power.astype(bf16), v_ref[...]) * (1.0 / total))
        c_f[here, :] = context
        c_heads[here, :] = context.astype(bf16)
        logs = jnp.broadcast_to(top + jnp.log(total), (T2, C))
        for h in range(2):
            lse[h:h + 1, here] = jnp.transpose(logs[h * T:(h + 1) * T, :])[0:1, :]

    share_c = Share(7, c_heads.at[pl.ds(0, T)])

    def attend_and_send(i):
        k = 7 - i
        attend(ps(k))

        @pl.when(k > 0)
        def _():
            share_c.batch.send(c_heads.at[block_of(ps(k), T)], c_tok.at[:, block_of(s, C)], share_c.slot, (ps(k), z))
    loop(8, attend_and_send)
    spread_up.pass_on()
    spread_dn.start()
    c_tok[:, block_of(s, C)] = c_heads[block_of(s, T), :]
    gather_o.wait()
    share_c.wait()

    a_buf = r.a_buf
    a_buf[...] = mm(c_tok[...], w_o[...])
    n1, y1, r1, y_all = r.n1, r.y1, r.r1, r.y_all

    def norm(h):
        centre = h - jnp.mean(h, axis=-1, keepdims=True)
        root = lax.rsqrt(jnp.mean(centre * centre, axis=-1, keepdims=True) + norm_epsilon)
        return centre * root, root

    def first_norm(i):
        rows = pl.ds(at(i, R), R)
        normal, root = norm(x_ref[rows, :].astype(f32) + a_buf[rows, :] + row(OUTPUT_BIAS))
        out = normal * row(FIRST_GAIN) + row(FIRST_SHIFT)
        n1[rows, :] = normal
        r1[rows, :] = jnp.broadcast_to(root, (R, C))
        y1[rows, :] = out
        y_all[pl.ds(pl.multiple_of(s * T + i * R, R), R), :] = out.astype(bf16)
    loop(T // R, first_norm, 4)
    gather_y = Gather(lambda o: y_all.at[block_of(o, T)], False)
    gather_y.start()
    c_all = r.c_all
    gather_c = Gather(lambda o: c_all.at[block_of(o, T)])
    c_all[block_of(s, T), :] = c_tok[...]

    u_buf, g_ref, d_ref, du_ref, dz_all = r.u_buf, r.g, r.d, r.du, r.dz_all
    parts, mid = r.parts, r.mid
    spread_up.wait()
    E = 32

    def lift(j):
        q = chip_of(j)
        u_buf[...] = mm(y_all[block_of(q, T2), :], w_up[...])

        def chunk(i):
            rows = pl.ds(at(i, E), E)
            there = pl.ds(pl.multiple_of(q * T2 + i * E, E), E)
            u = u_buf[rows, :] + row(UP_BIAS, F)
            share = 0.5 + 0.5 * lax.erf(u * (0.5 ** 0.5))
            g_ref[there, :] = (u * share).astype(bf16)
            d_ref[there, :] = share + u * (jnp.exp(-0.5 * u * u) * 0.3989422804014327)
        loop(T2 // E, chunk)

    def lower(j):
        parts[j] = mm(g_ref[block_of(chip_of(j), T2), :], w_dn[...]).astype(bf16)

    H = T // 2
    folds_z = [Scatter(parts, r.low0, mid, r.high0, i * H, H) for i in range(2)]
    y_t, g_t = r.y_t, r.g_t
    gather_y.wait(1)
    lift(0)
    gather_y.pass_near()
    gather_y.wait(3)
    lift(1)
    gather_y.wait(5)
    lift(2)
    spread_dn.pass_on()
    gather_y.pass_far()
    gather_c.start(c_tok)
    gather_y.wait(7)
    lift(3)
    turn(y_all, y_t)
    turn(g_ref, g_t)
    spread_dn.wait()
    for j in (3, 1, 2):
        lower(j)
        for fold in folds_z:
            fold.pair(j)
    for j in (3, 1, 2):
        folds_z[0].onward(j)
    folds_z[1].onward(3)
    lower(0)
    for fold in folds_z:
        fold.pair(0)
    folds_z[0].cross()
    folds_z[1].onward(1)
    folds_z[1].onward(2)
    folds_z[1].cross()
    folds_z[0].ready()

    dh2, out_ref = r.dh2, r.out

    def add_row(i, value):
        vecg[i:i + 1, :] = vecg[i:i + 1, :] + jnp.sum(value, axis=0, keepdims=True)

    def norm_back(incoming, normal, root, gain):
        scaled = incoming * gain
        return root * (scaled - jnp.mean(scaled, axis=-1, keepdims=True)
                       - normal * jnp.mean(scaled * normal, axis=-1, keepdims=True))

    def second_norm(i):
        start = at(i, R)
        rows = pl.ds(start, R)
        normal, root = norm(y1[rows, :] + folds_z[0].rows(start, R) + row(DOWN_BIAS))
        out_ref[rows, :] = (normal * row(SECOND_GAIN) + row(SECOND_SHIFT)).astype(bf16)
        e = ct_ref[rows, :].astype(f32)
        grad = norm_back(e, normal, root, row(SECOND_GAIN))
        dh2[rows, :] = grad
        dz = grad.astype(bf16)
        dz_all[pl.ds(pl.multiple_of(s * T + i * R, R), R), :] = dz
        add_row(3, dz.astype(f32))
        add_row(4, e * normal)
        add_row(5, e)
    gathers_dz = [Gather(lambda o, i=i: dz_all.at[block_of(2 * o + i, H)], False) for i in range(2)]
    loop(H // R, second_norm, 2)
    gathers_dz[0].start()
    folds_z[1].ready()
    loop(H // R, lambda i: second_norm(i + H // R), 2)
    gathers_dz[1].start()
    for fold in folds_z:
        fold.batch.close()

    colg = r.colg
    colg[...] = jnp.zeros((8, F), f32)

    def unlower(j):
        q = chip_of(j)
        u_buf[...] = mm(dz_all[block_of(q, T2), :], w_dn[...], NT)

        def chunk(i):
            rows = pl.ds(at(i, E), E)
            there = pl.ds(pl.multiple_of(q * T2 + i * E, E), E)
            du = (u_buf[rows, :] * d_ref[there, :]).astype(bf16)
            du_ref[there, :] = du
            colg[0:1, :] = colg[0:1, :] + jnp.sum(du.astype(f32), axis=0, keepdims=True)
        loop(T2 // E, chunk)

    def unlift(j):
        parts[j] = mm(du_ref[block_of(chip_of(j), T2), :], w_up[...], NT).astype(bf16)

    fold_y = Scatter(parts, r.low1, mid, r.high1)
    gd_part, gu_part = r.gd_part, r.gu_part
    folds_dn = [Fold(gd_part, r.gd_land, r.gd_pass, i * (UZ // 2), UZ // 2) for i in range(2)]
    folds_up = [Fold(gu_part, r.gu_land, r.gu_pass, i * (KW // 2), KW // 2) for i in range(2)]

    def down_grad(k):
        gd_part[pz(k)] = mm(g_t[block_of(pz(k), UZ), :], dz_all[...]).astype(bf16)

    def up_grad(k):
        gu_part[pz(k)] = mm(y_t[block_of(pz(k), KW), :], du_ref[...]).astype(bf16)

    def dz_wait(k):
        for gather in gathers_dz:
            gather.wait(k)
    dz_wait(1)
    unlower(0)
    unlift(0)
    fold_y.pair(0)
    gathers_dz[0].pass_near()
    gathers_dz[1].pass_near()
    dz_wait(3)
    unlower(1)
    unlift(1)
    fold_y.pair(1)
    gathers_dz[0].pass_far()
    dz_wait(5)
    unlower(2)
    fold_y.onward(1)
    unlift(2)
    fold_y.pair(2)
    gathers_dz[1].pass_far()
    fold_y.onward(2)
    dz_wait(7)
    down_grad(3)
    down_grad(1)
    folds_dn[0].start()
    folds_dn[1].start()
    unlower(3)
    unlift(3)
    fold_y.pair(3)
    up_grad(3)
    fold_y.onward(3)

    up_grad(1)
    down_grad(2)
    fold_y.cross()
    folds_dn[0].middle()
    folds_up[0].start()
    down_grad(0)
    up_grad(2)
    up_grad(0)
    fold_y.ready()

    dh1, da = r.dh1, r.da

    def first_back(i):
        start = at(i, R)
        rows = pl.ds(start, R)
        incoming = dh2[rows, :] + fold_y.rows(start, R)
        normal = n1[rows, :]
        grad = norm_back(incoming, normal, r1[rows, 0:1], row(FIRST_GAIN))
        dh1[rows, :] = grad
        low = grad.astype(bf16)
        da[rows, :] = low
        add_row(0, low.astype(f32))
        add_row(1, incoming * normal)
        add_row(2, incoming)
    loop(T // R, first_back, 2)
    fold_y.batch.close()

    dc_tok, dc = r.dc_tok, r.dc
    dc_tok[...] = mm(da[...], w_o[...], NT).astype(bf16)
    share_dc = Share(7, dc.at[pl.ds(0, T)])
    share_dc.plane(lambda o: dc_tok.at[:, block_of(o, C)], dc.at[block_of(s, T)])
    dc[block_of(s, T), :] = dc_tok[:, block_of(s, C)]
    da_cols = r.da_cols
    share_da = Share(7, da_cols.at[pl.ds(0, T)])
    share_da.plane(lambda o: da.at[:, block_of(o, C)], da_cols.at[block_of(s, T)])
    da_cols[block_of(s, T), :] = da[:, block_of(s, C)]
    vec_z, vec_all = r.vec_z, r.vec_all
    share_vec = Share(3, vec_z.at[0])
    for k in (2, 3, 1):
        share_vec.batch.send(vecg.at[:, block_of(pz(k), KW)], vec_z.at[z], share_vec.slot, (s, pz(k)))
    vec_z[z] = vecg[:, block_of(z, KW)]
    folds_dn[1].middle()
    folds_up[1].start()
    share_dc.wait()

    delta, dq, dproj = r.delta, r.dq, r.dproj

    def deltas(i):
        here = pl.ds(at(i, T), T)
        turned = jnp.transpose(dc[here, :].astype(f32) * c_f[here, :])
        delta[0:1, here] = jnp.sum(turned[:HEAD_DIM], axis=0, keepdims=True)
        delta[1:2, here] = jnp.sum(turned[HEAD_DIM:], axis=0, keepdims=True)
        dq[here, :] = jnp.zeros((T, C), f32)
    loop(L // T, deltas)

    def attend_back(i):
        here = pl.ds(at(i, T), T)
        same = same_document(here)
        k_here, v_here = k_ref[here, :], v_ref[here, :]
        keys, values, slopes = [], [], []
        for h in range(2):
            own = low_head if h == 0 else jnp.logical_not(low_head)
            nothing = jnp.zeros_like(k_here)
            key = jnp.where(own, k_here, nothing)
            weight = jnp.exp(jnp.where(same, mm(key, q_ref[...], NT), MASKED) - lse[h:h + 1, :])
            slope = mm(jnp.where(own, v_here, nothing), dc[...], NT) - delta[h:h + 1, :]
            slopes.append((weight * slope).astype(bf16))
            values.append(mm(weight.astype(bf16), dc[...]))
            keys.append(key)
        dv = jnp.where(low_head, values[0], values[1]).astype(bf16)
        dk = jnp.where(low_head, mm(slopes[0], q_ref[...]), mm(slopes[1], q_ref[...])).astype(bf16).astype(f32)
        dproj[here, 2 * C:] = dv
        dproj[here, C:2 * C] = (dk * cos_ref[here, :] - swapped(dk) * sin_ref[here, :]).astype(bf16)
        dq[...] = dq[...] + mm(jnp.concatenate(slopes, axis=0), jnp.concatenate(keys, axis=0), TN)

    gd_all, gu_all, go_all, gqk_all, gv_all = r.gd, r.gu, r.go, r.gqk, r.gv
    gather_gd = Gather(lambda o: gd_all.at[block_of(o, UZ)])
    gather_gu = Gather(lambda o: gu_all.at[o])
    gather_go = Gather(lambda o: go_all.at[:, block_of(o, C)])
    gather_gqk = Gather(lambda o: gqk_all.at[o])
    gather_gv = Gather(lambda o: gv_all.at[o])
    go_part = r.go_part
    fold_o = Fold(go_part, r.go_land, r.go_pass)

    def out_grad(k):
        go_part[pz(k)] = mm(c_all[:, block_of(pz(k), KW)], da_cols[...], TN).astype(bf16)

    def attend_back_and_fold(i):
        attend_back(i)

        @pl.when(i == 0)
        def _():
            gather_c.pass_near()

        @pl.when(i == 5)
        def _():
            for part in range(2):
                at_row = pl.multiple_of(s * UZ + part * (UZ // 2), UZ // 2)
                gd_all[pl.ds(at_row, UZ // 2), :] = folds_dn[part].finish()
            gather_gd.start()

        @pl.when(i == 6)
        def _():
            folds_up[0].middle()
            gather_c.pass_far()
    loop(L // T, attend_back_and_fold)


    def dq_rows(i):
        here = pl.ds(at(i, T), T)
        whole = (dq[here, :] * scale).astype(bf16).astype(f32)
        dproj[here, :C] = (whole * cos_ref[here, :] - swapped(whole) * sin_ref[here, :]).astype(bf16)
        colg[1:2, :3 * C] = colg[1:2, :3 * C] + jnp.sum(dproj[here, :].astype(f32), axis=0, keepdims=True)
    loop(L // T, dq_rows)

    gqk_part, gv_part = r.gqk_part, r.gv_part
    fold_qk = Fold(gqk_part, r.gqk_land, r.gqk_pass)
    fold_v = Fold(gv_part, r.gv_land, r.gv_pass)

    def projection_grad(k):
        grad = mm(x_t[block_of(pz(k), KW), :], dproj[...]).astype(bf16)
        gqk_part[pz(k)] = grad[:, :2 * C]
        gv_part[pz(k)] = grad[:, 2 * C:]
    projection_grad(3)
    projection_grad(1)
    fold_x = Scatter(parts, r.low2, mid, r.high2)

    def unproject(j):
        parts[j] = mm(dproj[block_of(chip_of(j), T2), :], w_qkv[...], NT).astype(bf16)
        fold_x.pair(j)
    fold_qk.start()
    unproject(3)
    unproject(1)
    fold_x.onward(3)
    folds_up[1].middle()
    fold_v.start()
    unproject(2)
    fold_x.onward(1)
    unproject(0)
    fold_x.onward(2)
    gather_c.wait()
    share_da.wait()
    for k in (3, 1):
        out_grad(k)
    fold_o.start()
    for k in (2, 0):
        out_grad(k)
    projection_grad(2)
    projection_grad(0)
    fold_x.cross()
    gather_gd.pass_near()
    col_z, col_own = r.col_z, r.col_own
    col_own[...] = jnp.zeros((8, C), f32)
    for i in range(Z):
        col_own[i:i + 1, :] = colg[0:1, i * C:(i + 1) * C]
    for i in range(3):
        col_own[Z + i:Z + i + 1, :] = colg[1:2, i * C:(i + 1) * C]
    share_col = Share(3, col_own)
    share_col.column(col_own, col_z.at[z])
    col_z[z] = col_own[...]
    share_vec.wait()
    vec_sum = r.vec_sum
    vec_sum[...] = vec_z[0] + vec_z[1] + vec_z[2] + vec_z[3]
    share_sum = Share(7, vec_sum)
    share_sum.plane(lambda o: vec_sum, vec_all.at[s])
    vec_all[s] = vec_sum[...]
    for i in range(2):
        gu_all[s, pl.ds(i * (KW // 2), KW // 2), :] = folds_up[i].finish()
    gather_gu.start()
    fold_qk.middle()
    inner = flip(zlow, zhigh) == 1

    @pl.when(inner)
    def _():
        fold_v.middle()
        fold_o.middle()
    gather_gd.pass_far()
    fold_x.ready()
    dx_ref = r.dx

    def input_back(i):
        start = at(i, R)
        rows = pl.ds(start, R)
        dx_ref[rows, :] = (dh1[rows, :] + fold_x.rows(start, R)).astype(bf16)
    loop(T // R, input_back, 2)
    gather_gd.wait()
    gather_gu.pass_near()

    @pl.when(jnp.logical_not(inner))
    def _():
        fold_v.middle()
    gqk_all[s] = fold_qk.finish()
    gather_gqk.start()

    @pl.when(jnp.logical_not(inner))
    def _():
        fold_o.middle()
    gv_all[s] = fold_v.finish()
    gather_gv.start()
    gather_gu.pass_far()
    go_all[:, block_of(s, C)] = fold_o.finish()
    gather_go.start()
    share_col.wait()
    col_all, col_sum = r.col_all, r.col_sum
    col_sum[...] = col_z[0] + col_z[1] + col_z[2] + col_z[3]
    share_cols = Share(7, col_sum)
    share_cols.plane(lambda o: col_sum, col_all.at[s])
    col_all[s] = col_sum[...]
    gather_gqk.pass_near()
    gather_gv.pass_near()
    gather_gu.wait()

    gather_go.pass_near()
    gather_gqk.pass_far()
    gather_gv.pass_far()
    share_sum.wait()
    share_cols.wait()
    total = vec_all[0]
    for o in range(1, S):
        total = total + vec_all[o]
    gsm = r.gsm
    gsm[...] = jnp.zeros(gsm.shape, f32)
    for start, i in wide:
        for half in range(KW // C):
            gsm[start + half:start + half + 1, :] = total[i:i + 1, half * C:(half + 1) * C]
    for o in range(S):
        at_row = first_row.up_bias + o
        gsm[at_row:at_row + 1, :] = col_all[o, pl.ds(z, 1), :]
    for i in range(per):
        number = z * per + i
        at_row = first_row.projection_bias + i
        gsm[at_row:at_row + 1, :] = col_all[number % S, pl.ds(Z + number // S, 1), :]
    gather_go.pass_far()
    gather_go.wait()
    gather_gqk.wait()
    gather_gv.wait()
    for batch in closing:
        batch.close()
    assert counter[0] <= LANDINGS and counter[1] <= BATCHES and counter[2] <= LOCAL, counter


def fused_shards(*args):
    (hidden_in, cotangent, segment_ids, projection, projection_bias, output_weight, output_bias, first_gain,
     first_shift, up_weight, up_bias, down_weight, down_bias, second_gain, second_shift) = args
    T, D = hidden_in.shape[1:]
    L = segment_ids.shape[1]
    KW = projection.shape[0]
    F = up_weight.shape[1] // 8
    C, Z = 128, 4
    UZ = F // Z
    small = dict(projection_bias=projection_bias, output_bias=output_bias, first_gain=first_gain,
                 first_shift=first_shift, up_bias=up_bias, down_bias=down_bias, second_gain=second_gain,
                 second_shift=second_shift)
    starts, at_row = {}, 0
    for name, value in small.items():
        starts[name] = at_row
        at_row += value.shape[0] // C
    rows = -(-at_row // 8) * 8
    half = HEAD_DIM // 2
    inverse = np.float32(10000.0) ** (np.float32(-2.0) * np.arange(half, dtype=np.float32) / np.float32(HEAD_DIM))
    angles = np.arange(L, dtype=np.float32)[:, None] * inverse.astype(np.float32)[None, :]
    cosine = np.tile(np.cos(angles), (1, C // half))
    sine = np.tile(np.concatenate([-np.sin(angles), np.sin(angles)], axis=1), (1, C // HEAD_DIM))

    inputs = dict(x=hidden_in[0], ct=cotangent[0], seg=segment_ids, cos=jnp.asarray(cosine), sin=jnp.asarray(sine),
                  b_projection=projection_bias.reshape(-1, C), b_output=output_bias[None], gain1=first_gain[None],
                  shift1=first_shift[None], b_up=up_bias[None], b_down=down_bias[None], gain2=second_gain[None],
                  shift2=second_shift[None], proj=projection, wo=output_weight, up=up_weight, dn=down_weight)
    outputs = dict(out=((T, D), bf16), dx=((T, D), bf16), gsm=((rows, C), f32), gqk=((8, KW, 2 * C), bf16), gv=((8, KW, C), bf16),
                   go=((KW, D), bf16), gu=((8, KW, F), bf16), gd=((8 * UZ, D), bf16))
    landed = dict(v_x=inputs["x"], v_ct=inputs["ct"], v_seg=segment_ids, v_cos=inputs["cos"], v_sin=inputs["sin"],
                  v_projection=inputs["b_projection"], v_output=inputs["b_output"], v_gain1=inputs["gain1"],
                  v_shift1=inputs["shift1"], v_up=inputs["b_up"], v_down=inputs["b_down"], v_gain2=inputs["gain2"],
                  v_shift2=inputs["shift2"])
    PART = (4, T, D)
    scratch = {name: (value.shape, value.dtype) for name, value in landed.items()}
    scratch.update(
        x_all=((L, D), bf16), x_t=((D, L), bf16), w_qkv=((D, 3 * C), bf16), st_proj=((KW, 3 * C), f32),
        w_o=((D, D), bf16), st_wo=((KW, C), f32), w_up=((D, F), bf16), st_up=((KW, F), f32),
        w_dn=((F, D), bf16), st_dn=((UZ, D), f32), small_all=((Z, rows, C), f32), vec=((8, D), f32),
        vecg=((8, D), f32), q=((L, C), bf16), k=((L, C), bf16), v=((L, C), bf16),
        seg_r=((8, L), f32), seg_c=((L, C), f32), small=((rows, C), f32), lse=((8, L), f32),
        delta=((8, L), f32), c_f=((L, C), f32), c_heads=((L, C), bf16), c_tok=((T, D), bf16),
        a_buf=((T, D), f32), n1=((T, D), f32), y1=((T, D), f32), r1=((T, C), f32),
        y_all=((L, D), bf16), y_t=((D, L), bf16), u_buf=((2 * T, F), f32), g=((L, F), bf16),
        g_t=((F, L), bf16), d=((L, F), f32), du=((L, F), bf16), dz_all=((L, D), bf16),
        parts=((4, 2 * T, D), bf16), mid=((4, T, D), bf16), dh2=((T, D), f32), dh1=((T, D), f32),
        colg=((8, F), f32), gd_part=((Z, UZ, D), bf16), gd_land=((3, UZ, D), bf16), gd_pass=((UZ, D), bf16),
        gu_part=((Z, KW, F), bf16), gu_land=((3, KW, F), bf16), gu_pass=((KW, F), bf16),
        go_part=((Z, KW, C), bf16), go_land=((3, KW, C), bf16), go_pass=((KW, C), bf16),
        gqk_part=((Z, KW, 2 * C), bf16), gqk_land=((3, KW, 2 * C), bf16), gqk_pass=((KW, 2 * C), bf16),
        gv_part=((Z, KW, C), bf16), gv_land=((3, KW, C), bf16), gv_pass=((KW, C), bf16),
        da=((T, D), bf16), dc_tok=((T, D), bf16), dc=((L, C), bf16),
        da_cols=((L, C), bf16), c_all=((L, D), bf16), dq=((L, C), f32), dproj=((L, 3 * C), bf16),
        vec_all=((8, 8, KW), f32), vec_z=((Z, 8, KW), f32), vec_sum=((8, KW), f32), col_own=((8, C), f32),
        col_z=((Z, 8, C), f32), col_sum=((8, C), f32), col_all=((8, 8, C), f32),
        low0=(PART, bf16), high0=(PART, bf16), low1=(PART, bf16), high1=(PART, bf16), low2=(PART, bf16),
        high2=(PART, bf16), ssem=(BATCHES,), rsem=(LANDINGS,), lsem=(LOCAL,))
    names = [*inputs, *outputs, *scratch]
    sizes = SimpleNamespace(names=names, T=T, D=D, L=L, F=F, first_row=SimpleNamespace(**starts))

    anywhere, near = pl.BlockSpec(memory_space=pl.ANY), pl.BlockSpec(memory_space=pltpu.VMEM)
    results = pl.pallas_call(
        partial(fused_layer, sizes),
        out_shape=[pltpu.VMEM(*what) for what in outputs.values()],
        in_specs=[anywhere] * len(inputs),
        out_specs=[near] * len(outputs),
        scratch_shapes=[pltpu.VMEM(*what) if len(what) == 2 else pltpu.SemaphoreType.DMA(what)
                        for what in scratch.values()],
        compiler_params=pltpu.CompilerParams(collective_id=0, has_side_effects=True, vmem_limit_bytes=57 << 20),
        name="fused_layer",
    )(*inputs.values())
    out, dx, gsm, gqk, gv, go, gu, gd = results
    wide = [jax.ShapeDtypeStruct(value.shape, f32) for value in (projection, output_weight, up_weight, down_weight)]
    narrow = [jax.ShapeDtypeStruct((1, value.shape[0]) if value is not projection_bias else (value.shape[0] // C, C), f32)
              for value in small.values()]
    sources = [out, dx, gqk, gv, go, gu, gd, gsm]
    outcomes = [out, dx] + wide + narrow
    results = pl.pallas_call(
        partial(widen, tuple(starts.values())),
        out_shape=[jax.ShapeDtypeStruct(value.shape, value.dtype) for value in outcomes],
        in_specs=[near] * len(sources),
        out_specs=[anywhere] * len(outcomes),
        scratch_shapes=[pltpu.VMEM(value.shape, value.dtype) for value in outcomes[2:]]
        + [pltpu.SemaphoreType.DMA((LOCAL,))],
        compiler_params=pltpu.CompilerParams(vmem_limit_bytes=20 << 20),
        name="widen",
    )(*sources)
    out, dx, gq, go, gu, gd = results[:6]
    pb, ob, g1, s1, ub, db, g2, s2 = [value.reshape(-1) for value in results[6:]]
    return (out[None], dx[None], gq, pb, go, ob, g1, s1, gu, ub, gd, db, g2, s2)


def widen(starts, *refs):
    held, results, made, outsem = refs[:8], refs[8:22], refs[22:34], refs[34]
    out, dx, gqk, gv, go, gu, gd, gsm = held
    C = gsm.shape[1]
    stores = []

    def store(ref, result):
        copy = pltpu.make_async_copy(ref, result, outsem.at[len(stores)])
        copy.start()
        stores.append(copy)

    def grouped(i, target, at, n, first):
        source, result = held[i], made[target]
        groups = source.shape[0]

        def step(j, carry):
            rows = pl.ds(pl.multiple_of(at + j * 32, 32), 32)
            for o in range(groups):
                for p in range(source.shape[2] // C):
                    lane = ((first + p) * groups + o) * C
                    result[rows, lane:lane + C] = source[o, rows, p * C:(p + 1) * C].astype(f32)
            return carry
        lax.fori_loop(0, n // 32, step, 0)

    def plain(i, target, at, n, _):
        source, result = held[i], made[target]

        def step(j, carry):
            rows = pl.ds(pl.multiple_of(at + j * 32, 32), 32)
            result[rows, :] = source[rows, :].astype(f32)
            return carry
        lax.fori_loop(0, n // 32, step, 0)

    store(out, results[0])
    store(dx, results[1])
    work = []
    for i, target, n, body, first in ((5, 2, 64, grouped, 0), (6, 3, 256, plain, 0), (2, 0, 64, grouped, 0),
                                      (3, 0, 64, grouped, 2), (4, 1, 256, plain, 0)):
        total = held[i].shape[-2]
        for at in range(0, total, n):
            work.append((i, target, at, n, body, first))
    for i, target, at, n, body, first in work:
        body(i, target, at, n, first)
        if i != 2:
            rows = pl.ds(at, n)
            store(made[target].at[rows], results[2 + target].at[rows])
    for start, ref, result in zip(starts, made[4:], results[6:]):
        if ref.shape[1] == C:
            ref[...] = gsm[start:start + ref.shape[0], :]
        else:
            for i in range(ref.shape[1] // C):
                ref[0:1, i * C:(i + 1) * C] = gsm[start + i:start + i + 1, :]
        store(ref, result)
    for copy in stores:
        copy.wait()


BATCHES = 34
LANDINGS = 155
LOCAL = 26


def fits(mesh):
    return mesh.shape["seq"] == 8 and mesh.shape["fsdp"] == 4


def solution(mesh):
    return jax.shard_map(
        fused_shards if fits(mesh) else shards,
        mesh=mesh,
        in_specs=(
            P("fsdp", "seq", None),
            P("fsdp", "seq", None),
            P("fsdp", None),
            P("fsdp", None),
            P("fsdp"),
            P("fsdp", None),
            P("fsdp"),
            P("fsdp"),
            P("fsdp"),
            P("fsdp", None),
            P("fsdp"),
            P("fsdp", None),
            P("fsdp"),
            P("fsdp"),
            P("fsdp"),
        ),
        out_specs=(
            P("fsdp", "seq", None),
            P("fsdp", "seq", None),
            P("fsdp", None),
            P("fsdp"),
            P("fsdp", None),
            P("fsdp"),
            P("fsdp"),
            P("fsdp"),
            P("fsdp", None),
            P("fsdp"),
            P("fsdp", None),
            P("fsdp"),
            P("fsdp"),
            P("fsdp"),
        ),
        check_vma=False,
    )
```

```python
from functools import partial

import jax
import jax.numpy as jnp
import numpy as np
import math
from types import SimpleNamespace
from jax import lax
from jax.experimental import pallas as pl
from jax.experimental.pallas import tpu as pltpu
from jax.sharding import PartitionSpec as P

HEADS = 16
HEAD_DIM = 64


norm_epsilon = 1e-05


def rotary(values, positions):
    half = values.shape[-1] // 2
    channel = jnp.arange(half).astype(jnp.float32)
    inverse = 10000.0 ** (-2.0 * channel / values.shape[-1])
    angles = positions[:, None] * inverse[None, :]
    cosine = jnp.cos(angles)[:, None, :]
    sine = jnp.sin(angles)[:, None, :]
    first = values[..., :half]
    second = values[..., half:]
    return jnp.concatenate(
        [first * cosine - second * sine, second * cosine + first * sine], axis=-1
    )


def rotary_back(grads, positions):
    unused, pullback = jax.vjp(lambda inner: rotary(inner, positions), grads)
    return pullback(grads)[0]


def norm_forward(values, gain, shift):
    centre = values - jnp.mean(values, axis=-1, keepdims=True)
    inverse_root = lax.rsqrt(jnp.mean(centre * centre, axis=-1, keepdims=True) + norm_epsilon)
    normal = centre * inverse_root
    return (normal * gain + shift, normal, inverse_root)


def norm_backward(incoming, normal, inverse_root, gain):
    gain_grad = jnp.sum(incoming * normal, axis=0)
    shift_grad = jnp.sum(incoming, axis=0)
    scaled = incoming * gain
    inner = (
        scaled
        - jnp.mean(scaled, axis=-1, keepdims=True)
        - normal * jnp.mean(scaled * normal, axis=-1, keepdims=True)
    )
    return (inner * inverse_root, gain_grad, shift_grad)


def shards(
    hidden_in,
    cotangent,
    segment_ids,
    projection,
    projection_bias,
    output_weight,
    output_bias,
    first_gain,
    first_shift,
    up_weight,
    up_bias,
    down_weight,
    down_bias,
    second_gain,
    second_shift,
):
    bf16 = jnp.bfloat16
    f32 = jnp.float32
    tokens = hidden_in[0]
    local_rows = tokens.shape[0]
    width = tokens.shape[1]
    seq_rank = lax.axis_index("seq")
    positions = (seq_rank * local_rows + jnp.arange(local_rows)).astype(f32)
    segments = segment_ids[0]
    scale = HEAD_DIM ** (-0.5)
    attention_full = (
        lax.all_gather(projection.astype(bf16), "fsdp", axis=0, tiled=True),
        lax.all_gather(projection_bias.astype(bf16), "fsdp", axis=0, tiled=True),
        lax.all_gather(output_weight.astype(bf16), "fsdp", axis=0, tiled=True),
        lax.all_gather(output_bias.astype(bf16), "fsdp", axis=0, tiled=True),
        lax.all_gather(first_gain.astype(bf16), "fsdp", axis=0, tiled=True),
        lax.all_gather(first_shift.astype(bf16), "fsdp", axis=0, tiled=True),
    )
    proj_weight = attention_full[0]
    projected = jnp.dot(tokens, proj_weight, preferred_element_type=f32) + attention_full[1].astype(
        f32
    )
    heads = projected.reshape(local_rows, 3, HEADS, HEAD_DIM)
    queries = rotary(heads[:, 0], positions)
    keys = rotary(heads[:, 1], positions)
    stacked = jnp.stack([queries, keys, heads[:, 2]]).astype(bf16)
    spread = lax.all_to_all(stacked, "seq", split_axis=2, concat_axis=1, tiled=True)
    query_all = spread[0]
    key_all = spread[1]
    value_all = spread[2]
    length = query_all.shape[0]
    local_heads = query_all.shape[1]
    block = min(512, length)
    count = length // block
    query_blocks = query_all.reshape(count, block, local_heads, HEAD_DIM)
    segment_blocks = segments.reshape(count, block)

    def scores_of(query_block, segment_block):
        raw = jnp.einsum("qhd,khd->hqk", query_block, key_all, preferred_element_type=f32) * scale
        allowed = segment_block[:, None] == segments[None, :]
        return jnp.where(allowed[None], raw, -1e30)

    def forward_block(pieces):
        query_block, segment_block = pieces
        scores = scores_of(query_block, segment_block)
        row_max = jnp.max(scores, axis=-1, keepdims=True)
        exponent = jnp.exp(scores - row_max)
        total = jnp.sum(exponent, axis=-1, keepdims=True)
        weights = exponent / total
        context = jnp.einsum(
            "hqk,khd->qhd", weights.astype(bf16), value_all, preferred_element_type=f32
        )
        return (context.astype(bf16), (row_max + jnp.log(total))[..., 0])

    context_blocks, log_totals = lax.map(forward_block, (query_blocks, segment_blocks))
    context_heads = context_blocks.reshape(length, local_heads, HEAD_DIM)
    context_tokens = lax.all_to_all(
        context_heads, "seq", split_axis=0, concat_axis=1, tiled=True
    ).reshape(local_rows, width)
    attended = jnp.dot(
        context_tokens, attention_full[2], preferred_element_type=f32
    ) + attention_full[3].astype(f32)
    gain_one = attention_full[4].astype(f32)
    normed_one, normal_one, inverse_one = norm_forward(
        tokens.astype(f32) + attended, gain_one, attention_full[5].astype(f32)
    )
    feed_full = (
        lax.all_gather(up_weight.astype(bf16), "fsdp", axis=0, tiled=True),
        lax.all_gather(up_bias.astype(bf16), "fsdp", axis=0, tiled=True),
        lax.all_gather(down_weight.astype(bf16), "fsdp", axis=0, tiled=True),
        lax.all_gather(down_bias.astype(bf16), "fsdp", axis=0, tiled=True),
        lax.all_gather(second_gain.astype(bf16), "fsdp", axis=0, tiled=True),
        lax.all_gather(second_shift.astype(bf16), "fsdp", axis=0, tiled=True),
    )
    normed_low = normed_one.astype(bf16)
    lifted = jnp.dot(normed_low, feed_full[0], preferred_element_type=f32) + feed_full[1].astype(
        f32
    )
    activated = jax.nn.gelu(lifted, approximate=False).astype(bf16)
    lowered = jnp.dot(activated, feed_full[2], preferred_element_type=f32) + feed_full[3].astype(
        f32
    )
    gain_two = feed_full[4].astype(f32)
    layer_out, normal_two, inverse_two = norm_forward(
        normed_one + lowered, gain_two, feed_full[5].astype(f32)
    )
    feed_back = (
        lax.all_gather(up_weight.astype(bf16), "fsdp", axis=0, tiled=True),
        lax.all_gather(up_bias.astype(bf16), "fsdp", axis=0, tiled=True),
        lax.all_gather(down_weight.astype(bf16), "fsdp", axis=0, tiled=True),
        lax.all_gather(down_bias.astype(bf16), "fsdp", axis=0, tiled=True),
        lax.all_gather(second_gain.astype(bf16), "fsdp", axis=0, tiled=True),
        lax.all_gather(second_shift.astype(bf16), "fsdp", axis=0, tiled=True),
    )
    attention_back = (
        lax.all_gather(projection.astype(bf16), "fsdp", axis=0, tiled=True),
        lax.all_gather(projection_bias.astype(bf16), "fsdp", axis=0, tiled=True),
        lax.all_gather(output_weight.astype(bf16), "fsdp", axis=0, tiled=True),
        lax.all_gather(output_bias.astype(bf16), "fsdp", axis=0, tiled=True),
        lax.all_gather(first_gain.astype(bf16), "fsdp", axis=0, tiled=True),
        lax.all_gather(first_shift.astype(bf16), "fsdp", axis=0, tiled=True),
    )
    grad_two, second_gain_grad, second_shift_grad = norm_backward(
        cotangent[0].astype(f32), normal_two, inverse_two, gain_two
    )
    lowered_grad = grad_two.astype(bf16)
    down_weight_grad = jnp.einsum("tf,td->fd", activated, lowered_grad, preferred_element_type=f32)
    down_bias_grad = jnp.sum(lowered_grad.astype(f32), axis=0)
    active_grad = jnp.einsum("td,fd->tf", lowered_grad, feed_back[2], preferred_element_type=f32)
    unused, gelu_pull = jax.vjp(partial(jax.nn.gelu, approximate=False), lifted)
    lifted_grad = gelu_pull(active_grad)[0].astype(bf16)
    up_weight_grad = jnp.einsum("td,tf->df", normed_low, lifted_grad, preferred_element_type=f32)
    up_bias_grad = jnp.sum(lifted_grad.astype(f32), axis=0)
    normed_grad = grad_two + jnp.einsum(
        "tf,df->td", lifted_grad, feed_back[0], preferred_element_type=f32
    )
    grad_one, first_gain_grad, first_shift_grad = norm_backward(
        normed_grad, normal_one, inverse_one, attention_back[4].astype(f32)
    )
    attended_grad = grad_one.astype(bf16)
    output_weight_grad = jnp.einsum(
        "tc,td->cd", context_tokens, attended_grad, preferred_element_type=f32
    )
    output_bias_grad = jnp.sum(attended_grad.astype(f32), axis=0)
    context_grad = jnp.einsum(
        "td,cd->tc", attended_grad, attention_back[2], preferred_element_type=f32
    ).astype(bf16)
    context_grad = context_grad.reshape(local_rows, HEADS, HEAD_DIM)
    context_grad_heads = lax.all_to_all(
        context_grad, "seq", split_axis=1, concat_axis=0, tiled=True
    )
    grad_blocks = context_grad_heads.reshape(count, block, local_heads, HEAD_DIM)

    def backward_block(carry, pieces):
        key_grad, value_grad = carry
        query_block, segment_block, grad_block, log_block = pieces
        scores = scores_of(query_block, segment_block)
        weights = jnp.exp(scores - log_block[..., None])
        value_grad = value_grad + jnp.einsum(
            "hqk,qhd->khd", weights.astype(bf16), grad_block, preferred_element_type=f32
        )
        weight_grad = jnp.einsum("qhd,khd->hqk", grad_block, value_all, preferred_element_type=f32)
        centre = jnp.sum(weights * weight_grad, axis=-1, keepdims=True)
        score_grad = (weights * (weight_grad - centre)).astype(bf16)
        query_grad = (
            jnp.einsum("hqk,khd->qhd", score_grad, key_all, preferred_element_type=f32) * scale
        )
        key_grad = (
            key_grad
            + jnp.einsum("hqk,qhd->khd", score_grad, query_block, preferred_element_type=f32)
            * scale
        )
        return ((key_grad, value_grad), query_grad)

    zeros_heads = jnp.zeros((length, local_heads, HEAD_DIM), f32)
    (key_grad, value_grad), query_grad = lax.scan(
        backward_block,
        (zeros_heads, zeros_heads),
        (query_blocks, segment_blocks, grad_blocks, log_totals),
    )
    query_grad = query_grad.reshape(length, local_heads, HEAD_DIM)
    stacked_grad = jnp.stack([query_grad, key_grad, value_grad]).astype(bf16)
    token_heads = lax.all_to_all(stacked_grad, "seq", split_axis=1, concat_axis=2, tiled=True)
    query_back = rotary_back(token_heads[0].astype(f32), positions)
    key_back = rotary_back(token_heads[1].astype(f32), positions)
    projected_grad = jnp.stack([query_back, key_back, token_heads[2].astype(f32)], axis=1)
    projected_grad = projected_grad.reshape(local_rows, 3 * width).astype(bf16)
    projection_grad = jnp.einsum("td,te->de", tokens, projected_grad, preferred_element_type=f32)
    projection_bias_grad = jnp.sum(projected_grad.astype(f32), axis=0)
    input_grad = grad_one + jnp.einsum(
        "te,de->td", projected_grad, attention_back[0], preferred_element_type=f32
    )
    every_shard = (
        lax.psum_scatter(
            projection_grad.astype(jnp.bfloat16), "fsdp", scatter_dimension=0, tiled=True
        ).astype(jnp.float32),
        lax.psum_scatter(
            projection_bias_grad.astype(jnp.bfloat16), "fsdp", scatter_dimension=0, tiled=True
        ).astype(jnp.float32),
        lax.psum_scatter(
            output_weight_grad.astype(jnp.bfloat16), "fsdp", scatter_dimension=0, tiled=True
        ).astype(jnp.float32),
        lax.psum_scatter(
            output_bias_grad.astype(jnp.bfloat16), "fsdp", scatter_dimension=0, tiled=True
        ).astype(jnp.float32),
        lax.psum_scatter(
            first_gain_grad.astype(jnp.bfloat16), "fsdp", scatter_dimension=0, tiled=True
        ).astype(jnp.float32),
        lax.psum_scatter(
            first_shift_grad.astype(jnp.bfloat16), "fsdp", scatter_dimension=0, tiled=True
        ).astype(jnp.float32),
        lax.psum_scatter(
            up_weight_grad.astype(jnp.bfloat16), "fsdp", scatter_dimension=0, tiled=True
        ).astype(jnp.float32),
        lax.psum_scatter(
            up_bias_grad.astype(jnp.bfloat16), "fsdp", scatter_dimension=0, tiled=True
        ).astype(jnp.float32),
        lax.psum_scatter(
            down_weight_grad.astype(jnp.bfloat16), "fsdp", scatter_dimension=0, tiled=True
        ).astype(jnp.float32),
        lax.psum_scatter(
            down_bias_grad.astype(jnp.bfloat16), "fsdp", scatter_dimension=0, tiled=True
        ).astype(jnp.float32),
        lax.psum_scatter(
            second_gain_grad.astype(jnp.bfloat16), "fsdp", scatter_dimension=0, tiled=True
        ).astype(jnp.float32),
        lax.psum_scatter(
            second_shift_grad.astype(jnp.bfloat16), "fsdp", scatter_dimension=0, tiled=True
        ).astype(jnp.float32),
    )
    finals = (
        lax.psum(every_shard[0].astype(jnp.bfloat16), "seq").astype(jnp.float32),
        lax.psum(every_shard[1].astype(jnp.bfloat16), "seq").astype(jnp.float32),
        lax.psum(every_shard[2].astype(jnp.bfloat16), "seq").astype(jnp.float32),
        lax.psum(every_shard[3].astype(jnp.bfloat16), "seq").astype(jnp.float32),
        lax.psum(every_shard[4].astype(jnp.bfloat16), "seq").astype(jnp.float32),
        lax.psum(every_shard[5].astype(jnp.bfloat16), "seq").astype(jnp.float32),
        lax.psum(every_shard[6].astype(jnp.bfloat16), "seq").astype(jnp.float32),
        lax.psum(every_shard[7].astype(jnp.bfloat16), "seq").astype(jnp.float32),
        lax.psum(every_shard[8].astype(jnp.bfloat16), "seq").astype(jnp.float32),
        lax.psum(every_shard[9].astype(jnp.bfloat16), "seq").astype(jnp.float32),
        lax.psum(every_shard[10].astype(jnp.bfloat16), "seq").astype(jnp.float32),
        lax.psum(every_shard[11].astype(jnp.bfloat16), "seq").astype(jnp.float32),
    )
    return (
        layer_out.astype(bf16)[None],
        input_grad.astype(bf16)[None],
        finals[0],
        finals[1],
        finals[2],
        finals[3],
        finals[4],
        finals[5],
        finals[6],
        finals[7],
        finals[8],
        finals[9],
        finals[10],
        finals[11],
    )


MESH = pl.DeviceIdType.MESH
NN = (((1,), (0,)), ((), ()))
NT = (((1,), (1,)), ((), ()))
TN = (((0,), (0,)), ((), ()))
f32 = jnp.float32
bf16 = jnp.bfloat16
MASKED = -1e30


def mm(left, right, dims=NN):
    return lax.dot_general(left, right, dims, preferred_element_type=f32)


def block_of(index, size):
    return pl.ds(pl.multiple_of(index * size, size), size)


def flip(bit, other):
    return bit + other - 2 * bit * other


def fused_layer(sizes, *refs):
    r = SimpleNamespace(**dict(zip(sizes.names, refs)))
    T, D, L, F = sizes.T, sizes.D, sizes.L, sizes.F
    S, Z = 8, 4
    KW = D // Z
    UZ = F // Z
    C = 128
    T2 = 2 * T
    first_row = sizes.first_row
    ssem, rsem, lsem = r.ssem, r.rsem, r.lsem

    s = lax.axis_index("seq")
    z = lax.axis_index("fsdp")
    core, xbit, ybit = s % 2, (s // 2) % 2, s // 4
    zlow, zhigh = z % 2, z // 2

    def ps(k):
        return flip(core, k % 2) + 2 * flip(xbit, (k // 2) % 2) + 4 * flip(ybit, k // 4)

    def pz(k):
        return flip(zlow, k % 2) + 2 * flip(zhigh, k // 2)

    inner = flip(zlow, zhigh) == 1

    def by_plane(for_inner, for_outer):
        pl.when(inner)(for_inner)
        pl.when(jnp.logical_not(inner))(for_outer)

    def chip_of(j):
        return flip(xbit, j % 2) + 2 * flip(ybit, j // 2)

    counter = [0, 0, 0]
    closing = []

    def take(which, n=1):
        counter[which] += n
        return counter[which] - n

    def landings(n=1):
        return take(0, n)

    def size(ref):
        return math.prod(ref.shape) * jnp.dtype(ref.dtype).itemsize

    def extent(n):
        if n <= size(r.c_f):
            return r.c_f.at[pl.ds(0, n * L // size(r.c_f))]
        return r.y_all.at[pl.ds(0, n * L // size(r.y_all))]

    def arrived(ref, slot):
        pltpu.make_async_copy(ref, ref, rsem.at[slot]).wait()

    class Batch:
        def __init__(self, count, like):
            self.slot, self.bytes, self.open = take(1), count * size(like), True
            self.one, self.shares = size(like), None
            closing.append(self)

        def drain(self, n):
            everything = extent(n)
            pltpu.make_async_copy(everything, everything, ssem.at[self.slot]).wait()

        def send(self, src, dst, slot, dev):
            pltpu.make_async_remote_copy(
                src_ref=src, dst_ref=dst, send_sem=ssem.at[self.slot], recv_sem=rsem.at[slot],
                device_id=dev, device_id_type=MESH).start()

        def close(self):
            if self.open and self.shares:
                by_plane(*[partial(self.drain, n * self.one) for n in self.shares])
            elif self.open:
                self.drain(self.bytes)
            self.open = False

    def local(src, dst):
        copy = pltpu.make_async_copy(src, dst, lsem.at[take(2)])
        copy.start()
        return copy

    class Gather:
        def __init__(self, place, at_once=True):
            self.place, self.at_once = place, at_once
            self.batch = Batch(7, place(0))
            self.near, self.across = landings(4), landings(2)
            self.other = landings() if at_once else landings(4)

        def part(self, ref, i):
            n = ref.shape[0] // 2
            return ref.at[pl.ds(i * n, n)]

        def start(self, src=None):
            mine = self.place(s)
            src = mine if src is None else src
            for slot, half, k in ((0, 0, 2), (3, 1, 4), (1, 1, 2), (2, 0, 4)):
                self.batch.send(self.part(src, half), self.part(mine, half), self.near + slot, (ps(k), z))
            self.batch.send(src, mine, self.other, (ps(1), z))

        def to_partner(self, k):
            there = self.place(ps(k))
            self.batch.send(there, there, self.other + (0 if self.at_once else k // 2), (ps(1), z))

        def pass_near(self):
            along_x, along_y = self.place(ps(2)), self.place(ps(4))
            first, second = self.part(along_x, 0), self.part(along_y, 1)
            arrived(first, self.near)
            self.batch.send(first, first, self.across, (ps(4), z))
            arrived(second, self.near + 3)
            self.batch.send(second, second, self.across + 1, (ps(2), z))
            arrived(self.part(along_x, 1), self.near + 1)
            self.to_partner(2)
            arrived(self.part(along_y, 0), self.near + 2)
            self.to_partner(4)

        def pass_far(self):
            far = self.place(ps(6))
            arrived(self.part(far, 0), self.across)
            arrived(self.part(far, 1), self.across + 1)
            self.to_partner(6)

        def pass_all(self):
            self.pass_near()
            self.pass_far()

        def wait(self, k=None):
            if self.at_once:
                arrived(extent(4 * size(self.place(0))), self.other)
            else:
                arrived(self.place(ps(k)), self.other + k // 2)

    class Spread:
        def __init__(self, place):
            self.place, self.batch, self.base = place, Batch(3, place(0)), landings(3)

        def start(self, *which):
            mine = self.place(z)
            for k in which or (2, 1):
                self.batch.send(mine, mine, self.base + k - 1, (s, pz(k)))

        def pass_on(self):
            there = self.place(pz(2))
            arrived(there, self.base + 1)
            self.batch.send(there, there, self.base + 2, (s, pz(1)))

        def meet(self):
            def for_inner():
                self.pass_on()
                self.start(3)
            by_plane(for_inner, lambda: arrived(self.place(pz(2)), self.base + 1))
            self.batch.shares = (4, 2)

        def wait(self):
            for k in (1, 3):
                arrived(self.place(pz(k)), self.base + k - 1)

        def wait_all(self):
            for k in (1, 2, 3):
                arrived(self.place(pz(k)), self.base + k - 1)

    class Fold:
        def __init__(self, parts, landing, passing, first=0, count=None):
            self.rows = pl.ds(first, count or passing.shape[0])
            self.parts, self.landing, self.passing = parts, landing, passing.at[self.rows]
            self.batch, self.base = Batch(3, self.passing), landings(3)

        def start(self):
            for i, k in ((1, 3), (0, 1)):
                self.batch.send(self.parts.at[pz(k), self.rows], self.landing.at[i, self.rows], self.base + i, (s, pz(1)))

        def middle(self):
            arrived(self.landing.at[1, self.rows], self.base + 1)
            self.passing[...] = (self.parts[pz(2), self.rows, :].astype(f32)
                                 + self.landing[1, self.rows, :].astype(f32)).astype(bf16)
            self.batch.send(self.passing, self.landing.at[2, self.rows], self.base + 2, (s, pz(2)))

        def finish(self):
            arrived(self.landing.at[0, self.rows], self.base)
            arrived(self.landing.at[2, self.rows], self.base + 2)
            return (self.parts[z, self.rows, :].astype(f32) + self.landing[0, self.rows, :].astype(f32)
                    + self.landing[2, self.rows, :].astype(f32)).astype(bf16)

    class Scatter:
        def __init__(self, parts, low, mid, high, first=0, count=T):
            self.parts, self.low, self.mid, self.high = parts, low, mid, high
            self.first, self.count, self.window = first, count, pl.ds(first, count)
            self.batch = Batch(7, mid.at[0, self.window])
            self.base, self.far, self.last = landings(4), landings(2), landings()

        def rows_of(self, which):
            return pl.ds(pl.multiple_of(which * T + self.first, self.count), self.count)

        def half(self, ref, j, i):
            return ref.at[j, self.window, pl.ds(i * (D // 2), D // 2)]

        def send(self, j, i, slot, k):
            self.batch.send(self.half(self.mid, j, i), self.half(self.high, j, i), slot, (ps(k), z))

        def pair(self, j):
            self.batch.send(self.parts.at[j, self.rows_of(1 - core)], self.low.at[j, self.window],
                            self.base + j, (ps(1), z))

        def onward(self, j):
            arrived(self.low.at[j, self.window], self.base + j)
            own = self.parts[j, self.rows_of(core), :].astype(f32)
            self.mid[j, self.window, :] = (own + self.low[j, self.window, :].astype(f32)).astype(bf16)
            if j == 1:
                self.send(1, 0, self.last, 2)
            elif j == 2:
                self.send(2, 1, self.last, 4)
            else:
                self.send(3, 0, self.far, 2)
                self.send(3, 1, self.far + 1, 4)

        def cross(self):
            for j, i, k in ((2, 0, 4), (1, 1, 2)):
                arrived(self.half(self.high, 3, i), self.far + i)
                ref = self.half(self.mid, j, i)
                ref[...] = (ref[...].astype(f32) + self.half(self.high, 3, i)[...].astype(f32)).astype(bf16)
                self.send(j, i, self.last, k)

        def ready(self):
            arrived(self.low.at[0, self.window], self.base)
            arrived(self.high.at[pl.ds(1, 2), self.window], self.last)

        def rows(self, at, n):
            own = self.parts[0, pl.ds(pl.multiple_of(core * T + at, n), n), :].astype(f32)
            total = own + self.low[0, pl.ds(at, n), :].astype(f32)
            for j in (1, 2):
                total = total + self.high[j, pl.ds(at, n), :].astype(f32)
            return total

    class Share:
        def __init__(self, count, like):
            self.count, self.batch, self.slot, self.bytes = count, Batch(count, like), landings(), count * size(like)

        def plane(self, src, dst):
            for k in (6, 7, 2, 3, 4, 5, 1):
                self.batch.send(src(ps(k)), dst, self.slot, (ps(k), z))

        def column(self, src, dst):
            for k in (2, 3, 1):
                self.batch.send(src, dst, self.slot, (s, pz(k)))

        def wait(self):
            arrived(extent(self.bytes), self.slot)

    def loop(count, body, unroll=1):
        def step(i, carry):
            body(i)
            return carry
        lax.fori_loop(0, count, step, 0, unroll=unroll)

    def at(i, n):
        return pl.multiple_of(i * n, n)

    def turn(src, dst):
        def one(i):
            dst[:, pl.ds(at(i, T), T)] = jnp.transpose(src[pl.ds(at(i, T), T), :])
        loop(L // T, one)

    vec, vecg = r.vec, r.vecg

    OUTPUT_BIAS, FIRST_GAIN, FIRST_SHIFT, DOWN_BIAS, SECOND_GAIN, SECOND_SHIFT, PROJECTION_BIAS, UP_BIAS = range(8)
    wide = ((first_row.output_bias, OUTPUT_BIAS), (first_row.first_gain, FIRST_GAIN),
            (first_row.first_shift, FIRST_SHIFT), (first_row.down_bias, DOWN_BIAS),
            (first_row.second_gain, SECOND_GAIN), (first_row.second_shift, SECOND_SHIFT))

    def row(i, width=D):
        return vec[i:i + 1, :width]

    lanes = lax.broadcasted_iota(jnp.int32, (T, C), 1)
    low_head = lanes < HEAD_DIM

    def swapped(w):
        low_half = lax.broadcasted_iota(jnp.int32, w.shape, 1) % HEAD_DIM < HEAD_DIM // 2
        return jnp.where(low_half, pltpu.roll(w, C - HEAD_DIM // 2, 1), pltpu.roll(w, HEAD_DIM // 2, 1))

    def stacked(w):
        nothing = jnp.zeros_like(w)
        return jnp.concatenate([jnp.where(low_head, w, nothing), jnp.where(low_head, nothing, w)], axis=0)

    def unstacked(w):
        return jnp.where(low_head, w[:T], w[T:])

    barrier = pltpu.get_barrier_semaphore()
    for k in range(1, S):
        pl.semaphore_signal(barrier, inc=1, device_id=(ps(k), z), device_id_type=MESH)
    for k in range(1, Z):
        pl.semaphore_signal(barrier, inc=1, device_id=(s, pz(k)), device_id_type=MESH)
    x_ref, ct_ref = r.v_x, r.v_ct
    x_load = local(r.x, x_ref)
    wo_load = local(r.wo.at[:, block_of(s, C)], r.st_wo)
    proj_loads = [local(r.proj.at[:, block_of(i * (D // C) + s, C)], r.st_proj.at[:, pl.ds(i * C, C)])
                  for i in range(3)]
    raw = ((r.b_projection, r.v_projection, first_row.projection_bias), (r.b_output, r.v_output, first_row.output_bias),
           (r.gain1, r.v_gain1, first_row.first_gain), (r.shift1, r.v_shift1, first_row.first_shift),
           (r.b_up, r.v_up, first_row.up_bias), (r.b_down, r.v_down, first_row.down_bias),
           (r.gain2, r.v_gain2, first_row.second_gain), (r.shift2, r.v_shift2, first_row.second_shift))
    raw_loads = [local(source, ref) for source, ref, _ in raw]
    seg_load = local(r.seg, r.v_seg)
    up_loads = [local(r.up.at[:, block_of(i * (D // C) + s, C)], r.st_up.at[:, pl.ds(i * C, C)])
                for i in range(Z)]
    dn_load = local(r.dn.at[block_of(s, UZ), :], r.st_dn)
    late_loads = [local(r.cos, r.v_cos), local(r.sin, r.v_sin), local(r.ct, ct_ref)]
    cos_ref, sin_ref = r.v_cos, r.v_sin

    x_all, w_qkv, w_o, w_up, w_dn = r.x_all, r.w_qkv, r.w_o, r.w_up, r.w_dn
    gather_x = Gather(lambda o: x_all.at[block_of(o, T)])
    spread_qkv = Spread(lambda p: w_qkv.at[block_of(p, KW)])
    spread_o = Spread(lambda p: w_o.at[block_of(p, KW), block_of(s, C)])
    spread_up = Spread(lambda p: w_up.at[block_of(p, KW)])
    spread_dn = Spread(lambda p: w_dn.at[block_of(p, UZ)])
    gather_o = Gather(lambda o: w_o.at[:, block_of(o, C)])
    wo_load.wait()
    w_o[block_of(z, KW), block_of(s, C)] = r.st_wo[...].astype(bf16)
    for copy in proj_loads:
        copy.wait()
    w_qkv[block_of(z, KW), :] = r.st_proj[...].astype(bf16)
    x_load.wait()
    pl.semaphore_wait(barrier, S + Z - 2)
    spread_o.start(2, 3, 1)
    spread_qkv.start()
    gather_x.start(x_ref)

    small, small_all, seg_c, seg_r = r.small, r.small_all, r.seg_c, r.seg_r
    for copy, (_, ref, start) in zip(raw_loads, raw):
        copy.wait()
        if ref.shape[1] == C:
            small[start:start + ref.shape[0], :] = ref[...].astype(bf16).astype(f32)
        else:
            for i in range(ref.shape[1] // C):
                small[start + i:start + i + 1, :] = ref[0:1, i * C:(i + 1) * C].astype(bf16).astype(f32)
    x_all[block_of(s, T), :] = x_ref[...]
    vecg[...] = jnp.zeros((8, D), f32)
    seg_load.wait()
    seg_r[...] = jnp.broadcast_to(r.v_seg[...].astype(f32), (8, L))

    def seg_turn(i):
        here = pl.ds(at(i, T), T)
        seg_c[here, :] = jnp.transpose(jnp.broadcast_to(seg_r[0:1, here], (T, T)))
    loop(L // T, seg_turn)
    for copy in up_loads:
        copy.wait()
    w_up[block_of(z, KW), :] = r.st_up[...].astype(bf16)
    dn_load.wait()
    w_dn[block_of(z, UZ), :] = r.st_dn[...].astype(bf16)
    share_small = Share(3, small)
    small_all[z] = small[...]

    gather_x.pass_near()
    spread_o.wait_all()
    gather_o.start()
    gather_x.pass_far()
    gather_x.wait()
    spread_qkv.pass_on()
    share_small.column(small, small_all.at[z])
    spread_up.start()
    x_t = r.x_t
    turn(x_all, x_t)
    for copy in late_loads:
        copy.wait()
    gather_o.pass_near()
    spread_qkv.wait()
    share_small.wait()
    for p in range(Z):
        for start, i in wide:
            for half in range(KW // C):
                at_row = start + half
                lane = (p * (KW // C) + half) * C
                vec[i:i + 1, lane:lane + C] = small_all[p, at_row:at_row + 1, :]
        vec[7:8, p * C:(p + 1) * C] = small_all[p, pl.ds(first_row.up_bias + s, 1), :]
    per = 3 * D // (C * Z)
    for t in range(3):
        number = t * (D // C) + s
        vec[6:7, t * C:(t + 1) * C] = small_all[number // per, pl.ds(first_row.projection_bias + number % per, 1), :]

    q_ref, k_ref, v_ref = r.q, r.k, r.v
    scale = HEAD_DIM ** -0.5

    def project(i):
        here = pl.ds(at(i, T2), T2)
        out = mm(x_all[here, :], w_qkv[...]) + row(PROJECTION_BIAS, 3 * C)
        cosine, sine = cos_ref[here, :], sin_ref[here, :]
        q0, k0 = out[:, :C], out[:, C:2 * C]
        q_ref[here, :] = ((q0 * cosine + swapped(q0) * sine).astype(bf16).astype(f32) * scale).astype(bf16)
        k_ref[here, :] = (k0 * cosine + swapped(k0) * sine).astype(bf16)
        v_ref[here, :] = out[:, 2 * C:].astype(bf16)
    loop(L // T2, project)
    gather_o.pass_far()

    lse, c_f, c_heads, c_tok = r.lse, r.c_f, r.c_heads, r.c_tok
    R = 16

    def same_document(here):
        return jnp.tile(seg_c[here, :], (1, L // C)) == seg_r[0:1, :]

    def both(w):
        return jnp.concatenate([w, w], axis=0)

    def attend(o):
        here = block_of(o, T)
        score = jnp.where(both(same_document(here)), mm(stacked(q_ref[here, :]), k_ref[...], NT), MASKED)
        top = jnp.max(score, axis=-1, keepdims=True)
        power = jnp.exp(score - top)
        total = jnp.sum(power, axis=-1, keepdims=True)
        context = unstacked(mm(power.astype(bf16), v_ref[...]) * (1.0 / total))
        c_f[here, :] = context
        c_heads[here, :] = context.astype(bf16)
        logs = jnp.broadcast_to(top + jnp.log(total), (T2, C))
        for h in range(2):
            lse[h:h + 1, here] = jnp.transpose(logs[h * T:(h + 1) * T, :])[0:1, :]

    share_c = Share(7, c_heads.at[pl.ds(0, T)])

    def attend_and_send(i):
        k = 7 - i
        attend(ps(k))

        @pl.when(k > 0)
        def _():
            share_c.batch.send(c_heads.at[block_of(ps(k), T)], c_tok.at[:, block_of(s, C)], share_c.slot, (ps(k), z))
    loop(8, attend_and_send)
    spread_up.meet()
    spread_dn.start()
    c_tok[:, block_of(s, C)] = c_heads[block_of(s, T), :]
    gather_o.wait()
    share_c.wait()

    a_buf = r.a_buf
    a_buf[...] = mm(c_tok[...], w_o[...])
    n1, y1, r1, y_all = r.n1, r.y1, r.r1, r.y_all

    def norm(h):
        centre = h - jnp.mean(h, axis=-1, keepdims=True)
        root = lax.rsqrt(jnp.mean(centre * centre, axis=-1, keepdims=True) + norm_epsilon)
        return centre * root, root

    def first_norm(i):
        rows = pl.ds(at(i, R), R)
        normal, root = norm(x_ref[rows, :].astype(f32) + a_buf[rows, :] + row(OUTPUT_BIAS))
        out = normal * row(FIRST_GAIN) + row(FIRST_SHIFT)
        n1[rows, :] = normal
        r1[rows, :] = jnp.broadcast_to(root, (R, C))
        y1[rows, :] = out
        y_all[pl.ds(pl.multiple_of(s * T + i * R, R), R), :] = out.astype(bf16)
    loop(T // R, first_norm, 4)
    gather_y = Gather(lambda o: y_all.at[block_of(o, T)], False)
    gather_y.start()
    c_all = r.c_all
    gather_c = Gather(lambda o: c_all.at[block_of(o, T)])
    c_all[block_of(s, T), :] = c_tok[...]

    u_buf, g_ref, d_ref, du_ref, dz_all = r.u_buf, r.g, r.d, r.du, r.dz_all
    parts, mid = r.parts, r.mid
    spread_up.wait()
    E = 32

    def lift(j):
        q = chip_of(j)
        u_buf[...] = mm(y_all[block_of(q, T2), :], w_up[...])

        def chunk(i):
            rows = pl.ds(at(i, E), E)
            there = pl.ds(pl.multiple_of(q * T2 + i * E, E), E)
            u = u_buf[rows, :] + row(UP_BIAS, F)
            share = 0.5 + 0.5 * lax.erf(u * (0.5 ** 0.5))
            g_ref[there, :] = (u * share).astype(bf16)
            d_ref[there, :] = share + u * (jnp.exp(-0.5 * u * u) * 0.3989422804014327)
        loop(T2 // E, chunk)

    def lower(j):
        parts[j] = mm(g_ref[block_of(chip_of(j), T2), :], w_dn[...]).astype(bf16)

    H = T // 2
    folds_z = [Scatter(parts, r.low0, mid, r.high0, i * H, H) for i in range(2)]
    y_t, g_t = r.y_t, r.g_t
    gather_y.wait(1)
    lift(0)
    gather_y.pass_near()
    gather_y.wait(3)
    lift(1)
    gather_y.wait(5)
    lift(2)
    spread_dn.meet()
    gather_y.pass_far()
    gather_c.start(c_tok)
    gather_y.wait(7)
    lift(3)
    turn(y_all, y_t)
    turn(g_ref, g_t)
    spread_dn.wait()
    for j in (3, 1, 2):
        lower(j)
        for fold in folds_z:
            fold.pair(j)
    for j in (3, 1, 2):
        folds_z[0].onward(j)
    folds_z[1].onward(3)
    lower(0)
    for fold in folds_z:
        fold.pair(0)
    folds_z[0].cross()
    folds_z[1].onward(1)
    folds_z[1].onward(2)
    folds_z[1].cross()
    folds_z[0].ready()

    dh2, out_ref = r.dh2, r.out

    def add_row(i, value):
        vecg[i:i + 1, :] = vecg[i:i + 1, :] + jnp.sum(value, axis=0, keepdims=True)

    def norm_back(incoming, normal, root, gain):
        scaled = incoming * gain
        return root * (scaled - jnp.mean(scaled, axis=-1, keepdims=True)
                       - normal * jnp.mean(scaled * normal, axis=-1, keepdims=True))

    def second_norm(i):
        start = at(i, R)
        rows = pl.ds(start, R)
        normal, root = norm(y1[rows, :] + folds_z[0].rows(start, R) + row(DOWN_BIAS))
        out_ref[rows, :] = (normal * row(SECOND_GAIN) + row(SECOND_SHIFT)).astype(bf16)
        e = ct_ref[rows, :].astype(f32)
        grad = norm_back(e, normal, root, row(SECOND_GAIN))
        dh2[rows, :] = grad
        dz = grad.astype(bf16)
        dz_all[pl.ds(pl.multiple_of(s * T + i * R, R), R), :] = dz
        add_row(3, dz.astype(f32))
        add_row(4, e * normal)
        add_row(5, e)
    gathers_dz = [Gather(lambda o, i=i: dz_all.at[block_of(2 * o + i, H)], False) for i in range(2)]
    loop(H // R, second_norm, 2)
    gathers_dz[0].start()
    folds_z[1].ready()
    loop(H // R, lambda i: second_norm(i + H // R), 2)
    gathers_dz[1].start()
    for fold in folds_z:
        fold.batch.close()

    colg = r.colg
    colg[...] = jnp.zeros((8, F), f32)

    def unlower(j):
        q = chip_of(j)
        u_buf[...] = mm(dz_all[block_of(q, T2), :], w_dn[...], NT)

        def chunk(i):
            rows = pl.ds(at(i, E), E)
            there = pl.ds(pl.multiple_of(q * T2 + i * E, E), E)
            du = (u_buf[rows, :] * d_ref[there, :]).astype(bf16)
            du_ref[there, :] = du
            colg[0:1, :] = colg[0:1, :] + jnp.sum(du.astype(f32), axis=0, keepdims=True)
        loop(T2 // E, chunk)

    def unlift(j):
        parts[j] = mm(du_ref[block_of(chip_of(j), T2), :], w_up[...], NT).astype(bf16)

    fold_y = Scatter(parts, r.low1, mid, r.high1)
    gd_part, gu_part = r.gd_part, r.gu_part
    folds_dn = [Fold(gd_part, r.gd_land, r.gd_pass, i * (UZ // 2), UZ // 2) for i in range(2)]
    folds_up = [Fold(gu_part, r.gu_land, r.gu_pass, i * (KW // 2), KW // 2) for i in range(2)]

    def down_grad(k):
        gd_part[pz(k)] = mm(g_t[block_of(pz(k), UZ), :], dz_all[...]).astype(bf16)

    def up_grad(k):
        gu_part[pz(k)] = mm(y_t[block_of(pz(k), KW), :], du_ref[...]).astype(bf16)

    def dz_wait(k):
        for gather in gathers_dz:
            gather.wait(k)
    dz_wait(1)
    unlower(0)
    unlift(0)
    fold_y.pair(0)
    gathers_dz[0].pass_near()
    gathers_dz[1].pass_near()
    dz_wait(3)
    unlower(1)
    unlift(1)
    fold_y.pair(1)
    gathers_dz[0].pass_far()
    dz_wait(5)
    unlower(2)
    fold_y.onward(1)
    unlift(2)
    fold_y.pair(2)
    gathers_dz[1].pass_far()
    fold_y.onward(2)
    dz_wait(7)
    down_grad(3)
    down_grad(1)
    folds_dn[0].start()
    folds_dn[1].start()
    unlower(3)
    unlift(3)
    fold_y.pair(3)
    up_grad(3)
    fold_y.onward(3)

    up_grad(1)
    down_grad(2)
    fold_y.cross()
    folds_dn[0].middle()
    folds_up[0].start()
    down_grad(0)
    up_grad(2)
    up_grad(0)
    fold_y.ready()

    dh1, da = r.dh1, r.da

    def first_back(i):
        start = at(i, R)
        rows = pl.ds(start, R)
        incoming = dh2[rows, :] + fold_y.rows(start, R)
        normal = n1[rows, :]
        grad = norm_back(incoming, normal, r1[rows, 0:1], row(FIRST_GAIN))
        dh1[rows, :] = grad
        low = grad.astype(bf16)
        da[rows, :] = low
        add_row(0, low.astype(f32))
        add_row(1, incoming * normal)
        add_row(2, incoming)
    loop(T // R, first_back, 2)
    fold_y.batch.close()

    dc_tok, dc = r.dc_tok, r.dc
    dc_tok[...] = mm(da[...], w_o[...], NT).astype(bf16)
    share_dc = Share(7, dc.at[pl.ds(0, T)])
    share_dc.plane(lambda o: dc_tok.at[:, block_of(o, C)], dc.at[block_of(s, T)])
    dc[block_of(s, T), :] = dc_tok[:, block_of(s, C)]
    da_cols = r.da_cols
    share_da = Share(7, da_cols.at[pl.ds(0, T)])
    share_da.plane(lambda o: da.at[:, block_of(o, C)], da_cols.at[block_of(s, T)])
    da_cols[block_of(s, T), :] = da[:, block_of(s, C)]
    vec_z, vec_all = r.vec_z, r.vec_all
    share_vec = Share(3, vec_z.at[0])
    for k in (2, 3, 1):
        share_vec.batch.send(vecg.at[:, block_of(pz(k), KW)], vec_z.at[z], share_vec.slot, (s, pz(k)))
    vec_z[z] = vecg[:, block_of(z, KW)]
    folds_dn[1].middle()
    folds_up[1].start()
    share_dc.wait()

    delta, dq, dproj = r.delta, r.dq, r.dproj

    def deltas(i):
        here = pl.ds(at(i, T), T)
        turned = jnp.transpose(dc[here, :].astype(f32) * c_f[here, :])
        delta[0:1, here] = jnp.sum(turned[:HEAD_DIM], axis=0, keepdims=True)
        delta[1:2, here] = jnp.sum(turned[HEAD_DIM:], axis=0, keepdims=True)
        dq[here, :] = jnp.zeros((T, C), f32)
    loop(L // T, deltas)

    def attend_back(i):
        here = pl.ds(at(i, T), T)
        same = same_document(here)
        k_here, v_here = k_ref[here, :], v_ref[here, :]
        keys, values, slopes = [], [], []
        for h in range(2):
            own = low_head if h == 0 else jnp.logical_not(low_head)
            nothing = jnp.zeros_like(k_here)
            key = jnp.where(own, k_here, nothing)
            weight = jnp.exp(jnp.where(same, mm(key, q_ref[...], NT), MASKED) - lse[h:h + 1, :])
            slope = mm(jnp.where(own, v_here, nothing), dc[...], NT) - delta[h:h + 1, :]
            slopes.append((weight * slope).astype(bf16))
            values.append(mm(weight.astype(bf16), dc[...]))
            keys.append(key)
        dv = jnp.where(low_head, values[0], values[1]).astype(bf16)
        dk = jnp.where(low_head, mm(slopes[0], q_ref[...]), mm(slopes[1], q_ref[...])).astype(bf16).astype(f32)
        dproj[here, 2 * C:] = dv
        dproj[here, C:2 * C] = (dk * cos_ref[here, :] - swapped(dk) * sin_ref[here, :]).astype(bf16)
        dq[...] = dq[...] + mm(jnp.concatenate(slopes, axis=0), jnp.concatenate(keys, axis=0), TN)

    gd_all, gu_all, go_all, gqk_all, gv_all = r.gd, r.gu, r.go, r.gqk, r.gv
    gather_gd = Gather(lambda o: gd_all.at[block_of(o, UZ)])
    gather_gu = Gather(lambda o: gu_all.at[o])
    gather_go = Gather(lambda o: go_all.at[:, block_of(o, C)])
    gather_gqk = Gather(lambda o: gqk_all.at[o])
    gather_gv = Gather(lambda o: gv_all.at[o])
    go_part = r.go_part
    fold_o = Fold(go_part, r.go_land, r.go_pass)

    def out_grad(k):
        go_part[pz(k)] = mm(c_all[:, block_of(pz(k), KW)], da_cols[...], TN).astype(bf16)

    def attend_back_and_fold(i):
        attend_back(i)

        @pl.when(i == 0)
        def _():
            gather_c.pass_near()

        @pl.when(i == 5)
        def _():
            for part in range(2):
                at_row = pl.multiple_of(s * UZ + part * (UZ // 2), UZ // 2)
                gd_all[pl.ds(at_row, UZ // 2), :] = folds_dn[part].finish()
            gather_gd.start()

        @pl.when(i == 6)
        def _():
            folds_up[0].middle()
            gather_c.pass_far()
    loop(L // T, attend_back_and_fold)


    def dq_rows(i):
        here = pl.ds(at(i, T), T)
        whole = (dq[here, :] * scale).astype(bf16).astype(f32)
        dproj[here, :C] = (whole * cos_ref[here, :] - swapped(whole) * sin_ref[here, :]).astype(bf16)
        colg[1:2, :3 * C] = colg[1:2, :3 * C] + jnp.sum(dproj[here, :].astype(f32), axis=0, keepdims=True)
    loop(L // T, dq_rows)

    gqk_part, gv_part = r.gqk_part, r.gv_part
    fold_qk = Fold(gqk_part, r.gqk_land, r.gqk_pass)
    fold_v = Fold(gv_part, r.gv_land, r.gv_pass)

    def projection_grad(k):
        grad = mm(x_t[block_of(pz(k), KW), :], dproj[...]).astype(bf16)
        gqk_part[pz(k)] = grad[:, :2 * C]
        gv_part[pz(k)] = grad[:, 2 * C:]
    projection_grad(3)
    projection_grad(1)
    fold_x = Scatter(parts, r.low2, mid, r.high2)

    def unproject(j):
        parts[j] = mm(dproj[block_of(chip_of(j), T2), :], w_qkv[...], NT).astype(bf16)
        fold_x.pair(j)
    fold_qk.start()
    unproject(3)
    unproject(1)
    fold_x.onward(3)
    folds_up[1].middle()
    fold_v.start()
    unproject(2)
    fold_x.onward(1)
    unproject(0)
    fold_x.onward(2)
    gather_c.wait()
    share_da.wait()
    for k in (3, 1):
        out_grad(k)
    fold_o.start()
    for k in (2, 0):
        out_grad(k)
    projection_grad(2)
    projection_grad(0)
    fold_x.cross()
    gather_gd.pass_near()
    col_z, col_own = r.col_z, r.col_own
    col_own[...] = jnp.zeros((8, C), f32)
    for i in range(Z):
        col_own[i:i + 1, :] = colg[0:1, i * C:(i + 1) * C]
    for i in range(3):
        col_own[Z + i:Z + i + 1, :] = colg[1:2, i * C:(i + 1) * C]
    share_col = Share(3, col_own)
    share_col.column(col_own, col_z.at[z])
    col_z[z] = col_own[...]
    share_vec.wait()
    vec_sum = r.vec_sum
    vec_sum[...] = vec_z[0] + vec_z[1] + vec_z[2] + vec_z[3]
    share_sum = Share(7, vec_sum)
    share_sum.plane(lambda o: vec_sum, vec_all.at[s])
    vec_all[s] = vec_sum[...]
    for i in range(2):
        gu_all[s, pl.ds(i * (KW // 2), KW // 2), :] = folds_up[i].finish()
    gather_gu.start()
    fold_qk.middle()

    @pl.when(inner)
    def _():
        fold_v.middle()
        fold_o.middle()
    gather_gd.pass_far()
    fold_x.ready()
    dx_ref = r.dx

    def input_back(i):
        start = at(i, R)
        rows = pl.ds(start, R)
        dx_ref[rows, :] = (dh1[rows, :] + fold_x.rows(start, R)).astype(bf16)
    loop(T // R, input_back, 2)
    gather_gd.wait()
    gather_gu.pass_near()

    @pl.when(jnp.logical_not(inner))
    def _():
        fold_v.middle()
    gqk_all[s] = fold_qk.finish()
    gather_gqk.start()

    @pl.when(jnp.logical_not(inner))
    def _():
        fold_o.middle()
    gv_all[s] = fold_v.finish()
    gather_gv.start()
    gather_gu.pass_far()
    go_all[:, block_of(s, C)] = fold_o.finish()
    gather_go.start()
    share_col.wait()
    col_all, col_sum = r.col_all, r.col_sum
    col_sum[...] = col_z[0] + col_z[1] + col_z[2] + col_z[3]
    share_cols = Share(7, col_sum)
    share_cols.plane(lambda o: col_sum, col_all.at[s])
    col_all[s] = col_sum[...]
    gather_gqk.pass_near()
    gather_gv.pass_near()
    gather_gu.wait()

    gather_go.pass_near()
    gather_gqk.pass_far()
    gather_gv.pass_far()
    share_sum.wait()
    share_cols.wait()
    total = vec_all[0]
    for o in range(1, S):
        total = total + vec_all[o]
    gsm = r.gsm
    gsm[...] = jnp.zeros(gsm.shape, f32)
    for start, i in wide:
        for half in range(KW // C):
            gsm[start + half:start + half + 1, :] = total[i:i + 1, half * C:(half + 1) * C]
    for o in range(S):
        at_row = first_row.up_bias + o
        gsm[at_row:at_row + 1, :] = col_all[o, pl.ds(z, 1), :]
    for i in range(per):
        number = z * per + i
        at_row = first_row.projection_bias + i
        gsm[at_row:at_row + 1, :] = col_all[number % S, pl.ds(Z + number // S, 1), :]
    gather_go.pass_far()
    gather_go.wait()
    gather_gqk.wait()
    gather_gv.wait()
    for batch in closing:
        batch.close()
    assert counter[0] <= LANDINGS and counter[1] <= BATCHES and counter[2] <= LOCAL, counter


def fused_shards(*args):
    (hidden_in, cotangent, segment_ids, projection, projection_bias, output_weight, output_bias, first_gain,
     first_shift, up_weight, up_bias, down_weight, down_bias, second_gain, second_shift) = args
    T, D = hidden_in.shape[1:]
    L = segment_ids.shape[1]
    KW = projection.shape[0]
    F = up_weight.shape[1] // 8
    C, Z = 128, 4
    UZ = F // Z
    small = dict(projection_bias=projection_bias, output_bias=output_bias, first_gain=first_gain,
                 first_shift=first_shift, up_bias=up_bias, down_bias=down_bias, second_gain=second_gain,
                 second_shift=second_shift)
    starts, at_row = {}, 0
    for name, value in small.items():
        starts[name] = at_row
        at_row += value.shape[0] // C
    rows = -(-at_row // 8) * 8
    half = HEAD_DIM // 2
    inverse = np.float32(10000.0) ** (np.float32(-2.0) * np.arange(half, dtype=np.float32) / np.float32(HEAD_DIM))
    angles = np.arange(L, dtype=np.float32)[:, None] * inverse.astype(np.float32)[None, :]
    cosine = np.tile(np.cos(angles), (1, C // half))
    sine = np.tile(np.concatenate([-np.sin(angles), np.sin(angles)], axis=1), (1, C // HEAD_DIM))

    inputs = dict(x=hidden_in[0], ct=cotangent[0], seg=segment_ids, cos=jnp.asarray(cosine), sin=jnp.asarray(sine),
                  b_projection=projection_bias.reshape(-1, C), b_output=output_bias[None], gain1=first_gain[None],
                  shift1=first_shift[None], b_up=up_bias[None], b_down=down_bias[None], gain2=second_gain[None],
                  shift2=second_shift[None], proj=projection, wo=output_weight, up=up_weight, dn=down_weight)
    outputs = dict(out=((T, D), bf16), dx=((T, D), bf16), gsm=((rows, C), f32), gqk=((8, KW, 2 * C), bf16), gv=((8, KW, C), bf16),
                   go=((KW, D), bf16), gu=((8, KW, F), bf16), gd=((8 * UZ, D), bf16))
    landed = dict(v_x=inputs["x"], v_ct=inputs["ct"], v_seg=segment_ids, v_cos=inputs["cos"], v_sin=inputs["sin"],
                  v_projection=inputs["b_projection"], v_output=inputs["b_output"], v_gain1=inputs["gain1"],
                  v_shift1=inputs["shift1"], v_up=inputs["b_up"], v_down=inputs["b_down"], v_gain2=inputs["gain2"],
                  v_shift2=inputs["shift2"])
    PART = (4, T, D)
    scratch = {name: (value.shape, value.dtype) for name, value in landed.items()}
    scratch.update(
        x_all=((L, D), bf16), x_t=((D, L), bf16), w_qkv=((D, 3 * C), bf16), st_proj=((KW, 3 * C), f32),
        w_o=((D, D), bf16), st_wo=((KW, C), f32), w_up=((D, F), bf16), st_up=((KW, F), f32),
        w_dn=((F, D), bf16), st_dn=((UZ, D), f32), small_all=((Z, rows, C), f32), vec=((8, D), f32),
        vecg=((8, D), f32), q=((L, C), bf16), k=((L, C), bf16), v=((L, C), bf16),
        seg_r=((8, L), f32), seg_c=((L, C), f32), small=((rows, C), f32), lse=((8, L), f32),
        delta=((8, L), f32), c_f=((L, C), f32), c_heads=((L, C), bf16), c_tok=((T, D), bf16),
        a_buf=((T, D), f32), n1=((T, D), f32), y1=((T, D), f32), r1=((T, C), f32),
        y_all=((L, D), bf16), y_t=((D, L), bf16), u_buf=((2 * T, F), f32), g=((L, F), bf16),
        g_t=((F, L), bf16), d=((L, F), f32), du=((L, F), bf16), dz_all=((L, D), bf16),
        parts=((4, 2 * T, D), bf16), mid=((4, T, D), bf16), dh2=((T, D), f32), dh1=((T, D), f32),
        colg=((8, F), f32), gd_part=((Z, UZ, D), bf16), gd_land=((3, UZ, D), bf16), gd_pass=((UZ, D), bf16),
        gu_part=((Z, KW, F), bf16), gu_land=((3, KW, F), bf16), gu_pass=((KW, F), bf16),
        go_part=((Z, KW, C), bf16), go_land=((3, KW, C), bf16), go_pass=((KW, C), bf16),
        gqk_part=((Z, KW, 2 * C), bf16), gqk_land=((3, KW, 2 * C), bf16), gqk_pass=((KW, 2 * C), bf16),
        gv_part=((Z, KW, C), bf16), gv_land=((3, KW, C), bf16), gv_pass=((KW, C), bf16),
        da=((T, D), bf16), dc_tok=((T, D), bf16), dc=((L, C), bf16),
        da_cols=((L, C), bf16), c_all=((L, D), bf16), dq=((L, C), f32), dproj=((L, 3 * C), bf16),
        vec_all=((8, 8, KW), f32), vec_z=((Z, 8, KW), f32), vec_sum=((8, KW), f32), col_own=((8, C), f32),
        col_z=((Z, 8, C), f32), col_sum=((8, C), f32), col_all=((8, 8, C), f32),
        low0=(PART, bf16), high0=(PART, bf16), low1=(PART, bf16), high1=(PART, bf16), low2=(PART, bf16),
        high2=(PART, bf16), ssem=(BATCHES,), rsem=(LANDINGS,), lsem=(LOCAL,))
    names = [*inputs, *outputs, *scratch]
    sizes = SimpleNamespace(names=names, T=T, D=D, L=L, F=F, first_row=SimpleNamespace(**starts))

    anywhere, near = pl.BlockSpec(memory_space=pl.ANY), pl.BlockSpec(memory_space=pltpu.VMEM)
    results = pl.pallas_call(
        partial(fused_layer, sizes),
        out_shape=[pltpu.VMEM(*what) for what in outputs.values()],
        in_specs=[anywhere] * len(inputs),
        out_specs=[near] * len(outputs),
        scratch_shapes=[pltpu.VMEM(*what) if len(what) == 2 else pltpu.SemaphoreType.DMA(what)
                        for what in scratch.values()],
        compiler_params=pltpu.CompilerParams(collective_id=0, has_side_effects=True, vmem_limit_bytes=57 << 20),
        name="fused_layer",
    )(*inputs.values())
    out, dx, gsm, gqk, gv, go, gu, gd = results
    wide = [jax.ShapeDtypeStruct(value.shape, f32) for value in (projection, output_weight, up_weight, down_weight)]
    narrow = [jax.ShapeDtypeStruct((1, value.shape[0]) if value is not projection_bias else (value.shape[0] // C, C), f32)
              for value in small.values()]
    sources = [out, dx, gqk, gv, go, gu, gd, gsm]
    outcomes = [out, dx] + wide + narrow
    results = pl.pallas_call(
        partial(widen, tuple(starts.values())),
        out_shape=[jax.ShapeDtypeStruct(value.shape, value.dtype) for value in outcomes],
        in_specs=[near] * len(sources),
        out_specs=[anywhere] * len(outcomes),
        scratch_shapes=[pltpu.VMEM(value.shape, value.dtype) for value in outcomes[2:]]
        + [pltpu.SemaphoreType.DMA((LOCAL,))],
        compiler_params=pltpu.CompilerParams(vmem_limit_bytes=20 << 20),
        name="widen",
    )(*sources)
    out, dx, gq, go, gu, gd = results[:6]
    pb, ob, g1, s1, ub, db, g2, s2 = [value.reshape(-1) for value in results[6:]]
    return (out[None], dx[None], gq, pb, go, ob, g1, s1, gu, ub, gd, db, g2, s2)


def widen(starts, *refs):
    held, results, made, outsem = refs[:8], refs[8:22], refs[22:34], refs[34]
    out, dx, gqk, gv, go, gu, gd, gsm = held
    C = gsm.shape[1]
    stores = []

    def store(ref, result):
        copy = pltpu.make_async_copy(ref, result, outsem.at[len(stores)])
        copy.start()
        stores.append(copy)

    def grouped(i, target, at, n, first):
        source, result = held[i], made[target]
        groups = source.shape[0]

        def step(j, carry):
            rows = pl.ds(pl.multiple_of(at + j * 32, 32), 32)
            for o in range(groups):
                for p in range(source.shape[2] // C):
                    lane = ((first + p) * groups + o) * C
                    result[rows, lane:lane + C] = source[o, rows, p * C:(p + 1) * C].astype(f32)
            return carry
        lax.fori_loop(0, n // 32, step, 0)

    def plain(i, target, at, n, _):
        source, result = held[i], made[target]

        def step(j, carry):
            rows = pl.ds(pl.multiple_of(at + j * 32, 32), 32)
            result[rows, :] = source[rows, :].astype(f32)
            return carry
        lax.fori_loop(0, n // 32, step, 0)

    store(out, results[0])
    store(dx, results[1])
    work = []
    for i, target, n, body, first in ((5, 2, 64, grouped, 0), (6, 3, 256, plain, 0), (2, 0, 64, grouped, 0),
                                      (3, 0, 64, grouped, 2), (4, 1, 256, plain, 0)):
        total = held[i].shape[-2]
        for at in range(0, total, n):
            work.append((i, target, at, n, body, first))
    for i, target, at, n, body, first in work:
        body(i, target, at, n, first)
        if i != 2:
            rows = pl.ds(at, n)
            store(made[target].at[rows], results[2 + target].at[rows])
    for start, ref, result in zip(starts, made[4:], results[6:]):
        if ref.shape[1] == C:
            ref[...] = gsm[start:start + ref.shape[0], :]
        else:
            for i in range(ref.shape[1] // C):
                ref[0:1, i * C:(i + 1) * C] = gsm[start + i:start + i + 1, :]
        store(ref, result)
    for copy in stores:
        copy.wait()


BATCHES = 34
LANDINGS = 155
LOCAL = 26


def fits(mesh):
    return mesh.shape["seq"] == 8 and mesh.shape["fsdp"] == 4


def solution(mesh):
    return jax.shard_map(
        fused_shards if fits(mesh) else shards,
        mesh=mesh,
        in_specs=(
            P("fsdp", "seq", None),
            P("fsdp", "seq", None),
            P("fsdp", None),
            P("fsdp", None),
            P("fsdp"),
            P("fsdp", None),
            P("fsdp"),
            P("fsdp"),
            P("fsdp"),
            P("fsdp", None),
            P("fsdp"),
            P("fsdp", None),
            P("fsdp"),
            P("fsdp"),
            P("fsdp"),
        ),
        out_specs=(
            P("fsdp", "seq", None),
            P("fsdp", "seq", None),
            P("fsdp", None),
            P("fsdp"),
            P("fsdp", None),
            P("fsdp"),
            P("fsdp"),
            P("fsdp"),
            P("fsdp", None),
            P("fsdp"),
            P("fsdp", None),
            P("fsdp"),
            P("fsdp"),
            P("fsdp"),
        ),
        check_vma=False,
    )
```

```python
from functools import partial

import jax
import jax.numpy as jnp
import numpy as np
import math
from types import SimpleNamespace
from jax import lax
from jax.experimental import pallas as pl
from jax.experimental.pallas import tpu as pltpu
from jax.sharding import PartitionSpec as P

HEADS = 16
HEAD_DIM = 64


norm_epsilon = 1e-05


def rotary(values, positions):
    half = values.shape[-1] // 2
    channel = jnp.arange(half).astype(jnp.float32)
    inverse = 10000.0 ** (-2.0 * channel / values.shape[-1])
    angles = positions[:, None] * inverse[None, :]
    cosine = jnp.cos(angles)[:, None, :]
    sine = jnp.sin(angles)[:, None, :]
    first = values[..., :half]
    second = values[..., half:]
    return jnp.concatenate(
        [first * cosine - second * sine, second * cosine + first * sine], axis=-1
    )


def rotary_back(grads, positions):
    unused, pullback = jax.vjp(lambda inner: rotary(inner, positions), grads)
    return pullback(grads)[0]


def norm_forward(values, gain, shift):
    centre = values - jnp.mean(values, axis=-1, keepdims=True)
    inverse_root = lax.rsqrt(jnp.mean(centre * centre, axis=-1, keepdims=True) + norm_epsilon)
    normal = centre * inverse_root
    return (normal * gain + shift, normal, inverse_root)


def norm_backward(incoming, normal, inverse_root, gain):
    gain_grad = jnp.sum(incoming * normal, axis=0)
    shift_grad = jnp.sum(incoming, axis=0)
    scaled = incoming * gain
    inner = (
        scaled
        - jnp.mean(scaled, axis=-1, keepdims=True)
        - normal * jnp.mean(scaled * normal, axis=-1, keepdims=True)
    )
    return (inner * inverse_root, gain_grad, shift_grad)


def shards(
    hidden_in,
    cotangent,
    segment_ids,
    projection,
    projection_bias,
    output_weight,
    output_bias,
    first_gain,
    first_shift,
    up_weight,
    up_bias,
    down_weight,
    down_bias,
    second_gain,
    second_shift,
):
    bf16 = jnp.bfloat16
    f32 = jnp.float32
    tokens = hidden_in[0]
    local_rows = tokens.shape[0]
    width = tokens.shape[1]
    seq_rank = lax.axis_index("seq")
    positions = (seq_rank * local_rows + jnp.arange(local_rows)).astype(f32)
    segments = segment_ids[0]
    scale = HEAD_DIM ** (-0.5)
    attention_full = (
        lax.all_gather(projection.astype(bf16), "fsdp", axis=0, tiled=True),
        lax.all_gather(projection_bias.astype(bf16), "fsdp", axis=0, tiled=True),
        lax.all_gather(output_weight.astype(bf16), "fsdp", axis=0, tiled=True),
        lax.all_gather(output_bias.astype(bf16), "fsdp", axis=0, tiled=True),
        lax.all_gather(first_gain.astype(bf16), "fsdp", axis=0, tiled=True),
        lax.all_gather(first_shift.astype(bf16), "fsdp", axis=0, tiled=True),
    )
    proj_weight = attention_full[0]
    projected = jnp.dot(tokens, proj_weight, preferred_element_type=f32) + attention_full[1].astype(
        f32
    )
    heads = projected.reshape(local_rows, 3, HEADS, HEAD_DIM)
    queries = rotary(heads[:, 0], positions)
    keys = rotary(heads[:, 1], positions)
    stacked = jnp.stack([queries, keys, heads[:, 2]]).astype(bf16)
    spread = lax.all_to_all(stacked, "seq", split_axis=2, concat_axis=1, tiled=True)
    query_all = spread[0]
    key_all = spread[1]
    value_all = spread[2]
    length = query_all.shape[0]
    local_heads = query_all.shape[1]
    block = min(512, length)
    count = length // block
    query_blocks = query_all.reshape(count, block, local_heads, HEAD_DIM)
    segment_blocks = segments.reshape(count, block)

    def scores_of(query_block, segment_block):
        raw = jnp.einsum("qhd,khd->hqk", query_block, key_all, preferred_element_type=f32) * scale
        allowed = segment_block[:, None] == segments[None, :]
        return jnp.where(allowed[None], raw, -1e30)

    def forward_block(pieces):
        query_block, segment_block = pieces
        scores = scores_of(query_block, segment_block)
        row_max = jnp.max(scores, axis=-1, keepdims=True)
        exponent = jnp.exp(scores - row_max)
        total = jnp.sum(exponent, axis=-1, keepdims=True)
        weights = exponent / total
        context = jnp.einsum(
            "hqk,khd->qhd", weights.astype(bf16), value_all, preferred_element_type=f32
        )
        return (context.astype(bf16), (row_max + jnp.log(total))[..., 0])

    context_blocks, log_totals = lax.map(forward_block, (query_blocks, segment_blocks))
    context_heads = context_blocks.reshape(length, local_heads, HEAD_DIM)
    context_tokens = lax.all_to_all(
        context_heads, "seq", split_axis=0, concat_axis=1, tiled=True
    ).reshape(local_rows, width)
    attended = jnp.dot(
        context_tokens, attention_full[2], preferred_element_type=f32
    ) + attention_full[3].astype(f32)
    gain_one = attention_full[4].astype(f32)
    normed_one, normal_one, inverse_one = norm_forward(
        tokens.astype(f32) + attended, gain_one, attention_full[5].astype(f32)
    )
    feed_full = (
        lax.all_gather(up_weight.astype(bf16), "fsdp", axis=0, tiled=True),
        lax.all_gather(up_bias.astype(bf16), "fsdp", axis=0, tiled=True),
        lax.all_gather(down_weight.astype(bf16), "fsdp", axis=0, tiled=True),
        lax.all_gather(down_bias.astype(bf16), "fsdp", axis=0, tiled=True),
        lax.all_gather(second_gain.astype(bf16), "fsdp", axis=0, tiled=True),
        lax.all_gather(second_shift.astype(bf16), "fsdp", axis=0, tiled=True),
    )
    normed_low = normed_one.astype(bf16)
    lifted = jnp.dot(normed_low, feed_full[0], preferred_element_type=f32) + feed_full[1].astype(
        f32
    )
    activated = jax.nn.gelu(lifted, approximate=False).astype(bf16)
    lowered = jnp.dot(activated, feed_full[2], preferred_element_type=f32) + feed_full[3].astype(
        f32
    )
    gain_two = feed_full[4].astype(f32)
    layer_out, normal_two, inverse_two = norm_forward(
        normed_one + lowered, gain_two, feed_full[5].astype(f32)
    )
    feed_back = (
        lax.all_gather(up_weight.astype(bf16), "fsdp", axis=0, tiled=True),
        lax.all_gather(up_bias.astype(bf16), "fsdp", axis=0, tiled=True),
        lax.all_gather(down_weight.astype(bf16), "fsdp", axis=0, tiled=True),
        lax.all_gather(down_bias.astype(bf16), "fsdp", axis=0, tiled=True),
        lax.all_gather(second_gain.astype(bf16), "fsdp", axis=0, tiled=True),
        lax.all_gather(second_shift.astype(bf16), "fsdp", axis=0, tiled=True),
    )
    attention_back = (
        lax.all_gather(projection.astype(bf16), "fsdp", axis=0, tiled=True),
        lax.all_gather(projection_bias.astype(bf16), "fsdp", axis=0, tiled=True),
        lax.all_gather(output_weight.astype(bf16), "fsdp", axis=0, tiled=True),
        lax.all_gather(output_bias.astype(bf16), "fsdp", axis=0, tiled=True),
        lax.all_gather(first_gain.astype(bf16), "fsdp", axis=0, tiled=True),
        lax.all_gather(first_shift.astype(bf16), "fsdp", axis=0, tiled=True),
    )
    grad_two, second_gain_grad, second_shift_grad = norm_backward(
        cotangent[0].astype(f32), normal_two, inverse_two, gain_two
    )
    lowered_grad = grad_two.astype(bf16)
    down_weight_grad = jnp.einsum("tf,td->fd", activated, lowered_grad, preferred_element_type=f32)
    down_bias_grad = jnp.sum(lowered_grad.astype(f32), axis=0)
    active_grad = jnp.einsum("td,fd->tf", lowered_grad, feed_back[2], preferred_element_type=f32)
    unused, gelu_pull = jax.vjp(partial(jax.nn.gelu, approximate=False), lifted)
    lifted_grad = gelu_pull(active_grad)[0].astype(bf16)
    up_weight_grad = jnp.einsum("td,tf->df", normed_low, lifted_grad, preferred_element_type=f32)
    up_bias_grad = jnp.sum(lifted_grad.astype(f32), axis=0)
    normed_grad = grad_two + jnp.einsum(
        "tf,df->td", lifted_grad, feed_back[0], preferred_element_type=f32
    )
    grad_one, first_gain_grad, first_shift_grad = norm_backward(
        normed_grad, normal_one, inverse_one, attention_back[4].astype(f32)
    )
    attended_grad = grad_one.astype(bf16)
    output_weight_grad = jnp.einsum(
        "tc,td->cd", context_tokens, attended_grad, preferred_element_type=f32
    )
    output_bias_grad = jnp.sum(attended_grad.astype(f32), axis=0)
    context_grad = jnp.einsum(
        "td,cd->tc", attended_grad, attention_back[2], preferred_element_type=f32
    ).astype(bf16)
    context_grad = context_grad.reshape(local_rows, HEADS, HEAD_DIM)
    context_grad_heads = lax.all_to_all(
        context_grad, "seq", split_axis=1, concat_axis=0, tiled=True
    )
    grad_blocks = context_grad_heads.reshape(count, block, local_heads, HEAD_DIM)

    def backward_block(carry, pieces):
        key_grad, value_grad = carry
        query_block, segment_block, grad_block, log_block = pieces
        scores = scores_of(query_block, segment_block)
        weights = jnp.exp(scores - log_block[..., None])
        value_grad = value_grad + jnp.einsum(
            "hqk,qhd->khd", weights.astype(bf16), grad_block, preferred_element_type=f32
        )
        weight_grad = jnp.einsum("qhd,khd->hqk", grad_block, value_all, preferred_element_type=f32)
        centre = jnp.sum(weights * weight_grad, axis=-1, keepdims=True)
        score_grad = (weights * (weight_grad - centre)).astype(bf16)
        query_grad = (
            jnp.einsum("hqk,khd->qhd", score_grad, key_all, preferred_element_type=f32) * scale
        )
        key_grad = (
            key_grad
            + jnp.einsum("hqk,qhd->khd", score_grad, query_block, preferred_element_type=f32)
            * scale
        )
        return ((key_grad, value_grad), query_grad)

    zeros_heads = jnp.zeros((length, local_heads, HEAD_DIM), f32)
    (key_grad, value_grad), query_grad = lax.scan(
        backward_block,
        (zeros_heads, zeros_heads),
        (query_blocks, segment_blocks, grad_blocks, log_totals),
    )
    query_grad = query_grad.reshape(length, local_heads, HEAD_DIM)
    stacked_grad = jnp.stack([query_grad, key_grad, value_grad]).astype(bf16)
    token_heads = lax.all_to_all(stacked_grad, "seq", split_axis=1, concat_axis=2, tiled=True)
    query_back = rotary_back(token_heads[0].astype(f32), positions)
    key_back = rotary_back(token_heads[1].astype(f32), positions)
    projected_grad = jnp.stack([query_back, key_back, token_heads[2].astype(f32)], axis=1)
    projected_grad = projected_grad.reshape(local_rows, 3 * width).astype(bf16)
    projection_grad = jnp.einsum("td,te->de", tokens, projected_grad, preferred_element_type=f32)
    projection_bias_grad = jnp.sum(projected_grad.astype(f32), axis=0)
    input_grad = grad_one + jnp.einsum(
        "te,de->td", projected_grad, attention_back[0], preferred_element_type=f32
    )
    every_shard = (
        lax.psum_scatter(
            projection_grad.astype(jnp.bfloat16), "fsdp", scatter_dimension=0, tiled=True
        ).astype(jnp.float32),
        lax.psum_scatter(
            projection_bias_grad.astype(jnp.bfloat16), "fsdp", scatter_dimension=0, tiled=True
        ).astype(jnp.float32),
        lax.psum_scatter(
            output_weight_grad.astype(jnp.bfloat16), "fsdp", scatter_dimension=0, tiled=True
        ).astype(jnp.float32),
        lax.psum_scatter(
            output_bias_grad.astype(jnp.bfloat16), "fsdp", scatter_dimension=0, tiled=True
        ).astype(jnp.float32),
        lax.psum_scatter(
            first_gain_grad.astype(jnp.bfloat16), "fsdp", scatter_dimension=0, tiled=True
        ).astype(jnp.float32),
        lax.psum_scatter(
            first_shift_grad.astype(jnp.bfloat16), "fsdp", scatter_dimension=0, tiled=True
        ).astype(jnp.float32),
        lax.psum_scatter(
            up_weight_grad.astype(jnp.bfloat16), "fsdp", scatter_dimension=0, tiled=True
        ).astype(jnp.float32),
        lax.psum_scatter(
            up_bias_grad.astype(jnp.bfloat16), "fsdp", scatter_dimension=0, tiled=True
        ).astype(jnp.float32),
        lax.psum_scatter(
            down_weight_grad.astype(jnp.bfloat16), "fsdp", scatter_dimension=0, tiled=True
        ).astype(jnp.float32),
        lax.psum_scatter(
            down_bias_grad.astype(jnp.bfloat16), "fsdp", scatter_dimension=0, tiled=True
        ).astype(jnp.float32),
        lax.psum_scatter(
            second_gain_grad.astype(jnp.bfloat16), "fsdp", scatter_dimension=0, tiled=True
        ).astype(jnp.float32),
        lax.psum_scatter(
            second_shift_grad.astype(jnp.bfloat16), "fsdp", scatter_dimension=0, tiled=True
        ).astype(jnp.float32),
    )
    finals = (
        lax.psum(every_shard[0].astype(jnp.bfloat16), "seq").astype(jnp.float32),
        lax.psum(every_shard[1].astype(jnp.bfloat16), "seq").astype(jnp.float32),
        lax.psum(every_shard[2].astype(jnp.bfloat16), "seq").astype(jnp.float32),
        lax.psum(every_shard[3].astype(jnp.bfloat16), "seq").astype(jnp.float32),
        lax.psum(every_shard[4].astype(jnp.bfloat16), "seq").astype(jnp.float32),
        lax.psum(every_shard[5].astype(jnp.bfloat16), "seq").astype(jnp.float32),
        lax.psum(every_shard[6].astype(jnp.bfloat16), "seq").astype(jnp.float32),
        lax.psum(every_shard[7].astype(jnp.bfloat16), "seq").astype(jnp.float32),
        lax.psum(every_shard[8].astype(jnp.bfloat16), "seq").astype(jnp.float32),
        lax.psum(every_shard[9].astype(jnp.bfloat16), "seq").astype(jnp.float32),
        lax.psum(every_shard[10].astype(jnp.bfloat16), "seq").astype(jnp.float32),
        lax.psum(every_shard[11].astype(jnp.bfloat16), "seq").astype(jnp.float32),
    )
    return (
        layer_out.astype(bf16)[None],
        input_grad.astype(bf16)[None],
        finals[0],
        finals[1],
        finals[2],
        finals[3],
        finals[4],
        finals[5],
        finals[6],
        finals[7],
        finals[8],
        finals[9],
        finals[10],
        finals[11],
    )


MESH = pl.DeviceIdType.MESH
NN = (((1,), (0,)), ((), ()))
NT = (((1,), (1,)), ((), ()))
TN = (((0,), (0,)), ((), ()))
f32 = jnp.float32
bf16 = jnp.bfloat16
MASKED = -1e30


def mm(left, right, dims=NN):
    return lax.dot_general(left, right, dims, preferred_element_type=f32)


def block_of(index, size):
    return pl.ds(pl.multiple_of(index * size, size), size)


def flip(bit, other):
    return bit + other - 2 * bit * other


def fused_layer(sizes, *refs):
    r = SimpleNamespace(**dict(zip(sizes.names, refs)))
    T, D, L, F = sizes.T, sizes.D, sizes.L, sizes.F
    S, Z = 8, 4
    KW = D // Z
    UZ = F // Z
    C = 128
    T2 = 2 * T
    first_row = sizes.first_row
    ssem, rsem, lsem = r.ssem, r.rsem, r.lsem

    s = lax.axis_index("seq")
    z = lax.axis_index("fsdp")
    core, xbit, ybit = s % 2, (s // 2) % 2, s // 4
    zlow, zhigh = z % 2, z // 2

    def ps(k):
        return flip(core, k % 2) + 2 * flip(xbit, (k // 2) % 2) + 4 * flip(ybit, k // 4)

    def pz(k):
        return flip(zlow, k % 2) + 2 * flip(zhigh, k // 2)

    inner = flip(zlow, zhigh) == 1

    def by_plane(for_inner, for_outer):
        pl.when(inner)(for_inner)
        pl.when(jnp.logical_not(inner))(for_outer)

    def chip_of(j):
        return flip(xbit, j % 2) + 2 * flip(ybit, j // 2)

    counter = [0, 0, 0]
    closing = []

    def take(which, n=1):
        counter[which] += n
        return counter[which] - n

    def landings(n=1):
        return take(0, n)

    def size(ref):
        return math.prod(ref.shape) * jnp.dtype(ref.dtype).itemsize

    def extent(n):
        if n <= size(r.c_f):
            return r.c_f.at[pl.ds(0, n * L // size(r.c_f))]
        return r.y_all.at[pl.ds(0, n * L // size(r.y_all))]

    def arrived(ref, slot):
        pltpu.make_async_copy(ref, ref, rsem.at[slot]).wait()

    class Batch:
        def __init__(self, count, like):
            self.slot, self.bytes, self.open = take(1), count * size(like), True
            self.one, self.shares = size(like), None
            closing.append(self)

        def drain(self, n):
            everything = extent(n)
            pltpu.make_async_copy(everything, everything, ssem.at[self.slot]).wait()

        def send(self, src, dst, slot, dev):
            pltpu.make_async_remote_copy(
                src_ref=src, dst_ref=dst, send_sem=ssem.at[self.slot], recv_sem=rsem.at[slot],
                device_id=dev, device_id_type=MESH).start()

        def close(self):
            if self.open and self.shares:
                by_plane(*[partial(self.drain, n * self.one) for n in self.shares])
            elif self.open:
                self.drain(self.bytes)
            self.open = False

    def local(src, dst):
        copy = pltpu.make_async_copy(src, dst, lsem.at[take(2)])
        copy.start()
        return copy

    class Gather:
        def __init__(self, place, at_once=True):
            self.place, self.at_once = place, at_once
            self.batch = Batch(7, place(0))
            self.near, self.across = landings(4), landings(2)
            self.other = landings() if at_once else landings(4)

        def part(self, ref, i):
            n = ref.shape[0] // 2
            return ref.at[pl.ds(i * n, n)]

        def start(self, src=None):
            mine = self.place(s)
            src = mine if src is None else src
            for slot, half, k in ((0, 0, 2), (3, 1, 4), (1, 1, 2), (2, 0, 4)):
                self.batch.send(self.part(src, half), self.part(mine, half), self.near + slot, (ps(k), z))
            self.batch.send(src, mine, self.other, (ps(1), z))

        def to_partner(self, k):
            there = self.place(ps(k))
            self.batch.send(there, there, self.other + (0 if self.at_once else k // 2), (ps(1), z))

        def pass_near(self):
            along_x, along_y = self.place(ps(2)), self.place(ps(4))
            first, second = self.part(along_x, 0), self.part(along_y, 1)
            arrived(first, self.near)
            self.batch.send(first, first, self.across, (ps(4), z))
            arrived(second, self.near + 3)
            self.batch.send(second, second, self.across + 1, (ps(2), z))
            arrived(self.part(along_x, 1), self.near + 1)
            self.to_partner(2)
            arrived(self.part(along_y, 0), self.near + 2)
            self.to_partner(4)

        def pass_far(self):
            far = self.place(ps(6))
            arrived(self.part(far, 0), self.across)
            arrived(self.part(far, 1), self.across + 1)
            self.to_partner(6)

        def pass_all(self):
            self.pass_near()
            self.pass_far()

        def wait(self, k=None):
            if self.at_once:
                arrived(extent(4 * size(self.place(0))), self.other)
            else:
                arrived(self.place(ps(k)), self.other + k // 2)

    class Spread:
        def __init__(self, place):
            self.place, self.batch, self.base = place, Batch(3, place(0)), landings(3)

        def start(self, *which):
            mine = self.place(z)
            for k in which or (2, 1):
                self.batch.send(mine, mine, self.base + k - 1, (s, pz(k)))

        def pass_on(self):
            there = self.place(pz(2))
            arrived(there, self.base + 1)
            self.batch.send(there, there, self.base + 2, (s, pz(1)))

        def meet(self):
            def for_inner():
                self.pass_on()
                self.start(3)
            by_plane(for_inner, lambda: arrived(self.place(pz(2)), self.base + 1))
            self.batch.shares = (4, 2)

        def wait(self):
            for k in (1, 3):
                arrived(self.place(pz(k)), self.base + k - 1)

        def wait_all(self):
            for k in (1, 2, 3):
                arrived(self.place(pz(k)), self.base + k - 1)

    class Fold:
        def __init__(self, parts, landing, passing, first=0, count=None):
            self.rows = pl.ds(first, count or passing.shape[0])
            self.parts, self.landing, self.passing = parts, landing, passing.at[self.rows]
            self.batch, self.base = Batch(3, self.passing), landings(3)

        def start(self):
            for i, k in ((1, 3), (0, 1)):
                self.batch.send(self.parts.at[pz(k), self.rows], self.landing.at[i, self.rows], self.base + i, (s, pz(1)))

        def middle(self):
            arrived(self.landing.at[1, self.rows], self.base + 1)
            self.passing[...] = (self.parts[pz(2), self.rows, :].astype(f32)
                                 + self.landing[1, self.rows, :].astype(f32)).astype(bf16)
            self.batch.send(self.passing, self.landing.at[2, self.rows], self.base + 2, (s, pz(2)))

        def finish(self):
            arrived(self.landing.at[0, self.rows], self.base)
            arrived(self.landing.at[2, self.rows], self.base + 2)
            return (self.parts[z, self.rows, :].astype(f32) + self.landing[0, self.rows, :].astype(f32)
                    + self.landing[2, self.rows, :].astype(f32)).astype(bf16)

    class FoldInner:
        def __init__(self, parts, landing, passing, first=0, count=None):
            self.rows = pl.ds(first, count or passing.shape[0])
            self.parts, self.landing, self.passing = parts, landing, passing.at[self.rows]
            self.batch, self.base = Batch(3, self.passing), landings(4)

            @pl.when(jnp.logical_not(inner))
            def _():
                landing[3, self.rows, :] = jnp.zeros(self.passing.shape, bf16)

        def send(self, slab, i, k):
            self.batch.send(self.parts.at[slab, self.rows], self.landing.at[i, self.rows], self.base + i, (s, pz(k)))

        def start(self):
            by_plane(lambda: None, lambda: self.send(pz(3), 1, 1))
            self.send(pz(1), 0, 1)
            by_plane(lambda: self.send(pz(3), 3, 3), lambda: None)

        def middle(self):
            def for_inner():
                arrived(self.landing.at[1, self.rows], self.base + 1)
                self.passing[...] = (self.parts[pz(2), self.rows, :].astype(f32)
                                     + self.landing[1, self.rows, :].astype(f32)).astype(bf16)
                self.batch.send(self.passing, self.landing.at[2, self.rows], self.base + 2, (s, pz(2)))
            by_plane(for_inner, lambda: self.send(pz(2), 2, 2))

        def finish(self):
            arrived(self.landing.at[0, self.rows], self.base)
            arrived(self.landing.at[2, self.rows], self.base + 2)
            pl.when(inner)(lambda: arrived(self.landing.at[3, self.rows], self.base + 3))
            total = self.parts[z, self.rows, :].astype(f32)
            for i in (0, 2, 3):
                total = total + self.landing[i, self.rows, :].astype(f32)
            return total.astype(bf16)

    class Scatter:
        def __init__(self, parts, low, mid, high, first=0, count=T):
            self.parts, self.low, self.mid, self.high = parts, low, mid, high
            self.first, self.count, self.window = first, count, pl.ds(first, count)
            self.batch = Batch(7, mid.at[0, self.window])
            self.base, self.far, self.last = landings(4), landings(2), landings()

        def rows_of(self, which):
            return pl.ds(pl.multiple_of(which * T + self.first, self.count), self.count)

        def half(self, ref, j, i):
            return ref.at[j, self.window, pl.ds(i * (D // 2), D // 2)]

        def send(self, j, i, slot, k):
            self.batch.send(self.half(self.mid, j, i), self.half(self.high, j, i), slot, (ps(k), z))

        def pair(self, j):
            self.batch.send(self.parts.at[j, self.rows_of(1 - core)], self.low.at[j, self.window],
                            self.base + j, (ps(1), z))

        def onward(self, j):
            arrived(self.low.at[j, self.window], self.base + j)
            own = self.parts[j, self.rows_of(core), :].astype(f32)
            self.mid[j, self.window, :] = (own + self.low[j, self.window, :].astype(f32)).astype(bf16)
            if j == 1:
                self.send(1, 0, self.last, 2)
            elif j == 2:
                self.send(2, 1, self.last, 4)
            else:
                self.send(3, 0, self.far, 2)
                self.send(3, 1, self.far + 1, 4)

        def cross(self):
            for j, i, k in ((2, 0, 4), (1, 1, 2)):
                arrived(self.half(self.high, 3, i), self.far + i)
                ref = self.half(self.mid, j, i)
                ref[...] = (ref[...].astype(f32) + self.half(self.high, 3, i)[...].astype(f32)).astype(bf16)
                self.send(j, i, self.last, k)

        def ready(self):
            arrived(self.low.at[0, self.window], self.base)
            arrived(self.high.at[pl.ds(1, 2), self.window], self.last)

        def rows(self, at, n):
            own = self.parts[0, pl.ds(pl.multiple_of(core * T + at, n), n), :].astype(f32)
            total = own + self.low[0, pl.ds(at, n), :].astype(f32)
            for j in (1, 2):
                total = total + self.high[j, pl.ds(at, n), :].astype(f32)
            return total

    class Share:
        def __init__(self, count, like):
            self.count, self.batch, self.slot, self.bytes = count, Batch(count, like), landings(), count * size(like)

        def plane(self, src, dst):
            for k in (6, 7, 2, 3, 4, 5, 1):
                self.batch.send(src(ps(k)), dst, self.slot, (ps(k), z))

        def column(self, src, dst):
            for k in (2, 3, 1):
                self.batch.send(src, dst, self.slot, (s, pz(k)))

        def wait(self):
            arrived(extent(self.bytes), self.slot)

    def loop(count, body, unroll=1):
        def step(i, carry):
            body(i)
            return carry
        lax.fori_loop(0, count, step, 0, unroll=unroll)

    def at(i, n):
        return pl.multiple_of(i * n, n)

    def turn(src, dst):
        def one(i):
            dst[:, pl.ds(at(i, T), T)] = jnp.transpose(src[pl.ds(at(i, T), T), :])
        loop(L // T, one)

    vec, vecg = r.vec, r.vecg

    OUTPUT_BIAS, FIRST_GAIN, FIRST_SHIFT, DOWN_BIAS, SECOND_GAIN, SECOND_SHIFT, PROJECTION_BIAS, UP_BIAS = range(8)
    wide = ((first_row.output_bias, OUTPUT_BIAS), (first_row.first_gain, FIRST_GAIN),
            (first_row.first_shift, FIRST_SHIFT), (first_row.down_bias, DOWN_BIAS),
            (first_row.second_gain, SECOND_GAIN), (first_row.second_shift, SECOND_SHIFT))

    def row(i, width=D):
        return vec[i:i + 1, :width]

    lanes = lax.broadcasted_iota(jnp.int32, (T, C), 1)
    low_head = lanes < HEAD_DIM

    def swapped(w):
        low_half = lax.broadcasted_iota(jnp.int32, w.shape, 1) % HEAD_DIM < HEAD_DIM // 2
        return jnp.where(low_half, pltpu.roll(w, C - HEAD_DIM // 2, 1), pltpu.roll(w, HEAD_DIM // 2, 1))

    def stacked(w):
        nothing = jnp.zeros_like(w)
        return jnp.concatenate([jnp.where(low_head, w, nothing), jnp.where(low_head, nothing, w)], axis=0)

    def unstacked(w):
        return jnp.where(low_head, w[:T], w[T:])

    barrier = pltpu.get_barrier_semaphore()
    for k in range(1, S):
        pl.semaphore_signal(barrier, inc=1, device_id=(ps(k), z), device_id_type=MESH)
    for k in range(1, Z):
        pl.semaphore_signal(barrier, inc=1, device_id=(s, pz(k)), device_id_type=MESH)
    x_ref, ct_ref = r.v_x, r.v_ct
    x_load = local(r.x, x_ref)
    wo_load = local(r.wo.at[:, block_of(s, C)], r.st_wo)
    proj_loads = [local(r.proj.at[:, block_of(i * (D // C) + s, C)], r.st_proj.at[:, pl.ds(i * C, C)])
                  for i in range(3)]
    raw = ((r.b_projection, r.v_projection, first_row.projection_bias), (r.b_output, r.v_output, first_row.output_bias),
           (r.gain1, r.v_gain1, first_row.first_gain), (r.shift1, r.v_shift1, first_row.first_shift),
           (r.b_up, r.v_up, first_row.up_bias), (r.b_down, r.v_down, first_row.down_bias),
           (r.gain2, r.v_gain2, first_row.second_gain), (r.shift2, r.v_shift2, first_row.second_shift))
    raw_loads = [local(source, ref) for source, ref, _ in raw]
    seg_load = local(r.seg, r.v_seg)
    up_loads = [local(r.up.at[:, block_of(i * (D // C) + s, C)], r.st_up.at[:, pl.ds(i * C, C)])
                for i in range(Z)]
    dn_load = local(r.dn.at[block_of(s, UZ), :], r.st_dn)
    late_loads = [local(r.cos, r.v_cos), local(r.sin, r.v_sin), local(r.ct, ct_ref)]
    cos_ref, sin_ref = r.v_cos, r.v_sin

    x_all, w_qkv, w_o, w_up, w_dn = r.x_all, r.w_qkv, r.w_o, r.w_up, r.w_dn
    gather_x = Gather(lambda o: x_all.at[block_of(o, T)])
    spread_qkv = Spread(lambda p: w_qkv.at[block_of(p, KW)])
    spread_o = Spread(lambda p: w_o.at[block_of(p, KW), block_of(s, C)])
    spread_up = Spread(lambda p: w_up.at[block_of(p, KW)])
    spread_dn = Spread(lambda p: w_dn.at[block_of(p, UZ)])
    gather_o = Gather(lambda o: w_o.at[:, block_of(o, C)])
    wo_load.wait()
    w_o[block_of(z, KW), block_of(s, C)] = r.st_wo[...].astype(bf16)
    for copy in proj_loads:
        copy.wait()
    w_qkv[block_of(z, KW), :] = r.st_proj[...].astype(bf16)
    x_load.wait()
    pl.semaphore_wait(barrier, S + Z - 2)
    spread_o.start(2, 3, 1)
    spread_qkv.start()
    gather_x.start(x_ref)

    small, small_all, seg_c, seg_r = r.small, r.small_all, r.seg_c, r.seg_r
    for copy, (_, ref, start) in zip(raw_loads, raw):
        copy.wait()
        if ref.shape[1] == C:
            small[start:start + ref.shape[0], :] = ref[...].astype(bf16).astype(f32)
        else:
            for i in range(ref.shape[1] // C):
                small[start + i:start + i + 1, :] = ref[0:1, i * C:(i + 1) * C].astype(bf16).astype(f32)
    x_all[block_of(s, T), :] = x_ref[...]
    vecg[...] = jnp.zeros((8, D), f32)
    seg_load.wait()
    seg_r[...] = jnp.broadcast_to(r.v_seg[...].astype(f32), (8, L))

    def seg_turn(i):
        here = pl.ds(at(i, T), T)
        seg_c[here, :] = jnp.transpose(jnp.broadcast_to(seg_r[0:1, here], (T, T)))
    loop(L // T, seg_turn)
    for copy in up_loads:
        copy.wait()
    w_up[block_of(z, KW), :] = r.st_up[...].astype(bf16)
    dn_load.wait()
    w_dn[block_of(z, UZ), :] = r.st_dn[...].astype(bf16)
    share_small = Share(3, small)
    small_all[z] = small[...]

    gather_x.pass_near()
    spread_o.wait_all()
    gather_o.start()
    gather_x.pass_far()
    gather_x.wait()
    spread_qkv.pass_on()
    share_small.column(small, small_all.at[z])
    spread_up.start()
    x_t = r.x_t
    turn(x_all, x_t)
    for copy in late_loads:
        copy.wait()
    gather_o.pass_near()
    spread_qkv.wait()
    share_small.wait()
    for p in range(Z):
        for start, i in wide:
            for half in range(KW // C):
                at_row = start + half
                lane = (p * (KW // C) + half) * C
                vec[i:i + 1, lane:lane + C] = small_all[p, at_row:at_row + 1, :]
        vec[7:8, p * C:(p + 1) * C] = small_all[p, pl.ds(first_row.up_bias + s, 1), :]
    per = 3 * D // (C * Z)
    for t in range(3):
        number = t * (D // C) + s
        vec[6:7, t * C:(t + 1) * C] = small_all[number // per, pl.ds(first_row.projection_bias + number % per, 1), :]

    q_ref, k_ref, v_ref = r.q, r.k, r.v
    scale = HEAD_DIM ** -0.5

    def project(i):
        here = pl.ds(at(i, T2), T2)
        out = mm(x_all[here, :], w_qkv[...]) + row(PROJECTION_BIAS, 3 * C)
        cosine, sine = cos_ref[here, :], sin_ref[here, :]
        q0, k0 = out[:, :C], out[:, C:2 * C]
        q_ref[here, :] = ((q0 * cosine + swapped(q0) * sine).astype(bf16).astype(f32) * scale).astype(bf16)
        k_ref[here, :] = (k0 * cosine + swapped(k0) * sine).astype(bf16)
        v_ref[here, :] = out[:, 2 * C:].astype(bf16)
    loop(L // T2, project)
    gather_o.pass_far()

    lse, c_f, c_heads, c_tok = r.lse, r.c_f, r.c_heads, r.c_tok
    R = 16

    def same_document(here):
        return jnp.tile(seg_c[here, :], (1, L // C)) == seg_r[0:1, :]

    def both(w):
        return jnp.concatenate([w, w], axis=0)

    def attend(o):
        here = block_of(o, T)
        score = jnp.where(both(same_document(here)), mm(stacked(q_ref[here, :]), k_ref[...], NT), MASKED)
        top = jnp.max(score, axis=-1, keepdims=True)
        power = jnp.exp(score - top)
        total = jnp.sum(power, axis=-1, keepdims=True)
        context = unstacked(mm(power.astype(bf16), v_ref[...]) * (1.0 / total))
        c_f[here, :] = context
        c_heads[here, :] = context.astype(bf16)
        logs = jnp.broadcast_to(top + jnp.log(total), (T2, C))
        for h in range(2):
            lse[h:h + 1, here] = jnp.transpose(logs[h * T:(h + 1) * T, :])[0:1, :]

    share_c = Share(7, c_heads.at[pl.ds(0, T)])

    def attend_and_send(i):
        k = 7 - i
        attend(ps(k))

        @pl.when(k > 0)
        def _():
            share_c.batch.send(c_heads.at[block_of(ps(k), T)], c_tok.at[:, block_of(s, C)], share_c.slot, (ps(k), z))
    loop(8, attend_and_send)
    spread_up.meet()
    spread_dn.start()
    c_tok[:, block_of(s, C)] = c_heads[block_of(s, T), :]
    gather_o.wait()
    share_c.wait()

    a_buf = r.a_buf
    a_buf[...] = mm(c_tok[...], w_o[...])
    n1, y1, r1, y_all = r.n1, r.y1, r.r1, r.y_all

    def norm(h):
        centre = h - jnp.mean(h, axis=-1, keepdims=True)
        root = lax.rsqrt(jnp.mean(centre * centre, axis=-1, keepdims=True) + norm_epsilon)
        return centre * root, root

    def first_norm(i):
        rows = pl.ds(at(i, R), R)
        normal, root = norm(x_ref[rows, :].astype(f32) + a_buf[rows, :] + row(OUTPUT_BIAS))
        out = normal * row(FIRST_GAIN) + row(FIRST_SHIFT)
        n1[rows, :] = normal
        r1[rows, :] = jnp.broadcast_to(root, (R, C))
        y1[rows, :] = out
        y_all[pl.ds(pl.multiple_of(s * T + i * R, R), R), :] = out.astype(bf16)
    loop(T // R, first_norm, 4)
    gather_y = Gather(lambda o: y_all.at[block_of(o, T)], False)
    gather_y.start()
    c_all = r.c_all
    gather_c = Gather(lambda o: c_all.at[block_of(o, T)])
    c_all[block_of(s, T), :] = c_tok[...]

    u_buf, g_ref, d_ref, du_ref, dz_all = r.u_buf, r.g, r.d, r.du, r.dz_all
    parts, mid = r.parts, r.mid
    spread_up.wait()
    E = 32

    def lift(j):
        q = chip_of(j)
        u_buf[...] = mm(y_all[block_of(q, T2), :], w_up[...])

        def chunk(i):
            rows = pl.ds(at(i, E), E)
            there = pl.ds(pl.multiple_of(q * T2 + i * E, E), E)
            u = u_buf[rows, :] + row(UP_BIAS, F)
            share = 0.5 + 0.5 * lax.erf(u * (0.5 ** 0.5))
            g_ref[there, :] = (u * share).astype(bf16)
            d_ref[there, :] = share + u * (jnp.exp(-0.5 * u * u) * 0.3989422804014327)
        loop(T2 // E, chunk)

    def lower(j):
        parts[j] = mm(g_ref[block_of(chip_of(j), T2), :], w_dn[...]).astype(bf16)

    H = T // 2
    folds_z = [Scatter(parts, r.low0, mid, r.high0, i * H, H) for i in range(2)]
    y_t, g_t = r.y_t, r.g_t
    gather_y.wait(1)
    lift(0)
    gather_y.pass_near()
    gather_y.wait(3)
    lift(1)
    gather_y.wait(5)
    lift(2)
    spread_dn.meet()
    gather_y.pass_far()
    gather_c.start(c_tok)
    gather_y.wait(7)
    lift(3)
    turn(y_all, y_t)
    turn(g_ref, g_t)
    spread_dn.wait()
    for j in (3, 1, 2):
        lower(j)
        for fold in folds_z:
            fold.pair(j)
    for j in (3, 1, 2):
        folds_z[0].onward(j)
    folds_z[1].onward(3)
    lower(0)
    for fold in folds_z:
        fold.pair(0)
    folds_z[0].cross()
    folds_z[1].onward(1)
    folds_z[1].onward(2)
    folds_z[1].cross()
    folds_z[0].ready()

    dh2, out_ref = r.dh2, r.out

    def add_row(i, value):
        vecg[i:i + 1, :] = vecg[i:i + 1, :] + jnp.sum(value, axis=0, keepdims=True)

    def norm_back(incoming, normal, root, gain):
        scaled = incoming * gain
        return root * (scaled - jnp.mean(scaled, axis=-1, keepdims=True)
                       - normal * jnp.mean(scaled * normal, axis=-1, keepdims=True))

    def second_norm(i):
        start = at(i, R)
        rows = pl.ds(start, R)
        normal, root = norm(y1[rows, :] + folds_z[0].rows(start, R) + row(DOWN_BIAS))
        out_ref[rows, :] = (normal * row(SECOND_GAIN) + row(SECOND_SHIFT)).astype(bf16)
        e = ct_ref[rows, :].astype(f32)
        grad = norm_back(e, normal, root, row(SECOND_GAIN))
        dh2[rows, :] = grad
        dz = grad.astype(bf16)
        dz_all[pl.ds(pl.multiple_of(s * T + i * R, R), R), :] = dz
        add_row(3, dz.astype(f32))
        add_row(4, e * normal)
        add_row(5, e)
    gathers_dz = [Gather(lambda o, i=i: dz_all.at[block_of(2 * o + i, H)], False) for i in range(2)]
    loop(H // R, second_norm, 2)
    gathers_dz[0].start()
    folds_z[1].ready()
    loop(H // R, lambda i: second_norm(i + H // R), 2)
    gathers_dz[1].start()
    for fold in folds_z:
        fold.batch.close()

    colg = r.colg
    colg[...] = jnp.zeros((8, F), f32)

    def unlower(j):
        q = chip_of(j)
        u_buf[...] = mm(dz_all[block_of(q, T2), :], w_dn[...], NT)

        def chunk(i):
            rows = pl.ds(at(i, E), E)
            there = pl.ds(pl.multiple_of(q * T2 + i * E, E), E)
            du = (u_buf[rows, :] * d_ref[there, :]).astype(bf16)
            du_ref[there, :] = du
            colg[0:1, :] = colg[0:1, :] + jnp.sum(du.astype(f32), axis=0, keepdims=True)
        loop(T2 // E, chunk)

    def unlift(j):
        parts[j] = mm(du_ref[block_of(chip_of(j), T2), :], w_up[...], NT).astype(bf16)

    fold_y = Scatter(parts, r.low1, mid, r.high1)
    gd_part, gu_part = r.gd_part, r.gu_part
    folds_dn = [Fold(gd_part, r.gd_land, r.gd_pass, i * (UZ // 2), UZ // 2) for i in range(2)]
    folds_up = [Fold(gu_part, r.gu_land, r.gu_pass, i * (KW // 2), KW // 2) for i in range(2)]

    def down_grad(k):
        gd_part[pz(k)] = mm(g_t[block_of(pz(k), UZ), :], dz_all[...]).astype(bf16)

    def up_grad(k):
        gu_part[pz(k)] = mm(y_t[block_of(pz(k), KW), :], du_ref[...]).astype(bf16)

    def dz_wait(k):
        for gather in gathers_dz:
            gather.wait(k)
    dz_wait(1)
    unlower(0)
    unlift(0)
    fold_y.pair(0)
    gathers_dz[0].pass_near()
    gathers_dz[1].pass_near()
    dz_wait(3)
    unlower(1)
    unlift(1)
    fold_y.pair(1)
    gathers_dz[0].pass_far()
    dz_wait(5)
    unlower(2)
    fold_y.onward(1)
    unlift(2)
    fold_y.pair(2)
    gathers_dz[1].pass_far()
    fold_y.onward(2)
    dz_wait(7)
    down_grad(3)
    down_grad(1)
    folds_dn[0].start()
    folds_dn[1].start()
    unlower(3)
    unlift(3)
    fold_y.pair(3)
    up_grad(3)
    fold_y.onward(3)

    up_grad(1)
    down_grad(2)
    fold_y.cross()
    folds_dn[0].middle()
    folds_up[0].start()
    down_grad(0)
    up_grad(2)
    up_grad(0)
    fold_y.ready()

    dh1, da = r.dh1, r.da

    def first_back(i):
        start = at(i, R)
        rows = pl.ds(start, R)
        incoming = dh2[rows, :] + fold_y.rows(start, R)
        normal = n1[rows, :]
        grad = norm_back(incoming, normal, r1[rows, 0:1], row(FIRST_GAIN))
        dh1[rows, :] = grad
        low = grad.astype(bf16)
        da[rows, :] = low
        add_row(0, low.astype(f32))
        add_row(1, incoming * normal)
        add_row(2, incoming)
    loop(T // R, first_back, 2)
    fold_y.batch.close()

    dc_tok, dc = r.dc_tok, r.dc
    dc_tok[...] = mm(da[...], w_o[...], NT).astype(bf16)
    share_dc = Share(7, dc.at[pl.ds(0, T)])
    share_dc.plane(lambda o: dc_tok.at[:, block_of(o, C)], dc.at[block_of(s, T)])
    dc[block_of(s, T), :] = dc_tok[:, block_of(s, C)]
    da_cols = r.da_cols
    share_da = Share(7, da_cols.at[pl.ds(0, T)])
    share_da.plane(lambda o: da.at[:, block_of(o, C)], da_cols.at[block_of(s, T)])
    da_cols[block_of(s, T), :] = da[:, block_of(s, C)]
    vec_z, vec_all = r.vec_z, r.vec_all
    share_vec = Share(3, vec_z.at[0])
    for k in (2, 3, 1):
        share_vec.batch.send(vecg.at[:, block_of(pz(k), KW)], vec_z.at[z], share_vec.slot, (s, pz(k)))
    vec_z[z] = vecg[:, block_of(z, KW)]
    folds_dn[1].middle()
    folds_up[1].start()
    share_dc.wait()

    delta, dq, dproj = r.delta, r.dq, r.dproj

    def deltas(i):
        here = pl.ds(at(i, T), T)
        turned = jnp.transpose(dc[here, :].astype(f32) * c_f[here, :])
        delta[0:1, here] = jnp.sum(turned[:HEAD_DIM], axis=0, keepdims=True)
        delta[1:2, here] = jnp.sum(turned[HEAD_DIM:], axis=0, keepdims=True)
        dq[here, :] = jnp.zeros((T, C), f32)
    loop(L // T, deltas)

    def attend_back(i):
        here = pl.ds(at(i, T), T)
        same = same_document(here)
        k_here, v_here = k_ref[here, :], v_ref[here, :]
        keys, values, slopes = [], [], []
        for h in range(2):
            own = low_head if h == 0 else jnp.logical_not(low_head)
            nothing = jnp.zeros_like(k_here)
            key = jnp.where(own, k_here, nothing)
            weight = jnp.exp(jnp.where(same, mm(key, q_ref[...], NT), MASKED) - lse[h:h + 1, :])
            slope = mm(jnp.where(own, v_here, nothing), dc[...], NT) - delta[h:h + 1, :]
            slopes.append((weight * slope).astype(bf16))
            values.append(mm(weight.astype(bf16), dc[...]))
            keys.append(key)
        dv = jnp.where(low_head, values[0], values[1]).astype(bf16)
        dk = jnp.where(low_head, mm(slopes[0], q_ref[...]), mm(slopes[1], q_ref[...])).astype(bf16).astype(f32)
        dproj[here, 2 * C:] = dv
        dproj[here, C:2 * C] = (dk * cos_ref[here, :] - swapped(dk) * sin_ref[here, :]).astype(bf16)
        dq[...] = dq[...] + mm(jnp.concatenate(slopes, axis=0), jnp.concatenate(keys, axis=0), TN)

    gd_all, gu_all, go_all, gqk_all, gv_all = r.gd, r.gu, r.go, r.gqk, r.gv
    gather_gd = Gather(lambda o: gd_all.at[block_of(o, UZ)])
    gather_gu = Gather(lambda o: gu_all.at[o])
    gather_go = Gather(lambda o: go_all.at[:, block_of(o, C)])
    gather_gqk = Gather(lambda o: gqk_all.at[o])
    gather_gv = Gather(lambda o: gv_all.at[o])
    go_part = r.go_part
    fold_o = FoldInner(go_part, r.go_land, r.go_pass)

    def out_grad(k):
        go_part[pz(k)] = mm(c_all[:, block_of(pz(k), KW)], da_cols[...], TN).astype(bf16)

    def attend_back_and_fold(i):
        attend_back(i)

        @pl.when(i == 0)
        def _():
            gather_c.pass_near()

        @pl.when(i == 5)
        def _():
            for part in range(2):
                at_row = pl.multiple_of(s * UZ + part * (UZ // 2), UZ // 2)
                gd_all[pl.ds(at_row, UZ // 2), :] = folds_dn[part].finish()
            gather_gd.start()

        @pl.when(i == 6)
        def _():
            folds_up[0].middle()
            gather_c.pass_far()
    loop(L // T, attend_back_and_fold)


    def dq_rows(i):
        here = pl.ds(at(i, T), T)
        whole = (dq[here, :] * scale).astype(bf16).astype(f32)
        dproj[here, :C] = (whole * cos_ref[here, :] - swapped(whole) * sin_ref[here, :]).astype(bf16)
        colg[1:2, :3 * C] = colg[1:2, :3 * C] + jnp.sum(dproj[here, :].astype(f32), axis=0, keepdims=True)
    loop(L // T, dq_rows)

    gqk_part, gv_part = r.gqk_part, r.gv_part
    fold_qk = Fold(gqk_part, r.gqk_land, r.gqk_pass)
    fold_v = FoldInner(gv_part, r.gv_land, r.gv_pass)

    def projection_grad(k):
        grad = mm(x_t[block_of(pz(k), KW), :], dproj[...]).astype(bf16)
        gqk_part[pz(k)] = grad[:, :2 * C]
        gv_part[pz(k)] = grad[:, 2 * C:]
    projection_grad(3)
    projection_grad(1)
    fold_x = Scatter(parts, r.low2, mid, r.high2)

    def unproject(j):
        parts[j] = mm(dproj[block_of(chip_of(j), T2), :], w_qkv[...], NT).astype(bf16)
        fold_x.pair(j)
    fold_qk.start()
    unproject(3)
    unproject(1)
    fold_x.onward(3)
    folds_up[1].middle()
    fold_v.start()
    unproject(2)
    fold_x.onward(1)
    unproject(0)
    fold_x.onward(2)
    gather_c.wait()
    share_da.wait()
    for k in (3, 1):
        out_grad(k)
    fold_o.start()
    for k in (2, 0):
        out_grad(k)
    projection_grad(2)
    projection_grad(0)
    fold_x.cross()
    gather_gd.pass_near()
    col_z, col_own = r.col_z, r.col_own
    col_own[...] = jnp.zeros((8, C), f32)
    for i in range(Z):
        col_own[i:i + 1, :] = colg[0:1, i * C:(i + 1) * C]
    for i in range(3):
        col_own[Z + i:Z + i + 1, :] = colg[1:2, i * C:(i + 1) * C]
    share_col = Share(3, col_own)
    share_col.column(col_own, col_z.at[z])
    col_z[z] = col_own[...]
    share_vec.wait()
    vec_sum = r.vec_sum
    vec_sum[...] = vec_z[0] + vec_z[1] + vec_z[2] + vec_z[3]
    share_sum = Share(7, vec_sum)
    share_sum.plane(lambda o: vec_sum, vec_all.at[s])
    vec_all[s] = vec_sum[...]
    for i in range(2):
        gu_all[s, pl.ds(i * (KW // 2), KW // 2), :] = folds_up[i].finish()
    gather_gu.start()
    fold_qk.middle()

    fold_v.middle()
    fold_o.middle()
    gather_gd.pass_far()
    fold_x.ready()
    dx_ref = r.dx

    def input_back(i):
        start = at(i, R)
        rows = pl.ds(start, R)
        dx_ref[rows, :] = (dh1[rows, :] + fold_x.rows(start, R)).astype(bf16)
    loop(T // R, input_back, 2)
    gather_gd.wait()
    gather_gu.pass_near()

    gqk_all[s] = fold_qk.finish()
    gather_gqk.start()

    gv_all[s] = fold_v.finish()
    gather_gv.start()
    gather_gu.pass_far()
    go_all[:, block_of(s, C)] = fold_o.finish()
    gather_go.start()
    share_col.wait()
    col_all, col_sum = r.col_all, r.col_sum
    col_sum[...] = col_z[0] + col_z[1] + col_z[2] + col_z[3]
    share_cols = Share(7, col_sum)
    share_cols.plane(lambda o: col_sum, col_all.at[s])
    col_all[s] = col_sum[...]
    gather_gqk.pass_near()
    gather_gv.pass_near()
    gather_gu.wait()

    gather_go.pass_near()
    gather_gqk.pass_far()
    gather_gv.pass_far()
    share_sum.wait()
    share_cols.wait()
    total = vec_all[0]
    for o in range(1, S):
        total = total + vec_all[o]
    gsm = r.gsm
    gsm[...] = jnp.zeros(gsm.shape, f32)
    for start, i in wide:
        for half in range(KW // C):
            gsm[start + half:start + half + 1, :] = total[i:i + 1, half * C:(half + 1) * C]
    for o in range(S):
        at_row = first_row.up_bias + o
        gsm[at_row:at_row + 1, :] = col_all[o, pl.ds(z, 1), :]
    for i in range(per):
        number = z * per + i
        at_row = first_row.projection_bias + i
        gsm[at_row:at_row + 1, :] = col_all[number % S, pl.ds(Z + number // S, 1), :]
    gather_go.pass_far()
    gather_go.wait()
    gather_gqk.wait()
    gather_gv.wait()
    for batch in closing:
        batch.close()
    assert counter[0] <= LANDINGS and counter[1] <= BATCHES and counter[2] <= LOCAL, counter


def fused_shards(*args):
    (hidden_in, cotangent, segment_ids, projection, projection_bias, output_weight, output_bias, first_gain,
     first_shift, up_weight, up_bias, down_weight, down_bias, second_gain, second_shift) = args
    T, D = hidden_in.shape[1:]
    L = segment_ids.shape[1]
    KW = projection.shape[0]
    F = up_weight.shape[1] // 8
    C, Z = 128, 4
    UZ = F // Z
    small = dict(projection_bias=projection_bias, output_bias=output_bias, first_gain=first_gain,
                 first_shift=first_shift, up_bias=up_bias, down_bias=down_bias, second_gain=second_gain,
                 second_shift=second_shift)
    starts, at_row = {}, 0
    for name, value in small.items():
        starts[name] = at_row
        at_row += value.shape[0] // C
    rows = -(-at_row // 8) * 8
    half = HEAD_DIM // 2
    inverse = np.float32(10000.0) ** (np.float32(-2.0) * np.arange(half, dtype=np.float32) / np.float32(HEAD_DIM))
    angles = np.arange(L, dtype=np.float32)[:, None] * inverse.astype(np.float32)[None, :]
    cosine = np.tile(np.cos(angles), (1, C // half))
    sine = np.tile(np.concatenate([-np.sin(angles), np.sin(angles)], axis=1), (1, C // HEAD_DIM))

    inputs = dict(x=hidden_in[0], ct=cotangent[0], seg=segment_ids, cos=jnp.asarray(cosine), sin=jnp.asarray(sine),
                  b_projection=projection_bias.reshape(-1, C), b_output=output_bias[None], gain1=first_gain[None],
                  shift1=first_shift[None], b_up=up_bias[None], b_down=down_bias[None], gain2=second_gain[None],
                  shift2=second_shift[None], proj=projection, wo=output_weight, up=up_weight, dn=down_weight)
    outputs = dict(out=((T, D), bf16), dx=((T, D), bf16), gsm=((rows, C), f32), gqk=((8, KW, 2 * C), bf16), gv=((8, KW, C), bf16),
                   go=((KW, D), bf16), gu=((8, KW, F), bf16), gd=((8 * UZ, D), bf16))
    landed = dict(v_x=inputs["x"], v_ct=inputs["ct"], v_seg=segment_ids, v_cos=inputs["cos"], v_sin=inputs["sin"],
                  v_projection=inputs["b_projection"], v_output=inputs["b_output"], v_gain1=inputs["gain1"],
                  v_shift1=inputs["shift1"], v_up=inputs["b_up"], v_down=inputs["b_down"], v_gain2=inputs["gain2"],
                  v_shift2=inputs["shift2"])
    PART = (4, T, D)
    scratch = {name: (value.shape, value.dtype) for name, value in landed.items()}
    scratch.update(
        x_all=((L, D), bf16), x_t=((D, L), bf16), w_qkv=((D, 3 * C), bf16), st_proj=((KW, 3 * C), f32),
        w_o=((D, D), bf16), st_wo=((KW, C), f32), w_up=((D, F), bf16), st_up=((KW, F), f32),
        w_dn=((F, D), bf16), st_dn=((UZ, D), f32), small_all=((Z, rows, C), f32), vec=((8, D), f32),
        vecg=((8, D), f32), q=((L, C), bf16), k=((L, C), bf16), v=((L, C), bf16),
        seg_r=((8, L), f32), seg_c=((L, C), f32), small=((rows, C), f32), lse=((8, L), f32),
        delta=((8, L), f32), c_f=((L, C), f32), c_heads=((L, C), bf16), c_tok=((T, D), bf16),
        a_buf=((T, D), f32), n1=((T, D), f32), y1=((T, D), f32), r1=((T, C), f32),
        y_all=((L, D), bf16), y_t=((D, L), bf16), u_buf=((2 * T, F), f32), g=((L, F), bf16),
        g_t=((F, L), bf16), d=((L, F), f32), du=((L, F), bf16), dz_all=((L, D), bf16),
        parts=((4, 2 * T, D), bf16), mid=((4, T, D), bf16), dh2=((T, D), f32), dh1=((T, D), f32),
        colg=((8, F), f32), gd_part=((Z, UZ, D), bf16), gd_land=((3, UZ, D), bf16), gd_pass=((UZ, D), bf16),
        gu_part=((Z, KW, F), bf16), gu_land=((3, KW, F), bf16), gu_pass=((KW, F), bf16),
        go_part=((Z, KW, C), bf16), go_land=((4, KW, C), bf16), go_pass=((KW, C), bf16),
        gqk_part=((Z, KW, 2 * C), bf16), gqk_land=((3, KW, 2 * C), bf16), gqk_pass=((KW, 2 * C), bf16),
        gv_part=((Z, KW, C), bf16), gv_land=((4, KW, C), bf16), gv_pass=((KW, C), bf16),
        da=((T, D), bf16), dc_tok=((T, D), bf16), dc=((L, C), bf16),
        da_cols=((L, C), bf16), c_all=((L, D), bf16), dq=((L, C), f32), dproj=((L, 3 * C), bf16),
        vec_all=((8, 8, KW), f32), vec_z=((Z, 8, KW), f32), vec_sum=((8, KW), f32), col_own=((8, C), f32),
        col_z=((Z, 8, C), f32), col_sum=((8, C), f32), col_all=((8, 8, C), f32),
        low0=(PART, bf16), high0=(PART, bf16), low1=(PART, bf16), high1=(PART, bf16), low2=(PART, bf16),
        high2=(PART, bf16), ssem=(BATCHES,), rsem=(LANDINGS,), lsem=(LOCAL,))
    names = [*inputs, *outputs, *scratch]
    sizes = SimpleNamespace(names=names, T=T, D=D, L=L, F=F, first_row=SimpleNamespace(**starts))

    anywhere, near = pl.BlockSpec(memory_space=pl.ANY), pl.BlockSpec(memory_space=pltpu.VMEM)
    results = pl.pallas_call(
        partial(fused_layer, sizes),
        out_shape=[pltpu.VMEM(*what) for what in outputs.values()],
        in_specs=[anywhere] * len(inputs),
        out_specs=[near] * len(outputs),
        scratch_shapes=[pltpu.VMEM(*what) if len(what) == 2 else pltpu.SemaphoreType.DMA(what)
                        for what in scratch.values()],
        compiler_params=pltpu.CompilerParams(collective_id=0, has_side_effects=True, vmem_limit_bytes=57 << 20),
        name="fused_layer",
    )(*inputs.values())
    out, dx, gsm, gqk, gv, go, gu, gd = results
    wide = [jax.ShapeDtypeStruct(value.shape, f32) for value in (projection, output_weight, up_weight, down_weight)]
    narrow = [jax.ShapeDtypeStruct((1, value.shape[0]) if value is not projection_bias else (value.shape[0] // C, C), f32)
              for value in small.values()]
    sources = [out, dx, gqk, gv, go, gu, gd, gsm]
    outcomes = [out, dx] + wide + narrow
    results = pl.pallas_call(
        partial(widen, tuple(starts.values())),
        out_shape=[jax.ShapeDtypeStruct(value.shape, value.dtype) for value in outcomes],
        in_specs=[near] * len(sources),
        out_specs=[anywhere] * len(outcomes),
        scratch_shapes=[pltpu.VMEM(value.shape, value.dtype) for value in outcomes[2:]]
        + [pltpu.SemaphoreType.DMA((LOCAL,))],
        compiler_params=pltpu.CompilerParams(vmem_limit_bytes=20 << 20),
        name="widen",
    )(*sources)
    out, dx, gq, go, gu, gd = results[:6]
    pb, ob, g1, s1, ub, db, g2, s2 = [value.reshape(-1) for value in results[6:]]
    return (out[None], dx[None], gq, pb, go, ob, g1, s1, gu, ub, gd, db, g2, s2)


def widen(starts, *refs):
    held, results, made, outsem = refs[:8], refs[8:22], refs[22:34], refs[34]
    out, dx, gqk, gv, go, gu, gd, gsm = held
    C = gsm.shape[1]
    stores = []

    def store(ref, result):
        copy = pltpu.make_async_copy(ref, result, outsem.at[len(stores)])
        copy.start()
        stores.append(copy)

    def grouped(i, target, at, n, first):
        source, result = held[i], made[target]
        groups = source.shape[0]

        def step(j, carry):
            rows = pl.ds(pl.multiple_of(at + j * 32, 32), 32)
            for o in range(groups):
                for p in range(source.shape[2] // C):
                    lane = ((first + p) * groups + o) * C
                    result[rows, lane:lane + C] = source[o, rows, p * C:(p + 1) * C].astype(f32)
            return carry
        lax.fori_loop(0, n // 32, step, 0)

    def plain(i, target, at, n, _):
        source, result = held[i], made[target]

        def step(j, carry):
            rows = pl.ds(pl.multiple_of(at + j * 32, 32), 32)
            result[rows, :] = source[rows, :].astype(f32)
            return carry
        lax.fori_loop(0, n // 32, step, 0)

    store(out, results[0])
    store(dx, results[1])
    work = []
    for i, target, n, body, first in ((5, 2, 64, grouped, 0), (6, 3, 256, plain, 0), (2, 0, 64, grouped, 0),
                                      (3, 0, 64, grouped, 2), (4, 1, 256, plain, 0)):
        total = held[i].shape[-2]
        for at in range(0, total, n):
            work.append((i, target, at, n, body, first))
    for i, target, at, n, body, first in work:
        body(i, target, at, n, first)
        if i != 2:
            rows = pl.ds(at, n)
            store(made[target].at[rows], results[2 + target].at[rows])
    for start, ref, result in zip(starts, made[4:], results[6:]):
        if ref.shape[1] == C:
            ref[...] = gsm[start:start + ref.shape[0], :]
        else:
            for i in range(ref.shape[1] // C):
                ref[0:1, i * C:(i + 1) * C] = gsm[start + i:start + i + 1, :]
        store(ref, result)
    for copy in stores:
        copy.wait()


BATCHES = 34
LANDINGS = 157
LOCAL = 26


def fits(mesh):
    return mesh.shape["seq"] == 8 and mesh.shape["fsdp"] == 4


def solution(mesh):
    return jax.shard_map(
        fused_shards if fits(mesh) else shards,
        mesh=mesh,
        in_specs=(
            P("fsdp", "seq", None),
            P("fsdp", "seq", None),
            P("fsdp", None),
            P("fsdp", None),
            P("fsdp"),
            P("fsdp", None),
            P("fsdp"),
            P("fsdp"),
            P("fsdp"),
            P("fsdp", None),
            P("fsdp"),
            P("fsdp", None),
            P("fsdp"),
            P("fsdp"),
            P("fsdp"),
        ),
        out_specs=(
            P("fsdp", "seq", None),
            P("fsdp", "seq", None),
            P("fsdp", None),
            P("fsdp"),
            P("fsdp", None),
            P("fsdp"),
            P("fsdp"),
            P("fsdp"),
            P("fsdp", None),
            P("fsdp"),
            P("fsdp", None),
            P("fsdp"),
            P("fsdp"),
            P("fsdp"),
        ),
        check_vma=False,
    )
```
